32 devices in a mesh: section: 2 (over y), dp: 4 (over x, core), tensor: 4 (over z).
Axes of the slice: x: 2, y: 2, z: 4, core: 2. Of those that a mesh axis runs over, the one named last changes fastest.
Arguments:
- acts_in: bfloat16 [4, 1024, 4, 1024], P(None, 'tensor', 'dp'), may hold values from -6 to 6
- cotangent: bfloat16 [4, 1024, 4, 1024], P(None, 'tensor', 'dp'), may hold values from -6 to 6
- norm_gains: float32 [2, 2, 1024], P('section', None, ('dp', 'tensor')), may hold values from 0.5 to 1.5
- vec_bias: float32 [2, 4, 1024], P('section', None, ('dp', 'tensor')), may hold values from -1.8 to 1.8
- w_qkv: bfloat16 [2, 1024, 3072], P('section', 'dp', 'tensor'), may hold values from -0.25 to 0.25
- b_qkv: bfloat16 [2, 16, 192], P('section', 'tensor', 'dp'), may hold values from -1.796875 to 1.796875
- w_out: bfloat16 [2, 1024, 1024], P('section', 'tensor', 'dp'), may hold values from -0.75 to 0.75
- w_up: bfloat16 [2, 1024, 4096], P('section', 'dp', 'tensor'), may hold values from -0.1875 to 0.1875
- b_up: bfloat16 [2, 32, 128], P('section', 'tensor', 'dp'), may hold values from -1.796875 to 1.796875
- w_down: bfloat16 [2, 4096, 1024], P('section', 'tensor', 'dp'), may hold values from -0.09375 to 0.09375
Outputs:
- acts_out: bfloat16 [2, 4, 1024, 4, 1024], P('section', None, 'tensor', 'dp')
- grad_in: bfloat16 [2, 4, 1024, 4, 1024], P('section', None, 'tensor', 'dp')
- grad_norm_gains: float32 [2, 2, 1024], P('section', None, ('dp', 'tensor'))
- grad_vec_bias: float32 [2, 4, 1024], P('section', None, ('dp', 'tensor'))
- grad_w_qkv: float32 [2, 1024, 3072], P('section', 'dp', 'tensor')
- grad_b_qkv: float32 [2, 16, 192], P('section', 'tensor', 'dp')
- grad_w_out: float32 [2, 1024, 1024], P('section', 'tensor', 'dp')
- grad_w_up: float32 [2, 1024, 4096], P('section', 'dp', 'tensor')
- grad_b_up: float32 [2, 32, 128], P('section', 'tensor', 'dp')
- grad_w_down: float32 [2, 4096, 1024], P('section', 'tensor', 'dp')
The draws below stay inside these ranges and needn't reach their ends.
All inputs are finite; a program needn't handle non-finite values.
Results may differ from the reference program's by a relative error of at most 0.025.
Values may be sent and summed in bfloat16 or wider, within the bound.
No kernel may reach another device: no remote copies, remote signals or barrier semaphores. Data moves between devices by JAX's collectives and lax.ppermute only.
A program may use at most 384 MiB of HBM per device.

```python
import math
import jax
import jax.numpy as jnp
from jax import lax

D = 1024
HEADS = 16
DH = 64
ROT = 16
FF = 4096
BIAS_COLS = 128
SEQ_LEN = 1024
QBLOCK = 512
MICRO = 4
SECTIONS = 2
SEQS = 4


def steps_of(own_key, extent, cuts, low, largest):
    level = 1.0
    for axis_at, parts in cuts:
        draws = jax.random.uniform(jax.random.fold_in(jax.random.fold_in(own_key, 6), axis_at), (parts,), jnp.float32, low / len(cuts), largest / len(cuts))
        level = level * jnp.repeat(jnp.exp(draws), extent[axis_at] // parts).reshape((-1,) + (1,) * (len(extent) - 1 - axis_at))
    return level


def noise(rng, extent, scale, bound, cuts=(), kind=jnp.bfloat16):
    factor_of = steps_of(rng, extent, cuts, -0.22, 0.18) if cuts else 1.0
    drawn = jax.random.normal(rng, extent, jnp.float32) * scale * factor_of
    return jnp.minimum(jnp.maximum(drawn, -bound), bound).astype(kind)


def setup_inputs(seed: int = 0) -> dict:
    key_list = jax.random.split(jax.random.key(seed), 11)
    acts_in = noise(key_list[0], (MICRO, SEQ_LEN, SEQS, D), 1.0, 6.0, ((1, 4), (2, 4)))
    cotangent = noise(key_list[1], (MICRO, SEQ_LEN, SEQS, D), 1.0, 6.0, ((1, 4), (2, 4)))
    norm_gains = jnp.clip(1.0 + 0.1 * jax.random.normal(key_list[2], (SECTIONS, 2, D), jnp.float32), 0.5, 1.5)
    vec_bias = noise(key_list[3], (SECTIONS, 4, D), 0.3, 1.8, ((0, 2), (2, 16)), jnp.float32)
    w_qkv = noise(key_list[4], (SECTIONS, D, 3 * D), (D // 2) ** -0.5, 0.25, ((0, 2), (1, 4), (2, 4)))
    b_qkv = noise(key_list[5], (SECTIONS, HEADS, 3 * DH), 0.3, 1.796875, ((0, 2), (1, 4), (2, 4)))
    w_out = noise(key_list[6], (SECTIONS, D, D), (D // 16) ** -0.5, 0.75, ((0, 2), (1, 4), (2, 4)))
    w_up = noise(key_list[7], (SECTIONS, D, FF), D ** -0.5, 0.1875, ((0, 2), (1, 4), (2, 4)))
    b_up = noise(key_list[8], (SECTIONS, FF // BIAS_COLS, BIAS_COLS), 0.3, 1.796875, ((0, 2), (1, 4), (2, 4)))
    w_down = noise(key_list[9], (SECTIONS, FF, D), FF ** -0.5, 0.09375, ((0, 2), (1, 4), (2, 4)))
    return dict(acts_in=acts_in, cotangent=cotangent, norm_gains=norm_gains, vec_bias=vec_bias, w_qkv=w_qkv, b_qkv=b_qkv, w_out=w_out, w_up=w_up, b_up=b_up, w_down=w_down)


HIGHEST = lax.Precision.HIGHEST
NORM_EPS = 1e-05
ROPE_BASE = 10000.0
MASK_FILL = -1e+30

@jax.custom_vjp
def low(v):
    return lax.optimization_barrier(v.astype(jnp.bfloat16)).astype(jnp.float32)

@jax.custom_vjp
def low_back(v):
    return v

def low_keep(v):
    return (low(v), None)

def low_pass(kept, grad):
    return (grad,)

def back_keep(v):
    return (v, None)

def back_low(kept, grad):
    return (low(grad),)
low.defvjp(low_keep, low_pass)
low_back.defvjp(back_keep, back_low)

def layer_norm(values, norm_gain, norm_shift):
    average = lax.optimization_barrier(jnp.mean(values, axis=-1, keepdims=True))
    centred = values - average
    variance = lax.optimization_barrier(jnp.mean(centred * centred, axis=-1, keepdims=True))
    return centred * lax.rsqrt(variance + NORM_EPS) * norm_gain + norm_shift

def rotary_tables(length):
    half_rot = ROT // 2
    frequency = jnp.exp(jnp.arange(half_rot, dtype=jnp.float32) * (-2.0 * math.log(ROPE_BASE) / ROT))
    angles = jnp.arange(length, dtype=jnp.float32)[:, None] * frequency[None, :]
    return (jnp.cos(angles), jnp.sin(angles))

def rotate(values, cosine, sine_tab):
    half_rot = ROT // 2
    low_half = values[..., :half_rot]
    high_half = values[..., half_rot:ROT]
    return jnp.concatenate([low_half * cosine - high_half * sine_tab, high_half * cosine + low_half * sine_tab, values[..., ROT:]], axis=-1)

def matmul(left, right):
    return jnp.einsum('...d,de->...e', left, right, precision=HIGHEST)

def attention(queries, key_rows, val_rows):
    batch, length, head_count, head_dim = queries.shape
    block_rows = min(QBLOCK, length)
    block_count = length // block_rows
    score_scale = head_dim ** (-0.5)
    query_blocks = queries.reshape(batch, block_count, block_rows, head_count, head_dim).transpose(1, 0, 2, 3, 4)
    block_starts = jnp.arange(block_count, dtype=jnp.int32) * block_rows
    key_pos = jnp.arange(length, dtype=jnp.int32)

    @jax.checkpoint
    def one_block(pieces):
        query_block, first_row = pieces
        scores = low_back(score_scale * jnp.einsum('bqhd,bkhd->bhqk', query_block, key_rows, precision=HIGHEST))
        row_pos = first_row + jnp.arange(block_rows, dtype=jnp.int32)
        allowed = key_pos[None, :] <= row_pos[:, None]
        scores = jnp.where(allowed, scores, MASK_FILL)
        probability = low(jax.nn.softmax(scores, axis=-1))
        return jnp.einsum('bhqk,bkhd->bqhd', probability, val_rows, precision=HIGHEST)
    blocks_out = lax.map(one_block, (query_blocks, block_starts))
    return blocks_out.transpose(1, 0, 2, 3, 4).reshape(batch, length, head_count * head_dim)

def layer_forward(values, params):
    norm_gain, vector_bias, mat_qkv, bias_qkv, mat_out, mat_up, bias_up, mat_down = params
    batch, length, model_width = values.shape
    head_count = bias_qkv.shape[0]
    head_dim = bias_qkv.shape[1] // 3
    normed_attn = low(layer_norm(values, norm_gain[0], vector_bias[0]))
    normed_mlp = low(layer_norm(values, norm_gain[1], vector_bias[1]))
    projected = low_back(matmul(normed_attn, mat_qkv) + bias_qkv.reshape(-1))
    projected = projected.reshape(batch, length, head_count, 3, head_dim)
    cosine, sine_tab = rotary_tables(length)
    cosine = cosine[None, :, None, :]
    sine_tab = sine_tab[None, :, None, :]
    queries = low(rotate(projected[:, :, :, 0], cosine, sine_tab))
    key_rows = low(rotate(projected[:, :, :, 1], cosine, sine_tab))
    val_rows = low(projected[:, :, :, 2])
    context = low_back(low(attention(queries, key_rows, val_rows)))
    up_proj = low_back(matmul(normed_mlp, mat_up) + bias_up.reshape(-1))
    activated = low(jax.nn.gelu(up_proj, approximate=False))
    return values + matmul(context, mat_out) + vector_bias[2] + matmul(activated, mat_down) + vector_bias[3]

def reference(acts_in, cotangent, norm_gains, vec_bias, w_qkv, b_qkv, w_out, w_up, b_up, w_down):
    params = tuple((item.astype(jnp.float32) for item in (norm_gains, vec_bias, w_qkv, b_qkv, w_out, w_up, b_up, w_down)))
    first_params = tuple((item[0] for item in params))
    second_params = tuple((item[1] for item in params))
    seq_total = MICRO * SEQS
    inputs = acts_in.transpose(0, 2, 1, 3).reshape(seq_total, SEQ_LEN, D)
    cot_rows = cotangent.transpose(0, 2, 1, 3).reshape(seq_total, SEQ_LEN, D)

    def two_layers(first_in, offset, params_one, params_two):
        first_out = layer_forward(first_in, params_one)
        handoff = low_back(low(first_out))
        return (handoff, layer_forward(handoff + offset, params_two))

    def one_sequence(running, sequence):
        seq_in, seq_cot = sequence
        seq_in = seq_in.astype(jnp.float32)[None]
        seq_cot = seq_cot.astype(jnp.float32)[None]
        offset = jnp.zeros_like(seq_in)
        (handoff, second_out), pullback = jax.vjp(two_layers, seq_in, offset, first_params, second_params)
        grad_first, grad_offset, grads_one, grads_two = pullback((jnp.zeros_like(handoff), seq_cot))
        running = jax.tree.map(lambda c, a, b: c + jnp.stack([a, b]), running, grads_one, grads_two)
        return (running, (handoff[0].astype(jnp.bfloat16), second_out[0].astype(jnp.bfloat16), grad_first[0].astype(jnp.bfloat16), grad_offset[0].astype(jnp.bfloat16)))
    zeros_init = tuple((jnp.zeros_like(item) for item in params))
    gradients, (handoffs, seconds, grads_first, grads_offset) = lax.scan(one_sequence, zeros_init, (inputs, cot_rows))

    def arrange(stacked):
        return stacked.reshape(MICRO, SEQS, SEQ_LEN, D).transpose(0, 2, 1, 3)
    acts_out = jnp.stack([arrange(handoffs), arrange(seconds)])
    grad_in = jnp.stack([arrange(grads_first), arrange(grads_offset)])
    return (acts_out, grad_in, gradients[0], gradients[1], gradients[2], gradients[3], gradients[4], gradients[5], gradients[6], gradients[7])
```

```python
from functools import partial
import math

import jax
import jax.numpy as jnp
from jax import lax
from jax.experimental import pallas as pl
from jax.experimental.pallas import tpu as pltpu
from jax.sharding import PartitionSpec as P

ROT = 16
QBLOCK = 512
MICRO = 4


NORM_EPS = 1e-05
ROPE_BASE = 10000.0
MASK_FILL = -1e30


def from_behind(value, axis, by):
    length = lax.axis_size(axis)
    pairs = [(i, i + by) for i in range(length) if 0 <= i + by < length]
    return lax.ppermute(value, axis, pairs)


def layer_norm(values, norm_gain, norm_shift):
    average = jnp.mean(values, axis=-1, keepdims=True)
    centred = values - average
    variance = jnp.mean(centred * centred, axis=-1, keepdims=True)
    return centred * lax.rsqrt(variance + NORM_EPS) * norm_gain + norm_shift


def both_norms(values, gain_attn, shift_attn, gain_mlp, shift_mlp):
    return (layer_norm(values, gain_attn, shift_attn), layer_norm(values, gain_mlp, shift_mlp))


def rotary_tables(length):
    half_rot = ROT // 2
    frequency = jnp.exp(
        jnp.arange(half_rot, dtype=jnp.float32) * (-2.0 * math.log(ROPE_BASE) / ROT)
    )
    angles = jnp.arange(length, dtype=jnp.float32)[:, None] * frequency[None, :]
    return (jnp.cos(angles), jnp.sin(angles))


def rotate(values, cosine, sine_tab):
    half_rot = ROT // 2
    low_half = values[..., :half_rot]
    high_half = values[..., half_rot:ROT]
    return jnp.concatenate(
        [
            low_half * cosine - high_half * sine_tab,
            high_half * cosine + low_half * sine_tab,
            values[..., ROT:],
        ],
        axis=-1,
    )


def rotate_back(grads_rot, cosine, sine_tab):
    half_rot = ROT // 2
    low_half = grads_rot[..., :half_rot]
    high_half = grads_rot[..., half_rot:ROT]
    return jnp.concatenate(
        [
            low_half * cosine + high_half * sine_tab,
            high_half * cosine - low_half * sine_tab,
            grads_rot[..., ROT:],
        ],
        axis=-1,
    )


def causal_scores(queries, key_rows, first_row, score_scale):
    block_rows = queries.shape[0]
    last_row = key_rows.shape[0]
    scores = (
        jnp.einsum("qshd,kshd->shqk", queries, key_rows, preferred_element_type=jnp.float32)
        * score_scale
    )
    row_pos = first_row + jnp.arange(block_rows, dtype=jnp.int32)
    col_pos = jnp.arange(last_row, dtype=jnp.int32)
    allowed = col_pos[None, :] <= row_pos[:, None]
    return (scores, allowed)


def attend(queries, key_rows, val_rows):
    length = queries.shape[0]
    block_rows = min(QBLOCK, length)
    score_scale = queries.shape[-1] ** (-0.5)
    outputs = []
    totals = []
    for block_index in range(length // block_rows):
        first_row = block_index * block_rows
        last_row = first_row + block_rows
        scores, allowed = causal_scores(
            queries[first_row:last_row], key_rows[:last_row], first_row, score_scale
        )
        scores = jnp.where(allowed, scores, MASK_FILL)
        highest = jnp.max(scores, axis=-1, keepdims=True)
        exponent = jnp.exp(scores - highest)
        denominator = jnp.sum(exponent, axis=-1, keepdims=True)
        probability = (exponent / denominator).astype(jnp.bfloat16)
        block_out = jnp.einsum(
            "shqk,kshd->qshd", probability, val_rows[:last_row], preferred_element_type=jnp.float32
        )
        outputs.append(block_out.astype(jnp.bfloat16))
        totals.append((highest + jnp.log(denominator))[..., 0])
    context = jnp.concatenate(outputs, axis=0)
    return (context.reshape(length, context.shape[1], -1), jnp.concatenate(totals, axis=-1))


def attend_back(queries, key_rows, val_rows, d_context, log_total):
    length = queries.shape[0]
    block_rows = min(QBLOCK, length)
    score_scale = queries.shape[-1] ** (-0.5)
    grad_query_list = []
    grad_keys = jnp.zeros(queries.shape, jnp.float32)
    grad_vals = jnp.zeros(queries.shape, jnp.float32)
    for block_index in range(length // block_rows):
        first_row = block_index * block_rows
        last_row = first_row + block_rows
        query_block = queries[first_row:last_row]
        scores, allowed = causal_scores(query_block, key_rows[:last_row], first_row, score_scale)
        probability = jnp.where(
            allowed, jnp.exp(scores - log_total[:, :, first_row:last_row, None]), 0.0
        )
        d_block = d_context[first_row:last_row]
        d_prob = jnp.einsum(
            "qshd,kshd->shqk", d_block, val_rows[:last_row], preferred_element_type=jnp.float32
        )
        delta = jnp.sum(probability * d_prob, axis=-1, keepdims=True)
        d_scores = (probability * (d_prob - delta)).astype(jnp.bfloat16)
        grad_query_list.append(
            jnp.einsum(
                "shqk,kshd->qshd", d_scores, key_rows[:last_row], preferred_element_type=jnp.float32
            )
            * score_scale
        )
        grad_keys = grad_keys.at[:last_row].add(
            jnp.einsum("shqk,qshd->kshd", d_scores, query_block, preferred_element_type=jnp.float32)
            * score_scale
        )
        grad_vals = grad_vals.at[:last_row].add(
            jnp.einsum(
                "shqk,qshd->kshd",
                probability.astype(jnp.bfloat16),
                d_block,
                preferred_element_type=jnp.float32,
            )
        )
    return (jnp.concatenate(grad_query_list, axis=0), grad_keys, grad_vals)


def local(acts_in, cotangent, norm_gains, vec_bias, w_qkv, b_qkv, w_out, w_up, b_up, w_down):
    section_index = lax.axis_index("section")
    own_start = lax.axis_index("tensor") * acts_in.shape[1]
    local_len = acts_in.shape[1]
    seq_count = acts_in.shape[2]
    model_width = acts_in.shape[3]
    length = local_len * lax.axis_size("tensor")
    all_rows = length * seq_count
    gain_full, bias_full = (
        lax.all_gather(norm_gains[0], ("dp", "tensor"), axis=1, tiled=True),
        lax.all_gather(vec_bias[0], ("dp", "tensor"), axis=1, tiled=True),
    )
    mat_qkv, bias_qkv, mat_out, mat_up, bias_up, mat_down = (
        lax.all_gather(w_qkv[0], "dp", axis=0, tiled=True),
        lax.all_gather(b_qkv[0], "dp", axis=1, tiled=True),
        lax.all_gather(w_out[0], "dp", axis=1, tiled=True),
        lax.all_gather(w_up[0], "dp", axis=0, tiled=True),
        lax.all_gather(b_up[0], "dp", axis=1, tiled=True),
        lax.all_gather(w_down[0], "dp", axis=1, tiled=True),
    )
    head_count = bias_qkv.shape[0]
    head_dim = bias_qkv.shape[1] // 3
    qkv_shift = bias_qkv.reshape(-1).astype(jnp.float32)
    up_shift = bias_up.reshape(-1).astype(jnp.float32)
    cosine, sine_tab = rotary_tables(length)
    cosine = cosine[:, None, None, :]
    sine_tab = sine_tab[:, None, None, :]
    received = jnp.zeros_like(acts_in[0])
    stash_list = []
    out_list = []
    for moment in range(MICRO + 1):
        own_rows = acts_in[min(moment, MICRO - 1)]
        inputs = jnp.where(section_index == 0, own_rows, received)
        forward_gathered = lax.all_gather(inputs, "tensor", axis=0, tiled=True)
        full_attn, full_mlp = both_norms(
            forward_gathered.astype(jnp.float32),
            gain_full[0],
            bias_full[0],
            gain_full[1],
            bias_full[1],
        )
        forward_normed_attn = full_attn.astype(jnp.bfloat16)
        forward_normed_mlp = full_mlp.astype(jnp.bfloat16)
        forward_flat_attn = forward_normed_attn.reshape(all_rows, model_width)
        forward_flat_mlp = forward_normed_mlp.reshape(all_rows, model_width)
        projected = (
            jnp.dot(forward_flat_attn, mat_qkv, preferred_element_type=jnp.float32) + qkv_shift
        )
        projected = projected.reshape(length, seq_count, head_count, 3, head_dim)
        forward_queries = rotate(projected[:, :, :, 0], cosine, sine_tab).astype(jnp.bfloat16)
        forward_key_rows = rotate(projected[:, :, :, 1], cosine, sine_tab).astype(jnp.bfloat16)
        forward_val_rows = projected[:, :, :, 2].astype(jnp.bfloat16)
        forward_context, forward_log_total = attend(
            forward_queries, forward_key_rows, forward_val_rows
        )
        forward_up_proj = (
            jnp.dot(forward_flat_mlp, mat_up, preferred_element_type=jnp.float32) + up_shift
        )
        forward_activated = jax.nn.gelu(forward_up_proj, approximate=False).astype(jnp.bfloat16)
        active_rows = forward_activated.reshape(length, seq_count, -1)
        context_part = forward_context.reshape(lax.axis_size("tensor") * local_len * seq_count, -1)
        active_part = active_rows.reshape(lax.axis_size("tensor") * local_len * seq_count, -1)
        summed = jnp.dot(context_part, mat_out, preferred_element_type=jnp.float32) + jnp.dot(
            active_part, mat_down, preferred_element_type=jnp.float32
        )
        mixed_sum = lax.psum_scatter(
            summed.reshape(lax.axis_size("tensor") * local_len, seq_count, model_width),
            "tensor",
            scatter_dimension=0,
            tiled=True,
        )
        result = inputs.astype(jnp.float32) + mixed_sum + bias_full[2] + bias_full[3]
        forward_stashed = (
            forward_gathered,
            forward_normed_attn,
            forward_normed_mlp,
            forward_queries,
            forward_key_rows,
            forward_val_rows,
            forward_context,
            forward_log_total,
            forward_up_proj,
            forward_activated,
        )
        result, stashed = (result.astype(jnp.bfloat16), forward_stashed)
        stash_list.append(stashed)
        out_list.append(result)
        if moment < MICRO:
            received = from_behind(result, "section", 1)
    stash_all = jax.tree.map(lambda *parts: jnp.stack(parts), *stash_list)
    acts_local = lax.dynamic_slice_in_dim(jnp.stack(out_list), section_index, MICRO, 0)
    back_received = jnp.zeros_like(cotangent[0])
    grad_list = []
    weight_sums = None
    vector_sums = None
    for moment in range(MICRO + 1):
        micro_index = moment - 1 + section_index
        is_valid = (micro_index >= 0) & (micro_index < MICRO)
        source_clock = jnp.clip(micro_index + section_index, 0, MICRO)
        stashed = jax.tree.map(
            lambda part: lax.dynamic_index_in_dim(part, source_clock, 0, keepdims=False), stash_all
        )
        upstream = jnp.where(section_index == 1, cotangent[min(moment, MICRO - 1)], back_received)
        (
            gathered,
            normed_attn,
            normed_mlp,
            queries,
            key_rows,
            val_rows,
            context,
            log_total,
            up_proj,
            activated,
        ) = stashed
        backward_inputs = lax.dynamic_slice_in_dim(gathered, own_start, local_len, 0)
        upstream_rows = lax.all_gather(upstream, "tensor", axis=0, tiled=True)
        flat_grad = upstream_rows.reshape(all_rows, model_width)
        d_context = jnp.dot(flat_grad, mat_out.T, preferred_element_type=jnp.float32).astype(
            jnp.bfloat16
        )
        d_context = d_context.reshape(length, seq_count, head_count, head_dim)
        d_active = jnp.dot(flat_grad, mat_down.T, preferred_element_type=jnp.float32)
        _, gelu_pullback = jax.vjp(partial(jax.nn.gelu, approximate=False), up_proj)
        d_up = gelu_pullback(d_active)[0].astype(jnp.bfloat16)
        grad_query, grad_key, grad_val = attend_back(
            queries, key_rows, val_rows, d_context, log_total
        )
        d_qkv = jnp.stack(
            [
                rotate_back(grad_query, cosine, sine_tab),
                rotate_back(grad_key, cosine, sine_tab),
                grad_val,
            ],
            axis=3,
        ).astype(jnp.bfloat16)
        d_qkv_flat = d_qkv.reshape(all_rows, -1)
        d_qkv_rows = d_qkv.reshape(length, seq_count, -1)
        d_up_rows = d_up.reshape(length, seq_count, -1)
        flat_attn = normed_attn.reshape(all_rows, model_width)
        flat_mlp = normed_mlp.reshape(all_rows, model_width)
        weight_terms = (
            jnp.einsum("tc,te->ce", flat_attn, d_qkv_flat, preferred_element_type=jnp.float32),
            jnp.sum(d_qkv_flat.astype(jnp.float32), axis=0).reshape(bias_qkv.shape),
            jnp.einsum(
                "tc,te->ce",
                context.reshape(all_rows, -1),
                flat_grad,
                preferred_element_type=jnp.float32,
            ),
            jnp.einsum("tc,te->ce", flat_mlp, d_up, preferred_element_type=jnp.float32),
            jnp.sum(d_up.astype(jnp.float32), axis=0).reshape(bias_up.shape),
            jnp.einsum("tc,te->ce", activated, flat_grad, preferred_element_type=jnp.float32),
        )
        attn_part = d_qkv_rows.reshape(lax.axis_size("tensor") * local_len * seq_count, -1)
        mlp_part = d_up_rows.reshape(lax.axis_size("tensor") * local_len * seq_count, -1)
        joined = jnp.concatenate(
            [
                jnp.dot(attn_part, mat_qkv.T, preferred_element_type=jnp.float32),
                jnp.dot(mlp_part, mat_up.T, preferred_element_type=jnp.float32),
            ],
            axis=-1,
        )
        d_normed = lax.psum_scatter(
            joined.reshape(lax.axis_size("tensor") * local_len, seq_count, 2 * model_width).astype(
                jnp.bfloat16
            ),
            "tensor",
            scatter_dimension=0,
            tiled=True,
        ).astype(jnp.float32)
        _, norm_pullback = jax.vjp(
            both_norms,
            backward_inputs.astype(jnp.float32),
            gain_full[0],
            bias_full[0],
            gain_full[1],
            bias_full[1],
        )
        d_local, d_gain_attn, d_shift_attn, d_gain_mlp, d_shift_mlp = norm_pullback(
            (d_normed[..., :model_width], d_normed[..., model_width:])
        )
        upstream_float = upstream.astype(jnp.float32)
        d_inputs = (upstream_float + d_local).astype(jnp.bfloat16)
        out_shift = jnp.sum(upstream_float, axis=(0, 1))
        vector_terms = (
            jnp.stack([d_gain_attn, d_gain_mlp]),
            jnp.stack([d_shift_attn, d_shift_mlp, out_shift, out_shift]),
        )
        d_inputs, weight_terms, vector_terms = (d_inputs, weight_terms, vector_terms)
        grad_list.append(d_inputs)
        if moment < MICRO:
            back_received = from_behind(d_inputs, "section", -1)
        weight_terms = tuple((jnp.where(is_valid, term, 0.0) for term in weight_terms))
        vector_terms = tuple((jnp.where(is_valid, term, 0.0) for term in vector_terms))
        if moment == 0:
            weight_sums = tuple(weight_terms)
            vector_sums = vector_terms
        else:
            weight_sums = tuple((a + b for a, b in zip(weight_sums, weight_terms)))
            vector_sums = tuple((a + b for a, b in zip(vector_sums, vector_terms)))
    sum_qkv, sum_bqkv, sum_out, sum_up, sum_bup, sum_down = weight_sums
    share_qkv, share_bqkv, share_out, share_up, share_bup, share_down = (
        lax.psum_scatter(
            sum_qkv.astype(jnp.bfloat16), "dp", scatter_dimension=0, tiled=True
        ).astype(jnp.float32),
        lax.psum_scatter(
            sum_bqkv.astype(jnp.bfloat16), "dp", scatter_dimension=1, tiled=True
        ).astype(jnp.float32),
        lax.psum_scatter(
            sum_out.astype(jnp.bfloat16), "dp", scatter_dimension=1, tiled=True
        ).astype(jnp.float32),
        lax.psum_scatter(sum_up.astype(jnp.bfloat16), "dp", scatter_dimension=0, tiled=True).astype(
            jnp.float32
        ),
        lax.psum_scatter(
            sum_bup.astype(jnp.bfloat16), "dp", scatter_dimension=1, tiled=True
        ).astype(jnp.float32),
        lax.psum_scatter(
            sum_down.astype(jnp.bfloat16), "dp", scatter_dimension=1, tiled=True
        ).astype(jnp.float32),
    )
    grad_local = lax.dynamic_slice_in_dim(jnp.stack(grad_list), 1 - section_index, MICRO, 0)
    gain_share, bias_share = (
        lax.psum_scatter(vector_sums[0], ("dp", "tensor"), scatter_dimension=1, tiled=True),
        lax.psum_scatter(vector_sums[1], ("dp", "tensor"), scatter_dimension=1, tiled=True),
    )
    return (
        acts_local[None],
        grad_local[None],
        gain_share[None],
        bias_share[None],
        share_qkv[None],
        share_bqkv[None],
        share_out[None],
        share_up[None],
        share_bup[None],
        share_down[None],
    )


FAR_ORDER = (0, 2, 3, 1)
VMEM_LIMIT = 60 * 1024 * 1024
ROW_BLOCK = 256
CHUNKS = 2


def ring(value, axis, by):
    length = lax.axis_size(axis)
    return lax.ppermute(value, axis, [(i, (i + by) % length) for i in range(length)])


def swap(value, axis, bit):
    length = lax.axis_size(axis)
    return lax.ppermute(value, axis, [(i, i ^ bit) for i in range(length)])


def pick(value, index, axis=0):
    return lax.dynamic_index_in_dim(value, index, axis, keepdims=False)


def place(value, block, index):
    return lax.dynamic_update_index_in_dim(value, block, index, 0)


def relative(values, own):
    parts = values.reshape(values.shape[:-1] + (4, values.shape[-1] // 4))
    axis = parts.ndim - 2
    picked = [pick(parts, jnp.bitwise_xor(own, k), axis) for k in range(4)]
    return jnp.concatenate(picked, axis=-1)


def exchange(blocks, own):
    rows = blocks.shape[1]
    half = rows // 2
    far = pick(blocks, (own + 2) % 4)
    ahead = jnp.concatenate([pick(blocks, (own + 1) % 4), far[:half]], axis=0)
    behind = jnp.concatenate([pick(blocks, (own + 3) % 4), far[half:]], axis=0)
    from_left = ring(ahead, "tensor", 1)
    from_right = ring(behind, "tensor", -1)
    first = ring(from_left[rows:], "tensor", 1)
    second = ring(from_right[rows:], "tensor", -1)
    result = jnp.zeros_like(blocks)
    result = place(result, pick(blocks, own), own)
    result = place(result, from_left[:rows], (own + 3) % 4)
    result = place(result, from_right[:rows], (own + 1) % 4)
    return place(result, jnp.concatenate([first, second], axis=0), (own + 2) % 4)


def gather_across_first(shard):
    pair = jnp.stack([shard, swap(shard, "dp", 2)])
    left = ring(pair, "tensor", 1)
    right = ring(pair, "tensor", -1)
    far = jnp.stack([ring(left[0], "tensor", 1), ring(right[1], "tensor", -1)])
    mine = jnp.stack([pair, left, right, far])
    return jnp.stack([mine, swap(mine, "dp", 1)], axis=2)


def gather_along_first(shard):
    half = shard.shape[0] // 2
    left = ring(shard, "tensor", 1)
    right = ring(shard, "tensor", -1)
    own_far = swap(shard, "dp", 2)
    far = jnp.concatenate(
        [ring(left[:half], "tensor", 1), ring(right[half:], "tensor", -1)], axis=0
    )
    mine = jnp.stack(
        [
            jnp.stack([shard, own_far]),
            jnp.stack([left, swap(left, "dp", 2)]),
            jnp.stack([right, swap(right, "dp", 2)]),
            jnp.stack([far, swap(far, "dp", 2)]),
        ]
    )
    return jnp.stack([mine, swap(mine, "dp", 1)], axis=2)


def add_wide(left, right):
    return (left.astype(jnp.float32) + right.astype(jnp.float32)).astype(jnp.bfloat16)


def reduce_ring(blocks):
    own, left, right, far = blocks
    half = own.shape[0] // 2
    to_right = ring(far[:half], "tensor", 1)
    to_left = ring(far[half:], "tensor", -1)
    right = jnp.concatenate([add_wide(right[:half], to_right), right[half:]], axis=0)
    left = jnp.concatenate([left[:half], add_wide(left[half:], to_left)], axis=0)
    got_left = ring(right, "tensor", 1)
    got_right = ring(left, "tensor", -1)
    total = own.astype(jnp.float32) + got_left.astype(jnp.float32) + got_right.astype(jnp.float32)
    return total.astype(jnp.bfloat16)


def reduce_core(grads):
    return add_wide(grads[:, 0], swap(grads[:, 1], "dp", 1))


def reduce_across_last(grads):
    shared = reduce_core(grads)
    own = reduce_ring([shared[:, :, k] for k in range(4)])
    return add_wide(own[0], swap(own[1], "dp", 2))


def reduce_along_last(grads):
    shared = reduce_core(grads)
    own = add_wide(shared[0], swap(shared[1], "dp", 2))
    return reduce_ring([own[:, k] for k in range(4)])


def normalised(x):
    average = jnp.mean(x, axis=-1, keepdims=True)
    centred = x - average
    variance = jnp.mean(centred * centred, axis=-1, keepdims=True)
    inverse = lax.rsqrt(variance + NORM_EPS)
    return centred * inverse, inverse


def nt_dot(left, right):
    return lax.dot_general(
        left, right, (((1,), (1,)), ((), ())), preferred_element_type=jnp.float32
    )


def tn_dot(left, right):
    return lax.dot_general(
        left, right, (((0,), (0,)), ((), ())), preferred_element_type=jnp.float32
    )


def nn_dot(left, right):
    return jnp.dot(left, right, preferred_element_type=jnp.float32)


def turn(values, cosine, low_sine, high_sine):
    lanes = values.shape[-1]
    return (
        values * cosine
        + pltpu.roll(values, ROT // 2, 1) * low_sine
        + pltpu.roll(values, lanes - ROT // 2, 1) * high_sine
    )


def call(body, name, grid, ins, outs, scratch=(), limit=VMEM_LIMIT):
    return pl.pallas_call(
        body,
        name=name,
        grid=grid,
        in_specs=[pl.BlockSpec(block, index) for _, block, index in ins],
        out_specs=[pl.BlockSpec(block, index) for _, _, block, index in outs],
        out_shape=[jax.ShapeDtypeStruct(shape, kind) for shape, kind, _, _ in outs],
        scratch_shapes=list(scratch),
        compiler_params=pltpu.CompilerParams(
            vmem_limit_bytes=limit, dimension_semantics=("arbitrary",) * len(grid)
        ),
    )(*[array for array, _, _ in ins])


def whole(array):
    return (array, array.shape, lambda *_: (0,) * array.ndim)


def rows_of(array, first=0, block=ROW_BLOCK):
    base = first // block
    return (array, (block, array.shape[1]), lambda i: (i + base, 0))


def qkv_body(x, vecs, shift, cos, low, high, w, ln_a, ln_m, qkv):
    hat, _ = normalised(x[...].astype(jnp.float32))
    attn = (hat * vecs[0:1, :] + vecs[1:2, :]).astype(jnp.bfloat16)
    ln_a[...] = attn
    ln_m[...] = (hat * vecs[2:3, :] + vecs[3:4, :]).astype(jnp.bfloat16)
    out = nn_dot(attn, w[...]) + shift[...]
    for block in range(qkv.shape[1] // 384):
        for part in range(3):
            at = block * 384 + part * 128
            piece = out[:, at : at + 128]
            if part < 2:
                piece = turn(piece, cos[...], low[...], high[...])
            qkv[:, at : at + 128] = piece.astype(jnp.bfloat16)


def run_qkv(x, vecs, shift, tables, w, first):
    rows, width = x.shape
    cols = w.shape[1]
    bf = jnp.bfloat16
    own = lambda i: (i, 0)
    return call(
        qkv_body,
        "norm_qkv",
        (rows // ROW_BLOCK,),
        [rows_of(x), whole(vecs), whole(shift)]
        + [rows_of(t, first) for t in tables]
        + [whole(w)],
        [
            ((rows, width), bf, (ROW_BLOCK, width), own),
            ((rows, width), bf, (ROW_BLOCK, width), own),
            ((rows, cols), bf, (ROW_BLOCK, cols), own),
        ],
    )


def attend_body(q, k, v, ctx, lse):
    length = q.shape[0]
    step = ROW_BLOCK
    for head in range(2):
        lanes = slice(head * 64, head * 64 + 64)
        keys = k[:, lanes]
        vals = v[:, lanes]
        for at in range(0, length, step):
            end = at + step
            queries = q[at:end, lanes] * jnp.bfloat16(0.125)
            scores = nt_dot(queries, keys[:end])
            row = lax.broadcasted_iota(jnp.int32, (step, step), 0)
            col = lax.broadcasted_iota(jnp.int32, (step, step), 1)
            last = jnp.where(col <= row, scores[:, at:], MASK_FILL)
            scores = last if at == 0 else jnp.concatenate([scores[:, :at], last], axis=1)
            top = jnp.max(scores, axis=1, keepdims=True)
            power = jnp.exp(scores - top)
            total = jnp.sum(power, axis=1, keepdims=True)
            probs = (power * (1.0 / total)).astype(jnp.bfloat16)
            ctx[at:end, lanes] = nn_dot(probs, vals[:end]).astype(jnp.bfloat16)
            level = jnp.broadcast_to(top + jnp.log(total), (step, 128))
            lse[0, head : head + 1, at:end] = level.T[0:1]


def run_attend(qkv):
    length, cols = qkv.shape
    groups = cols // 384
    return call(
        attend_body,
        "attend",
        (groups,),
        [
            (qkv, (length, 128), lambda i: (0, 3 * i)),
            (qkv, (length, 128), lambda i: (0, 3 * i + 1)),
            (qkv, (length, 128), lambda i: (0, 3 * i + 2)),
        ],
        [
            ((length, groups * 128), jnp.bfloat16, (length, 128), lambda i: (0, i)),
            ((groups, 8, length), jnp.float32, (1, 8, length), lambda i: (i, 0, 0)),
        ],
    )


ERF_TOP = (
    0.00022905065861350646,
    0.0034082910107109506,
    0.050955695062380861,
    0.18520832239976145,
    1.128379143519084,
)
ERF_BOTTOM = (
    -1.1791602954361697e-7,
    0.000023547966471313185,
    0.0010179625278914885,
    0.014070470171167667,
    0.11098505178285362,
    0.49746925110067538,
    1.0,
)


def erf(x):
    x = jnp.clip(x, -3.7439211627767994, 3.7439211627767994)
    square = x * x
    top = jnp.full_like(x, ERF_TOP[0])
    for term in ERF_TOP[1:]:
        top = top * square + term
    bottom = jnp.full_like(x, ERF_BOTTOM[0])
    for term in ERF_BOTTOM[1:]:
        bottom = bottom * square + term
    return x * top / bottom


def mlp_body(ctx, ln_m, shift, w_out, w_up, w_down, act, slope, part):
    up = nn_dot(ln_m[...], w_up[...]) + shift[...]
    half_erf = 0.5 * erf(up * (2.0**-0.5)) + 0.5
    bell = jnp.exp(up * up * -0.5) * ((2.0 * math.pi) ** -0.5)
    active = (up * half_erf).astype(jnp.bfloat16)
    act[...] = active
    slope[...] = (half_erf + up * bell).astype(jnp.bfloat16)
    part[...] = (nt_dot(ctx[...], w_out[...]) + nt_dot(active, w_down[...])).astype(jnp.bfloat16)


def run_mlp(ctx, ln_m, shift, w_out, w_up, w_down, first, rows):
    width = ln_m.shape[1]
    cols = w_up.shape[1]
    bf = jnp.bfloat16
    own = lambda i: (i, 0)
    return call(
        mlp_body,
        "mlp_out",
        (rows // ROW_BLOCK,),
        [
            rows_of(ctx, first),
            rows_of(ln_m, first),
            whole(shift),
            whole(w_out),
            whole(w_up),
            whole(w_down),
        ],
        [
            ((rows, cols), bf, (ROW_BLOCK, cols), own),
            ((rows, cols), bf, (ROW_BLOCK, cols), own),
            ((rows, width), bf, (ROW_BLOCK, width), own),
        ],
    )


def mlp_back_body(g, slope, w_out, w_down, d_up, d_ctx, sum_up, sum_g):
    grad = g[...]
    du = (nn_dot(grad, w_down[...]) * slope[...].astype(jnp.float32)).astype(jnp.bfloat16)
    d_up[...] = du
    d_ctx[...] = nn_dot(grad, w_out[...]).astype(jnp.bfloat16)

    @pl.when(pl.program_id(0) == 0)
    def _():
        sum_up[...] = jnp.zeros_like(sum_up)
        sum_g[...] = jnp.zeros_like(sum_g)

    sum_up[...] += jnp.sum(du.astype(jnp.float32), axis=0, keepdims=True)
    sum_g[...] += jnp.sum(grad.astype(jnp.float32), axis=0, keepdims=True)


def run_mlp_back(g, slope, w_out, w_down):
    rows, width = g.shape
    cols, heads = w_down.shape[1], w_out.shape[1]
    bf = jnp.bfloat16
    own = lambda i: (i, 0)
    fixed = lambda i: (0, 0)
    return call(
        mlp_back_body,
        "mlp_back",
        (rows // ROW_BLOCK,),
        [rows_of(g), rows_of(slope), whole(w_out), whole(w_down)],
        [
            ((rows, cols), bf, (ROW_BLOCK, cols), own),
            ((rows, heads), bf, (ROW_BLOCK, heads), own),
            ((1, cols), jnp.float32, (1, cols), fixed),
            ((1, width), jnp.float32, (1, width), fixed),
        ],
    )


def attend_back_body(q, k, v, d_ctx, lse, cos, low, high, d_qkv, sums, dk_sum, dv_sum, dq_all):
    length = q.shape[0]
    step = ROW_BLOCK
    for head in range(2):
        lanes = slice(head * 64, head * 64 + 64)
        keys = k[:, lanes]
        vals = v[:, lanes]
        dk_sum[:, lanes] = jnp.zeros((length, 64), jnp.float32)
        dv_sum[:, lanes] = jnp.zeros((length, 64), jnp.float32)
        for at in range(0, length, step):
            end = at + step
            queries = q[at:end, lanes] * jnp.bfloat16(0.125)
            grads = d_ctx[at:end, lanes]
            scores = nt_dot(keys[:end], queries)
            power = jnp.exp(scores - lse[0, head : head + 1, at:end])
            key = lax.broadcasted_iota(jnp.int32, (step, step), 0)
            row = lax.broadcasted_iota(jnp.int32, (step, step), 1)
            last = jnp.where(key <= row, power[at:], 0.0)
            probs = last if at == 0 else jnp.concatenate([power[:at], last], axis=0)
            d_probs = nt_dot(vals[:end], grads)
            delta = jnp.sum(probs * d_probs, axis=0, keepdims=True)
            d_scores = (probs * (d_probs - delta)).astype(jnp.bfloat16)
            dv_sum[:end, lanes] += nn_dot(probs.astype(jnp.bfloat16), grads)
            dk_sum[:end, lanes] += nn_dot(d_scores, queries)
            dq_all[at:end, lanes] = tn_dot(d_scores, keys[:end]) * 0.125
    dq = turn(dq_all[...], cos[...], -low[...], -high[...]).astype(jnp.bfloat16)
    dk = turn(dk_sum[...], cos[...], -low[...], -high[...]).astype(jnp.bfloat16)
    dv = dv_sum[...].astype(jnp.bfloat16)
    for part, piece in enumerate((dq, dk, dv)):
        at = part * 128
        d_qkv[:, at : at + 128] = piece
        sums[:, at : at + 128] = jnp.sum(piece.astype(jnp.float32), axis=0, keepdims=True)


def run_attend_back(qkv, d_ctx, lse, tables):
    length, cols = qkv.shape
    groups = cols // 384
    wide = pltpu.VMEM((length, 128), jnp.float32)
    return call(
        attend_back_body,
        "attend_back",
        (groups,),
        [
            (qkv, (length, 128), lambda i: (0, 3 * i)),
            (qkv, (length, 128), lambda i: (0, 3 * i + 1)),
            (qkv, (length, 128), lambda i: (0, 3 * i + 2)),
            (d_ctx, (length, 128), lambda i: (0, i)),
            (lse, (1, 8, length), lambda i: (i, 0, 0)),
        ]
        + [whole(t) for t in tables],
        [
            ((length, cols), jnp.bfloat16, (length, 384), lambda i: (0, i)),
            ((1, cols), jnp.float32, (1, 384), lambda i: (0, i)),
        ],
        [wide, wide, wide],
    )


def norm_back_body(x, d_qkv, d_up, vecs, w_qkv, w_up, part, sums):
    hat, inverse = normalised(x[...].astype(jnp.float32))
    d_attn = nt_dot(d_qkv[...], w_qkv[...])
    d_mlp = nt_dot(d_up[...], w_up[...])

    @pl.when(pl.program_id(0) == 0)
    def _():
        sums[...] = jnp.zeros_like(sums)

    for row, term in enumerate((d_attn * hat, d_mlp * hat, d_attn, d_mlp)):
        sums[row : row + 1, :] += jnp.sum(term, axis=0, keepdims=True)
    d_hat = d_attn * vecs[0:1, :] + d_mlp * vecs[2:3, :]
    along = jnp.mean(d_hat * hat, axis=-1, keepdims=True)
    level = jnp.mean(d_hat, axis=-1, keepdims=True)
    part[...] = (inverse * (d_hat - level - hat * along)).astype(jnp.bfloat16)


def run_norm_back(x, d_qkv, d_up, vecs, w_qkv, w_up, first, rows):
    width = x.shape[1]
    return call(
        norm_back_body,
        "norm_back",
        (rows // ROW_BLOCK,),
        [
            rows_of(x, first),
            rows_of(d_qkv, first),
            rows_of(d_up, first),
            whole(vecs),
            whole(w_qkv),
            whole(w_up),
        ],
        [
            ((rows, width), jnp.bfloat16, (ROW_BLOCK, width), lambda i: (i, 0)),
            ((8, width), jnp.float32, (8, width), lambda i: (0, 0)),
        ],
    )


def turn_tables(length):
    cosine, sine_tab = rotary_tables(length)
    zero = jnp.zeros_like(sine_tab)
    rest = jnp.zeros((length, 64 - ROT), jnp.float32)
    cos = jnp.concatenate([cosine, cosine, rest + 1.0], axis=1)
    low = jnp.concatenate([zero, sine_tab, rest], axis=1)
    high = jnp.concatenate([-sine_tab, zero, rest], axis=1)
    return tuple(jnp.concatenate([t, t], axis=1) for t in (cos, low, high))


def by_sequence(
    acts_in, cotangent, norm_gains, vec_bias, w_qkv, b_qkv, w_out, w_up, b_up, w_down
):
    section = lax.axis_index("section")
    across = lax.axis_index("dp")
    along = lax.axis_index("tensor")
    first_section = section == 0
    width = acts_in.shape[3]
    rows = w_qkv.shape[1]
    positions = acts_in.shape[1]
    length = 4 * positions
    heads = b_qkv.shape[1]
    bf = jnp.bfloat16

    qkv_halves = (
        w_qkv[0].reshape(rows, 2, 2, 3, 64).transpose(1, 0, 3, 2, 4).reshape(2, rows, -1)
    )
    out_halves = w_out[0].T.reshape(rows, 2, -1).transpose(1, 0, 2)
    up_halves = w_up[0].reshape(rows, 2, -1).transpose(1, 0, 2)
    down_halves = w_down[0].T.reshape(rows, 2, -1).transpose(1, 0, 2)
    n_qkv, n_out, n_up = qkv_halves.shape[2], out_halves.shape[2], up_halves.shape[2]

    def both_layers(halves):
        keep = pick(halves, section)
        got = swap(pick(halves, 1 - section), "section", 1)
        return jnp.where(first_section, keep, got), jnp.where(first_section, got, keep)

    small = jnp.concatenate(
        [
            norm_gains[0].reshape(-1),
            vec_bias[0].reshape(-1),
            b_qkv[0].reshape(-1).astype(jnp.float32),
            b_up[0].reshape(-1).astype(jnp.float32),
        ]
    )
    other = swap(small, "section", 1)
    small = jnp.where(first_section, jnp.stack([small, other]), jnp.stack([other, small]))
    small = jnp.stack([small, swap(small, "dp", 1)])
    small = jnp.concatenate([small, swap(small, "dp", 2)])
    small = jnp.stack(
        [small, ring(small, "tensor", 1), ring(small, "tensor", -1), ring(small, "tensor", 2)]
    )

    narrow = jnp.stack([jnp.concatenate([qkv_halves[h], out_halves[h]], axis=1) for h in (0, 1)])
    broad = jnp.stack([jnp.concatenate([up_halves[h], down_halves[h]], axis=1) for h in (0, 1)])
    narrow_shards = both_layers(narrow)
    acts = exchange(acts_in[:, :, 0, :], along).reshape(length, width)
    acts = relative(acts, across)
    broad_shards = both_layers(broad)

    def join(pieces, start, size):
        part = pieces[..., start : start + size]
        return part.transpose(1, 2, 3, 0, 4).reshape(width, -1)

    mats = []
    for layer in (0, 1):
        pieces = gather_across_first(narrow_shards[layer])
        mat_qkv, mat_out = join(pieces, 0, n_qkv), join(pieces, n_qkv, n_out)
        pieces = gather_along_first(broad_shards[layer])
        mats.append((mat_qkv, mat_out, join(pieces, 0, n_up), join(pieces, n_up, n_up)))
        if layer == 0:
            grads_in = exchange(cotangent[:, :, 0, :], along).reshape(length, width)
            grads_in = relative(grads_in, across)

    share = norm_gains.shape[2]
    vec_part = small[..., : 6 * share].reshape(4, 4, 2, 6, share)
    offsets = jnp.array(FAR_ORDER, jnp.int32)
    order = jnp.stack([pick(offsets, (k - along) % 4) for k in range(4)])
    vec_part = jnp.stack([pick(vec_part, order[k]) for k in range(4)])
    vecs_full = vec_part.transpose(2, 3, 1, 0, 4).reshape(2, 6, width)
    at = 6 * share
    share_q = b_qkv.shape[2]
    dp_order = [jnp.bitwise_xor(across, k) for k in range(4)]
    qkv_bias = small[..., at : at + heads * share_q].reshape(4, 4, 2, heads, share_q)
    qkv_bias = jnp.stack([pick(qkv_bias, i, 1) for i in dp_order], axis=1)
    qkv_bias = qkv_bias.transpose(2, 0, 3, 1, 4).reshape(2, 4, 2, heads // 2, 3, 64)
    qkv_bias = pick(qkv_bias, section, 2).transpose(0, 1, 3, 2, 4).reshape(2, 1, -1)
    at += heads * share_q
    bias_rows, share_u = b_up.shape[1], b_up.shape[2]
    up_bias = small[..., at : at + bias_rows * share_u].reshape(4, 4, 2, bias_rows, share_u)
    up_bias = jnp.stack([pick(up_bias, i, 1) for i in dp_order], axis=1)
    up_bias = up_bias.transpose(2, 0, 3, 1, 4).reshape(2, 4, 2, bias_rows // 2, 4 * share_u)
    up_bias = pick(up_bias, section, 2).reshape(2, 1, -1)
    zero_rows = jnp.zeros((4, width), jnp.float32)

    tables = turn_tables(length)
    chunk = length // CHUNKS
    starts = [i * chunk for i in range(CHUNKS)]

    inputs = [acts[a : a + chunk] for a in starts]
    kept = []
    for layer in (0, 1):
        mat_qkv, mat_out, mat_up, mat_down = mats[layer]
        full = vecs_full[layer]
        vecs = jnp.concatenate(
            [full[0:1], full[2:3], full[1:2], full[3:4], zero_rows], axis=0
        )
        pieces = [
            run_qkv(inputs[i], vecs, qkv_bias[layer], tables, mat_qkv, starts[i])
            for i in range(CHUNKS)
        ]
        ln_a, ln_m, qkv = (jnp.concatenate(p, axis=0) for p in zip(*pieces))
        ctx, lse = run_attend(qkv)
        acts_list, slopes, outs = [], [], []
        for i in range(CHUNKS):
            act, slope, part = run_mlp(
                ctx, ln_m, up_bias[layer], mat_out, mat_up, mat_down, starts[i], chunk
            )
            got = swap(part, "section", 1)
            total = part.astype(jnp.float32) + got.astype(jnp.float32)
            total = inputs[i].astype(jnp.float32) + total + (full[4] + full[5])
            outs.append(total.astype(bf))
            acts_list.append(act)
            slopes.append(slope)
        kept.append(
            (inputs, vecs, ln_a, ln_m, qkv, ctx, lse, jnp.concatenate(acts_list), slopes, outs)
        )
        inputs = outs

    upstream = [grads_in[a : a + chunk] for a in starts]
    reduced = [None, None]
    vectors = [None, None]
    layer_grads = [None, None]
    for layer in (1, 0):
        mat_qkv, mat_out, mat_up, mat_down = mats[layer]
        x_list, vecs, ln_a, ln_m, qkv, ctx, lse, act, slopes, _ = kept[layer]
        pieces = [
            run_mlp_back(upstream[i], slopes[i], mat_out, mat_down) for i in range(CHUNKS)
        ]
        d_up, d_ctx = (jnp.concatenate(p, axis=0) for p in list(zip(*pieces))[:2])
        sum_up = sum(p[2] for p in pieces)
        sum_g = sum(p[3] for p in pieces)
        g_full = jnp.concatenate(upstream, axis=0)
        d_qkv, sum_qkv = run_attend_back(qkv, d_ctx, lse, tables)
        x_full = jnp.concatenate(x_list, axis=0)
        downs, norm_sums = [], 0.0
        for i in range(CHUNKS):
            part, sums = run_norm_back(
                x_full, d_qkv, d_up, vecs, mat_qkv, mat_up, starts[i], chunk
            )
            got = swap(part, "section", 1)
            total = part.astype(jnp.float32) + got.astype(jnp.float32)
            downs.append((upstream[i].astype(jnp.float32) + total).astype(bf))
            norm_sums = norm_sums + sums[:4]

        def split(left, right):
            grad = tn_dot(left, right).astype(bf)
            return grad.reshape(2, 2, rows, 4, -1)

        broad_grad = jnp.concatenate([split(ln_m, d_up), split(g_full, act)], axis=-1)
        narrow_grad = jnp.concatenate([split(ln_a, d_qkv), split(g_full, ctx)], axis=-1)
        reduced[layer] = (reduce_across_last(narrow_grad), reduce_along_last(broad_grad))
        vectors[layer] = (norm_sums, sum_g, sum_qkv, sum_up)
        layer_grads[layer] = jnp.concatenate(downs, axis=0)
        upstream = downs

    def deliver(values):
        return exchange(relative(values, across).reshape(4, positions, width), along)

    acts_local = deliver(
        jnp.where(first_section, jnp.concatenate(kept[0][9]), jnp.concatenate(kept[1][9]))
    )
    grad_local = deliver(jnp.where(first_section, layer_grads[0], layer_grads[1]))

    def whole_layer(first, second):
        keep = jnp.where(first_section, first, second)
        got = swap(jnp.where(first_section, second, first), "section", 1)
        keep, got = keep.astype(jnp.float32), got.astype(jnp.float32)
        return jnp.where(first_section, jnp.stack([keep, got], 1), jnp.stack([got, keep], 1))

    narrow_out = whole_layer(reduced[0][0], reduced[1][0])
    broad_out = whole_layer(reduced[0][1], reduced[1][1])
    grad_qkv = narrow_out[..., :n_qkv].reshape(rows, 2, 3, 2, 64)
    grad_qkv = grad_qkv.transpose(0, 1, 3, 2, 4).reshape(rows, -1)
    grad_out = narrow_out[..., n_qkv:].reshape(rows, -1).T
    grad_up = broad_out[..., :n_up].reshape(rows, -1)
    grad_down = broad_out[..., n_up:].reshape(rows, -1).T

    flat = []
    for norm_sums, sum_g, sum_qkv, sum_up in vectors:
        feature = relative(jnp.concatenate([norm_sums, sum_g], axis=0), across)
        q_sum = sum_qkv.reshape(4, 3, 2, 64).transpose(0, 2, 1, 3).reshape(4, -1)
        both = jnp.concatenate([q_sum, sum_up.reshape(4, -1)], axis=1)
        both = jnp.stack([pick(both, order[k]) for k in range(4)])
        flat.append(jnp.concatenate([feature.reshape(-1), both.reshape(-1)]))
    flat = jnp.stack(flat)
    for axis, bit in (("dp", 1), ("dp", 2), ("tensor", 1), ("tensor", 2)):
        flat = flat + swap(flat, axis, bit)
    keep = pick(flat, section)
    mine = pick(flat, 1 - section)
    got = swap(mine, "section", 1)
    n_feature = 5 * width
    feature_own = keep[:n_feature].reshape(5, width)
    feature = feature_own[:4] + got[: 4 * width].reshape(4, width)
    place_at = (across * 4 + along) * share
    gain_share = lax.dynamic_slice_in_dim(feature[:2], place_at, share, 1)
    shifts = jnp.concatenate([feature[2:4], feature_own[4:5], feature_own[4:5]], axis=0)
    bias_share = lax.dynamic_slice_in_dim(shifts, place_at, share, 1)
    low_half = jnp.where(first_section, keep, got)[n_feature:].reshape(4, -1)
    high_half = jnp.where(first_section, got, keep)[n_feature:].reshape(4, -1)
    halves = jnp.stack([pick(low_half, along), pick(high_half, along)])
    n_head = (heads // 2) * 192
    head_sums = halves[:, :n_head].reshape(heads, 192)
    head_share = lax.dynamic_slice_in_dim(head_sums, across * share_q, share_q, 1)
    unit_sums = halves[:, n_head:].reshape(bias_rows, 4 * share_u)
    unit_share = lax.dynamic_slice_in_dim(unit_sums, across * share_u, share_u, 1)
    return (
        acts_local[None, :, :, None],
        grad_local[None, :, :, None],
        gain_share[None],
        bias_share[None],
        grad_qkv[None],
        head_share[None],
        grad_out[None],
        grad_up[None],
        unit_share[None],
        grad_down[None],
    )


def fits(mesh, args):
    acts_in, b_qkv = args[0], args[5]
    sizes = dict(mesh.shape)
    return (
        sizes["section"] == 2
        and sizes["dp"] == 4
        and sizes["tensor"] == MICRO
        and MICRO == 4
        and acts_in.shape[2] == sizes["dp"]
        and b_qkv.shape[1] == 16
        and b_qkv.shape[2] == 192
        and acts_in.shape[1] % (CHUNKS * ROW_BLOCK) == 0
    )


def solution(mesh):
    placed = (
        P(None, "tensor", "dp", None),
        P(None, "tensor", "dp", None),
        P("section", None, ("dp", "tensor")),
        P("section", None, ("dp", "tensor")),
        P("section", "dp", "tensor"),
        P("section", "tensor", "dp"),
        P("section", "tensor", "dp"),
        P("section", "dp", "tensor"),
        P("section", "tensor", "dp"),
        P("section", "tensor", "dp"),
    )
    def wrap(body):
        return jax.shard_map(
            body,
            mesh=mesh,
            in_specs=placed,
            out_specs=(
                P("section", None, "tensor", "dp", None),
                P("section", None, "tensor", "dp", None),
                P("section", None, ("dp", "tensor")),
                P("section", None, ("dp", "tensor")),
                P("section", "dp", "tensor"),
                P("section", "tensor", "dp"),
                P("section", "tensor", "dp"),
                P("section", "dp", "tensor"),
                P("section", "tensor", "dp"),
                P("section", "tensor", "dp"),
            ),
            check_vma=False,
        )

    return lambda *args: wrap(by_sequence if fits(mesh, args) else local)(*args)
```

```python
from functools import partial
import math

import jax
import jax.numpy as jnp
from jax import lax
from jax.experimental import pallas as pl
from jax.experimental.pallas import tpu as pltpu
from jax.sharding import PartitionSpec as P

ROT = 16
QBLOCK = 512
MICRO = 4


NORM_EPS = 1e-05
ROPE_BASE = 10000.0
MASK_FILL = -1e30


def from_behind(value, axis, by):
    length = lax.axis_size(axis)
    pairs = [(i, i + by) for i in range(length) if 0 <= i + by < length]
    return lax.ppermute(value, axis, pairs)


def layer_norm(values, norm_gain, norm_shift):
    average = jnp.mean(values, axis=-1, keepdims=True)
    centred = values - average
    variance = jnp.mean(centred * centred, axis=-1, keepdims=True)
    return centred * lax.rsqrt(variance + NORM_EPS) * norm_gain + norm_shift


def both_norms(values, gain_attn, shift_attn, gain_mlp, shift_mlp):
    return (layer_norm(values, gain_attn, shift_attn), layer_norm(values, gain_mlp, shift_mlp))


def rotary_tables(length):
    half_rot = ROT // 2
    frequency = jnp.exp(
        jnp.arange(half_rot, dtype=jnp.float32) * (-2.0 * math.log(ROPE_BASE) / ROT)
    )
    angles = jnp.arange(length, dtype=jnp.float32)[:, None] * frequency[None, :]
    return (jnp.cos(angles), jnp.sin(angles))


def rotate(values, cosine, sine_tab):
    half_rot = ROT // 2
    low_half = values[..., :half_rot]
    high_half = values[..., half_rot:ROT]
    return jnp.concatenate(
        [
            low_half * cosine - high_half * sine_tab,
            high_half * cosine + low_half * sine_tab,
            values[..., ROT:],
        ],
        axis=-1,
    )


def rotate_back(grads_rot, cosine, sine_tab):
    half_rot = ROT // 2
    low_half = grads_rot[..., :half_rot]
    high_half = grads_rot[..., half_rot:ROT]
    return jnp.concatenate(
        [
            low_half * cosine + high_half * sine_tab,
            high_half * cosine - low_half * sine_tab,
            grads_rot[..., ROT:],
        ],
        axis=-1,
    )


def causal_scores(queries, key_rows, first_row, score_scale):
    block_rows = queries.shape[0]
    last_row = key_rows.shape[0]
    scores = (
        jnp.einsum("qshd,kshd->shqk", queries, key_rows, preferred_element_type=jnp.float32)
        * score_scale
    )
    row_pos = first_row + jnp.arange(block_rows, dtype=jnp.int32)
    col_pos = jnp.arange(last_row, dtype=jnp.int32)
    allowed = col_pos[None, :] <= row_pos[:, None]
    return (scores, allowed)


def attend(queries, key_rows, val_rows):
    length = queries.shape[0]
    block_rows = min(QBLOCK, length)
    score_scale = queries.shape[-1] ** (-0.5)
    outputs = []
    totals = []
    for block_index in range(length // block_rows):
        first_row = block_index * block_rows
        last_row = first_row + block_rows
        scores, allowed = causal_scores(
            queries[first_row:last_row], key_rows[:last_row], first_row, score_scale
        )
        scores = jnp.where(allowed, scores, MASK_FILL)
        highest = jnp.max(scores, axis=-1, keepdims=True)
        exponent = jnp.exp(scores - highest)
        denominator = jnp.sum(exponent, axis=-1, keepdims=True)
        probability = (exponent / denominator).astype(jnp.bfloat16)
        block_out = jnp.einsum(
            "shqk,kshd->qshd", probability, val_rows[:last_row], preferred_element_type=jnp.float32
        )
        outputs.append(block_out.astype(jnp.bfloat16))
        totals.append((highest + jnp.log(denominator))[..., 0])
    context = jnp.concatenate(outputs, axis=0)
    return (context.reshape(length, context.shape[1], -1), jnp.concatenate(totals, axis=-1))


def attend_back(queries, key_rows, val_rows, d_context, log_total):
    length = queries.shape[0]
    block_rows = min(QBLOCK, length)
    score_scale = queries.shape[-1] ** (-0.5)
    grad_query_list = []
    grad_keys = jnp.zeros(queries.shape, jnp.float32)
    grad_vals = jnp.zeros(queries.shape, jnp.float32)
    for block_index in range(length // block_rows):
        first_row = block_index * block_rows
        last_row = first_row + block_rows
        query_block = queries[first_row:last_row]
        scores, allowed = causal_scores(query_block, key_rows[:last_row], first_row, score_scale)
        probability = jnp.where(
            allowed, jnp.exp(scores - log_total[:, :, first_row:last_row, None]), 0.0
        )
        d_block = d_context[first_row:last_row]
        d_prob = jnp.einsum(
            "qshd,kshd->shqk", d_block, val_rows[:last_row], preferred_element_type=jnp.float32
        )
        delta = jnp.sum(probability * d_prob, axis=-1, keepdims=True)
        d_scores = (probability * (d_prob - delta)).astype(jnp.bfloat16)
        grad_query_list.append(
            jnp.einsum(
                "shqk,kshd->qshd", d_scores, key_rows[:last_row], preferred_element_type=jnp.float32
            )
            * score_scale
        )
        grad_keys = grad_keys.at[:last_row].add(
            jnp.einsum("shqk,qshd->kshd", d_scores, query_block, preferred_element_type=jnp.float32)
            * score_scale
        )
        grad_vals = grad_vals.at[:last_row].add(
            jnp.einsum(
                "shqk,qshd->kshd",
                probability.astype(jnp.bfloat16),
                d_block,
                preferred_element_type=jnp.float32,
            )
        )
    return (jnp.concatenate(grad_query_list, axis=0), grad_keys, grad_vals)


def local(acts_in, cotangent, norm_gains, vec_bias, w_qkv, b_qkv, w_out, w_up, b_up, w_down):
    section_index = lax.axis_index("section")
    own_start = lax.axis_index("tensor") * acts_in.shape[1]
    local_len = acts_in.shape[1]
    seq_count = acts_in.shape[2]
    model_width = acts_in.shape[3]
    length = local_len * lax.axis_size("tensor")
    all_rows = length * seq_count
    gain_full, bias_full = (
        lax.all_gather(norm_gains[0], ("dp", "tensor"), axis=1, tiled=True),
        lax.all_gather(vec_bias[0], ("dp", "tensor"), axis=1, tiled=True),
    )
    mat_qkv, bias_qkv, mat_out, mat_up, bias_up, mat_down = (
        lax.all_gather(w_qkv[0], "dp", axis=0, tiled=True),
        lax.all_gather(b_qkv[0], "dp", axis=1, tiled=True),
        lax.all_gather(w_out[0], "dp", axis=1, tiled=True),
        lax.all_gather(w_up[0], "dp", axis=0, tiled=True),
        lax.all_gather(b_up[0], "dp", axis=1, tiled=True),
        lax.all_gather(w_down[0], "dp", axis=1, tiled=True),
    )
    head_count = bias_qkv.shape[0]
    head_dim = bias_qkv.shape[1] // 3
    qkv_shift = bias_qkv.reshape(-1).astype(jnp.float32)
    up_shift = bias_up.reshape(-1).astype(jnp.float32)
    cosine, sine_tab = rotary_tables(length)
    cosine = cosine[:, None, None, :]
    sine_tab = sine_tab[:, None, None, :]
    received = jnp.zeros_like(acts_in[0])
    stash_list = []
    out_list = []
    for moment in range(MICRO + 1):
        own_rows = acts_in[min(moment, MICRO - 1)]
        inputs = jnp.where(section_index == 0, own_rows, received)
        forward_gathered = lax.all_gather(inputs, "tensor", axis=0, tiled=True)
        full_attn, full_mlp = both_norms(
            forward_gathered.astype(jnp.float32),
            gain_full[0],
            bias_full[0],
            gain_full[1],
            bias_full[1],
        )
        forward_normed_attn = full_attn.astype(jnp.bfloat16)
        forward_normed_mlp = full_mlp.astype(jnp.bfloat16)
        forward_flat_attn = forward_normed_attn.reshape(all_rows, model_width)
        forward_flat_mlp = forward_normed_mlp.reshape(all_rows, model_width)
        projected = (
            jnp.dot(forward_flat_attn, mat_qkv, preferred_element_type=jnp.float32) + qkv_shift
        )
        projected = projected.reshape(length, seq_count, head_count, 3, head_dim)
        forward_queries = rotate(projected[:, :, :, 0], cosine, sine_tab).astype(jnp.bfloat16)
        forward_key_rows = rotate(projected[:, :, :, 1], cosine, sine_tab).astype(jnp.bfloat16)
        forward_val_rows = projected[:, :, :, 2].astype(jnp.bfloat16)
        forward_context, forward_log_total = attend(
            forward_queries, forward_key_rows, forward_val_rows
        )
        forward_up_proj = (
            jnp.dot(forward_flat_mlp, mat_up, preferred_element_type=jnp.float32) + up_shift
        )
        forward_activated = jax.nn.gelu(forward_up_proj, approximate=False).astype(jnp.bfloat16)
        active_rows = forward_activated.reshape(length, seq_count, -1)
        context_part = forward_context.reshape(lax.axis_size("tensor") * local_len * seq_count, -1)
        active_part = active_rows.reshape(lax.axis_size("tensor") * local_len * seq_count, -1)
        summed = jnp.dot(context_part, mat_out, preferred_element_type=jnp.float32) + jnp.dot(
            active_part, mat_down, preferred_element_type=jnp.float32
        )
        mixed_sum = lax.psum_scatter(
            summed.reshape(lax.axis_size("tensor") * local_len, seq_count, model_width),
            "tensor",
            scatter_dimension=0,
            tiled=True,
        )
        result = inputs.astype(jnp.float32) + mixed_sum + bias_full[2] + bias_full[3]
        forward_stashed = (
            forward_gathered,
            forward_normed_attn,
            forward_normed_mlp,
            forward_queries,
            forward_key_rows,
            forward_val_rows,
            forward_context,
            forward_log_total,
            forward_up_proj,
            forward_activated,
        )
        result, stashed = (result.astype(jnp.bfloat16), forward_stashed)
        stash_list.append(stashed)
        out_list.append(result)
        if moment < MICRO:
            received = from_behind(result, "section", 1)
    stash_all = jax.tree.map(lambda *parts: jnp.stack(parts), *stash_list)
    acts_local = lax.dynamic_slice_in_dim(jnp.stack(out_list), section_index, MICRO, 0)
    back_received = jnp.zeros_like(cotangent[0])
    grad_list = []
    weight_sums = None
    vector_sums = None
    for moment in range(MICRO + 1):
        micro_index = moment - 1 + section_index
        is_valid = (micro_index >= 0) & (micro_index < MICRO)
        source_clock = jnp.clip(micro_index + section_index, 0, MICRO)
        stashed = jax.tree.map(
            lambda part: lax.dynamic_index_in_dim(part, source_clock, 0, keepdims=False), stash_all
        )
        upstream = jnp.where(section_index == 1, cotangent[min(moment, MICRO - 1)], back_received)
        (
            gathered,
            normed_attn,
            normed_mlp,
            queries,
            key_rows,
            val_rows,
            context,
            log_total,
            up_proj,
            activated,
        ) = stashed
        backward_inputs = lax.dynamic_slice_in_dim(gathered, own_start, local_len, 0)
        upstream_rows = lax.all_gather(upstream, "tensor", axis=0, tiled=True)
        flat_grad = upstream_rows.reshape(all_rows, model_width)
        d_context = jnp.dot(flat_grad, mat_out.T, preferred_element_type=jnp.float32).astype(
            jnp.bfloat16
        )
        d_context = d_context.reshape(length, seq_count, head_count, head_dim)
        d_active = jnp.dot(flat_grad, mat_down.T, preferred_element_type=jnp.float32)
        _, gelu_pullback = jax.vjp(partial(jax.nn.gelu, approximate=False), up_proj)
        d_up = gelu_pullback(d_active)[0].astype(jnp.bfloat16)
        grad_query, grad_key, grad_val = attend_back(
            queries, key_rows, val_rows, d_context, log_total
        )
        d_qkv = jnp.stack(
            [
                rotate_back(grad_query, cosine, sine_tab),
                rotate_back(grad_key, cosine, sine_tab),
                grad_val,
            ],
            axis=3,
        ).astype(jnp.bfloat16)
        d_qkv_flat = d_qkv.reshape(all_rows, -1)
        d_qkv_rows = d_qkv.reshape(length, seq_count, -1)
        d_up_rows = d_up.reshape(length, seq_count, -1)
        flat_attn = normed_attn.reshape(all_rows, model_width)
        flat_mlp = normed_mlp.reshape(all_rows, model_width)
        weight_terms = (
            jnp.einsum("tc,te->ce", flat_attn, d_qkv_flat, preferred_element_type=jnp.float32),
            jnp.sum(d_qkv_flat.astype(jnp.float32), axis=0).reshape(bias_qkv.shape),
            jnp.einsum(
                "tc,te->ce",
                context.reshape(all_rows, -1),
                flat_grad,
                preferred_element_type=jnp.float32,
            ),
            jnp.einsum("tc,te->ce", flat_mlp, d_up, preferred_element_type=jnp.float32),
            jnp.sum(d_up.astype(jnp.float32), axis=0).reshape(bias_up.shape),
            jnp.einsum("tc,te->ce", activated, flat_grad, preferred_element_type=jnp.float32),
        )
        attn_part = d_qkv_rows.reshape(lax.axis_size("tensor") * local_len * seq_count, -1)
        mlp_part = d_up_rows.reshape(lax.axis_size("tensor") * local_len * seq_count, -1)
        joined = jnp.concatenate(
            [
                jnp.dot(attn_part, mat_qkv.T, preferred_element_type=jnp.float32),
                jnp.dot(mlp_part, mat_up.T, preferred_element_type=jnp.float32),
            ],
            axis=-1,
        )
        d_normed = lax.psum_scatter(
            joined.reshape(lax.axis_size("tensor") * local_len, seq_count, 2 * model_width).astype(
                jnp.bfloat16
            ),
            "tensor",
            scatter_dimension=0,
            tiled=True,
        ).astype(jnp.float32)
        _, norm_pullback = jax.vjp(
            both_norms,
            backward_inputs.astype(jnp.float32),
            gain_full[0],
            bias_full[0],
            gain_full[1],
            bias_full[1],
        )
        d_local, d_gain_attn, d_shift_attn, d_gain_mlp, d_shift_mlp = norm_pullback(
            (d_normed[..., :model_width], d_normed[..., model_width:])
        )
        upstream_float = upstream.astype(jnp.float32)
        d_inputs = (upstream_float + d_local).astype(jnp.bfloat16)
        out_shift = jnp.sum(upstream_float, axis=(0, 1))
        vector_terms = (
            jnp.stack([d_gain_attn, d_gain_mlp]),
            jnp.stack([d_shift_attn, d_shift_mlp, out_shift, out_shift]),
        )
        d_inputs, weight_terms, vector_terms = (d_inputs, weight_terms, vector_terms)
        grad_list.append(d_inputs)
        if moment < MICRO:
            back_received = from_behind(d_inputs, "section", -1)
        weight_terms = tuple((jnp.where(is_valid, term, 0.0) for term in weight_terms))
        vector_terms = tuple((jnp.where(is_valid, term, 0.0) for term in vector_terms))
        if moment == 0:
            weight_sums = tuple(weight_terms)
            vector_sums = vector_terms
        else:
            weight_sums = tuple((a + b for a, b in zip(weight_sums, weight_terms)))
            vector_sums = tuple((a + b for a, b in zip(vector_sums, vector_terms)))
    sum_qkv, sum_bqkv, sum_out, sum_up, sum_bup, sum_down = weight_sums
    share_qkv, share_bqkv, share_out, share_up, share_bup, share_down = (
        lax.psum_scatter(
            sum_qkv.astype(jnp.bfloat16), "dp", scatter_dimension=0, tiled=True
        ).astype(jnp.float32),
        lax.psum_scatter(
            sum_bqkv.astype(jnp.bfloat16), "dp", scatter_dimension=1, tiled=True
        ).astype(jnp.float32),
        lax.psum_scatter(
            sum_out.astype(jnp.bfloat16), "dp", scatter_dimension=1, tiled=True
        ).astype(jnp.float32),
        lax.psum_scatter(sum_up.astype(jnp.bfloat16), "dp", scatter_dimension=0, tiled=True).astype(
            jnp.float32
        ),
        lax.psum_scatter(
            sum_bup.astype(jnp.bfloat16), "dp", scatter_dimension=1, tiled=True
        ).astype(jnp.float32),
        lax.psum_scatter(
            sum_down.astype(jnp.bfloat16), "dp", scatter_dimension=1, tiled=True
        ).astype(jnp.float32),
    )
    grad_local = lax.dynamic_slice_in_dim(jnp.stack(grad_list), 1 - section_index, MICRO, 0)
    gain_share, bias_share = (
        lax.psum_scatter(vector_sums[0], ("dp", "tensor"), scatter_dimension=1, tiled=True),
        lax.psum_scatter(vector_sums[1], ("dp", "tensor"), scatter_dimension=1, tiled=True),
    )
    return (
        acts_local[None],
        grad_local[None],
        gain_share[None],
        bias_share[None],
        share_qkv[None],
        share_bqkv[None],
        share_out[None],
        share_up[None],
        share_bup[None],
        share_down[None],
    )


FAR_ORDER = (0, 2, 3, 1)
VMEM_LIMIT = 60 * 1024 * 1024
ROW_BLOCK = 256
CHUNKS = 2


def ring(value, axis, by):
    length = lax.axis_size(axis)
    return lax.ppermute(value, axis, [(i, (i + by) % length) for i in range(length)])


def swap(value, axis, bit):
    length = lax.axis_size(axis)
    return lax.ppermute(value, axis, [(i, i ^ bit) for i in range(length)])


def pick(value, index, axis=0):
    return lax.dynamic_index_in_dim(value, index, axis, keepdims=False)


def place(value, block, index):
    return lax.dynamic_update_index_in_dim(value, block, index, 0)


def relative(values, own):
    size = values.shape[-1] // 4
    picked = [
        lax.dynamic_slice_in_dim(values, jnp.bitwise_xor(own, k) * size, size, values.ndim - 1)
        for k in range(4)
    ]
    return jnp.concatenate(picked, axis=-1)


def after(values, *earlier):
    return lax.optimization_barrier((values, earlier))[0]


def exchange(blocks, own):
    rows = blocks.shape[1]
    half = rows // 2
    far = pick(blocks, (own + 2) % 4)
    ahead = jnp.concatenate([pick(blocks, (own + 1) % 4), far[:half]], axis=0)
    behind = jnp.concatenate([pick(blocks, (own + 3) % 4), far[half:]], axis=0)
    from_left = ring(ahead, "tensor", 1)
    from_right = ring(behind, "tensor", -1)
    first = ring(from_left[rows:], "tensor", 1)
    second = ring(from_right[rows:], "tensor", -1)
    result = jnp.zeros_like(blocks)
    result = place(result, pick(blocks, own), own)
    result = place(result, from_left[:rows], (own + 3) % 4)
    result = place(result, from_right[:rows], (own + 1) % 4)
    return place(result, jnp.concatenate([first, second], axis=0), (own + 2) % 4)


def with_other_core(pieces):
    return tuple(pieces) + tuple(swap(piece, "dp", 1) for piece in pieces)


def gather_across_first(shard):
    pair = jnp.stack([shard, swap(shard, "dp", 2)])
    left = ring(pair, "tensor", 1)
    right = ring(pair, "tensor", -1)
    far = jnp.stack([ring(left[0], "tensor", 1), ring(right[1], "tensor", -1)])
    return with_other_core((pair, left, right, far))


def gather_along_first(shard):
    half = shard.shape[0] // 2
    left = ring(shard, "tensor", 1)
    right = ring(shard, "tensor", -1)
    far = jnp.concatenate(
        [ring(left[:half], "tensor", 1), ring(right[half:], "tensor", -1)], axis=0
    )
    pieces = [jnp.stack([part, swap(part, "dp", 2)]) for part in (shard, left, right, far)]
    return with_other_core(pieces)


def add_wide(left, right):
    return (left.astype(jnp.float32) + right.astype(jnp.float32)).astype(jnp.bfloat16)


def reduce_ring(blocks):
    own, left, right, far = blocks
    half = own.shape[0] // 2
    to_right = ring(far[:half], "tensor", 1)
    to_left = ring(far[half:], "tensor", -1)
    right = jnp.concatenate([add_wide(right[:half], to_right), right[half:]], axis=0)
    left = jnp.concatenate([left[:half], add_wide(left[half:], to_left)], axis=0)
    got_left = ring(right, "tensor", 1)
    got_right = ring(left, "tensor", -1)
    total = own.astype(jnp.float32) + got_left.astype(jnp.float32) + got_right.astype(jnp.float32)
    return total.astype(jnp.bfloat16)


def reduce_across_last(shared):
    own = reduce_ring([shared[k] for k in range(4)])
    return add_wide(own[0], swap(own[1], "dp", 2))


def reduce_along_last(shared):
    own = add_wide(shared[:, 0], swap(shared[:, 1], "dp", 2))
    return reduce_ring([own[k] for k in range(4)])


def normalised(x):
    average = jnp.mean(x, axis=-1, keepdims=True)
    centred = x - average
    variance = jnp.mean(centred * centred, axis=-1, keepdims=True)
    inverse = lax.rsqrt(variance + NORM_EPS)
    return centred * inverse, inverse


def nt_dot(left, right):
    return lax.dot_general(
        left, right, (((1,), (1,)), ((), ())), preferred_element_type=jnp.float32
    )


def tn_dot(left, right):
    return lax.dot_general(
        left, right, (((0,), (0,)), ((), ())), preferred_element_type=jnp.float32
    )


def nn_dot(left, right):
    return jnp.dot(left, right, preferred_element_type=jnp.float32)


def turn(values, cosine, low_sine, high_sine):
    lanes = values.shape[-1]
    return (
        values * cosine
        + pltpu.roll(values, ROT // 2, 1) * low_sine
        + pltpu.roll(values, lanes - ROT // 2, 1) * high_sine
    )


def call(body, name, grid, ins, outs, scratch=(), filled=()):
    count = len(ins)

    def run(*refs):
        body(*refs[:count], *refs[count + len(filled) :])

    return pl.pallas_call(
        run,
        name=name,
        grid=grid,
        in_specs=[pl.BlockSpec(block, index) for _, block, index in ins]
        + [pl.BlockSpec(memory_space=pl.ANY)] * len(filled),
        out_specs=[pl.BlockSpec(block, index) for _, _, block, index in outs],
        out_shape=[jax.ShapeDtypeStruct(shape, kind) for shape, kind, _, _ in outs],
        scratch_shapes=list(scratch),
        input_output_aliases={count + i: i for i in range(len(filled))},
        compiler_params=pltpu.CompilerParams(
            vmem_limit_bytes=VMEM_LIMIT, dimension_semantics=("arbitrary",) * len(grid)
        ),
    )(*[array for array, _, _ in ins], *filled)


def whole(array):
    return (array, array.shape, lambda *_: (0,) * array.ndim)


def matrix(pieces, size, block):
    shape = (2, pieces[0].shape[1], size)
    return [(piece, shape, lambda *_: (0, 0, block)) for piece in pieces]


def room(pieces, size):
    return pltpu.VMEM((4 * pieces[0].shape[1], 4 * size), jnp.bfloat16)


def assemble(refs, target):
    _, rows, size = refs[0].shape
    for core in range(2):
        for offset in range(4):
            for side in range(2):
                at = (2 * side + core) * rows
                target[at : at + rows, offset * size : (offset + 1) * size] = refs[
                    core * 4 + offset
                ][side]


def rows_of(array, first=0, block=ROW_BLOCK):
    base = first // block
    return (array, (block, array.shape[1]), lambda i: (i + base, 0))


def qkv_body(x, vecs, shift, cos, low, high, *rest):
    ln_a, ln_m, qkv, w = rest[8:]

    @pl.when(pl.program_id(0) == 0)
    def _():
        assemble(rest[:8], w)

    hat, _ = normalised(x[...].astype(jnp.float32))
    attn = (hat * vecs[0:1, :] + vecs[1:2, :]).astype(jnp.bfloat16)
    ln_a[...] = attn
    ln_m[...] = (hat * vecs[2:3, :] + vecs[3:4, :]).astype(jnp.bfloat16)
    out = nn_dot(attn, w[...]) + shift[...]
    for block in range(qkv.shape[1] // 384):
        for part in range(3):
            at = block * 384 + part * 128
            piece = out[:, at : at + 128]
            if part < 2:
                piece = turn(piece, cos[...], low[...], high[...])
            qkv[:, at : at + 128] = piece.astype(jnp.bfloat16)


def run_qkv(source, vecs, shift, tables, pieces, at, rows, filled):
    x, first = source
    width = x.shape[1]
    length = tables[0].shape[0]
    cols = shift.shape[1]
    bf = jnp.bfloat16
    base = at // ROW_BLOCK
    own = lambda i: (i + base, 0)
    return call(
        qkv_body,
        "norm_qkv",
        (rows // ROW_BLOCK,),
        [rows_of(x, first), whole(vecs), whole(shift)]
        + [rows_of(t, at) for t in tables]
        + matrix(pieces, cols // 4, 0),
        [
            ((length, width), bf, (ROW_BLOCK, width), own),
            ((length, width), bf, (ROW_BLOCK, width), own),
            ((length, cols), bf, (ROW_BLOCK, cols), own),
        ],
        [room(pieces, cols // 4)],
        filled,
    )


def attend_body(q, k, v, ctx, lse):
    length = q.shape[0]
    step = ROW_BLOCK
    for head in range(2):
        lanes = slice(head * 64, head * 64 + 64)
        keys = k[:, lanes]
        vals = v[:, lanes]
        for at in range(0, length, step):
            end = at + step
            queries = q[at:end, lanes] * jnp.bfloat16(0.125)
            scores = nt_dot(queries, keys[:end])
            row = lax.broadcasted_iota(jnp.int32, (step, step), 0)
            col = lax.broadcasted_iota(jnp.int32, (step, step), 1)
            last = jnp.where(col <= row, scores[:, at:], MASK_FILL)
            scores = last if at == 0 else jnp.concatenate([scores[:, :at], last], axis=1)
            top = jnp.max(scores, axis=1, keepdims=True)
            power = jnp.exp(scores - top)
            total = jnp.sum(power, axis=1, keepdims=True)
            probs = (power * (1.0 / total)).astype(jnp.bfloat16)
            ctx[at:end, lanes] = nn_dot(probs, vals[:end]).astype(jnp.bfloat16)
            level = jnp.broadcast_to(top + jnp.log(total), (step, 128))
            lse[0, head : head + 1, at:end] = level.T[0:1]


def run_attend(qkv):
    length, cols = qkv.shape
    groups = cols // 384
    return call(
        attend_body,
        "attend",
        (groups,),
        [
            (qkv, (length, 128), lambda i: (0, 3 * i)),
            (qkv, (length, 128), lambda i: (0, 3 * i + 1)),
            (qkv, (length, 128), lambda i: (0, 3 * i + 2)),
        ],
        [
            ((length, groups * 128), jnp.bfloat16, (length, 128), lambda i: (0, i)),
            ((groups, 8, length), jnp.float32, (1, 8, length), lambda i: (i, 0, 0)),
        ],
    )


ERF_TOP = (
    0.00022905065861350646,
    0.0034082910107109506,
    0.050955695062380861,
    0.18520832239976145,
    1.128379143519084,
)
ERF_BOTTOM = (
    -1.1791602954361697e-7,
    0.000023547966471313185,
    0.0010179625278914885,
    0.014070470171167667,
    0.11098505178285362,
    0.49746925110067538,
    1.0,
)


def erf(x):
    x = jnp.clip(x, -3.7439211627767994, 3.7439211627767994)
    square = x * x
    top = jnp.full_like(x, ERF_TOP[0])
    for term in ERF_TOP[1:]:
        top = top * square + term
    bottom = jnp.full_like(x, ERF_BOTTOM[0])
    for term in ERF_BOTTOM[1:]:
        bottom = bottom * square + term
    return x * top / bottom


def mlp_body(ctx, ln_m, shift, *rest):
    act, slope, part, w_out, w_up, w_down = rest[24:]

    @pl.when(pl.program_id(0) == 0)
    def _():
        assemble(rest[:8], w_out)
        assemble(rest[8:16], w_up)
        assemble(rest[16:24], w_down)

    up = nn_dot(ln_m[...], w_up[...]) + shift[...]
    half_erf = 0.5 * erf(up * (2.0**-0.5)) + 0.5
    bell = jnp.exp(up * up * -0.5) * ((2.0 * math.pi) ** -0.5)
    active = (up * half_erf).astype(jnp.bfloat16)
    act[...] = active
    slope[...] = (half_erf + up * bell).astype(jnp.bfloat16)
    part[...] = (nt_dot(ctx[...], w_out[...]) + nt_dot(active, w_down[...])).astype(jnp.bfloat16)


def run_mlp(ctx, ln_m, shift, narrow, broad, at, rows, filled):
    length, width = ln_m.shape
    cols, heads = shift.shape[1], ctx.shape[1]
    bf = jnp.bfloat16
    base = at // ROW_BLOCK
    own = lambda i: (i + base, 0)
    return call(
        mlp_body,
        "mlp_out",
        (rows // ROW_BLOCK,),
        [rows_of(ctx, at), rows_of(ln_m, at), whole(shift)]
        + matrix(narrow, heads // 4, 3)
        + matrix(broad, cols // 4, 0)
        + matrix(broad, cols // 4, 1),
        [
            ((length, cols), bf, (ROW_BLOCK, cols), own),
            ((length, cols), bf, (ROW_BLOCK, cols), own),
            ((rows, width), bf, (ROW_BLOCK, width), lambda i: (i, 0)),
        ],
        [room(narrow, heads // 4), room(broad, cols // 4), room(broad, cols // 4)],
        filled,
    )


def mlp_back_body(g, slope, *rest):
    d_up, d_ctx, sum_up, sum_g, w_out, w_down = rest[16:]

    @pl.when(pl.program_id(0) == 0)
    def _():
        assemble(rest[:8], w_out)
        assemble(rest[8:16], w_down)
        sum_up[...] = jnp.zeros_like(sum_up)
        sum_g[...] = jnp.zeros_like(sum_g)

    grad = g[...]
    du = (nn_dot(grad, w_down[...]) * slope[...].astype(jnp.float32)).astype(jnp.bfloat16)
    d_up[...] = du
    d_ctx[...] = nn_dot(grad, w_out[...]).astype(jnp.bfloat16)
    sum_up[...] += jnp.sum(du.astype(jnp.float32), axis=0, keepdims=True)
    sum_g[...] += jnp.sum(grad.astype(jnp.float32), axis=0, keepdims=True)


def run_mlp_back(source, slope, narrow, broad, at, rows, heads, filled):
    g, first = source
    width = g.shape[1]
    length, cols = slope.shape
    bf = jnp.bfloat16
    base = at // ROW_BLOCK
    own = lambda i: (i + base, 0)
    fixed = lambda i: (0, 0)
    return call(
        mlp_back_body,
        "mlp_back",
        (rows // ROW_BLOCK,),
        [rows_of(g, first), rows_of(slope, at)]
        + matrix(narrow, heads // 4, 3)
        + matrix(broad, cols // 4, 1),
        [
            ((length, cols), bf, (ROW_BLOCK, cols), own),
            ((length, heads), bf, (ROW_BLOCK, heads), own),
            ((1, cols), jnp.float32, (1, cols), fixed),
            ((1, width), jnp.float32, (1, width), fixed),
        ],
        [room(narrow, heads // 4), room(broad, cols // 4)],
        filled,
    )


def attend_back_body(q, k, v, d_ctx, lse, cos, low, high, d_qkv, sums, dk_sum, dv_sum, dq_all):
    length = q.shape[0]
    step = ROW_BLOCK
    for head in range(2):
        lanes = slice(head * 64, head * 64 + 64)
        keys = k[:, lanes]
        vals = v[:, lanes]
        dk_sum[:, lanes] = jnp.zeros((length, 64), jnp.float32)
        dv_sum[:, lanes] = jnp.zeros((length, 64), jnp.float32)
        for at in range(0, length, step):
            end = at + step
            queries = q[at:end, lanes] * jnp.bfloat16(0.125)
            grads = d_ctx[at:end, lanes]
            scores = nt_dot(keys[:end], queries)
            power = jnp.exp(scores - lse[0, head : head + 1, at:end])
            key = lax.broadcasted_iota(jnp.int32, (step, step), 0)
            row = lax.broadcasted_iota(jnp.int32, (step, step), 1)
            last = jnp.where(key <= row, power[at:], 0.0)
            probs = last if at == 0 else jnp.concatenate([power[:at], last], axis=0)
            d_probs = nt_dot(vals[:end], grads)
            delta = jnp.sum(probs * d_probs, axis=0, keepdims=True)
            d_scores = (probs * (d_probs - delta)).astype(jnp.bfloat16)
            dv_sum[:end, lanes] += nn_dot(probs.astype(jnp.bfloat16), grads)
            dk_sum[:end, lanes] += nn_dot(d_scores, queries)
            dq_all[at:end, lanes] = tn_dot(d_scores, keys[:end]) * 0.125
    dq = turn(dq_all[...], cos[...], -low[...], -high[...]).astype(jnp.bfloat16)
    dk = turn(dk_sum[...], cos[...], -low[...], -high[...]).astype(jnp.bfloat16)
    dv = dv_sum[...].astype(jnp.bfloat16)
    for part, piece in enumerate((dq, dk, dv)):
        at = part * 128
        d_qkv[:, at : at + 128] = piece
        sums[:, at : at + 128] = jnp.sum(piece.astype(jnp.float32), axis=0, keepdims=True)


def run_attend_back(qkv, d_ctx, lse, tables):
    length, cols = qkv.shape
    groups = cols // 384
    wide = pltpu.VMEM((length, 128), jnp.float32)
    return call(
        attend_back_body,
        "attend_back",
        (groups,),
        [
            (qkv, (length, 128), lambda i: (0, 3 * i)),
            (qkv, (length, 128), lambda i: (0, 3 * i + 1)),
            (qkv, (length, 128), lambda i: (0, 3 * i + 2)),
            (d_ctx, (length, 128), lambda i: (0, i)),
            (lse, (1, 8, length), lambda i: (i, 0, 0)),
        ]
        + [whole(t) for t in tables],
        [
            ((length, cols), jnp.bfloat16, (length, 384), lambda i: (0, i)),
            ((1, cols), jnp.float32, (1, 384), lambda i: (0, i)),
        ],
        [wide, wide, wide],
    )


def norm_back_body(x, d_qkv, d_up, vecs, *rest):
    part, sums, w_qkv, w_up = rest[16:]

    @pl.when(pl.program_id(0) == 0)
    def _():
        assemble(rest[:8], w_qkv)
        assemble(rest[8:16], w_up)
        sums[...] = jnp.zeros_like(sums)

    hat, inverse = normalised(x[...].astype(jnp.float32))
    d_attn = nt_dot(d_qkv[...], w_qkv[...])
    d_mlp = nt_dot(d_up[...], w_up[...])
    for row, term in enumerate((d_attn * hat, d_mlp * hat, d_attn, d_mlp)):
        sums[row : row + 1, :] += jnp.sum(term, axis=0, keepdims=True)
    d_hat = d_attn * vecs[0:1, :] + d_mlp * vecs[2:3, :]
    along = jnp.mean(d_hat * hat, axis=-1, keepdims=True)
    level = jnp.mean(d_hat, axis=-1, keepdims=True)
    part[...] = (inverse * (d_hat - level - hat * along)).astype(jnp.bfloat16)


def run_norm_back(source, d_qkv, d_up, vecs, narrow, broad, at, rows):
    x, first = source
    width = x.shape[1]
    n_qkv, n_up = d_qkv.shape[1] // 4, d_up.shape[1] // 4
    return call(
        norm_back_body,
        "norm_back",
        (rows // ROW_BLOCK,),
        [rows_of(x, first), rows_of(d_qkv, at), rows_of(d_up, at), whole(vecs)]
        + matrix(narrow, n_qkv, 0)
        + matrix(broad, n_up, 0),
        [
            ((rows, width), jnp.bfloat16, (ROW_BLOCK, width), lambda i: (i, 0)),
            ((8, width), jnp.float32, (8, width), lambda i: (0, 0)),
        ],
        [room(narrow, n_qkv), room(broad, n_up)],
    )


def weight_grad_body(cuts, *refs):
    a_refs, b_refs, rest = refs[: sum(cuts)], refs[sum(cuts) :], refs[sum(cuts) + 2 :]
    keep, send, turned_one, turned_two = rest
    groups = (a_refs[: cuts[0]], a_refs[cuts[0] :])

    @pl.when(pl.program_id(0) == 0)
    def _():
        for group, turned in zip(groups, (turned_one, turned_two)):
            at = 0
            for ref in group:
                turned[:, at : at + ref.shape[0]] = ref[...].T
                at += ref.shape[0]

    at = 0
    rows = keep.shape[2]
    for turned, right in zip((turned_one, turned_two), b_refs[:2]):
        size = right.shape[1]
        grad = nn_dot(turned[...], right[...]).astype(jnp.bfloat16)
        for side in range(2):
            first = 2 * side * rows
            keep[0, side, :, at : at + size] = grad[first : first + rows]
            send[0, side, :, at : at + size] = grad[first + rows : first + 2 * rows]
        at += size


def run_weight_grad(lefts, rights):
    length, width = rights[0].shape[0], lefts[0][0].shape[1]
    sizes = [right.shape[1] // 4 for right in rights]
    shape = (4, 2, width // 4, sum(sizes))
    out = (shape, jnp.bfloat16, (1,) + shape[1:], lambda i: (i, 0, 0, 0))
    turned = pltpu.VMEM((width, length), jnp.bfloat16)
    return call(
        partial(weight_grad_body, tuple(len(group) for group in lefts)),
        "weight_grad",
        (4,),
        [whole(left) for group in lefts for left in group]
        + [(r, (length, n), lambda i: (0, i)) for r, n in zip(rights, sizes)],
        [out, out],
        [turned, turned],
    )


def turn_tables(length):
    cosine, sine_tab = rotary_tables(length)
    zero = jnp.zeros_like(sine_tab)
    rest = jnp.zeros((length, 64 - ROT), jnp.float32)
    cos = jnp.concatenate([cosine, cosine, rest + 1.0], axis=1)
    low = jnp.concatenate([zero, sine_tab, rest], axis=1)
    high = jnp.concatenate([-sine_tab, zero, rest], axis=1)
    return tuple(jnp.concatenate([t, t], axis=1) for t in (cos, low, high))


def by_sequence(
    acts_in, cotangent, norm_gains, vec_bias, w_qkv, b_qkv, w_out, w_up, b_up, w_down
):
    section = lax.axis_index("section")
    across = lax.axis_index("dp")
    along = lax.axis_index("tensor")
    first_section = section == 0
    width = acts_in.shape[3]
    rows = w_qkv.shape[1]
    positions = acts_in.shape[1]
    length = 4 * positions
    heads = b_qkv.shape[1]
    bf = jnp.bfloat16

    qkv_halves = (
        w_qkv[0].reshape(rows, 2, 2, 3, 64).transpose(1, 0, 3, 2, 4).reshape(2, rows, -1)
    )
    out_halves = w_out[0].T.reshape(rows, 2, -1).transpose(1, 0, 2)
    up_halves = w_up[0].reshape(rows, 2, -1).transpose(1, 0, 2)
    down_halves = w_down[0].T.reshape(rows, 2, -1).transpose(1, 0, 2)
    n_qkv, n_out, n_up = qkv_halves.shape[2], out_halves.shape[2], up_halves.shape[2]

    def both_layers(halves):
        keep = pick(halves, section)
        got = swap(pick(halves, 1 - section), "section", 1)
        return jnp.where(first_section, keep, got), jnp.where(first_section, got, keep)

    small = jnp.concatenate(
        [
            norm_gains[0].reshape(-1),
            vec_bias[0].reshape(-1),
            b_qkv[0].reshape(-1).astype(jnp.float32),
            b_up[0].reshape(-1).astype(jnp.float32),
        ]
    )
    other = swap(small, "section", 1)
    small = jnp.where(first_section, jnp.stack([small, other]), jnp.stack([other, small]))
    small = jnp.stack([small, swap(small, "dp", 1)])
    small = jnp.concatenate([small, swap(small, "dp", 2)])
    small = jnp.stack(
        [small, ring(small, "tensor", 1), ring(small, "tensor", -1), ring(small, "tensor", 2)]
    )

    narrow = jnp.stack([jnp.concatenate([qkv_halves[h], out_halves[h]], axis=1) for h in (0, 1)])
    broad = jnp.stack([jnp.concatenate([up_halves[h], down_halves[h]], axis=1) for h in (0, 1)])
    narrow_shards = both_layers(narrow)
    acts = exchange(acts_in[:, :, 0, :], along).reshape(length, width)
    acts = relative(acts, across)
    broad_shards = both_layers(broad)

    mats = [(gather_across_first(narrow_shards[0]), gather_along_first(broad_shards[0]))]
    later = after((narrow_shards[1], broad_shards[1]), mats[0][1][:4])
    mats.append((gather_across_first(later[0]), gather_along_first(later[1])))

    share = norm_gains.shape[2]
    vec_part = small[..., : 6 * share].reshape(4, 4, 2, 6, share)
    offsets = jnp.array(FAR_ORDER, jnp.int32)
    order = jnp.stack([pick(offsets, (k - along) % 4) for k in range(4)])
    vec_part = jnp.stack([pick(vec_part, order[k]) for k in range(4)])
    vecs_full = vec_part.transpose(2, 3, 1, 0, 4).reshape(2, 6, width)
    at = 6 * share
    share_q = b_qkv.shape[2]
    dp_order = [jnp.bitwise_xor(across, k) for k in range(4)]
    qkv_bias = small[..., at : at + heads * share_q].reshape(4, 4, 2, heads, share_q)
    qkv_bias = jnp.stack([pick(qkv_bias, i, 1) for i in dp_order], axis=1)
    qkv_bias = qkv_bias.transpose(2, 0, 3, 1, 4).reshape(2, 4, 2, heads // 2, 3, 64)
    qkv_bias = pick(qkv_bias, section, 2).transpose(0, 1, 3, 2, 4).reshape(2, 1, -1)
    at += heads * share_q
    bias_rows, share_u = b_up.shape[1], b_up.shape[2]
    up_bias = small[..., at : at + bias_rows * share_u].reshape(4, 4, 2, bias_rows, share_u)
    up_bias = jnp.stack([pick(up_bias, i, 1) for i in dp_order], axis=1)
    up_bias = up_bias.transpose(2, 0, 3, 1, 4).reshape(2, 4, 2, bias_rows // 2, 4 * share_u)
    up_bias = pick(up_bias, section, 2).reshape(2, 1, -1)
    zero_rows = jnp.zeros((4, width), jnp.float32)

    tables = turn_tables(length)
    chunk = length // CHUNKS
    starts = [i * chunk for i in range(CHUNKS)]

    sources = [(acts, a) for a in starts]
    inputs = [acts[a : a + chunk] for a in starts]
    kept = []
    grads_in = None
    for layer in (0, 1):
        narrow, broad = mats[layer]
        full = vecs_full[layer]
        vecs = jnp.concatenate(
            [full[0:1], full[2:3], full[1:2], full[3:4], zero_rows], axis=0
        )
        first = ()
        for i in range(CHUNKS):
            first = run_qkv(
                sources[i], vecs, qkv_bias[layer], tables, narrow, starts[i], chunk, first
            )
        ln_a, ln_m, qkv = first
        if layer == 1:
            qkv = after(qkv, grads_in)
        ctx, lse = run_attend(qkv)
        if layer == 0:
            given = after(cotangent[:, :, 0, :], ctx, mats[1][1][:4])
            grads_in = exchange(given, along).reshape(length, width)
            grads_in = relative(grads_in, across)
        outs, first = [], ()
        for i in range(CHUNKS):
            *first, part = run_mlp(
                ctx, ln_m, up_bias[layer], narrow, broad, starts[i], chunk, first
            )
            got = swap(part, "section", 1)
            total = part.astype(jnp.float32) + got.astype(jnp.float32)
            total = inputs[i].astype(jnp.float32) + total + (full[4] + full[5])
            outs.append(total.astype(bf))
        kept.append((sources, vecs, ln_a, ln_m, qkv, ctx, lse, *first, outs))
        inputs = outs
        sources = [(out, 0) for out in outs]

    def deliver(values):
        return exchange(relative(values, across).reshape(4, positions, width), along)

    acts_local = deliver(
        jnp.where(first_section, jnp.concatenate(kept[0][9]), jnp.concatenate(kept[1][9]))
    )

    sources = [(grads_in, a) for a in starts]
    upstream = [grads_in[a : a + chunk] for a in starts]
    whole_up = [grads_in]
    reduced = [None, None]
    vectors = [None, None]
    layer_grads = [None, None]
    for layer in (1, 0):
        narrow, broad = mats[layer]
        x_list, vecs, ln_a, ln_m, qkv, ctx, lse, act, slope, _ = kept[layer]
        first, sum_up, sum_g = (), 0.0, 0.0
        if layer == 0:
            sources = [(after(down, acts_local), at) for down, at in sources]
        for i in range(CHUNKS):
            *first, up_term, g_term = run_mlp_back(
                sources[i], slope, narrow, broad, starts[i], chunk, ctx.shape[1], first
            )
            sum_up, sum_g = sum_up + up_term, sum_g + g_term
        d_up, d_ctx = first
        if layer == 0:
            keep, send = run_weight_grad([[ln_m], whole_up], [d_up, act])
            broad_sum = add_wide(keep, swap(send, "dp", 1))
            d_ctx = after(d_ctx, keep)
        d_qkv, sum_qkv = run_attend_back(qkv, d_ctx, lse, tables)
        downs, norm_sums = [], 0.0
        for i in range(CHUNKS):
            part, sums = run_norm_back(
                x_list[i], d_qkv, d_up, vecs, narrow, broad, starts[i], chunk
            )
            got = swap(part, "section", 1)
            total = part.astype(jnp.float32) + got.astype(jnp.float32)
            downs.append((upstream[i].astype(jnp.float32) + total).astype(bf))
            norm_sums = norm_sums + sums[:4]
        if layer == 1:
            keep, send = run_weight_grad([[ln_m], whole_up], [d_up, act])
            broad_sum = add_wide(keep, swap(send, "dp", 1))
        keep, send = run_weight_grad([[ln_a], whole_up], [d_qkv, ctx])
        narrow_sum = add_wide(keep, swap(send, "dp", 1))
        reduced[layer] = (reduce_across_last(narrow_sum), reduce_along_last(broad_sum))
        vectors[layer] = (norm_sums, sum_g, sum_qkv, sum_up)
        layer_grads[layer] = jnp.concatenate(downs, axis=0)
        upstream = downs
        whole_up = downs
        sources = [(down, 0) for down in downs]

    grad_local = deliver(jnp.where(first_section, layer_grads[0], layer_grads[1]))

    def whole_layer(first, second):
        keep = jnp.where(first_section, first, second)
        got = swap(jnp.where(first_section, second, first), "section", 1)
        keep, got = keep.astype(jnp.float32), got.astype(jnp.float32)
        return jnp.where(first_section, jnp.stack([keep, got], 1), jnp.stack([got, keep], 1))

    narrow_out = whole_layer(reduced[0][0], reduced[1][0])
    broad_out = whole_layer(reduced[0][1], reduced[1][1])
    grad_qkv = narrow_out[..., :n_qkv].reshape(rows, 2, 3, 2, 64)
    grad_qkv = grad_qkv.transpose(0, 1, 3, 2, 4).reshape(rows, -1)
    grad_out = narrow_out[..., n_qkv:].reshape(rows, -1).T
    grad_up = broad_out[..., :n_up].reshape(rows, -1)
    grad_down = broad_out[..., n_up:].reshape(rows, -1).T

    flat = []
    for norm_sums, sum_g, sum_qkv, sum_up in vectors:
        feature = relative(jnp.concatenate([norm_sums, sum_g], axis=0), across)
        q_sum = sum_qkv.reshape(4, 3, 2, 64).transpose(0, 2, 1, 3).reshape(4, -1)
        both = jnp.concatenate([q_sum, sum_up.reshape(4, -1)], axis=1)
        both = jnp.stack([pick(both, order[k]) for k in range(4)])
        flat.append(jnp.concatenate([feature.reshape(-1), both.reshape(-1)]))
    flat = jnp.stack(flat)
    for axis, bit in (("dp", 1), ("dp", 2), ("tensor", 1), ("tensor", 2)):
        flat = flat + swap(flat, axis, bit)
    keep = pick(flat, section)
    mine = pick(flat, 1 - section)
    got = swap(mine, "section", 1)
    n_feature = 5 * width
    feature_own = keep[:n_feature].reshape(5, width)
    feature = feature_own[:4] + got[: 4 * width].reshape(4, width)
    place_at = (across * 4 + along) * share
    gain_share = lax.dynamic_slice_in_dim(feature[:2], place_at, share, 1)
    shifts = jnp.concatenate([feature[2:4], feature_own[4:5], feature_own[4:5]], axis=0)
    bias_share = lax.dynamic_slice_in_dim(shifts, place_at, share, 1)
    low_half = jnp.where(first_section, keep, got)[n_feature:].reshape(4, -1)
    high_half = jnp.where(first_section, got, keep)[n_feature:].reshape(4, -1)
    halves = jnp.stack([pick(low_half, along), pick(high_half, along)])
    n_head = (heads // 2) * 192
    head_sums = halves[:, :n_head].reshape(heads, 192)
    head_share = lax.dynamic_slice_in_dim(head_sums, across * share_q, share_q, 1)
    unit_sums = halves[:, n_head:].reshape(bias_rows, 4 * share_u)
    unit_share = lax.dynamic_slice_in_dim(unit_sums, across * share_u, share_u, 1)
    return (
        acts_local[None, :, :, None],
        grad_local[None, :, :, None],
        gain_share[None],
        bias_share[None],
        grad_qkv[None],
        head_share[None],
        grad_out[None],
        grad_up[None],
        unit_share[None],
        grad_down[None],
    )


def fits(mesh, args):
    acts_in, b_qkv = args[0], args[5]
    sizes = dict(mesh.shape)
    return (
        sizes["section"] == 2
        and sizes["dp"] == 4
        and sizes["tensor"] == MICRO
        and MICRO == 4
        and acts_in.shape[2] == sizes["dp"]
        and b_qkv.shape[1] == 16
        and b_qkv.shape[2] == 192
        and acts_in.shape[1] % (CHUNKS * ROW_BLOCK) == 0
    )


def solution(mesh):
    placed = (
        P(None, "tensor", "dp", None),
        P(None, "tensor", "dp", None),
        P("section", None, ("dp", "tensor")),
        P("section", None, ("dp", "tensor")),
        P("section", "dp", "tensor"),
        P("section", "tensor", "dp"),
        P("section", "tensor", "dp"),
        P("section", "dp", "tensor"),
        P("section", "tensor", "dp"),
        P("section", "tensor", "dp"),
    )
    def wrap(body):
        return jax.shard_map(
            body,
            mesh=mesh,
            in_specs=placed,
            out_specs=(
                P("section", None, "tensor", "dp", None),
                P("section", None, "tensor", "dp", None),
                P("section", None, ("dp", "tensor")),
                P("section", None, ("dp", "tensor")),
                P("section", "dp", "tensor"),
                P("section", "tensor", "dp"),
                P("section", "tensor", "dp"),
                P("section", "dp", "tensor"),
                P("section", "tensor", "dp"),
                P("section", "tensor", "dp"),
            ),
            check_vma=False,
        )

    return lambda *args: wrap(by_sequence if fits(mesh, args) else local)(*args)
```

```python
from functools import partial
import math

import jax
import jax.numpy as jnp
from jax import lax
from jax.experimental import pallas as pl
from jax.experimental.pallas import tpu as pltpu
from jax.sharding import PartitionSpec as P

ROT = 16
QBLOCK = 512
MICRO = 4


NORM_EPS = 1e-05
ROPE_BASE = 10000.0
MASK_FILL = -1e30


def from_behind(value, axis, by):
    length = lax.axis_size(axis)
    pairs = [(i, i + by) for i in range(length) if 0 <= i + by < length]
    return lax.ppermute(value, axis, pairs)


def layer_norm(values, norm_gain, norm_shift):
    average = jnp.mean(values, axis=-1, keepdims=True)
    centred = values - average
    variance = jnp.mean(centred * centred, axis=-1, keepdims=True)
    return centred * lax.rsqrt(variance + NORM_EPS) * norm_gain + norm_shift


def both_norms(values, gain_attn, shift_attn, gain_mlp, shift_mlp):
    return (layer_norm(values, gain_attn, shift_attn), layer_norm(values, gain_mlp, shift_mlp))


def rotary_tables(length):
    half_rot = ROT // 2
    frequency = jnp.exp(
        jnp.arange(half_rot, dtype=jnp.float32) * (-2.0 * math.log(ROPE_BASE) / ROT)
    )
    angles = jnp.arange(length, dtype=jnp.float32)[:, None] * frequency[None, :]
    return (jnp.cos(angles), jnp.sin(angles))


def rotate(values, cosine, sine_tab):
    half_rot = ROT // 2
    low_half = values[..., :half_rot]
    high_half = values[..., half_rot:ROT]
    return jnp.concatenate(
        [
            low_half * cosine - high_half * sine_tab,
            high_half * cosine + low_half * sine_tab,
            values[..., ROT:],
        ],
        axis=-1,
    )


def rotate_back(grads_rot, cosine, sine_tab):
    half_rot = ROT // 2
    low_half = grads_rot[..., :half_rot]
    high_half = grads_rot[..., half_rot:ROT]
    return jnp.concatenate(
        [
            low_half * cosine + high_half * sine_tab,
            high_half * cosine - low_half * sine_tab,
            grads_rot[..., ROT:],
        ],
        axis=-1,
    )


def causal_scores(queries, key_rows, first_row, score_scale):
    block_rows = queries.shape[0]
    last_row = key_rows.shape[0]
    scores = (
        jnp.einsum("qshd,kshd->shqk", queries, key_rows, preferred_element_type=jnp.float32)
        * score_scale
    )
    row_pos = first_row + jnp.arange(block_rows, dtype=jnp.int32)
    col_pos = jnp.arange(last_row, dtype=jnp.int32)
    allowed = col_pos[None, :] <= row_pos[:, None]
    return (scores, allowed)


def attend(queries, key_rows, val_rows):
    length = queries.shape[0]
    block_rows = min(QBLOCK, length)
    score_scale = queries.shape[-1] ** (-0.5)
    outputs = []
    totals = []
    for block_index in range(length // block_rows):
        first_row = block_index * block_rows
        last_row = first_row + block_rows
        scores, allowed = causal_scores(
            queries[first_row:last_row], key_rows[:last_row], first_row, score_scale
        )
        scores = jnp.where(allowed, scores, MASK_FILL)
        highest = jnp.max(scores, axis=-1, keepdims=True)
        exponent = jnp.exp(scores - highest)
        denominator = jnp.sum(exponent, axis=-1, keepdims=True)
        probability = (exponent / denominator).astype(jnp.bfloat16)
        block_out = jnp.einsum(
            "shqk,kshd->qshd", probability, val_rows[:last_row], preferred_element_type=jnp.float32
        )
        outputs.append(block_out.astype(jnp.bfloat16))
        totals.append((highest + jnp.log(denominator))[..., 0])
    context = jnp.concatenate(outputs, axis=0)
    return (context.reshape(length, context.shape[1], -1), jnp.concatenate(totals, axis=-1))


def attend_back(queries, key_rows, val_rows, d_context, log_total):
    length = queries.shape[0]
    block_rows = min(QBLOCK, length)
    score_scale = queries.shape[-1] ** (-0.5)
    grad_query_list = []
    grad_keys = jnp.zeros(queries.shape, jnp.float32)
    grad_vals = jnp.zeros(queries.shape, jnp.float32)
    for block_index in range(length // block_rows):
        first_row = block_index * block_rows
        last_row = first_row + block_rows
        query_block = queries[first_row:last_row]
        scores, allowed = causal_scores(query_block, key_rows[:last_row], first_row, score_scale)
        probability = jnp.where(
            allowed, jnp.exp(scores - log_total[:, :, first_row:last_row, None]), 0.0
        )
        d_block = d_context[first_row:last_row]
        d_prob = jnp.einsum(
            "qshd,kshd->shqk", d_block, val_rows[:last_row], preferred_element_type=jnp.float32
        )
        delta = jnp.sum(probability * d_prob, axis=-1, keepdims=True)
        d_scores = (probability * (d_prob - delta)).astype(jnp.bfloat16)
        grad_query_list.append(
            jnp.einsum(
                "shqk,kshd->qshd", d_scores, key_rows[:last_row], preferred_element_type=jnp.float32
            )
            * score_scale
        )
        grad_keys = grad_keys.at[:last_row].add(
            jnp.einsum("shqk,qshd->kshd", d_scores, query_block, preferred_element_type=jnp.float32)
            * score_scale
        )
        grad_vals = grad_vals.at[:last_row].add(
            jnp.einsum(
                "shqk,qshd->kshd",
                probability.astype(jnp.bfloat16),
                d_block,
                preferred_element_type=jnp.float32,
            )
        )
    return (jnp.concatenate(grad_query_list, axis=0), grad_keys, grad_vals)


def local(acts_in, cotangent, norm_gains, vec_bias, w_qkv, b_qkv, w_out, w_up, b_up, w_down):
    section_index = lax.axis_index("section")
    own_start = lax.axis_index("tensor") * acts_in.shape[1]
    local_len = acts_in.shape[1]
    seq_count = acts_in.shape[2]
    model_width = acts_in.shape[3]
    length = local_len * lax.axis_size("tensor")
    all_rows = length * seq_count
    gain_full, bias_full = (
        lax.all_gather(norm_gains[0], ("dp", "tensor"), axis=1, tiled=True),
        lax.all_gather(vec_bias[0], ("dp", "tensor"), axis=1, tiled=True),
    )
    mat_qkv, bias_qkv, mat_out, mat_up, bias_up, mat_down = (
        lax.all_gather(w_qkv[0], "dp", axis=0, tiled=True),
        lax.all_gather(b_qkv[0], "dp", axis=1, tiled=True),
        lax.all_gather(w_out[0], "dp", axis=1, tiled=True),
        lax.all_gather(w_up[0], "dp", axis=0, tiled=True),
        lax.all_gather(b_up[0], "dp", axis=1, tiled=True),
        lax.all_gather(w_down[0], "dp", axis=1, tiled=True),
    )
    head_count = bias_qkv.shape[0]
    head_dim = bias_qkv.shape[1] // 3
    qkv_shift = bias_qkv.reshape(-1).astype(jnp.float32)
    up_shift = bias_up.reshape(-1).astype(jnp.float32)
    cosine, sine_tab = rotary_tables(length)
    cosine = cosine[:, None, None, :]
    sine_tab = sine_tab[:, None, None, :]
    received = jnp.zeros_like(acts_in[0])
    stash_list = []
    out_list = []
    for moment in range(MICRO + 1):
        own_rows = acts_in[min(moment, MICRO - 1)]
        inputs = jnp.where(section_index == 0, own_rows, received)
        forward_gathered = lax.all_gather(inputs, "tensor", axis=0, tiled=True)
        full_attn, full_mlp = both_norms(
            forward_gathered.astype(jnp.float32),
            gain_full[0],
            bias_full[0],
            gain_full[1],
            bias_full[1],
        )
        forward_normed_attn = full_attn.astype(jnp.bfloat16)
        forward_normed_mlp = full_mlp.astype(jnp.bfloat16)
        forward_flat_attn = forward_normed_attn.reshape(all_rows, model_width)
        forward_flat_mlp = forward_normed_mlp.reshape(all_rows, model_width)
        projected = (
            jnp.dot(forward_flat_attn, mat_qkv, preferred_element_type=jnp.float32) + qkv_shift
        )
        projected = projected.reshape(length, seq_count, head_count, 3, head_dim)
        forward_queries = rotate(projected[:, :, :, 0], cosine, sine_tab).astype(jnp.bfloat16)
        forward_key_rows = rotate(projected[:, :, :, 1], cosine, sine_tab).astype(jnp.bfloat16)
        forward_val_rows = projected[:, :, :, 2].astype(jnp.bfloat16)
        forward_context, forward_log_total = attend(
            forward_queries, forward_key_rows, forward_val_rows
        )
        forward_up_proj = (
            jnp.dot(forward_flat_mlp, mat_up, preferred_element_type=jnp.float32) + up_shift
        )
        forward_activated = jax.nn.gelu(forward_up_proj, approximate=False).astype(jnp.bfloat16)
        active_rows = forward_activated.reshape(length, seq_count, -1)
        context_part = forward_context.reshape(lax.axis_size("tensor") * local_len * seq_count, -1)
        active_part = active_rows.reshape(lax.axis_size("tensor") * local_len * seq_count, -1)
        summed = jnp.dot(context_part, mat_out, preferred_element_type=jnp.float32) + jnp.dot(
            active_part, mat_down, preferred_element_type=jnp.float32
        )
        mixed_sum = lax.psum_scatter(
            summed.reshape(lax.axis_size("tensor") * local_len, seq_count, model_width),
            "tensor",
            scatter_dimension=0,
            tiled=True,
        )
        result = inputs.astype(jnp.float32) + mixed_sum + bias_full[2] + bias_full[3]
        forward_stashed = (
            forward_gathered,
            forward_normed_attn,
            forward_normed_mlp,
            forward_queries,
            forward_key_rows,
            forward_val_rows,
            forward_context,
            forward_log_total,
            forward_up_proj,
            forward_activated,
        )
        result, stashed = (result.astype(jnp.bfloat16), forward_stashed)
        stash_list.append(stashed)
        out_list.append(result)
        if moment < MICRO:
            received = from_behind(result, "section", 1)
    stash_all = jax.tree.map(lambda *parts: jnp.stack(parts), *stash_list)
    acts_local = lax.dynamic_slice_in_dim(jnp.stack(out_list), section_index, MICRO, 0)
    back_received = jnp.zeros_like(cotangent[0])
    grad_list = []
    weight_sums = None
    vector_sums = None
    for moment in range(MICRO + 1):
        micro_index = moment - 1 + section_index
        is_valid = (micro_index >= 0) & (micro_index < MICRO)
        source_clock = jnp.clip(micro_index + section_index, 0, MICRO)
        stashed = jax.tree.map(
            lambda part: lax.dynamic_index_in_dim(part, source_clock, 0, keepdims=False), stash_all
        )
        upstream = jnp.where(section_index == 1, cotangent[min(moment, MICRO - 1)], back_received)
        (
            gathered,
            normed_attn,
            normed_mlp,
            queries,
            key_rows,
            val_rows,
            context,
            log_total,
            up_proj,
            activated,
        ) = stashed
        backward_inputs = lax.dynamic_slice_in_dim(gathered, own_start, local_len, 0)
        upstream_rows = lax.all_gather(upstream, "tensor", axis=0, tiled=True)
        flat_grad = upstream_rows.reshape(all_rows, model_width)
        d_context = jnp.dot(flat_grad, mat_out.T, preferred_element_type=jnp.float32).astype(
            jnp.bfloat16
        )
        d_context = d_context.reshape(length, seq_count, head_count, head_dim)
        d_active = jnp.dot(flat_grad, mat_down.T, preferred_element_type=jnp.float32)
        _, gelu_pullback = jax.vjp(partial(jax.nn.gelu, approximate=False), up_proj)
        d_up = gelu_pullback(d_active)[0].astype(jnp.bfloat16)
        grad_query, grad_key, grad_val = attend_back(
            queries, key_rows, val_rows, d_context, log_total
        )
        d_qkv = jnp.stack(
            [
                rotate_back(grad_query, cosine, sine_tab),
                rotate_back(grad_key, cosine, sine_tab),
                grad_val,
            ],
            axis=3,
        ).astype(jnp.bfloat16)
        d_qkv_flat = d_qkv.reshape(all_rows, -1)
        d_qkv_rows = d_qkv.reshape(length, seq_count, -1)
        d_up_rows = d_up.reshape(length, seq_count, -1)
        flat_attn = normed_attn.reshape(all_rows, model_width)
        flat_mlp = normed_mlp.reshape(all_rows, model_width)
        weight_terms = (
            jnp.einsum("tc,te->ce", flat_attn, d_qkv_flat, preferred_element_type=jnp.float32),
            jnp.sum(d_qkv_flat.astype(jnp.float32), axis=0).reshape(bias_qkv.shape),
            jnp.einsum(
                "tc,te->ce",
                context.reshape(all_rows, -1),
                flat_grad,
                preferred_element_type=jnp.float32,
            ),
            jnp.einsum("tc,te->ce", flat_mlp, d_up, preferred_element_type=jnp.float32),
            jnp.sum(d_up.astype(jnp.float32), axis=0).reshape(bias_up.shape),
            jnp.einsum("tc,te->ce", activated, flat_grad, preferred_element_type=jnp.float32),
        )
        attn_part = d_qkv_rows.reshape(lax.axis_size("tensor") * local_len * seq_count, -1)
        mlp_part = d_up_rows.reshape(lax.axis_size("tensor") * local_len * seq_count, -1)
        joined = jnp.concatenate(
            [
                jnp.dot(attn_part, mat_qkv.T, preferred_element_type=jnp.float32),
                jnp.dot(mlp_part, mat_up.T, preferred_element_type=jnp.float32),
            ],
            axis=-1,
        )
        d_normed = lax.psum_scatter(
            joined.reshape(lax.axis_size("tensor") * local_len, seq_count, 2 * model_width).astype(
                jnp.bfloat16
            ),
            "tensor",
            scatter_dimension=0,
            tiled=True,
        ).astype(jnp.float32)
        _, norm_pullback = jax.vjp(
            both_norms,
            backward_inputs.astype(jnp.float32),
            gain_full[0],
            bias_full[0],
            gain_full[1],
            bias_full[1],
        )
        d_local, d_gain_attn, d_shift_attn, d_gain_mlp, d_shift_mlp = norm_pullback(
            (d_normed[..., :model_width], d_normed[..., model_width:])
        )
        upstream_float = upstream.astype(jnp.float32)
        d_inputs = (upstream_float + d_local).astype(jnp.bfloat16)
        out_shift = jnp.sum(upstream_float, axis=(0, 1))
        vector_terms = (
            jnp.stack([d_gain_attn, d_gain_mlp]),
            jnp.stack([d_shift_attn, d_shift_mlp, out_shift, out_shift]),
        )
        d_inputs, weight_terms, vector_terms = (d_inputs, weight_terms, vector_terms)
        grad_list.append(d_inputs)
        if moment < MICRO:
            back_received = from_behind(d_inputs, "section", -1)
        weight_terms = tuple((jnp.where(is_valid, term, 0.0) for term in weight_terms))
        vector_terms = tuple((jnp.where(is_valid, term, 0.0) for term in vector_terms))
        if moment == 0:
            weight_sums = tuple(weight_terms)
            vector_sums = vector_terms
        else:
            weight_sums = tuple((a + b for a, b in zip(weight_sums, weight_terms)))
            vector_sums = tuple((a + b for a, b in zip(vector_sums, vector_terms)))
    sum_qkv, sum_bqkv, sum_out, sum_up, sum_bup, sum_down = weight_sums
    share_qkv, share_bqkv, share_out, share_up, share_bup, share_down = (
        lax.psum_scatter(
            sum_qkv.astype(jnp.bfloat16), "dp", scatter_dimension=0, tiled=True
        ).astype(jnp.float32),
        lax.psum_scatter(
            sum_bqkv.astype(jnp.bfloat16), "dp", scatter_dimension=1, tiled=True
        ).astype(jnp.float32),
        lax.psum_scatter(
            sum_out.astype(jnp.bfloat16), "dp", scatter_dimension=1, tiled=True
        ).astype(jnp.float32),
        lax.psum_scatter(sum_up.astype(jnp.bfloat16), "dp", scatter_dimension=0, tiled=True).astype(
            jnp.float32
        ),
        lax.psum_scatter(
            sum_bup.astype(jnp.bfloat16), "dp", scatter_dimension=1, tiled=True
        ).astype(jnp.float32),
        lax.psum_scatter(
            sum_down.astype(jnp.bfloat16), "dp", scatter_dimension=1, tiled=True
        ).astype(jnp.float32),
    )
    grad_local = lax.dynamic_slice_in_dim(jnp.stack(grad_list), 1 - section_index, MICRO, 0)
    gain_share, bias_share = (
        lax.psum_scatter(vector_sums[0], ("dp", "tensor"), scatter_dimension=1, tiled=True),
        lax.psum_scatter(vector_sums[1], ("dp", "tensor"), scatter_dimension=1, tiled=True),
    )
    return (
        acts_local[None],
        grad_local[None],
        gain_share[None],
        bias_share[None],
        share_qkv[None],
        share_bqkv[None],
        share_out[None],
        share_up[None],
        share_bup[None],
        share_down[None],
    )


FAR_ORDER = (0, 2, 3, 1)
VMEM_LIMIT = 60 * 1024 * 1024
ROW_BLOCK = 256
CHUNKS = 2
MICROSECOND = 1_000_000_000


def ring(value, axis, by):
    length = lax.axis_size(axis)
    return lax.ppermute(value, axis, [(i, (i + by) % length) for i in range(length)])


def swap(value, axis, bit):
    length = lax.axis_size(axis)
    return lax.ppermute(value, axis, [(i, i ^ bit) for i in range(length)])


def pick(value, index, axis=0):
    return lax.dynamic_index_in_dim(value, index, axis, keepdims=False)


def place(value, block, index):
    return lax.dynamic_update_index_in_dim(value, block, index, 0)


def relative(values, own):
    size = values.shape[-1] // 4
    picked = [
        lax.dynamic_slice_in_dim(values, jnp.bitwise_xor(own, k) * size, size, values.ndim - 1)
        for k in range(4)
    ]
    return jnp.concatenate(picked, axis=-1)


class Clock:
    def __init__(self):
        self.ended = ()

    def hold(self, value):
        return lax.optimization_barrier((value, self.ended))[0]

    def tick(self, *ended):
        self.ended = ended


def exchange_near(blocks, own, hold):
    half = blocks.shape[1] // 2
    far = pick(blocks, (own + 2) % 4)
    ahead = jnp.concatenate([pick(blocks, (own + 1) % 4), far[:half]], axis=0)
    behind = jnp.concatenate([pick(blocks, (own + 3) % 4), far[half:]], axis=0)
    return ring(hold(ahead), "tensor", 1), ring(hold(behind), "tensor", -1)


def exchange_far(near, hold):
    rows = near[0].shape[0] * 2 // 3
    first = ring(hold(near[0][rows:]), "tensor", 1)
    second = ring(hold(near[1][rows:]), "tensor", -1)
    return first, second


def exchanged(blocks, near, far, own):
    rows = blocks.shape[1]
    result = jnp.zeros_like(blocks)
    result = place(result, pick(blocks, own), own)
    result = place(result, near[0][:rows], (own + 3) % 4)
    result = place(result, near[1][:rows], (own + 1) % 4)
    return place(result, jnp.concatenate(far, axis=0), (own + 2) % 4)


def add_wide(left, right):
    return (left.astype(jnp.float32) + right.astype(jnp.float32)).astype(jnp.bfloat16)


def ring_first(blocks, hold):
    far = blocks[3]
    half = far.shape[0] // 2
    to_right = ring(hold(far[:half]), "tensor", 1)
    to_left = ring(hold(far[half:]), "tensor", -1)
    return to_right, to_left


def ring_second(blocks, got, hold):
    _, left, right, _ = blocks
    half = left.shape[0] // 2
    right = jnp.concatenate([add_wide(right[:half], got[0]), right[half:]], axis=0)
    left = jnp.concatenate([left[:half], add_wide(left[half:], got[1])], axis=0)
    return ring(hold(right), "tensor", 1), ring(hold(left), "tensor", -1)


def ring_total(own, got):
    total = own.astype(jnp.float32) + got[0].astype(jnp.float32) + got[1].astype(jnp.float32)
    return total.astype(jnp.bfloat16)


def normalised(x):
    average = jnp.mean(x, axis=-1, keepdims=True)
    centred = x - average
    variance = jnp.mean(centred * centred, axis=-1, keepdims=True)
    inverse = lax.rsqrt(variance + NORM_EPS)
    return centred * inverse, inverse


def nt_dot(left, right):
    return lax.dot_general(
        left, right, (((1,), (1,)), ((), ())), preferred_element_type=jnp.float32
    )


def tn_dot(left, right):
    return lax.dot_general(
        left, right, (((0,), (0,)), ((), ())), preferred_element_type=jnp.float32
    )


def nn_dot(left, right):
    return jnp.dot(left, right, preferred_element_type=jnp.float32)


def turn(values, cosine, low_sine, high_sine):
    lanes = values.shape[-1]
    return (
        values * cosine
        + pltpu.roll(values, ROT // 2, 1) * low_sine
        + pltpu.roll(values, lanes - ROT // 2, 1) * high_sine
    )


def call(body, name, flops, grid, ins, outs, scratch=(), filled=()):
    count = len(ins)

    def run(*refs):
        body(*refs[:count], *refs[count + len(filled) :])

    return pl.pallas_call(
        run,
        name=name,
        grid=grid,
        in_specs=[pl.BlockSpec(block, index) for _, block, index in ins]
        + [pl.BlockSpec(memory_space=pl.ANY)] * len(filled),
        out_specs=[pl.BlockSpec(block, index) for _, _, block, index in outs],
        out_shape=[jax.ShapeDtypeStruct(shape, kind) for shape, kind, _, _ in outs],
        scratch_shapes=list(scratch),
        input_output_aliases={count + i: i for i in range(len(filled))},
        cost_estimate=pl.CostEstimate(flops=flops, bytes_accessed=1 << 20, transcendentals=0),
        compiler_params=pltpu.CompilerParams(
            vmem_limit_bytes=VMEM_LIMIT, dimension_semantics=("arbitrary",) * len(grid)
        ),
    )(*[array for array, _, _ in ins], *filled)


def whole(array):
    return (array, array.shape, lambda *_: (0,) * array.ndim)


def matrix(pieces, size, block):
    shape = (2, pieces[0].shape[1], size)
    return [(piece, shape, lambda *_: (0, 0, block)) for piece in pieces]


def room(pieces, size):
    return pltpu.VMEM((4 * pieces[0].shape[1], 4 * size), jnp.bfloat16)


def assemble(refs, target):
    _, rows, size = refs[0].shape
    for core in range(2):
        for offset in range(4):
            for side in range(2):
                at = (2 * side + core) * rows
                target[at : at + rows, offset * size : (offset + 1) * size] = refs[
                    core * 4 + offset
                ][side]


def rows_of(array, first=0, block=ROW_BLOCK):
    base = first // block
    return (array, (block, array.shape[1]), lambda i: (i + base, 0))


def qkv_body(x, vecs, shift, cos, low, high, *rest):
    ln_a, ln_m, qkv, w = rest[8:]

    @pl.when(pl.program_id(0) == 0)
    def _():
        assemble(rest[:8], w)

    hat, _ = normalised(x[...].astype(jnp.float32))
    attn = (hat * vecs[0:1, :] + vecs[1:2, :]).astype(jnp.bfloat16)
    ln_a[...] = attn
    ln_m[...] = (hat * vecs[2:3, :] + vecs[3:4, :]).astype(jnp.bfloat16)
    out = nn_dot(attn, w[...]) + shift[...]
    for block in range(qkv.shape[1] // 384):
        for part in range(3):
            at = block * 384 + part * 128
            piece = out[:, at : at + 128]
            if part < 2:
                piece = turn(piece, cos[...], low[...], high[...])
            qkv[:, at : at + 128] = piece.astype(jnp.bfloat16)


def run_qkv(source, vecs, shift, tables, pieces, at, rows, filled):
    x, first = source
    width = x.shape[1]
    length = tables[0].shape[0]
    cols = shift.shape[1]
    bf = jnp.bfloat16
    base = at // ROW_BLOCK
    own = lambda i: (i + base, 0)
    return call(
        qkv_body,
        "norm_qkv",
        rows * 13 * MICROSECOND // 1024,
        (rows // ROW_BLOCK,),
        [rows_of(x, first), whole(vecs), whole(shift)]
        + [rows_of(t, at) for t in tables]
        + matrix(pieces, cols // 4, 0),
        [
            ((length, width), bf, (ROW_BLOCK, width), own),
            ((length, width), bf, (ROW_BLOCK, width), own),
            ((length, cols), bf, (ROW_BLOCK, cols), own),
        ],
        [room(pieces, cols // 4)],
        filled,
    )


def attend_body(q, k, v, ctx, lse):
    length = q.shape[0]
    step = ROW_BLOCK
    for head in range(2):
        lanes = slice(head * 64, head * 64 + 64)
        keys = k[:, lanes]
        vals = v[:, lanes]
        for at in range(0, length, step):
            end = at + step
            queries = q[at:end, lanes] * jnp.bfloat16(0.125)
            scores = nt_dot(queries, keys[:end])
            row = lax.broadcasted_iota(jnp.int32, (step, step), 0)
            col = lax.broadcasted_iota(jnp.int32, (step, step), 1)
            last = jnp.where(col <= row, scores[:, at:], MASK_FILL)
            scores = last if at == 0 else jnp.concatenate([scores[:, :at], last], axis=1)
            top = jnp.max(scores, axis=1, keepdims=True)
            power = jnp.exp(scores - top)
            total = jnp.sum(power, axis=1, keepdims=True)
            probs = (power * (1.0 / total)).astype(jnp.bfloat16)
            ctx[at:end, lanes] = nn_dot(probs, vals[:end]).astype(jnp.bfloat16)
            level = jnp.broadcast_to(top + jnp.log(total), (step, 128))
            lse[0, head : head + 1, at:end] = level.T[0:1]


def run_attend(qkv):
    length, cols = qkv.shape
    groups = cols // 384
    return call(
        attend_body,
        "attend",
        length * 19 * MICROSECOND // 1024,
        (groups,),
        [
            (qkv, (length, 128), lambda i: (0, 3 * i)),
            (qkv, (length, 128), lambda i: (0, 3 * i + 1)),
            (qkv, (length, 128), lambda i: (0, 3 * i + 2)),
        ],
        [
            ((length, groups * 128), jnp.bfloat16, (length, 128), lambda i: (0, i)),
            ((groups, 8, length), jnp.float32, (1, 8, length), lambda i: (i, 0, 0)),
        ],
    )


ERF_TOP = (
    0.00022905065861350646,
    0.0034082910107109506,
    0.050955695062380861,
    0.18520832239976145,
    1.128379143519084,
)
ERF_BOTTOM = (
    -1.1791602954361697e-7,
    0.000023547966471313185,
    0.0010179625278914885,
    0.014070470171167667,
    0.11098505178285362,
    0.49746925110067538,
    1.0,
)


def erf(x):
    x = jnp.clip(x, -3.7439211627767994, 3.7439211627767994)
    square = x * x
    top = jnp.full_like(x, ERF_TOP[0])
    for term in ERF_TOP[1:]:
        top = top * square + term
    bottom = jnp.full_like(x, ERF_BOTTOM[0])
    for term in ERF_BOTTOM[1:]:
        bottom = bottom * square + term
    return x * top / bottom


def mlp_body(ctx, ln_m, shift, *rest):
    act, slope, part, w_out, w_up, w_down = rest[24:]

    @pl.when(pl.program_id(0) == 0)
    def _():
        assemble(rest[:8], w_out)
        assemble(rest[8:16], w_up)
        assemble(rest[16:24], w_down)

    up = nn_dot(ln_m[...], w_up[...]) + shift[...]
    half_erf = 0.5 * erf(up * (2.0**-0.5)) + 0.5
    bell = jnp.exp(up * up * -0.5) * ((2.0 * math.pi) ** -0.5)
    active = (up * half_erf).astype(jnp.bfloat16)
    act[...] = active
    slope[...] = (half_erf + up * bell).astype(jnp.bfloat16)
    part[...] = (nt_dot(ctx[...], w_out[...]) + nt_dot(active, w_down[...])).astype(jnp.bfloat16)


def run_mlp(ctx, ln_m, shift, narrow, broad, at, rows, filled):
    length, width = ln_m.shape
    cols, heads = shift.shape[1], ctx.shape[1]
    bf = jnp.bfloat16
    base = at // ROW_BLOCK
    own = lambda i: (i + base, 0)
    return call(
        mlp_body,
        "mlp_out",
        rows * 32 * MICROSECOND // 1024,
        (rows // ROW_BLOCK,),
        [rows_of(ctx, at), rows_of(ln_m, at), whole(shift)]
        + matrix(narrow, heads // 4, 3)
        + matrix(broad, cols // 4, 0)
        + matrix(broad, cols // 4, 1),
        [
            ((length, cols), bf, (ROW_BLOCK, cols), own),
            ((length, cols), bf, (ROW_BLOCK, cols), own),
            ((rows, width), bf, (ROW_BLOCK, width), lambda i: (i, 0)),
        ],
        [room(narrow, heads // 4), room(broad, cols // 4), room(broad, cols // 4)],
        filled,
    )


def mlp_back_body(g, slope, *rest):
    d_up, d_ctx, sum_up, sum_g, w_out, w_down = rest[16:]

    @pl.when(pl.program_id(0) == 0)
    def _():
        assemble(rest[:8], w_out)
        assemble(rest[8:16], w_down)
        sum_up[...] = jnp.zeros_like(sum_up)
        sum_g[...] = jnp.zeros_like(sum_g)

    grad = g[...]
    du = (nn_dot(grad, w_down[...]) * slope[...].astype(jnp.float32)).astype(jnp.bfloat16)
    d_up[...] = du
    d_ctx[...] = nn_dot(grad, w_out[...]).astype(jnp.bfloat16)
    sum_up[...] += jnp.sum(du.astype(jnp.float32), axis=0, keepdims=True)
    sum_g[...] += jnp.sum(grad.astype(jnp.float32), axis=0, keepdims=True)


def run_mlp_back(source, slope, narrow, broad, at, rows, heads, filled):
    g, first = source
    width = g.shape[1]
    length, cols = slope.shape
    bf = jnp.bfloat16
    base = at // ROW_BLOCK
    own = lambda i: (i + base, 0)
    fixed = lambda i: (0, 0)
    return call(
        mlp_back_body,
        "mlp_back",
        rows * 15 * MICROSECOND // 1024,
        (rows // ROW_BLOCK,),
        [rows_of(g, first), rows_of(slope, at)]
        + matrix(narrow, heads // 4, 3)
        + matrix(broad, cols // 4, 1),
        [
            ((length, cols), bf, (ROW_BLOCK, cols), own),
            ((length, heads), bf, (ROW_BLOCK, heads), own),
            ((1, cols), jnp.float32, (1, cols), fixed),
            ((1, width), jnp.float32, (1, width), fixed),
        ],
        [room(narrow, heads // 4), room(broad, cols // 4)],
        filled,
    )


def attend_back_body(q, k, v, d_ctx, lse, cos, low, high, d_qkv, sums, dk_sum, dv_sum, dq_all):
    length = q.shape[0]
    step = ROW_BLOCK
    for head in range(2):
        lanes = slice(head * 64, head * 64 + 64)
        keys = k[:, lanes]
        vals = v[:, lanes]
        dk_sum[:, lanes] = jnp.zeros((length, 64), jnp.float32)
        dv_sum[:, lanes] = jnp.zeros((length, 64), jnp.float32)
        for at in range(0, length, step):
            end = at + step
            queries = q[at:end, lanes] * jnp.bfloat16(0.125)
            grads = d_ctx[at:end, lanes]
            scores = nt_dot(keys[:end], queries)
            power = jnp.exp(scores - lse[0, head : head + 1, at:end])
            key = lax.broadcasted_iota(jnp.int32, (step, step), 0)
            row = lax.broadcasted_iota(jnp.int32, (step, step), 1)
            last = jnp.where(key <= row, power[at:], 0.0)
            probs = last if at == 0 else jnp.concatenate([power[:at], last], axis=0)
            d_probs = nt_dot(vals[:end], grads)
            delta = jnp.sum(probs * d_probs, axis=0, keepdims=True)
            d_scores = (probs * (d_probs - delta)).astype(jnp.bfloat16)
            dv_sum[:end, lanes] += nn_dot(probs.astype(jnp.bfloat16), grads)
            dk_sum[:end, lanes] += nn_dot(d_scores, queries)
            dq_all[at:end, lanes] = tn_dot(d_scores, keys[:end]) * 0.125
    dq = turn(dq_all[...], cos[...], -low[...], -high[...]).astype(jnp.bfloat16)
    dk = turn(dk_sum[...], cos[...], -low[...], -high[...]).astype(jnp.bfloat16)
    dv = dv_sum[...].astype(jnp.bfloat16)
    for part, piece in enumerate((dq, dk, dv)):
        at = part * 128
        d_qkv[:, at : at + 128] = piece
        sums[:, at : at + 128] = jnp.sum(piece.astype(jnp.float32), axis=0, keepdims=True)


def run_attend_back(qkv, d_ctx, lse, tables):
    length, cols = qkv.shape
    groups = cols // 384
    wide = pltpu.VMEM((length, 128), jnp.float32)
    return call(
        attend_back_body,
        "attend_back",
        length * 26 * MICROSECOND // 1024,
        (groups,),
        [
            (qkv, (length, 128), lambda i: (0, 3 * i)),
            (qkv, (length, 128), lambda i: (0, 3 * i + 1)),
            (qkv, (length, 128), lambda i: (0, 3 * i + 2)),
            (d_ctx, (length, 128), lambda i: (0, i)),
            (lse, (1, 8, length), lambda i: (i, 0, 0)),
        ]
        + [whole(t) for t in tables],
        [
            ((length, cols), jnp.bfloat16, (length, 384), lambda i: (0, i)),
            ((1, cols), jnp.float32, (1, 384), lambda i: (0, i)),
        ],
        [wide, wide, wide],
    )


def norm_back_body(x, d_qkv, d_up, vecs, *rest):
    part, sums, w_qkv, w_up = rest[16:]

    @pl.when(pl.program_id(0) == 0)
    def _():
        assemble(rest[:8], w_qkv)
        assemble(rest[8:16], w_up)
        sums[...] = jnp.zeros_like(sums)

    hat, inverse = normalised(x[...].astype(jnp.float32))
    d_attn = nt_dot(d_qkv[...], w_qkv[...])
    d_mlp = nt_dot(d_up[...], w_up[...])
    for row, term in enumerate((d_attn * hat, d_mlp * hat, d_attn, d_mlp)):
        sums[row : row + 1, :] += jnp.sum(term, axis=0, keepdims=True)
    d_hat = d_attn * vecs[0:1, :] + d_mlp * vecs[2:3, :]
    along = jnp.mean(d_hat * hat, axis=-1, keepdims=True)
    level = jnp.mean(d_hat, axis=-1, keepdims=True)
    part[...] = (inverse * (d_hat - level - hat * along)).astype(jnp.bfloat16)


def run_norm_back(source, d_qkv, d_up, vecs, narrow, broad, at, rows):
    x, first = source
    width = x.shape[1]
    n_qkv, n_up = d_qkv.shape[1] // 4, d_up.shape[1] // 4
    return call(
        norm_back_body,
        "norm_back",
        rows * 21 * MICROSECOND // 1024,
        (rows // ROW_BLOCK,),
        [rows_of(x, first), rows_of(d_qkv, at), rows_of(d_up, at), whole(vecs)]
        + matrix(narrow, n_qkv, 0)
        + matrix(broad, n_up, 0),
        [
            ((rows, width), jnp.bfloat16, (ROW_BLOCK, width), lambda i: (i, 0)),
            ((8, width), jnp.float32, (8, width), lambda i: (0, 0)),
        ],
        [room(narrow, n_qkv), room(broad, n_up)],
    )


def weight_grad_body(cuts, *refs):
    a_refs, b_refs, rest = refs[: sum(cuts)], refs[sum(cuts) :], refs[sum(cuts) + 2 :]
    keep, send, turned_one, turned_two = rest
    groups = (a_refs[: cuts[0]], a_refs[cuts[0] :])

    @pl.when(pl.program_id(0) == 0)
    def _():
        for group, turned in zip(groups, (turned_one, turned_two)):
            at = 0
            for ref in group:
                turned[:, at : at + ref.shape[0]] = ref[...].T
                at += ref.shape[0]

    at = 0
    rows = keep.shape[2]
    for turned, right in zip((turned_one, turned_two), b_refs[:2]):
        size = right.shape[1]
        grad = nn_dot(turned[...], right[...]).astype(jnp.bfloat16)
        for side in range(2):
            first = 2 * side * rows
            keep[0, side, :, at : at + size] = grad[first : first + rows]
            send[0, side, :, at : at + size] = grad[first + rows : first + 2 * rows]
        at += size


def run_weight_grad(lefts, rights):
    length, width = rights[0].shape[0], lefts[0][0].shape[1]
    sizes = [right.shape[1] // 4 for right in rights]
    shape = (4, 2, width // 4, sum(sizes))
    out = (shape, jnp.bfloat16, (1,) + shape[1:], lambda i: (i, 0, 0, 0))
    turned = pltpu.VMEM((width, length), jnp.bfloat16)
    return call(
        partial(weight_grad_body, tuple(len(group) for group in lefts)),
        "weight_grad",
        length * 14 * MICROSECOND // 1024,
        (4,),
        [whole(left) for group in lefts for left in group]
        + [(r, (length, n), lambda i: (0, i)) for r, n in zip(rights, sizes)],
        [out, out],
        [turned, turned],
    )


def turn_tables(length):
    cosine, sine_tab = rotary_tables(length)
    zero = jnp.zeros_like(sine_tab)
    rest = jnp.zeros((length, 64 - ROT), jnp.float32)
    cos = jnp.concatenate([cosine, cosine, rest + 1.0], axis=1)
    low = jnp.concatenate([zero, sine_tab, rest], axis=1)
    high = jnp.concatenate([-sine_tab, zero, rest], axis=1)
    return tuple(jnp.concatenate([t, t], axis=1) for t in (cos, low, high))


def by_sequence(
    acts_in, cotangent, norm_gains, vec_bias, w_qkv, b_qkv, w_out, w_up, b_up, w_down
):
    section = lax.axis_index("section")
    across = lax.axis_index("dp")
    along = lax.axis_index("tensor")
    first_section = section == 0
    width = acts_in.shape[3]
    rows = w_qkv.shape[1]
    positions = acts_in.shape[1]
    length = 4 * positions
    heads = b_qkv.shape[1]
    bf = jnp.bfloat16

    qkv_halves = (
        w_qkv[0].reshape(rows, 2, 2, 3, 64).transpose(1, 0, 3, 2, 4).reshape(2, rows, -1)
    )
    out_halves = w_out[0].T.reshape(rows, 2, -1).transpose(1, 0, 2)
    up_halves = w_up[0].reshape(rows, 2, -1).transpose(1, 0, 2)
    down_halves = w_down[0].T.reshape(rows, 2, -1).transpose(1, 0, 2)
    n_qkv, n_out, n_up = qkv_halves.shape[2], out_halves.shape[2], up_halves.shape[2]

    narrow = jnp.stack([jnp.concatenate([qkv_halves[h], out_halves[h]], axis=1) for h in (0, 1)])
    broad = jnp.stack([jnp.concatenate([up_halves[h], down_halves[h]], axis=1) for h in (0, 1)])
    small = jnp.concatenate(
        [
            norm_gains[0].reshape(-1),
            vec_bias[0].reshape(-1),
            b_qkv[0].reshape(-1).astype(jnp.float32),
            b_up[0].reshape(-1).astype(jnp.float32),
        ]
    )
    clock = Clock()
    hold, tick = clock.hold, clock.tick

    def pass_half(halves):
        return swap(hold(pick(halves, 1 - section)), "section", 1)

    def by_layer(halves, got):
        keep = pick(halves, section)
        return jnp.where(first_section, keep, got), jnp.where(first_section, got, keep)

    def x_swap(value):
        return swap(hold(value), "dp", 2)

    def core_swap(value):
        return swap(hold(value), "dp", 1)

    def y_swap(value):
        return swap(hold(value), "section", 1)

    def both_ways(value):
        value = hold(value)
        return ring(value, "tensor", 1), ring(value, "tensor", -1)

    def far_narrow(left, right):
        return ring(hold(left[0]), "tensor", 1), ring(hold(right[1]), "tensor", -1)

    def far_broad(left, right):
        half = left.shape[0] // 2
        return ring(hold(left[:half]), "tensor", 1), ring(hold(right[half:]), "tensor", -1)

    got_narrow = pass_half(narrow)
    got_small = swap(small, "section", 1)
    tick(got_narrow, got_small)
    narrow_shards = by_layer(narrow, got_narrow)
    small = jnp.where(first_section, jnp.stack([small, got_small]), jnp.stack([got_small, small]))
    blocks = acts_in[:, :, 0, :]
    near = exchange_near(blocks, along, hold)
    got_broad = pass_half(broad)
    pair = jnp.stack([narrow_shards[0], x_swap(narrow_shards[0])])
    small = jnp.stack([small, core_swap(small)])
    small = jnp.concatenate([small, swap(small, "dp", 2)])
    tick(near, got_broad, pair, small)
    broad_shards = by_layer(broad, got_broad)
    far = exchange_far(near, hold)
    left, right = both_ways(pair)
    broad_own = jnp.stack([broad_shards[0], x_swap(broad_shards[0])])
    small = jnp.stack([small, swap(hold(small), "tensor", 1)])
    small = jnp.concatenate([small, swap(small, "tensor", 2)])
    tick(far, left, right, broad_own, small)
    acts = exchanged(blocks, near, far, along).reshape(length, width)
    acts = relative(acts, across)
    narrow_far = far_narrow(left, right)
    others = [core_swap(pair), core_swap(left), core_swap(right)]
    tick(narrow_far, others)
    narrow_far = jnp.stack(narrow_far)
    others.append(core_swap(narrow_far))
    narrow_zero = (pair, left, right, narrow_far, *others)
    tick(others[3])

    share = norm_gains.shape[2]
    vec_part = small[..., : 6 * share].reshape(4, 4, 2, 6, share)
    offsets = jnp.array(FAR_ORDER, jnp.int32)
    order = jnp.stack([pick(offsets, (k - along) % 4) for k in range(4)])
    slots = [jnp.bitwise_xor((along + k) % 4, along) for k in (0, 3, 1, 2)]
    vec_part = jnp.stack([pick(vec_part, jnp.bitwise_xor(along, k)) for k in range(4)])
    vecs_full = vec_part.transpose(2, 3, 1, 0, 4).reshape(2, 6, width)
    at = 6 * share
    share_q = b_qkv.shape[2]
    dp_order = [jnp.bitwise_xor(across, k) for k in range(4)]
    qkv_bias = small[..., at : at + heads * share_q].reshape(4, 4, 2, heads, share_q)
    qkv_bias = jnp.stack([pick(qkv_bias, k) for k in slots])
    qkv_bias = jnp.stack([pick(qkv_bias, i, 1) for i in dp_order], axis=1)
    qkv_bias = qkv_bias.transpose(2, 0, 3, 1, 4).reshape(2, 4, 2, heads // 2, 3, 64)
    qkv_bias = pick(qkv_bias, section, 2).transpose(0, 1, 3, 2, 4).reshape(2, 1, -1)
    at += heads * share_q
    bias_rows, share_u = b_up.shape[1], b_up.shape[2]
    up_bias = small[..., at : at + bias_rows * share_u].reshape(4, 4, 2, bias_rows, share_u)
    up_bias = jnp.stack([pick(up_bias, k) for k in slots])
    up_bias = jnp.stack([pick(up_bias, i, 1) for i in dp_order], axis=1)
    up_bias = up_bias.transpose(2, 0, 3, 1, 4).reshape(2, 4, 2, bias_rows // 2, 4 * share_u)
    up_bias = pick(up_bias, section, 2).reshape(2, 1, -1)
    zero_rows = jnp.zeros((4, width), jnp.float32)

    tables = turn_tables(length)
    chunk = length // CHUNKS
    starts = [i * chunk for i in range(CHUNKS)]

    all_vecs = [
        jnp.concatenate([v[0:1], v[2:3], v[1:2], v[3:4], zero_rows], axis=0) for v in vecs_full
    ]

    def project(layer, i, source, pieces, filled):
        return run_qkv(
            source, all_vecs[layer], qkv_bias[layer], tables, pieces, starts[i], chunk, filled
        )

    def feed(layer, i, ctx, ln_m, narrow, broad, filled):
        *filled, part = run_mlp(
            hold(ctx), ln_m, up_bias[layer], narrow, broad, starts[i], chunk, filled
        )
        return filled, part

    def join(layer, before, part, got):
        total = part.astype(jnp.float32) + got.astype(jnp.float32)
        full = vecs_full[layer]
        return (before.astype(jnp.float32) + total + (full[4] + full[5])).astype(bf)

    acts = hold(acts)
    first = project(0, 0, (acts, 0), narrow_zero, ())
    first = project(0, 1, (acts, chunk), narrow_zero, first)
    broad_left, broad_right = both_ways(broad_shards[0])
    tick(first, broad_left, broad_right)
    ln_a0, ln_m0, qkv0 = first
    ctx0, lse0 = run_attend(hold(qkv0))
    broad_far = far_broad(broad_left, broad_right)
    got_left, got_right = x_swap(broad_left), x_swap(broad_right)
    tick(ctx0, broad_far, got_left, got_right)
    broad_left = jnp.stack([broad_left, got_left])
    broad_right = jnp.stack([broad_right, got_right])
    broad_far = jnp.concatenate(broad_far, axis=0)
    got_far = x_swap(broad_far)
    others = [core_swap(broad_own), core_swap(broad_left), core_swap(broad_right)]
    tick(got_far, others)
    broad_far = jnp.stack([broad_far, got_far])
    others.append(core_swap(broad_far))
    broad_zero = (broad_own, broad_left, broad_right, broad_far, *others)
    pair = jnp.stack([narrow_shards[1], x_swap(narrow_shards[1])])
    tick(others[3], pair)
    first, part_a = feed(0, 0, ctx0, ln_m0, narrow_zero, broad_zero, ())
    broad_left, broad_right = both_ways(broad_shards[1])
    tick(part_a, broad_left, broad_right)
    first, part_b = feed(0, 1, ctx0, ln_m0, narrow_zero, broad_zero, first)
    act0, slope0 = first
    got_a = y_swap(part_a)
    left, right = both_ways(pair)
    got_own = x_swap(broad_shards[1])
    tick(part_b, got_a, left, right, got_own)
    got_b = y_swap(part_b)
    narrow_far = far_narrow(left, right)
    got_left = x_swap(broad_left)
    others = [core_swap(pair), core_swap(left), core_swap(right)]
    x1_a = join(0, acts[:chunk], part_a, got_a)
    tick(got_b, narrow_far, got_left, others)
    x1_b = join(0, acts[chunk:], part_b, got_b)
    narrow_far = jnp.stack(narrow_far)
    others.append(core_swap(narrow_far))
    narrow_one = (pair, left, right, narrow_far, *others)
    tick(others[3], x1_a, x1_b)

    first = project(1, 0, (hold(x1_a), 0), narrow_one, ())
    first = project(1, 1, (x1_b, 0), narrow_one, first)
    ln_a1, ln_m1, qkv1 = first
    broad_far = far_broad(broad_left, broad_right)
    got_right = x_swap(broad_right)
    tick(first, broad_far, got_right)
    ctx1, lse1 = run_attend(hold(qkv1))
    broad_own = jnp.stack([broad_shards[1], got_own])
    broad_left = jnp.stack([broad_left, got_left])
    broad_right = jnp.stack([broad_right, got_right])
    broad_far = jnp.concatenate(broad_far, axis=0)
    got_far = x_swap(broad_far)
    others = [core_swap(broad_own), core_swap(broad_left), core_swap(broad_right)]
    tick(ctx1, got_far, others)
    broad_far = jnp.stack([broad_far, got_far])
    others.append(core_swap(broad_far))
    broad_one = (broad_own, broad_left, broad_right, broad_far, *others)
    tick(others[3])
    first, part_a = feed(1, 0, ctx1, ln_m1, narrow_one, broad_one, ())
    blocks = cotangent[:, :, 0, :]
    near = exchange_near(blocks, along, hold)
    tick(part_a, near)
    first, part_b = feed(1, 1, ctx1, ln_m1, narrow_one, broad_one, first)
    act1, slope1 = first
    far = exchange_far(near, hold)
    got_a = y_swap(part_a)
    tick(part_b, far, got_a)

    grads = exchanged(blocks, near, far, along).reshape(length, width)
    grads = hold(relative(grads, across))
    n_heads = ctx0.shape[1]

    def back(i, source, slope, narrow, broad, filled):
        *filled, up_term, g_term = run_mlp_back(
            source, slope, narrow, broad, starts[i], chunk, n_heads, filled
        )
        return filled, up_term, g_term

    first, up_a, g_a = back(0, (grads, 0), slope1, narrow_one, broad_one, ())
    first, up_b, g_b = back(1, (grads, chunk), slope1, narrow_one, broad_one, first)
    d_up1, d_ctx1 = first
    sums_one = [None, g_a + g_b, None, up_a + up_b]
    got_b = y_swap(part_b)
    tick(first, got_b)
    x2 = jnp.concatenate(
        [join(1, x1_a, part_a, got_a), join(1, x1_b, part_b, got_b)], axis=0
    )
    x1 = jnp.concatenate([x1_a, x1_b], axis=0)

    def to_blocks(values):
        return relative(values, across).reshape(4, positions, width)

    out_blocks = to_blocks(jnp.where(first_section, x1, x2))
    d_qkv1, sums_one[2] = run_attend_back(qkv1, hold(d_ctx1), lse1, tables)
    out_near = exchange_near(out_blocks, along, hold)
    tick(d_qkv1, out_near)
    part_a, sum_a = run_norm_back(
        (x1_a, 0), hold(d_qkv1), d_up1, all_vecs[1], narrow_one, broad_one, 0, chunk
    )
    out_far = exchange_far(out_near, hold)
    tick(part_a, out_far)
    acts_local = exchanged(out_blocks, out_near, out_far, along)
    part_b, sum_b = run_norm_back(
        (x1_b, 0), hold(d_qkv1), d_up1, all_vecs[1], narrow_one, broad_one, chunk, chunk
    )
    sums_one[0] = (sum_a + sum_b)[:4]
    keep_broad, send = run_weight_grad([[hold(ln_m1)], [grads]], [d_up1, act1])
    got_a = y_swap(part_a)
    tick(part_b, keep_broad, got_a)
    keep_narrow, send_narrow = run_weight_grad([[hold(ln_a1)], [grads]], [d_qkv1, ctx1])
    got_b = y_swap(part_b)
    got_core = core_swap(send)
    tick(keep_narrow, got_b, got_core)

    def lower(above, part, got):
        total = part.astype(jnp.float32) + got.astype(jnp.float32)
        return (above.astype(jnp.float32) + total).astype(bf)

    g1_a = hold(lower(grads[:chunk], part_a, got_a))
    g1_b = hold(lower(grads[chunk:], part_b, got_b))
    broad_sum = add_wide(keep_broad, got_core)
    first, up_a, g_a = back(0, (g1_a, 0), slope0, narrow_zero, broad_zero, ())
    first, up_b, g_b = back(1, (g1_b, 0), slope0, narrow_zero, broad_zero, first)
    d_up0, d_ctx0 = first
    sums_zero = [None, g_a + g_b, None, up_a + up_b]
    got_core = core_swap(send_narrow)
    got_x = [x_swap(broad_sum[2:, 1])]
    tick(first, got_core, got_x)
    narrow_sum = add_wide(keep_narrow, got_core)
    narrow_sum = [narrow_sum[k] for k in range(4)]
    keep_broad, send = run_weight_grad([[hold(ln_m0)], [g1_a, g1_b]], [d_up0, act0])
    narrow_got = ring_first(narrow_sum, hold)
    got_x.append(x_swap(broad_sum[:2, 1]))
    tick(keep_broad, narrow_got, got_x)

    def after_x(total, got):
        late = add_wide(total[2:, 0], got[0])
        early = add_wide(total[:2, 0], got[1])
        return [early[0], early[1], late[0], late[1]]

    broad_one_sum = after_x(broad_sum, got_x)
    d_qkv0, sums_zero[2] = run_attend_back(qkv0, hold(d_ctx0), lse0, tables)
    narrow_got = ring_second(narrow_sum, narrow_got, hold)
    broad_got = ring_first(broad_one_sum, hold)
    got_core = core_swap(send)
    tick(d_qkv0, narrow_got, broad_got, got_core)
    narrow_total = ring_total(narrow_sum[0], narrow_got)
    broad_sum = add_wide(keep_broad, got_core)
    part_a, sum_a = run_norm_back(
        (acts, 0), hold(d_qkv0), d_up0, all_vecs[0], narrow_zero, broad_zero, 0, chunk
    )
    broad_got = ring_second(broad_one_sum, broad_got, hold)
    got_x = x_swap(narrow_total[1])
    tick(part_a, broad_got, got_x)
    one_narrow = add_wide(narrow_total[0], got_x)
    one_broad = ring_total(broad_one_sum[0], broad_got)
    part_b, sum_b = run_norm_back(
        (acts, chunk), hold(d_qkv0), d_up0, all_vecs[0], narrow_zero, broad_zero, chunk, chunk
    )
    sums_zero[0] = (sum_a + sum_b)[:4]
    keep_narrow, send_narrow = run_weight_grad([[hold(ln_a0)], [g1_a, g1_b]], [d_qkv0, ctx0])
    got_a = y_swap(part_a)
    got_x = [x_swap(broad_sum[2:, 1])]
    tick(part_b, keep_narrow, got_a, got_x)

    flat = []
    for norm_sums, sum_g, sum_qkv, sum_up in (sums_zero, sums_one):
        feature = relative(jnp.concatenate([norm_sums, sum_g], axis=0), across)
        q_sum = sum_qkv.reshape(4, 3, 2, 64).transpose(0, 2, 1, 3).reshape(4, -1)
        both = jnp.concatenate([q_sum, sum_up.reshape(4, -1)], axis=1)
        both = jnp.stack([pick(both, order[k]) for k in range(4)])
        flat.append(jnp.concatenate([feature.reshape(-1), both.reshape(-1)]))
    flat = jnp.stack(flat)
    got_b = y_swap(part_b)
    got_x.append(x_swap(broad_sum[:2, 1]))
    late = add_wide(broad_sum[2:, 0], got_x[0])
    broad_got = ring_first([None, None, late[0], late[1]], hold)
    got_core = core_swap(send_narrow)
    tick(got_b, got_x, broad_got, got_core)
    flat = flat + core_swap(flat)
    early = add_wide(broad_sum[:2, 0], got_x[1])
    broad_zero_sum = [early[0], early[1], late[0], late[1]]
    narrow_sum = add_wide(keep_narrow, got_core)
    narrow_sum = [narrow_sum[k] for k in range(4)]
    grads_low = jnp.concatenate([lower(g1_a, part_a, got_a), lower(g1_b, part_b, got_b)], axis=0)
    g1 = jnp.concatenate([g1_a, g1_b], axis=0)
    out_blocks = to_blocks(jnp.where(first_section, grads_low, g1))
    narrow_got = ring_first(narrow_sum, hold)
    broad_got = ring_second(broad_zero_sum, broad_got, hold)
    tick(narrow_got, broad_got, flat)
    flat = flat + x_swap(flat)
    zero_broad = ring_total(broad_zero_sum[0], broad_got)
    narrow_got = ring_second(narrow_sum, narrow_got, hold)
    out_near = exchange_near(out_blocks, along, hold)
    broad_send = y_swap(jnp.where(first_section, one_broad, zero_broad))
    tick(narrow_got, out_near, broad_send, flat)
    flat = flat + swap(hold(flat), "tensor", 1)
    narrow_total = ring_total(narrow_sum[0], narrow_got)
    out_far = exchange_far(out_near, hold)
    zero_narrow = add_wide(narrow_total[0], x_swap(narrow_total[1]))
    tick(out_far, zero_narrow, flat)
    flat = flat + swap(hold(flat), "tensor", 2)
    grad_local = exchanged(out_blocks, out_near, out_far, along)
    narrow_send = y_swap(jnp.where(first_section, one_narrow, zero_narrow))

    def whole_layer(keep_pair, got):
        keep = jnp.where(first_section, *keep_pair).astype(jnp.float32)
        got = got.astype(jnp.float32)
        return jnp.where(first_section, jnp.stack([keep, got], 1), jnp.stack([got, keep], 1))

    narrow_out = whole_layer((zero_narrow, one_narrow), narrow_send)
    broad_out = whole_layer((zero_broad, one_broad), broad_send)
    grad_qkv = narrow_out[..., :n_qkv].reshape(rows, 2, 3, 2, 64)
    grad_qkv = grad_qkv.transpose(0, 1, 3, 2, 4).reshape(rows, -1)
    grad_out = narrow_out[..., n_qkv:].reshape(rows, -1).T
    grad_up = broad_out[..., :n_up].reshape(rows, -1)
    grad_down = broad_out[..., n_up:].reshape(rows, -1).T

    keep = pick(flat, section)
    mine = pick(flat, 1 - section)
    got = swap(mine, "section", 1)
    n_feature = 5 * width
    feature_own = keep[:n_feature].reshape(5, width)
    feature = feature_own[:4] + got[: 4 * width].reshape(4, width)
    place_at = (across * 4 + along) * share
    gain_share = lax.dynamic_slice_in_dim(feature[:2], place_at, share, 1)
    shifts = jnp.concatenate([feature[2:4], feature_own[4:5], feature_own[4:5]], axis=0)
    bias_share = lax.dynamic_slice_in_dim(shifts, place_at, share, 1)
    low_half = jnp.where(first_section, keep, got)[n_feature:].reshape(4, -1)
    high_half = jnp.where(first_section, got, keep)[n_feature:].reshape(4, -1)
    halves = jnp.stack([pick(low_half, along), pick(high_half, along)])
    n_head = (heads // 2) * 192
    head_sums = halves[:, :n_head].reshape(heads, 192)
    head_share = lax.dynamic_slice_in_dim(head_sums, across * share_q, share_q, 1)
    unit_sums = halves[:, n_head:].reshape(bias_rows, 4 * share_u)
    unit_share = lax.dynamic_slice_in_dim(unit_sums, across * share_u, share_u, 1)
    return (
        acts_local[None, :, :, None],
        grad_local[None, :, :, None],
        gain_share[None],
        bias_share[None],
        grad_qkv[None],
        head_share[None],
        grad_out[None],
        grad_up[None],
        unit_share[None],
        grad_down[None],
    )


def fits(mesh, args):
    acts_in, b_qkv = args[0], args[5]
    sizes = dict(mesh.shape)
    return (
        sizes["section"] == 2
        and sizes["dp"] == 4
        and sizes["tensor"] == MICRO
        and MICRO == 4
        and acts_in.shape[2] == sizes["dp"]
        and b_qkv.shape[1] == 16
        and b_qkv.shape[2] == 192
        and acts_in.shape[1] % (CHUNKS * ROW_BLOCK) == 0
    )


def solution(mesh):
    placed = (
        P(None, "tensor", "dp", None),
        P(None, "tensor", "dp", None),
        P("section", None, ("dp", "tensor")),
        P("section", None, ("dp", "tensor")),
        P("section", "dp", "tensor"),
        P("section", "tensor", "dp"),
        P("section", "tensor", "dp"),
        P("section", "dp", "tensor"),
        P("section", "tensor", "dp"),
        P("section", "tensor", "dp"),
    )
    def wrap(body):
        return jax.shard_map(
            body,
            mesh=mesh,
            in_specs=placed,
            out_specs=(
                P("section", None, "tensor", "dp", None),
                P("section", None, "tensor", "dp", None),
                P("section", None, ("dp", "tensor")),
                P("section", None, ("dp", "tensor")),
                P("section", "dp", "tensor"),
                P("section", "tensor", "dp"),
                P("section", "tensor", "dp"),
                P("section", "dp", "tensor"),
                P("section", "tensor", "dp"),
                P("section", "tensor", "dp"),
            ),
            check_vma=False,
        )

    return lambda *args: wrap(by_sequence if fits(mesh, args) else local)(*args)
```

```python
from functools import partial
import math

import jax
import jax.numpy as jnp
from jax import lax
from jax.experimental import pallas as pl
from jax.experimental.pallas import tpu as pltpu
from jax.sharding import PartitionSpec as P

ROT = 16
QBLOCK = 512
MICRO = 4


NORM_EPS = 1e-05
ROPE_BASE = 10000.0
MASK_FILL = -1e30


def from_behind(value, axis, by):
    length = lax.axis_size(axis)
    pairs = [(i, i + by) for i in range(length) if 0 <= i + by < length]
    return lax.ppermute(value, axis, pairs)


def layer_norm(values, norm_gain, norm_shift):
    average = jnp.mean(values, axis=-1, keepdims=True)
    centred = values - average
    variance = jnp.mean(centred * centred, axis=-1, keepdims=True)
    return centred * lax.rsqrt(variance + NORM_EPS) * norm_gain + norm_shift


def both_norms(values, gain_attn, shift_attn, gain_mlp, shift_mlp):
    return (layer_norm(values, gain_attn, shift_attn), layer_norm(values, gain_mlp, shift_mlp))


def rotary_tables(length):
    half_rot = ROT // 2
    frequency = jnp.exp(
        jnp.arange(half_rot, dtype=jnp.float32) * (-2.0 * math.log(ROPE_BASE) / ROT)
    )
    angles = jnp.arange(length, dtype=jnp.float32)[:, None] * frequency[None, :]
    return (jnp.cos(angles), jnp.sin(angles))


def rotate(values, cosine, sine_tab):
    half_rot = ROT // 2
    low_half = values[..., :half_rot]
    high_half = values[..., half_rot:ROT]
    return jnp.concatenate(
        [
            low_half * cosine - high_half * sine_tab,
            high_half * cosine + low_half * sine_tab,
            values[..., ROT:],
        ],
        axis=-1,
    )


def rotate_back(grads_rot, cosine, sine_tab):
    half_rot = ROT // 2
    low_half = grads_rot[..., :half_rot]
    high_half = grads_rot[..., half_rot:ROT]
    return jnp.concatenate(
        [
            low_half * cosine + high_half * sine_tab,
            high_half * cosine - low_half * sine_tab,
            grads_rot[..., ROT:],
        ],
        axis=-1,
    )


def causal_scores(queries, key_rows, first_row, score_scale):
    block_rows = queries.shape[0]
    last_row = key_rows.shape[0]
    scores = (
        jnp.einsum("qshd,kshd->shqk", queries, key_rows, preferred_element_type=jnp.float32)
        * score_scale
    )
    row_pos = first_row + jnp.arange(block_rows, dtype=jnp.int32)
    col_pos = jnp.arange(last_row, dtype=jnp.int32)
    allowed = col_pos[None, :] <= row_pos[:, None]
    return (scores, allowed)


def attend(queries, key_rows, val_rows):
    length = queries.shape[0]
    block_rows = min(QBLOCK, length)
    score_scale = queries.shape[-1] ** (-0.5)
    outputs = []
    totals = []
    for block_index in range(length // block_rows):
        first_row = block_index * block_rows
        last_row = first_row + block_rows
        scores, allowed = causal_scores(
            queries[first_row:last_row], key_rows[:last_row], first_row, score_scale
        )
        scores = jnp.where(allowed, scores, MASK_FILL)
        highest = jnp.max(scores, axis=-1, keepdims=True)
        exponent = jnp.exp(scores - highest)
        denominator = jnp.sum(exponent, axis=-1, keepdims=True)
        probability = (exponent / denominator).astype(jnp.bfloat16)
        block_out = jnp.einsum(
            "shqk,kshd->qshd", probability, val_rows[:last_row], preferred_element_type=jnp.float32
        )
        outputs.append(block_out.astype(jnp.bfloat16))
        totals.append((highest + jnp.log(denominator))[..., 0])
    context = jnp.concatenate(outputs, axis=0)
    return (context.reshape(length, context.shape[1], -1), jnp.concatenate(totals, axis=-1))


def attend_back(queries, key_rows, val_rows, d_context, log_total):
    length = queries.shape[0]
    block_rows = min(QBLOCK, length)
    score_scale = queries.shape[-1] ** (-0.5)
    grad_query_list = []
    grad_keys = jnp.zeros(queries.shape, jnp.float32)
    grad_vals = jnp.zeros(queries.shape, jnp.float32)
    for block_index in range(length // block_rows):
        first_row = block_index * block_rows
        last_row = first_row + block_rows
        query_block = queries[first_row:last_row]
        scores, allowed = causal_scores(query_block, key_rows[:last_row], first_row, score_scale)
        probability = jnp.where(
            allowed, jnp.exp(scores - log_total[:, :, first_row:last_row, None]), 0.0
        )
        d_block = d_context[first_row:last_row]
        d_prob = jnp.einsum(
            "qshd,kshd->shqk", d_block, val_rows[:last_row], preferred_element_type=jnp.float32
        )
        delta = jnp.sum(probability * d_prob, axis=-1, keepdims=True)
        d_scores = (probability * (d_prob - delta)).astype(jnp.bfloat16)
        grad_query_list.append(
            jnp.einsum(
                "shqk,kshd->qshd", d_scores, key_rows[:last_row], preferred_element_type=jnp.float32
            )
            * score_scale
        )
        grad_keys = grad_keys.at[:last_row].add(
            jnp.einsum("shqk,qshd->kshd", d_scores, query_block, preferred_element_type=jnp.float32)
            * score_scale
        )
        grad_vals = grad_vals.at[:last_row].add(
            jnp.einsum(
                "shqk,qshd->kshd",
                probability.astype(jnp.bfloat16),
                d_block,
                preferred_element_type=jnp.float32,
            )
        )
    return (jnp.concatenate(grad_query_list, axis=0), grad_keys, grad_vals)


def local(acts_in, cotangent, norm_gains, vec_bias, w_qkv, b_qkv, w_out, w_up, b_up, w_down):
    section_index = lax.axis_index("section")
    own_start = lax.axis_index("tensor") * acts_in.shape[1]
    local_len = acts_in.shape[1]
    seq_count = acts_in.shape[2]
    model_width = acts_in.shape[3]
    length = local_len * lax.axis_size("tensor")
    all_rows = length * seq_count
    gain_full, bias_full = (
        lax.all_gather(norm_gains[0], ("dp", "tensor"), axis=1, tiled=True),
        lax.all_gather(vec_bias[0], ("dp", "tensor"), axis=1, tiled=True),
    )
    mat_qkv, bias_qkv, mat_out, mat_up, bias_up, mat_down = (
        lax.all_gather(w_qkv[0], "dp", axis=0, tiled=True),
        lax.all_gather(b_qkv[0], "dp", axis=1, tiled=True),
        lax.all_gather(w_out[0], "dp", axis=1, tiled=True),
        lax.all_gather(w_up[0], "dp", axis=0, tiled=True),
        lax.all_gather(b_up[0], "dp", axis=1, tiled=True),
        lax.all_gather(w_down[0], "dp", axis=1, tiled=True),
    )
    head_count = bias_qkv.shape[0]
    head_dim = bias_qkv.shape[1] // 3
    qkv_shift = bias_qkv.reshape(-1).astype(jnp.float32)
    up_shift = bias_up.reshape(-1).astype(jnp.float32)
    cosine, sine_tab = rotary_tables(length)
    cosine = cosine[:, None, None, :]
    sine_tab = sine_tab[:, None, None, :]
    received = jnp.zeros_like(acts_in[0])
    stash_list = []
    out_list = []
    for moment in range(MICRO + 1):
        own_rows = acts_in[min(moment, MICRO - 1)]
        inputs = jnp.where(section_index == 0, own_rows, received)
        forward_gathered = lax.all_gather(inputs, "tensor", axis=0, tiled=True)
        full_attn, full_mlp = both_norms(
            forward_gathered.astype(jnp.float32),
            gain_full[0],
            bias_full[0],
            gain_full[1],
            bias_full[1],
        )
        forward_normed_attn = full_attn.astype(jnp.bfloat16)
        forward_normed_mlp = full_mlp.astype(jnp.bfloat16)
        forward_flat_attn = forward_normed_attn.reshape(all_rows, model_width)
        forward_flat_mlp = forward_normed_mlp.reshape(all_rows, model_width)
        projected = (
            jnp.dot(forward_flat_attn, mat_qkv, preferred_element_type=jnp.float32) + qkv_shift
        )
        projected = projected.reshape(length, seq_count, head_count, 3, head_dim)
        forward_queries = rotate(projected[:, :, :, 0], cosine, sine_tab).astype(jnp.bfloat16)
        forward_key_rows = rotate(projected[:, :, :, 1], cosine, sine_tab).astype(jnp.bfloat16)
        forward_val_rows = projected[:, :, :, 2].astype(jnp.bfloat16)
        forward_context, forward_log_total = attend(
            forward_queries, forward_key_rows, forward_val_rows
        )
        forward_up_proj = (
            jnp.dot(forward_flat_mlp, mat_up, preferred_element_type=jnp.float32) + up_shift
        )
        forward_activated = jax.nn.gelu(forward_up_proj, approximate=False).astype(jnp.bfloat16)
        active_rows = forward_activated.reshape(length, seq_count, -1)
        context_part = forward_context.reshape(lax.axis_size("tensor") * local_len * seq_count, -1)
        active_part = active_rows.reshape(lax.axis_size("tensor") * local_len * seq_count, -1)
        summed = jnp.dot(context_part, mat_out, preferred_element_type=jnp.float32) + jnp.dot(
            active_part, mat_down, preferred_element_type=jnp.float32
        )
        mixed_sum = lax.psum_scatter(
            summed.reshape(lax.axis_size("tensor") * local_len, seq_count, model_width),
            "tensor",
            scatter_dimension=0,
            tiled=True,
        )
        result = inputs.astype(jnp.float32) + mixed_sum + bias_full[2] + bias_full[3]
        forward_stashed = (
            forward_gathered,
            forward_normed_attn,
            forward_normed_mlp,
            forward_queries,
            forward_key_rows,
            forward_val_rows,
            forward_context,
            forward_log_total,
            forward_up_proj,
            forward_activated,
        )
        result, stashed = (result.astype(jnp.bfloat16), forward_stashed)
        stash_list.append(stashed)
        out_list.append(result)
        if moment < MICRO:
            received = from_behind(result, "section", 1)
    stash_all = jax.tree.map(lambda *parts: jnp.stack(parts), *stash_list)
    acts_local = lax.dynamic_slice_in_dim(jnp.stack(out_list), section_index, MICRO, 0)
    back_received = jnp.zeros_like(cotangent[0])
    grad_list = []
    weight_sums = None
    vector_sums = None
    for moment in range(MICRO + 1):
        micro_index = moment - 1 + section_index
        is_valid = (micro_index >= 0) & (micro_index < MICRO)
        source_clock = jnp.clip(micro_index + section_index, 0, MICRO)
        stashed = jax.tree.map(
            lambda part: lax.dynamic_index_in_dim(part, source_clock, 0, keepdims=False), stash_all
        )
        upstream = jnp.where(section_index == 1, cotangent[min(moment, MICRO - 1)], back_received)
        (
            gathered,
            normed_attn,
            normed_mlp,
            queries,
            key_rows,
            val_rows,
            context,
            log_total,
            up_proj,
            activated,
        ) = stashed
        backward_inputs = lax.dynamic_slice_in_dim(gathered, own_start, local_len, 0)
        upstream_rows = lax.all_gather(upstream, "tensor", axis=0, tiled=True)
        flat_grad = upstream_rows.reshape(all_rows, model_width)
        d_context = jnp.dot(flat_grad, mat_out.T, preferred_element_type=jnp.float32).astype(
            jnp.bfloat16
        )
        d_context = d_context.reshape(length, seq_count, head_count, head_dim)
        d_active = jnp.dot(flat_grad, mat_down.T, preferred_element_type=jnp.float32)
        _, gelu_pullback = jax.vjp(partial(jax.nn.gelu, approximate=False), up_proj)
        d_up = gelu_pullback(d_active)[0].astype(jnp.bfloat16)
        grad_query, grad_key, grad_val = attend_back(
            queries, key_rows, val_rows, d_context, log_total
        )
        d_qkv = jnp.stack(
            [
                rotate_back(grad_query, cosine, sine_tab),
                rotate_back(grad_key, cosine, sine_tab),
                grad_val,
            ],
            axis=3,
        ).astype(jnp.bfloat16)
        d_qkv_flat = d_qkv.reshape(all_rows, -1)
        d_qkv_rows = d_qkv.reshape(length, seq_count, -1)
        d_up_rows = d_up.reshape(length, seq_count, -1)
        flat_attn = normed_attn.reshape(all_rows, model_width)
        flat_mlp = normed_mlp.reshape(all_rows, model_width)
        weight_terms = (
            jnp.einsum("tc,te->ce", flat_attn, d_qkv_flat, preferred_element_type=jnp.float32),
            jnp.sum(d_qkv_flat.astype(jnp.float32), axis=0).reshape(bias_qkv.shape),
            jnp.einsum(
                "tc,te->ce",
                context.reshape(all_rows, -1),
                flat_grad,
                preferred_element_type=jnp.float32,
            ),
            jnp.einsum("tc,te->ce", flat_mlp, d_up, preferred_element_type=jnp.float32),
            jnp.sum(d_up.astype(jnp.float32), axis=0).reshape(bias_up.shape),
            jnp.einsum("tc,te->ce", activated, flat_grad, preferred_element_type=jnp.float32),
        )
        attn_part = d_qkv_rows.reshape(lax.axis_size("tensor") * local_len * seq_count, -1)
        mlp_part = d_up_rows.reshape(lax.axis_size("tensor") * local_len * seq_count, -1)
        joined = jnp.concatenate(
            [
                jnp.dot(attn_part, mat_qkv.T, preferred_element_type=jnp.float32),
                jnp.dot(mlp_part, mat_up.T, preferred_element_type=jnp.float32),
            ],
            axis=-1,
        )
        d_normed = lax.psum_scatter(
            joined.reshape(lax.axis_size("tensor") * local_len, seq_count, 2 * model_width).astype(
                jnp.bfloat16
            ),
            "tensor",
            scatter_dimension=0,
            tiled=True,
        ).astype(jnp.float32)
        _, norm_pullback = jax.vjp(
            both_norms,
            backward_inputs.astype(jnp.float32),
            gain_full[0],
            bias_full[0],
            gain_full[1],
            bias_full[1],
        )
        d_local, d_gain_attn, d_shift_attn, d_gain_mlp, d_shift_mlp = norm_pullback(
            (d_normed[..., :model_width], d_normed[..., model_width:])
        )
        upstream_float = upstream.astype(jnp.float32)
        d_inputs = (upstream_float + d_local).astype(jnp.bfloat16)
        out_shift = jnp.sum(upstream_float, axis=(0, 1))
        vector_terms = (
            jnp.stack([d_gain_attn, d_gain_mlp]),
            jnp.stack([d_shift_attn, d_shift_mlp, out_shift, out_shift]),
        )
        d_inputs, weight_terms, vector_terms = (d_inputs, weight_terms, vector_terms)
        grad_list.append(d_inputs)
        if moment < MICRO:
            back_received = from_behind(d_inputs, "section", -1)
        weight_terms = tuple((jnp.where(is_valid, term, 0.0) for term in weight_terms))
        vector_terms = tuple((jnp.where(is_valid, term, 0.0) for term in vector_terms))
        if moment == 0:
            weight_sums = tuple(weight_terms)
            vector_sums = vector_terms
        else:
            weight_sums = tuple((a + b for a, b in zip(weight_sums, weight_terms)))
            vector_sums = tuple((a + b for a, b in zip(vector_sums, vector_terms)))
    sum_qkv, sum_bqkv, sum_out, sum_up, sum_bup, sum_down = weight_sums
    share_qkv, share_bqkv, share_out, share_up, share_bup, share_down = (
        lax.psum_scatter(
            sum_qkv.astype(jnp.bfloat16), "dp", scatter_dimension=0, tiled=True
        ).astype(jnp.float32),
        lax.psum_scatter(
            sum_bqkv.astype(jnp.bfloat16), "dp", scatter_dimension=1, tiled=True
        ).astype(jnp.float32),
        lax.psum_scatter(
            sum_out.astype(jnp.bfloat16), "dp", scatter_dimension=1, tiled=True
        ).astype(jnp.float32),
        lax.psum_scatter(sum_up.astype(jnp.bfloat16), "dp", scatter_dimension=0, tiled=True).astype(
            jnp.float32
        ),
        lax.psum_scatter(
            sum_bup.astype(jnp.bfloat16), "dp", scatter_dimension=1, tiled=True
        ).astype(jnp.float32),
        lax.psum_scatter(
            sum_down.astype(jnp.bfloat16), "dp", scatter_dimension=1, tiled=True
        ).astype(jnp.float32),
    )
    grad_local = lax.dynamic_slice_in_dim(jnp.stack(grad_list), 1 - section_index, MICRO, 0)
    gain_share, bias_share = (
        lax.psum_scatter(vector_sums[0], ("dp", "tensor"), scatter_dimension=1, tiled=True),
        lax.psum_scatter(vector_sums[1], ("dp", "tensor"), scatter_dimension=1, tiled=True),
    )
    return (
        acts_local[None],
        grad_local[None],
        gain_share[None],
        bias_share[None],
        share_qkv[None],
        share_bqkv[None],
        share_out[None],
        share_up[None],
        share_bup[None],
        share_down[None],
    )


FAR_ORDER = (0, 2, 3, 1)
VMEM_LIMIT = 60 * 1024 * 1024
ROW_BLOCK = 256
CHUNKS = 2
MICROSECOND = 1_000_000_000


def ring(value, axis, by):
    length = lax.axis_size(axis)
    return lax.ppermute(value, axis, [(i, (i + by) % length) for i in range(length)])


def swap(value, axis, bit):
    length = lax.axis_size(axis)
    return lax.ppermute(value, axis, [(i, i ^ bit) for i in range(length)])


def pick(value, index, axis=0):
    return lax.dynamic_index_in_dim(value, index, axis, keepdims=False)


def place(value, block, index):
    return lax.dynamic_update_index_in_dim(value, block, index, 0)


def relative(values, own):
    size = values.shape[-1] // 4
    picked = [
        lax.dynamic_slice_in_dim(values, jnp.bitwise_xor(own, k) * size, size, values.ndim - 1)
        for k in range(4)
    ]
    return jnp.concatenate(picked, axis=-1)


class Clock:
    def __init__(self):
        self.ended = ()

    def hold(self, value):
        return lax.optimization_barrier((value, self.ended))[0]

    def tick(self, *ended):
        self.ended = ended


def exchange_near(blocks, own, hold):
    half = blocks.shape[1] // 2
    far = pick(blocks, (own + 2) % 4)
    ahead = jnp.concatenate([pick(blocks, (own + 1) % 4), far[:half]], axis=0)
    behind = jnp.concatenate([pick(blocks, (own + 3) % 4), far[half:]], axis=0)
    return ring(hold(ahead), "tensor", 1), ring(hold(behind), "tensor", -1)


def exchange_far(near, hold):
    rows = near[0].shape[0] * 2 // 3
    first = ring(hold(near[0][rows:]), "tensor", 1)
    second = ring(hold(near[1][rows:]), "tensor", -1)
    return first, second


def exchanged(blocks, near, far, own):
    rows = blocks.shape[1]
    result = jnp.zeros_like(blocks)
    result = place(result, pick(blocks, own), own)
    result = place(result, near[0][:rows], (own + 3) % 4)
    result = place(result, near[1][:rows], (own + 1) % 4)
    return place(result, jnp.concatenate(far, axis=0), (own + 2) % 4)


def add_wide(left, right):
    return (left.astype(jnp.float32) + right.astype(jnp.float32)).astype(jnp.bfloat16)


def ring_first(blocks, hold):
    far = blocks[3]
    half = far.shape[0] // 2
    to_right = ring(hold(far[:half]), "tensor", 1)
    to_left = ring(hold(far[half:]), "tensor", -1)
    return to_right, to_left


def ring_second(blocks, got, hold):
    _, left, right, _ = blocks
    half = left.shape[0] // 2
    right = jnp.concatenate([add_wide(right[:half], got[0]), right[half:]], axis=0)
    left = jnp.concatenate([left[:half], add_wide(left[half:], got[1])], axis=0)
    return ring(hold(right), "tensor", 1), ring(hold(left), "tensor", -1)


def ring_total(own, got):
    total = own.astype(jnp.float32) + got[0].astype(jnp.float32) + got[1].astype(jnp.float32)
    return total.astype(jnp.bfloat16)


def normalised(x):
    average = jnp.mean(x, axis=-1, keepdims=True)
    centred = x - average
    variance = jnp.mean(centred * centred, axis=-1, keepdims=True)
    inverse = lax.rsqrt(variance + NORM_EPS)
    return centred * inverse, inverse


def nt_dot(left, right):
    return lax.dot_general(
        left, right, (((1,), (1,)), ((), ())), preferred_element_type=jnp.float32
    )


def tn_dot(left, right):
    return lax.dot_general(
        left, right, (((0,), (0,)), ((), ())), preferred_element_type=jnp.float32
    )


def nn_dot(left, right):
    return jnp.dot(left, right, preferred_element_type=jnp.float32)


def turn(values, cosine, low_sine, high_sine):
    lanes = values.shape[-1]
    return (
        values * cosine
        + pltpu.roll(values, ROT // 2, 1) * low_sine
        + pltpu.roll(values, lanes - ROT // 2, 1) * high_sine
    )


def call(body, name, flops, grid, ins, outs, scratch=(), filled=()):
    count = len(ins)

    def run(*refs):
        body(*refs[:count], *refs[count + len(filled) :])

    return pl.pallas_call(
        run,
        name=name,
        grid=grid,
        in_specs=[pl.BlockSpec(block, index) for _, block, index in ins]
        + [pl.BlockSpec(memory_space=pl.ANY)] * len(filled),
        out_specs=[pl.BlockSpec(block, index) for _, _, block, index in outs],
        out_shape=[jax.ShapeDtypeStruct(shape, kind) for shape, kind, _, _ in outs],
        scratch_shapes=list(scratch),
        input_output_aliases={count + i: i for i in range(len(filled))},
        cost_estimate=pl.CostEstimate(flops=flops, bytes_accessed=1 << 20, transcendentals=0),
        compiler_params=pltpu.CompilerParams(
            vmem_limit_bytes=VMEM_LIMIT, dimension_semantics=("arbitrary",) * len(grid)
        ),
    )(*[array for array, _, _ in ins], *filled)


def whole(array):
    return (array, array.shape, lambda *_: (0,) * array.ndim)


def matrix(pieces, size, block):
    shape = (2, pieces[0].shape[1], size)
    return [(piece, shape, lambda *_: (0, 0, block)) for piece in pieces]


def room(pieces, size):
    return pltpu.VMEM((4 * pieces[0].shape[1], 4 * size), jnp.bfloat16)


def assemble(refs, target):
    _, rows, size = refs[0].shape
    for core in range(2):
        for offset in range(4):
            for side in range(2):
                at = (2 * side + core) * rows
                target[at : at + rows, offset * size : (offset + 1) * size] = refs[
                    core * 4 + offset
                ][side]


def rows_of(array, first=0, block=ROW_BLOCK):
    base = first // block
    return (array, (block, array.shape[1]), lambda i: (i + base, 0))


def qkv_body(x, vecs, shift, cos, low, high, *rest):
    ln_a, ln_m, qkv, w = rest[8:]

    @pl.when(pl.program_id(0) == 0)
    def _():
        assemble(rest[:8], w)

    hat, _ = normalised(x[...].astype(jnp.float32))
    attn = (hat * vecs[0:1, :] + vecs[1:2, :]).astype(jnp.bfloat16)
    ln_a[...] = attn
    ln_m[...] = (hat * vecs[2:3, :] + vecs[3:4, :]).astype(jnp.bfloat16)
    out = nn_dot(attn, w[...]) + shift[...]
    for block in range(qkv.shape[1] // 384):
        for part in range(3):
            at = block * 384 + part * 128
            piece = out[:, at : at + 128]
            if part < 2:
                piece = turn(piece, cos[...], low[...], high[...])
            qkv[:, at : at + 128] = piece.astype(jnp.bfloat16)


def run_qkv(source, vecs, shift, tables, pieces, at, rows, filled):
    x, first = source
    width = x.shape[1]
    length = tables[0].shape[0]
    cols = shift.shape[1]
    bf = jnp.bfloat16
    base = at // ROW_BLOCK
    own = lambda i: (i + base, 0)
    return call(
        qkv_body,
        "norm_qkv",
        rows * 13 * MICROSECOND // 1024,
        (rows // ROW_BLOCK,),
        [rows_of(x, first), whole(vecs), whole(shift)]
        + [rows_of(t, at) for t in tables]
        + matrix(pieces, cols // 4, 0),
        [
            ((length, width), bf, (ROW_BLOCK, width), own),
            ((length, width), bf, (ROW_BLOCK, width), own),
            ((length, cols), bf, (ROW_BLOCK, cols), own),
        ],
        [room(pieces, cols // 4)],
        filled,
    )


def attend_body(q, k, v, ctx, lse):
    length = q.shape[0]
    step = ROW_BLOCK
    for head in range(2):
        lanes = slice(head * 64, head * 64 + 64)
        keys = k[:, lanes]
        vals = v[:, lanes]
        for at in range(0, length, step):
            end = at + step
            queries = q[at:end, lanes] * jnp.bfloat16(0.125)
            scores = nt_dot(queries, keys[:end])
            row = lax.broadcasted_iota(jnp.int32, (step, step), 0)
            col = lax.broadcasted_iota(jnp.int32, (step, step), 1)
            last = jnp.where(col <= row, scores[:, at:], MASK_FILL)
            scores = last if at == 0 else jnp.concatenate([scores[:, :at], last], axis=1)
            top = jnp.max(scores, axis=1, keepdims=True)
            power = jnp.exp(scores - top)
            total = jnp.sum(power, axis=1, keepdims=True)
            probs = (power * (1.0 / total)).astype(jnp.bfloat16)
            ctx[at:end, lanes] = nn_dot(probs, vals[:end]).astype(jnp.bfloat16)
            level = jnp.broadcast_to(top + jnp.log(total), (step, 128))
            lse[0, head : head + 1, at:end] = level.T[0:1]


def run_attend(qkv):
    length, cols = qkv.shape
    groups = cols // 384
    return call(
        attend_body,
        "attend",
        length * 19 * MICROSECOND // 1024,
        (groups,),
        [
            (qkv, (length, 128), lambda i: (0, 3 * i)),
            (qkv, (length, 128), lambda i: (0, 3 * i + 1)),
            (qkv, (length, 128), lambda i: (0, 3 * i + 2)),
        ],
        [
            ((length, groups * 128), jnp.bfloat16, (length, 128), lambda i: (0, i)),
            ((groups, 8, length), jnp.float32, (1, 8, length), lambda i: (i, 0, 0)),
        ],
    )


ERF_TOP = (
    0.00022905065861350646,
    0.0034082910107109506,
    0.050955695062380861,
    0.18520832239976145,
    1.128379143519084,
)
ERF_BOTTOM = (
    -1.1791602954361697e-7,
    0.000023547966471313185,
    0.0010179625278914885,
    0.014070470171167667,
    0.11098505178285362,
    0.49746925110067538,
    1.0,
)


def erf(x):
    x = jnp.clip(x, -3.7439211627767994, 3.7439211627767994)
    square = x * x
    top = jnp.full_like(x, ERF_TOP[0])
    for term in ERF_TOP[1:]:
        top = top * square + term
    bottom = jnp.full_like(x, ERF_BOTTOM[0])
    for term in ERF_BOTTOM[1:]:
        bottom = bottom * square + term
    return x * top / bottom


def mlp_body(ctx, ln_m, shift, *rest):
    act, slope, part, w_out, w_up, w_down = rest[24:]

    @pl.when(pl.program_id(0) == 0)
    def _():
        assemble(rest[:8], w_out)
        assemble(rest[8:16], w_up)
        assemble(rest[16:24], w_down)

    up = nn_dot(ln_m[...], w_up[...]) + shift[...]
    half_erf = 0.5 * erf(up * (2.0**-0.5)) + 0.5
    bell = jnp.exp(up * up * -0.5) * ((2.0 * math.pi) ** -0.5)
    active = (up * half_erf).astype(jnp.bfloat16)
    act[...] = active
    slope[...] = (half_erf + up * bell).astype(jnp.bfloat16)
    part[...] = (nt_dot(ctx[...], w_out[...]) + nt_dot(active, w_down[...])).astype(jnp.bfloat16)


def run_mlp(ctx, ln_m, shift, narrow, broad, at, rows, filled):
    length, width = ln_m.shape
    cols, heads = shift.shape[1], ctx.shape[1]
    bf = jnp.bfloat16
    base = at // ROW_BLOCK
    own = lambda i: (i + base, 0)
    return call(
        mlp_body,
        "mlp_out",
        rows * 32 * MICROSECOND // 1024,
        (rows // ROW_BLOCK,),
        [rows_of(ctx, at), rows_of(ln_m, at), whole(shift)]
        + matrix(narrow, heads // 4, 3)
        + matrix(broad, cols // 4, 0)
        + matrix(broad, cols // 4, 1),
        [
            ((length, cols), bf, (ROW_BLOCK, cols), own),
            ((length, cols), bf, (ROW_BLOCK, cols), own),
            ((rows, width), bf, (ROW_BLOCK, width), lambda i: (i, 0)),
        ],
        [room(narrow, heads // 4), room(broad, cols // 4), room(broad, cols // 4)],
        filled,
    )


def mlp_back_body(g, slope, *rest):
    d_up, d_ctx, sum_up, sum_g, w_out, w_down = rest[16:]

    @pl.when(pl.program_id(0) == 0)
    def _():
        assemble(rest[:8], w_out)
        assemble(rest[8:16], w_down)
        sum_up[...] = jnp.zeros_like(sum_up)
        sum_g[...] = jnp.zeros_like(sum_g)

    grad = g[...]
    du = (nn_dot(grad, w_down[...]) * slope[...].astype(jnp.float32)).astype(jnp.bfloat16)
    d_up[...] = du
    d_ctx[...] = nn_dot(grad, w_out[...]).astype(jnp.bfloat16)
    sum_up[...] += jnp.sum(du.astype(jnp.float32), axis=0, keepdims=True)
    sum_g[...] += jnp.sum(grad.astype(jnp.float32), axis=0, keepdims=True)


def run_mlp_back(source, slope, narrow, broad, at, rows, heads, filled):
    g, first = source
    width = g.shape[1]
    length, cols = slope.shape
    bf = jnp.bfloat16
    base = at // ROW_BLOCK
    own = lambda i: (i + base, 0)
    fixed = lambda i: (0, 0)
    return call(
        mlp_back_body,
        "mlp_back",
        rows * 15 * MICROSECOND // 1024,
        (rows // ROW_BLOCK,),
        [rows_of(g, first), rows_of(slope, at)]
        + matrix(narrow, heads // 4, 3)
        + matrix(broad, cols // 4, 1),
        [
            ((length, cols), bf, (ROW_BLOCK, cols), own),
            ((length, heads), bf, (ROW_BLOCK, heads), own),
            ((1, cols), jnp.float32, (1, cols), fixed),
            ((1, width), jnp.float32, (1, width), fixed),
        ],
        [room(narrow, heads // 4), room(broad, cols // 4)],
        filled,
    )


def attend_back_body(q, k, v, d_ctx, lse, cos, low, high, d_qkv, sums, dk_sum, dv_sum, dq_all):
    length = q.shape[0]
    step = ROW_BLOCK
    for head in range(2):
        lanes = slice(head * 64, head * 64 + 64)
        keys = k[:, lanes]
        vals = v[:, lanes]
        dk_sum[:, lanes] = jnp.zeros((length, 64), jnp.float32)
        dv_sum[:, lanes] = jnp.zeros((length, 64), jnp.float32)
        for at in range(0, length, step):
            end = at + step
            queries = q[at:end, lanes] * jnp.bfloat16(0.125)
            grads = d_ctx[at:end, lanes]
            scores = nt_dot(keys[:end], queries)
            power = jnp.exp(scores - lse[0, head : head + 1, at:end])
            key = lax.broadcasted_iota(jnp.int32, (step, step), 0)
            row = lax.broadcasted_iota(jnp.int32, (step, step), 1)
            last = jnp.where(key <= row, power[at:], 0.0)
            probs = last if at == 0 else jnp.concatenate([power[:at], last], axis=0)
            d_probs = nt_dot(vals[:end], grads)
            delta = jnp.sum(probs * d_probs, axis=0, keepdims=True)
            d_scores = (probs * (d_probs - delta)).astype(jnp.bfloat16)
            dv_sum[:end, lanes] += nn_dot(probs.astype(jnp.bfloat16), grads)
            dk_sum[:end, lanes] += nn_dot(d_scores, queries)
            dq_all[at:end, lanes] = tn_dot(d_scores, keys[:end]) * 0.125
    dq = turn(dq_all[...], cos[...], -low[...], -high[...]).astype(jnp.bfloat16)
    dk = turn(dk_sum[...], cos[...], -low[...], -high[...]).astype(jnp.bfloat16)
    dv = dv_sum[...].astype(jnp.bfloat16)
    for part, piece in enumerate((dq, dk, dv)):
        at = part * 128
        d_qkv[:, at : at + 128] = piece
        sums[:, at : at + 128] = jnp.sum(piece.astype(jnp.float32), axis=0, keepdims=True)


def run_attend_back(qkv, d_ctx, lse, tables):
    length, cols = qkv.shape
    groups = cols // 384
    wide = pltpu.VMEM((length, 128), jnp.float32)
    return call(
        attend_back_body,
        "attend_back",
        length * 26 * MICROSECOND // 1024,
        (groups,),
        [
            (qkv, (length, 128), lambda i: (0, 3 * i)),
            (qkv, (length, 128), lambda i: (0, 3 * i + 1)),
            (qkv, (length, 128), lambda i: (0, 3 * i + 2)),
            (d_ctx, (length, 128), lambda i: (0, i)),
            (lse, (1, 8, length), lambda i: (i, 0, 0)),
        ]
        + [whole(t) for t in tables],
        [
            ((length, cols), jnp.bfloat16, (length, 384), lambda i: (0, i)),
            ((1, cols), jnp.float32, (1, 384), lambda i: (0, i)),
        ],
        [wide, wide, wide],
    )


def norm_back_body(x, d_qkv, d_up, vecs, *rest):
    part, sums, w_qkv, w_up = rest[16:]

    @pl.when(pl.program_id(0) == 0)
    def _():
        assemble(rest[:8], w_qkv)
        assemble(rest[8:16], w_up)
        sums[...] = jnp.zeros_like(sums)

    hat, inverse = normalised(x[...].astype(jnp.float32))
    d_attn = nt_dot(d_qkv[...], w_qkv[...])
    d_mlp = nt_dot(d_up[...], w_up[...])
    for row, term in enumerate((d_attn * hat, d_mlp * hat, d_attn, d_mlp)):
        sums[row : row + 1, :] += jnp.sum(term, axis=0, keepdims=True)
    d_hat = d_attn * vecs[0:1, :] + d_mlp * vecs[2:3, :]
    along = jnp.mean(d_hat * hat, axis=-1, keepdims=True)
    level = jnp.mean(d_hat, axis=-1, keepdims=True)
    part[...] = (inverse * (d_hat - level - hat * along)).astype(jnp.bfloat16)


def run_norm_back(source, d_qkv, d_up, vecs, narrow, broad, at, rows):
    x, first = source
    width = x.shape[1]
    n_qkv, n_up = d_qkv.shape[1] // 4, d_up.shape[1] // 4
    return call(
        norm_back_body,
        "norm_back",
        rows * 21 * MICROSECOND // 1024,
        (rows // ROW_BLOCK,),
        [rows_of(x, first), rows_of(d_qkv, at), rows_of(d_up, at), whole(vecs)]
        + matrix(narrow, n_qkv, 0)
        + matrix(broad, n_up, 0),
        [
            ((rows, width), jnp.bfloat16, (ROW_BLOCK, width), lambda i: (i, 0)),
            ((8, width), jnp.float32, (8, width), lambda i: (0, 0)),
        ],
        [room(narrow, n_qkv), room(broad, n_up)],
    )


def weight_grad_body(cuts, *refs):
    a_refs, b_refs, rest = refs[: sum(cuts)], refs[sum(cuts) :], refs[sum(cuts) + 2 :]
    keep, send, turned_one, turned_two = rest
    groups = (a_refs[: cuts[0]], a_refs[cuts[0] :])

    @pl.when(pl.program_id(0) == 0)
    def _():
        for group, turned in zip(groups, (turned_one, turned_two)):
            at = 0
            for ref in group:
                turned[:, at : at + ref.shape[0]] = ref[...].T
                at += ref.shape[0]

    at = 0
    rows = keep.shape[2]
    for turned, right in zip((turned_one, turned_two), b_refs[:2]):
        size = right.shape[1]
        grad = nn_dot(turned[...], right[...]).astype(jnp.bfloat16)
        for side in range(2):
            first = 2 * side * rows
            keep[0, side, :, at : at + size] = grad[first : first + rows]
            send[0, side, :, at : at + size] = grad[first + rows : first + 2 * rows]
        at += size


def run_weight_grad(lefts, rights):
    length, width = rights[0].shape[0], lefts[0][0].shape[1]
    sizes = [right.shape[1] // 4 for right in rights]
    shape = (4, 2, width // 4, sum(sizes))
    out = (shape, jnp.bfloat16, (1,) + shape[1:], lambda i: (i, 0, 0, 0))
    turned = pltpu.VMEM((width, length), jnp.bfloat16)
    return call(
        partial(weight_grad_body, tuple(len(group) for group in lefts)),
        "weight_grad",
        length * 14 * MICROSECOND // 1024,
        (4,),
        [whole(left) for group in lefts for left in group]
        + [(r, (length, n), lambda i: (0, i)) for r, n in zip(rights, sizes)],
        [out, out],
        [turned, turned],
    )


def turn_tables(length):
    cosine, sine_tab = rotary_tables(length)
    zero = jnp.zeros_like(sine_tab)
    rest = jnp.zeros((length, 64 - ROT), jnp.float32)
    cos = jnp.concatenate([cosine, cosine, rest + 1.0], axis=1)
    low = jnp.concatenate([zero, sine_tab, rest], axis=1)
    high = jnp.concatenate([-sine_tab, zero, rest], axis=1)
    return tuple(jnp.concatenate([t, t], axis=1) for t in (cos, low, high))


def by_sequence(
    acts_in, cotangent, norm_gains, vec_bias, w_qkv, b_qkv, w_out, w_up, b_up, w_down
):
    section = lax.axis_index("section")
    across = lax.axis_index("dp")
    along = lax.axis_index("tensor")
    first_section = section == 0
    width = acts_in.shape[3]
    rows = w_qkv.shape[1]
    positions = acts_in.shape[1]
    length = 4 * positions
    heads = b_qkv.shape[1]
    bf = jnp.bfloat16

    qkv_halves = (
        w_qkv[0].reshape(rows, 2, 2, 3, 64).transpose(1, 0, 3, 2, 4).reshape(2, rows, -1)
    )
    out_halves = w_out[0].T.reshape(rows, 2, -1).transpose(1, 0, 2)
    up_halves = w_up[0].reshape(rows, 2, -1).transpose(1, 0, 2)
    down_halves = w_down[0].T.reshape(rows, 2, -1).transpose(1, 0, 2)
    n_qkv, n_out, n_up = qkv_halves.shape[2], out_halves.shape[2], up_halves.shape[2]

    narrow = jnp.stack([jnp.concatenate([qkv_halves[h], out_halves[h]], axis=1) for h in (0, 1)])
    broad = jnp.stack([jnp.concatenate([up_halves[h], down_halves[h]], axis=1) for h in (0, 1)])
    small = jnp.concatenate(
        [
            norm_gains[0].reshape(-1),
            vec_bias[0].reshape(-1),
            b_qkv[0].reshape(-1).astype(jnp.float32),
            b_up[0].reshape(-1).astype(jnp.float32),
        ]
    )
    clock = Clock()
    hold, tick = clock.hold, clock.tick

    def pass_half(halves):
        return swap(hold(pick(halves, 1 - section)), "section", 1)

    def by_layer(halves, got):
        keep = pick(halves, section)
        return jnp.where(first_section, keep, got), jnp.where(first_section, got, keep)

    def x_swap(value):
        return swap(hold(value), "dp", 2)

    def core_swap(value):
        return swap(hold(value), "dp", 1)

    def y_swap(value):
        return swap(hold(value), "section", 1)

    def both_ways(value):
        value = hold(value)
        return ring(value, "tensor", 1), ring(value, "tensor", -1)

    def far_halves(left, right):
        half = left.shape[0] // 2
        return ring(hold(left[:half]), "tensor", 1), ring(hold(right[half:]), "tensor", -1)

    def own_half(blocks):
        return lax.dynamic_slice_in_dim(blocks, section * (width // 2), width // 2, 2)

    def both_halves(own, got):
        own = own.reshape(length, width // 2)
        got = got.reshape(length, width // 2)
        low = jnp.where(first_section, own, got)
        high = jnp.where(first_section, got, own)
        return relative(jnp.concatenate([low, high], axis=1), across)

    def stacked(own, got):
        return jnp.stack([own, got])

    got_narrow = pass_half(narrow)
    got_small = swap(small, "section", 1)
    blocks = own_half(acts_in[:, :, 0, :])
    near = exchange_near(blocks, along, hold)
    tick(got_narrow, got_small, near)
    narrow_shards = by_layer(narrow, got_narrow)
    small = jnp.where(first_section, jnp.stack([small, got_small]), jnp.stack([got_small, small]))
    left, right = both_ways(narrow_shards[0])
    far = exchange_far(near, hold)
    got_broad = pass_half(broad)
    got_own = x_swap(narrow_shards[0])
    small = jnp.stack([small, core_swap(small)])
    small = jnp.concatenate([small, swap(small, "dp", 2)])
    tick(left, right, far, got_broad, got_own, small)
    own_acts = exchanged(blocks, near, far, along)
    got_acts = y_swap(own_acts)
    narrow_far = far_halves(left, right)
    got_left, got_right = x_swap(left), x_swap(right)
    small = jnp.stack([small, swap(hold(small), "tensor", 1)])
    tick(narrow_far, got_left, got_right, small)
    broad_shards = by_layer(broad, got_broad)
    small = jnp.concatenate([small, swap(hold(small), "tensor", 2)])
    broad_left, broad_right = both_ways(broad_shards[0])
    narrow_far = jnp.concatenate(narrow_far, axis=0)
    got_far = x_swap(narrow_far)
    pieces = [
        stacked(narrow_shards[0], got_own),
        stacked(left, got_left),
        stacked(right, got_right),
    ]
    others = [core_swap(piece) for piece in pieces]
    tick(got_far, others, got_acts, small)
    acts = both_halves(own_acts, got_acts)
    pieces.append(stacked(narrow_far, got_far))
    others.append(core_swap(pieces[3]))
    got_own = x_swap(broad_shards[0])
    narrow_zero = (*pieces, *others)
    tick(others[3])

    share = norm_gains.shape[2]
    vec_part = small[..., : 6 * share].reshape(4, 4, 2, 6, share)
    offsets = jnp.array(FAR_ORDER, jnp.int32)
    order = jnp.stack([pick(offsets, (k - along) % 4) for k in range(4)])
    slots = [jnp.bitwise_xor((along + k) % 4, along) for k in (0, 3, 1, 2)]
    vec_part = jnp.stack([pick(vec_part, jnp.bitwise_xor(along, k)) for k in range(4)])
    vecs_full = vec_part.transpose(2, 3, 1, 0, 4).reshape(2, 6, width)
    at = 6 * share
    share_q = b_qkv.shape[2]
    dp_order = [jnp.bitwise_xor(across, k) for k in range(4)]
    qkv_bias = small[..., at : at + heads * share_q].reshape(4, 4, 2, heads, share_q)
    qkv_bias = jnp.stack([pick(qkv_bias, k) for k in slots])
    qkv_bias = jnp.stack([pick(qkv_bias, i, 1) for i in dp_order], axis=1)
    qkv_bias = qkv_bias.transpose(2, 0, 3, 1, 4).reshape(2, 4, 2, heads // 2, 3, 64)
    qkv_bias = pick(qkv_bias, section, 2).transpose(0, 1, 3, 2, 4).reshape(2, 1, -1)
    at += heads * share_q
    bias_rows, share_u = b_up.shape[1], b_up.shape[2]
    up_bias = small[..., at : at + bias_rows * share_u].reshape(4, 4, 2, bias_rows, share_u)
    up_bias = jnp.stack([pick(up_bias, k) for k in slots])
    up_bias = jnp.stack([pick(up_bias, i, 1) for i in dp_order], axis=1)
    up_bias = up_bias.transpose(2, 0, 3, 1, 4).reshape(2, 4, 2, bias_rows // 2, 4 * share_u)
    up_bias = pick(up_bias, section, 2).reshape(2, 1, -1)
    zero_rows = jnp.zeros((4, width), jnp.float32)

    tables = turn_tables(length)
    chunk = length // CHUNKS
    starts = [i * chunk for i in range(CHUNKS)]

    all_vecs = [
        jnp.concatenate([v[0:1], v[2:3], v[1:2], v[3:4], zero_rows], axis=0) for v in vecs_full
    ]

    def project(layer, i, source, pieces, filled):
        return run_qkv(
            source, all_vecs[layer], qkv_bias[layer], tables, pieces, starts[i], chunk, filled
        )

    def feed(layer, i, ctx, ln_m, narrow, broad, filled):
        *filled, part = run_mlp(
            hold(ctx), ln_m, up_bias[layer], narrow, broad, starts[i], chunk, filled
        )
        return filled, part

    def join(layer, before, part, got):
        total = part.astype(jnp.float32) + got.astype(jnp.float32)
        full = vecs_full[layer]
        return (before.astype(jnp.float32) + total + (full[4] + full[5])).astype(bf)

    acts = hold(acts)
    first = project(0, 0, (acts, 0), narrow_zero, ())
    tick(first, broad_left, broad_right)
    got_left = x_swap(broad_left)
    first = project(0, 1, (acts, chunk), narrow_zero, first)
    tick(first, got_own)
    ln_a0, ln_m0, qkv0 = first
    broad_far = far_halves(broad_left, broad_right)
    got_right = x_swap(broad_right)
    ctx0, lse0 = run_attend(hold(qkv0))
    tick(ctx0, broad_far, got_left, got_right)
    broad_far = jnp.concatenate(broad_far, axis=0)
    got_far = x_swap(broad_far)
    pieces = [
        stacked(broad_shards[0], got_own),
        stacked(broad_left, got_left),
        stacked(broad_right, got_right),
    ]
    others = [core_swap(piece) for piece in pieces]
    tick(got_far, others)
    pieces.append(stacked(broad_far, got_far))
    others.append(core_swap(pieces[3]))
    broad_zero = (*pieces, *others)
    tick(others[3])
    first, part_a = feed(0, 0, ctx0, ln_m0, narrow_zero, broad_zero, ())
    left, right = both_ways(narrow_shards[1])
    got_own = x_swap(narrow_shards[1])
    broad_own = x_swap(broad_shards[1])
    tick(part_a, left, right, got_own, broad_own)
    first, part_b = feed(0, 1, ctx0, ln_m0, narrow_zero, broad_zero, first)
    act0, slope0 = first
    got_a = y_swap(part_a)
    narrow_far = far_halves(left, right)
    broad_left, broad_right = both_ways(broad_shards[1])
    tick(part_b, got_a, narrow_far, broad_left, broad_right)
    got_b = y_swap(part_b)
    got_left, got_right = x_swap(left), x_swap(right)
    x1_a = join(0, acts[:chunk], part_a, got_a)
    tick(got_left, got_right)
    narrow_far = jnp.concatenate(narrow_far, axis=0)
    got_far = x_swap(narrow_far)
    pieces = [
        stacked(narrow_shards[1], got_own),
        stacked(left, got_left),
        stacked(right, got_right),
    ]
    others = [core_swap(piece) for piece in pieces]
    tick(got_b, got_far, others)
    x1_b = join(0, acts[chunk:], part_b, got_b)
    pieces.append(stacked(narrow_far, got_far))
    others.append(core_swap(pieces[3]))
    narrow_one = (*pieces, *others)
    tick(others[3], x1_a, x1_b)

    broad_far = far_halves(broad_left, broad_right)
    got_left = x_swap(broad_left)
    first = project(1, 0, (hold(x1_a), 0), narrow_one, ())
    first = project(1, 1, (x1_b, 0), narrow_one, first)
    ln_a1, ln_m1, qkv1 = first
    tick(first, broad_far, got_left)
    broad_far = jnp.concatenate(broad_far, axis=0)
    got_right, got_far = x_swap(broad_right), x_swap(broad_far)
    pieces = [stacked(broad_shards[1], broad_own), stacked(broad_left, got_left)]
    others = [core_swap(piece) for piece in pieces]
    ctx1, lse1 = run_attend(hold(qkv1))
    tick(ctx1, got_right, got_far, others)
    pieces += [stacked(broad_right, got_right), stacked(broad_far, got_far)]
    others += [core_swap(piece) for piece in pieces[2:]]
    broad_one = (*pieces, *others)
    tick(others[2:])
    first, part_a = feed(1, 0, ctx1, ln_m1, narrow_one, broad_one, ())
    blocks = own_half(cotangent[:, :, 0, :])
    near = exchange_near(blocks, along, hold)
    tick(part_a, near)
    first, part_b = feed(1, 1, ctx1, ln_m1, narrow_one, broad_one, first)
    act1, slope1 = first
    far = exchange_far(near, hold)
    tick(far)
    own_grads = exchanged(blocks, near, far, along)
    got_grads = y_swap(own_grads)
    tick(part_b, got_grads)

    grads = hold(both_halves(own_grads, got_grads))
    n_heads = ctx0.shape[1]

    def back(i, source, slope, narrow, broad, filled):
        *filled, up_term, g_term = run_mlp_back(
            source, slope, narrow, broad, starts[i], chunk, n_heads, filled
        )
        return filled, up_term, g_term

    first, up_a, g_a = back(0, (grads, 0), slope1, narrow_one, broad_one, ())
    first, up_b, g_b = back(1, (grads, chunk), slope1, narrow_one, broad_one, first)
    d_up1, d_ctx1 = first
    sums_one = [None, g_a + g_b, None, up_a + up_b]
    got_a = y_swap(part_a)
    tick(first, got_a)
    x1 = jnp.concatenate([x1_a, x1_b], axis=0)

    def to_blocks(values):
        return relative(values, across).reshape(4, positions, width)

    d_qkv1, sums_one[2] = run_attend_back(qkv1, hold(d_ctx1), lse1, tables)
    got_b = y_swap(part_b)
    tick(d_qkv1, got_b)
    x2 = jnp.concatenate(
        [join(1, x1_a, part_a, got_a), join(1, x1_b, hold(part_b), got_b)], axis=0
    )
    out_blocks = to_blocks(jnp.where(first_section, x1, x2))
    part_a, sum_a = run_norm_back(
        (x1_a, 0), hold(d_qkv1), d_up1, all_vecs[1], narrow_one, broad_one, 0, chunk
    )
    tick(part_a, out_blocks)
    got_a = y_swap(part_a)
    part_b, sum_b = run_norm_back(
        (x1_b, 0), hold(d_qkv1), d_up1, all_vecs[1], narrow_one, broad_one, chunk, chunk
    )
    sums_one[0] = (sum_a + sum_b)[:4]
    keep_broad, send = run_weight_grad([[hold(ln_m1)], [grads]], [d_up1, act1])
    tick(part_b, keep_broad, got_a)
    got_b = y_swap(part_b)
    got_core = core_swap(send)
    out_near = exchange_near(out_blocks, along, hold)
    keep_narrow, send_narrow = run_weight_grad([[hold(ln_a1)], [grads]], [d_qkv1, ctx1])
    tick(keep_narrow, got_b, got_core)

    def lower(above, part, got):
        total = part.astype(jnp.float32) + got.astype(jnp.float32)
        return (above.astype(jnp.float32) + total).astype(bf)

    g1_a = lower(grads[:chunk], hold(part_a), got_a)
    g1_b = lower(grads[chunk:], hold(part_b), got_b)
    broad_sum = add_wide(hold(keep_broad), got_core)
    got_core = core_swap(send_narrow)
    got_x = [x_swap(broad_sum[2:, 1])]
    first, up_a, g_a = back(0, (hold(g1_a), 0), slope0, narrow_zero, broad_zero, ())
    first, up_b, g_b = back(1, (g1_b, 0), slope0, narrow_zero, broad_zero, first)
    d_up0, d_ctx0 = first
    sums_zero = [None, g_a + g_b, None, up_a + up_b]
    tick(first, got_core, got_x, out_near)
    out_far = exchange_far(out_near, hold)
    narrow_sum = add_wide(hold(keep_narrow), got_core)
    got_narrow = x_swap(narrow_sum[:, 1])
    got_x.append(x_swap(broad_sum[:2, 1]))
    keep_broad, send = run_weight_grad([[hold(ln_m0)], [g1_a, g1_b]], [d_up0, act0])
    tick(keep_broad, out_far)

    def after_x(total, got):
        late = add_wide(total[2:, 0], got[0])
        early = add_wide(total[:2, 0], got[1])
        return [early[0], early[1], late[0], late[1]]

    got_core = core_swap(send)
    late = add_wide(hold(broad_sum[2:, 0]), got_x[0])
    broad_got = ring_first([None, None, late[0], late[1]], hold)
    d_qkv0, sums_zero[2] = run_attend_back(qkv0, hold(d_ctx0), lse0, tables)
    tick(d_qkv0, broad_got, got_core, got_x, got_narrow)
    early = add_wide(hold(broad_sum[:2, 0]), got_x[1])
    broad_one_sum = [early[0], early[1], late[0], late[1]]
    narrow_sum = add_wide(hold(narrow_sum[:, 0]), got_narrow)
    narrow_sum = [narrow_sum[k] for k in range(4)]
    broad_sum = add_wide(hold(keep_broad), got_core)
    got_x = [x_swap(broad_sum[2:, 1])]
    broad_got = ring_second(broad_one_sum, broad_got, hold)
    part_a, sum_a = run_norm_back(
        (acts, 0), hold(d_qkv0), d_up0, all_vecs[0], narrow_zero, broad_zero, 0, chunk
    )
    tick(part_a, broad_got)
    got_a = y_swap(part_a)
    narrow_got = ring_first(narrow_sum, hold)
    part_b, sum_b = run_norm_back(
        (acts, chunk), hold(d_qkv0), d_up0, all_vecs[0], narrow_zero, broad_zero, chunk, chunk
    )
    sums_zero[0] = (sum_a + sum_b)[:4]
    tick(part_b, got_x, narrow_got)
    got_b = y_swap(part_b)
    narrow_got = ring_second(narrow_sum, narrow_got, hold)
    got_x.append(x_swap(broad_sum[:2, 1]))
    keep_narrow, send_narrow = run_weight_grad([[hold(ln_a0)], [g1_a, g1_b]], [d_qkv0, ctx0])
    tick(keep_narrow, got_a, narrow_got)

    flat = []
    for norm_sums, sum_g, sum_qkv, sum_up in (sums_zero, sums_one):
        feature = relative(jnp.concatenate([norm_sums, sum_g], axis=0), across)
        q_sum = sum_qkv.reshape(4, 3, 2, 64).transpose(0, 2, 1, 3).reshape(4, -1)
        both = jnp.concatenate([q_sum, sum_up.reshape(4, -1)], axis=1)
        both = jnp.stack([pick(both, order[k]) for k in range(4)])
        flat.append(jnp.concatenate([feature.reshape(-1), both.reshape(-1)]))
    flat = jnp.stack(flat)
    got_core = core_swap(send_narrow)
    late = add_wide(hold(broad_sum[2:, 0]), got_x[0])
    broad_next = ring_first([None, None, late[0], late[1]], hold)
    tick(got_b, got_x, broad_next, got_core)
    early = add_wide(hold(broad_sum[:2, 0]), got_x[1])
    broad_zero_sum = [early[0], early[1], late[0], late[1]]
    grads_low = jnp.concatenate(
        [lower(g1_a, hold(part_a), got_a), lower(g1_b, hold(part_b), got_b)], axis=0
    )
    g1 = jnp.concatenate([g1_a, g1_b], axis=0)
    grad_blocks = to_blocks(jnp.where(first_section, grads_low, g1))
    tick(grad_blocks)
    grad_near = exchange_near(grad_blocks, along, hold)
    zero_sum = add_wide(keep_narrow, got_core)
    got_narrow = x_swap(zero_sum[:, 1])
    flat = flat + core_swap(flat)
    one_broad = ring_total(hold(broad_one_sum[0]), broad_got)
    one_narrow = ring_total(hold(narrow_sum[0]), narrow_got)
    acts_local = exchanged(hold(out_blocks), out_near, out_far, along)
    tick(grad_near, got_narrow, flat, acts_local)
    broad_next = ring_second(broad_zero_sum, broad_next, hold)
    zero_sum = add_wide(hold(zero_sum[:, 0]), got_narrow)
    zero_sum = [zero_sum[k] for k in range(4)]
    narrow_next = ring_first(zero_sum, hold)
    flat = flat + x_swap(flat)
    tick(narrow_next, broad_next, flat)
    zero_broad = ring_total(broad_zero_sum[0], broad_next)
    broad_send = y_swap(jnp.where(first_section, one_broad, zero_broad))
    narrow_next = ring_second(zero_sum, narrow_next, hold)
    grad_far = exchange_far(grad_near, hold)
    flat = flat + swap(hold(flat), "tensor", 1)
    tick(narrow_next, grad_far, broad_send, flat)
    zero_narrow = ring_total(zero_sum[0], narrow_next)
    narrow_send = y_swap(jnp.where(first_section, one_narrow, zero_narrow))
    flat = flat + swap(hold(flat), "tensor", 2)
    grad_local = exchanged(grad_blocks, grad_near, grad_far, along)

    def whole_layer(keep_pair, got):
        keep = jnp.where(first_section, *keep_pair).astype(jnp.float32)
        got = got.astype(jnp.float32)
        return jnp.where(first_section, jnp.stack([keep, got], 1), jnp.stack([got, keep], 1))

    narrow_out = whole_layer((zero_narrow, one_narrow), narrow_send)
    broad_out = whole_layer((zero_broad, one_broad), broad_send)
    grad_qkv = narrow_out[..., :n_qkv].reshape(rows, 2, 3, 2, 64)
    grad_qkv = grad_qkv.transpose(0, 1, 3, 2, 4).reshape(rows, -1)
    grad_out = narrow_out[..., n_qkv:].reshape(rows, -1).T
    grad_up = broad_out[..., :n_up].reshape(rows, -1)
    grad_down = broad_out[..., n_up:].reshape(rows, -1).T

    keep = pick(flat, section)
    mine = pick(flat, 1 - section)
    got = swap(mine, "section", 1)
    n_feature = 5 * width
    feature_own = keep[:n_feature].reshape(5, width)
    feature = feature_own[:4] + got[: 4 * width].reshape(4, width)
    place_at = (across * 4 + along) * share
    gain_share = lax.dynamic_slice_in_dim(feature[:2], place_at, share, 1)
    shifts = jnp.concatenate([feature[2:4], feature_own[4:5], feature_own[4:5]], axis=0)
    bias_share = lax.dynamic_slice_in_dim(shifts, place_at, share, 1)
    low_half = jnp.where(first_section, keep, got)[n_feature:].reshape(4, -1)
    high_half = jnp.where(first_section, got, keep)[n_feature:].reshape(4, -1)
    halves = jnp.stack([pick(low_half, along), pick(high_half, along)])
    n_head = (heads // 2) * 192
    head_sums = halves[:, :n_head].reshape(heads, 192)
    head_share = lax.dynamic_slice_in_dim(head_sums, across * share_q, share_q, 1)
    unit_sums = halves[:, n_head:].reshape(bias_rows, 4 * share_u)
    unit_share = lax.dynamic_slice_in_dim(unit_sums, across * share_u, share_u, 1)
    return (
        acts_local[None, :, :, None],
        grad_local[None, :, :, None],
        gain_share[None],
        bias_share[None],
        grad_qkv[None],
        head_share[None],
        grad_out[None],
        grad_up[None],
        unit_share[None],
        grad_down[None],
    )


def fits(mesh, args):
    acts_in, b_qkv = args[0], args[5]
    sizes = dict(mesh.shape)
    return (
        sizes["section"] == 2
        and sizes["dp"] == 4
        and sizes["tensor"] == MICRO
        and MICRO == 4
        and acts_in.shape[2] == sizes["dp"]
        and b_qkv.shape[1] == 16
        and b_qkv.shape[2] == 192
        and acts_in.shape[1] % (CHUNKS * ROW_BLOCK) == 0
    )


def solution(mesh):
    placed = (
        P(None, "tensor", "dp", None),
        P(None, "tensor", "dp", None),
        P("section", None, ("dp", "tensor")),
        P("section", None, ("dp", "tensor")),
        P("section", "dp", "tensor"),
        P("section", "tensor", "dp"),
        P("section", "tensor", "dp"),
        P("section", "dp", "tensor"),
        P("section", "tensor", "dp"),
        P("section", "tensor", "dp"),
    )
    def wrap(body):
        return jax.shard_map(
            body,
            mesh=mesh,
            in_specs=placed,
            out_specs=(
                P("section", None, "tensor", "dp", None),
                P("section", None, "tensor", "dp", None),
                P("section", None, ("dp", "tensor")),
                P("section", None, ("dp", "tensor")),
                P("section", "dp", "tensor"),
                P("section", "tensor", "dp"),
                P("section", "tensor", "dp"),
                P("section", "dp", "tensor"),
                P("section", "tensor", "dp"),
                P("section", "tensor", "dp"),
            ),
            check_vma=False,
        )

    return lambda *args: wrap(by_sequence if fits(mesh, args) else local)(*args)
```

```python
from functools import partial
import math

import jax
import jax.numpy as jnp
from jax import lax
from jax.experimental import pallas as pl
from jax.experimental.pallas import tpu as pltpu
from jax.sharding import PartitionSpec as P

ROT = 16
QBLOCK = 512
MICRO = 4


NORM_EPS = 1e-05
ROPE_BASE = 10000.0
MASK_FILL = -1e30


def from_behind(value, axis, by):
    length = lax.axis_size(axis)
    pairs = [(i, i + by) for i in range(length) if 0 <= i + by < length]
    return lax.ppermute(value, axis, pairs)


def layer_norm(values, norm_gain, norm_shift):
    average = jnp.mean(values, axis=-1, keepdims=True)
    centred = values - average
    variance = jnp.mean(centred * centred, axis=-1, keepdims=True)
    return centred * lax.rsqrt(variance + NORM_EPS) * norm_gain + norm_shift


def both_norms(values, gain_attn, shift_attn, gain_mlp, shift_mlp):
    return (layer_norm(values, gain_attn, shift_attn), layer_norm(values, gain_mlp, shift_mlp))


def rotary_tables(length):
    half_rot = ROT // 2
    frequency = jnp.exp(
        jnp.arange(half_rot, dtype=jnp.float32) * (-2.0 * math.log(ROPE_BASE) / ROT)
    )
    angles = jnp.arange(length, dtype=jnp.float32)[:, None] * frequency[None, :]
    return (jnp.cos(angles), jnp.sin(angles))


def rotate(values, cosine, sine_tab):
    half_rot = ROT // 2
    low_half = values[..., :half_rot]
    high_half = values[..., half_rot:ROT]
    return jnp.concatenate(
        [
            low_half * cosine - high_half * sine_tab,
            high_half * cosine + low_half * sine_tab,
            values[..., ROT:],
        ],
        axis=-1,
    )


def rotate_back(grads_rot, cosine, sine_tab):
    half_rot = ROT // 2
    low_half = grads_rot[..., :half_rot]
    high_half = grads_rot[..., half_rot:ROT]
    return jnp.concatenate(
        [
            low_half * cosine + high_half * sine_tab,
            high_half * cosine - low_half * sine_tab,
            grads_rot[..., ROT:],
        ],
        axis=-1,
    )


def causal_scores(queries, key_rows, first_row, score_scale):
    block_rows = queries.shape[0]
    last_row = key_rows.shape[0]
    scores = (
        jnp.einsum("qshd,kshd->shqk", queries, key_rows, preferred_element_type=jnp.float32)
        * score_scale
    )
    row_pos = first_row + jnp.arange(block_rows, dtype=jnp.int32)
    col_pos = jnp.arange(last_row, dtype=jnp.int32)
    allowed = col_pos[None, :] <= row_pos[:, None]
    return (scores, allowed)


def attend(queries, key_rows, val_rows):
    length = queries.shape[0]
    block_rows = min(QBLOCK, length)
    score_scale = queries.shape[-1] ** (-0.5)
    outputs = []
    totals = []
    for block_index in range(length // block_rows):
        first_row = block_index * block_rows
        last_row = first_row + block_rows
        scores, allowed = causal_scores(
            queries[first_row:last_row], key_rows[:last_row], first_row, score_scale
        )
        scores = jnp.where(allowed, scores, MASK_FILL)
        highest = jnp.max(scores, axis=-1, keepdims=True)
        exponent = jnp.exp(scores - highest)
        denominator = jnp.sum(exponent, axis=-1, keepdims=True)
        probability = (exponent / denominator).astype(jnp.bfloat16)
        block_out = jnp.einsum(
            "shqk,kshd->qshd", probability, val_rows[:last_row], preferred_element_type=jnp.float32
        )
        outputs.append(block_out.astype(jnp.bfloat16))
        totals.append((highest + jnp.log(denominator))[..., 0])
    context = jnp.concatenate(outputs, axis=0)
    return (context.reshape(length, context.shape[1], -1), jnp.concatenate(totals, axis=-1))


def attend_back(queries, key_rows, val_rows, d_context, log_total):
    length = queries.shape[0]
    block_rows = min(QBLOCK, length)
    score_scale = queries.shape[-1] ** (-0.5)
    grad_query_list = []
    grad_keys = jnp.zeros(queries.shape, jnp.float32)
    grad_vals = jnp.zeros(queries.shape, jnp.float32)
    for block_index in range(length // block_rows):
        first_row = block_index * block_rows
        last_row = first_row + block_rows
        query_block = queries[first_row:last_row]
        scores, allowed = causal_scores(query_block, key_rows[:last_row], first_row, score_scale)
        probability = jnp.where(
            allowed, jnp.exp(scores - log_total[:, :, first_row:last_row, None]), 0.0
        )
        d_block = d_context[first_row:last_row]
        d_prob = jnp.einsum(
            "qshd,kshd->shqk", d_block, val_rows[:last_row], preferred_element_type=jnp.float32
        )
        delta = jnp.sum(probability * d_prob, axis=-1, keepdims=True)
        d_scores = (probability * (d_prob - delta)).astype(jnp.bfloat16)
        grad_query_list.append(
            jnp.einsum(
                "shqk,kshd->qshd", d_scores, key_rows[:last_row], preferred_element_type=jnp.float32
            )
            * score_scale
        )
        grad_keys = grad_keys.at[:last_row].add(
            jnp.einsum("shqk,qshd->kshd", d_scores, query_block, preferred_element_type=jnp.float32)
            * score_scale
        )
        grad_vals = grad_vals.at[:last_row].add(
            jnp.einsum(
                "shqk,qshd->kshd",
                probability.astype(jnp.bfloat16),
                d_block,
                preferred_element_type=jnp.float32,
            )
        )
    return (jnp.concatenate(grad_query_list, axis=0), grad_keys, grad_vals)


def local(acts_in, cotangent, norm_gains, vec_bias, w_qkv, b_qkv, w_out, w_up, b_up, w_down):
    section_index = lax.axis_index("section")
    own_start = lax.axis_index("tensor") * acts_in.shape[1]
    local_len = acts_in.shape[1]
    seq_count = acts_in.shape[2]
    model_width = acts_in.shape[3]
    length = local_len * lax.axis_size("tensor")
    all_rows = length * seq_count
    gain_full, bias_full = (
        lax.all_gather(norm_gains[0], ("dp", "tensor"), axis=1, tiled=True),
        lax.all_gather(vec_bias[0], ("dp", "tensor"), axis=1, tiled=True),
    )
    mat_qkv, bias_qkv, mat_out, mat_up, bias_up, mat_down = (
        lax.all_gather(w_qkv[0], "dp", axis=0, tiled=True),
        lax.all_gather(b_qkv[0], "dp", axis=1, tiled=True),
        lax.all_gather(w_out[0], "dp", axis=1, tiled=True),
        lax.all_gather(w_up[0], "dp", axis=0, tiled=True),
        lax.all_gather(b_up[0], "dp", axis=1, tiled=True),
        lax.all_gather(w_down[0], "dp", axis=1, tiled=True),
    )
    head_count = bias_qkv.shape[0]
    head_dim = bias_qkv.shape[1] // 3
    qkv_shift = bias_qkv.reshape(-1).astype(jnp.float32)
    up_shift = bias_up.reshape(-1).astype(jnp.float32)
    cosine, sine_tab = rotary_tables(length)
    cosine = cosine[:, None, None, :]
    sine_tab = sine_tab[:, None, None, :]
    received = jnp.zeros_like(acts_in[0])
    stash_list = []
    out_list = []
    for moment in range(MICRO + 1):
        own_rows = acts_in[min(moment, MICRO - 1)]
        inputs = jnp.where(section_index == 0, own_rows, received)
        forward_gathered = lax.all_gather(inputs, "tensor", axis=0, tiled=True)
        full_attn, full_mlp = both_norms(
            forward_gathered.astype(jnp.float32),
            gain_full[0],
            bias_full[0],
            gain_full[1],
            bias_full[1],
        )
        forward_normed_attn = full_attn.astype(jnp.bfloat16)
        forward_normed_mlp = full_mlp.astype(jnp.bfloat16)
        forward_flat_attn = forward_normed_attn.reshape(all_rows, model_width)
        forward_flat_mlp = forward_normed_mlp.reshape(all_rows, model_width)
        projected = (
            jnp.dot(forward_flat_attn, mat_qkv, preferred_element_type=jnp.float32) + qkv_shift
        )
        projected = projected.reshape(length, seq_count, head_count, 3, head_dim)
        forward_queries = rotate(projected[:, :, :, 0], cosine, sine_tab).astype(jnp.bfloat16)
        forward_key_rows = rotate(projected[:, :, :, 1], cosine, sine_tab).astype(jnp.bfloat16)
        forward_val_rows = projected[:, :, :, 2].astype(jnp.bfloat16)
        forward_context, forward_log_total = attend(
            forward_queries, forward_key_rows, forward_val_rows
        )
        forward_up_proj = (
            jnp.dot(forward_flat_mlp, mat_up, preferred_element_type=jnp.float32) + up_shift
        )
        forward_activated = jax.nn.gelu(forward_up_proj, approximate=False).astype(jnp.bfloat16)
        active_rows = forward_activated.reshape(length, seq_count, -1)
        context_part = forward_context.reshape(lax.axis_size("tensor") * local_len * seq_count, -1)
        active_part = active_rows.reshape(lax.axis_size("tensor") * local_len * seq_count, -1)
        summed = jnp.dot(context_part, mat_out, preferred_element_type=jnp.float32) + jnp.dot(
            active_part, mat_down, preferred_element_type=jnp.float32
        )
        mixed_sum = lax.psum_scatter(
            summed.reshape(lax.axis_size("tensor") * local_len, seq_count, model_width),
            "tensor",
            scatter_dimension=0,
            tiled=True,
        )
        result = inputs.astype(jnp.float32) + mixed_sum + bias_full[2] + bias_full[3]
        forward_stashed = (
            forward_gathered,
            forward_normed_attn,
            forward_normed_mlp,
            forward_queries,
            forward_key_rows,
            forward_val_rows,
            forward_context,
            forward_log_total,
            forward_up_proj,
            forward_activated,
        )
        result, stashed = (result.astype(jnp.bfloat16), forward_stashed)
        stash_list.append(stashed)
        out_list.append(result)
        if moment < MICRO:
            received = from_behind(result, "section", 1)
    stash_all = jax.tree.map(lambda *parts: jnp.stack(parts), *stash_list)
    acts_local = lax.dynamic_slice_in_dim(jnp.stack(out_list), section_index, MICRO, 0)
    back_received = jnp.zeros_like(cotangent[0])
    grad_list = []
    weight_sums = None
    vector_sums = None
    for moment in range(MICRO + 1):
        micro_index = moment - 1 + section_index
        is_valid = (micro_index >= 0) & (micro_index < MICRO)
        source_clock = jnp.clip(micro_index + section_index, 0, MICRO)
        stashed = jax.tree.map(
            lambda part: lax.dynamic_index_in_dim(part, source_clock, 0, keepdims=False), stash_all
        )
        upstream = jnp.where(section_index == 1, cotangent[min(moment, MICRO - 1)], back_received)
        (
            gathered,
            normed_attn,
            normed_mlp,
            queries,
            key_rows,
            val_rows,
            context,
            log_total,
            up_proj,
            activated,
        ) = stashed
        backward_inputs = lax.dynamic_slice_in_dim(gathered, own_start, local_len, 0)
        upstream_rows = lax.all_gather(upstream, "tensor", axis=0, tiled=True)
        flat_grad = upstream_rows.reshape(all_rows, model_width)
        d_context = jnp.dot(flat_grad, mat_out.T, preferred_element_type=jnp.float32).astype(
            jnp.bfloat16
        )
        d_context = d_context.reshape(length, seq_count, head_count, head_dim)
        d_active = jnp.dot(flat_grad, mat_down.T, preferred_element_type=jnp.float32)
        _, gelu_pullback = jax.vjp(partial(jax.nn.gelu, approximate=False), up_proj)
        d_up = gelu_pullback(d_active)[0].astype(jnp.bfloat16)
        grad_query, grad_key, grad_val = attend_back(
            queries, key_rows, val_rows, d_context, log_total
        )
        d_qkv = jnp.stack(
            [
                rotate_back(grad_query, cosine, sine_tab),
                rotate_back(grad_key, cosine, sine_tab),
                grad_val,
            ],
            axis=3,
        ).astype(jnp.bfloat16)
        d_qkv_flat = d_qkv.reshape(all_rows, -1)
        d_qkv_rows = d_qkv.reshape(length, seq_count, -1)
        d_up_rows = d_up.reshape(length, seq_count, -1)
        flat_attn = normed_attn.reshape(all_rows, model_width)
        flat_mlp = normed_mlp.reshape(all_rows, model_width)
        weight_terms = (
            jnp.einsum("tc,te->ce", flat_attn, d_qkv_flat, preferred_element_type=jnp.float32),
            jnp.sum(d_qkv_flat.astype(jnp.float32), axis=0).reshape(bias_qkv.shape),
            jnp.einsum(
                "tc,te->ce",
                context.reshape(all_rows, -1),
                flat_grad,
                preferred_element_type=jnp.float32,
            ),
            jnp.einsum("tc,te->ce", flat_mlp, d_up, preferred_element_type=jnp.float32),
            jnp.sum(d_up.astype(jnp.float32), axis=0).reshape(bias_up.shape),
            jnp.einsum("tc,te->ce", activated, flat_grad, preferred_element_type=jnp.float32),
        )
        attn_part = d_qkv_rows.reshape(lax.axis_size("tensor") * local_len * seq_count, -1)
        mlp_part = d_up_rows.reshape(lax.axis_size("tensor") * local_len * seq_count, -1)
        joined = jnp.concatenate(
            [
                jnp.dot(attn_part, mat_qkv.T, preferred_element_type=jnp.float32),
                jnp.dot(mlp_part, mat_up.T, preferred_element_type=jnp.float32),
            ],
            axis=-1,
        )
        d_normed = lax.psum_scatter(
            joined.reshape(lax.axis_size("tensor") * local_len, seq_count, 2 * model_width).astype(
                jnp.bfloat16
            ),
            "tensor",
            scatter_dimension=0,
            tiled=True,
        ).astype(jnp.float32)
        _, norm_pullback = jax.vjp(
            both_norms,
            backward_inputs.astype(jnp.float32),
            gain_full[0],
            bias_full[0],
            gain_full[1],
            bias_full[1],
        )
        d_local, d_gain_attn, d_shift_attn, d_gain_mlp, d_shift_mlp = norm_pullback(
            (d_normed[..., :model_width], d_normed[..., model_width:])
        )
        upstream_float = upstream.astype(jnp.float32)
        d_inputs = (upstream_float + d_local).astype(jnp.bfloat16)
        out_shift = jnp.sum(upstream_float, axis=(0, 1))
        vector_terms = (
            jnp.stack([d_gain_attn, d_gain_mlp]),
            jnp.stack([d_shift_attn, d_shift_mlp, out_shift, out_shift]),
        )
        d_inputs, weight_terms, vector_terms = (d_inputs, weight_terms, vector_terms)
        grad_list.append(d_inputs)
        if moment < MICRO:
            back_received = from_behind(d_inputs, "section", -1)
        weight_terms = tuple((jnp.where(is_valid, term, 0.0) for term in weight_terms))
        vector_terms = tuple((jnp.where(is_valid, term, 0.0) for term in vector_terms))
        if moment == 0:
            weight_sums = tuple(weight_terms)
            vector_sums = vector_terms
        else:
            weight_sums = tuple((a + b for a, b in zip(weight_sums, weight_terms)))
            vector_sums = tuple((a + b for a, b in zip(vector_sums, vector_terms)))
    sum_qkv, sum_bqkv, sum_out, sum_up, sum_bup, sum_down = weight_sums
    share_qkv, share_bqkv, share_out, share_up, share_bup, share_down = (
        lax.psum_scatter(
            sum_qkv.astype(jnp.bfloat16), "dp", scatter_dimension=0, tiled=True
        ).astype(jnp.float32),
        lax.psum_scatter(
            sum_bqkv.astype(jnp.bfloat16), "dp", scatter_dimension=1, tiled=True
        ).astype(jnp.float32),
        lax.psum_scatter(
            sum_out.astype(jnp.bfloat16), "dp", scatter_dimension=1, tiled=True
        ).astype(jnp.float32),
        lax.psum_scatter(sum_up.astype(jnp.bfloat16), "dp", scatter_dimension=0, tiled=True).astype(
            jnp.float32
        ),
        lax.psum_scatter(
            sum_bup.astype(jnp.bfloat16), "dp", scatter_dimension=1, tiled=True
        ).astype(jnp.float32),
        lax.psum_scatter(
            sum_down.astype(jnp.bfloat16), "dp", scatter_dimension=1, tiled=True
        ).astype(jnp.float32),
    )
    grad_local = lax.dynamic_slice_in_dim(jnp.stack(grad_list), 1 - section_index, MICRO, 0)
    gain_share, bias_share = (
        lax.psum_scatter(vector_sums[0], ("dp", "tensor"), scatter_dimension=1, tiled=True),
        lax.psum_scatter(vector_sums[1], ("dp", "tensor"), scatter_dimension=1, tiled=True),
    )
    return (
        acts_local[None],
        grad_local[None],
        gain_share[None],
        bias_share[None],
        share_qkv[None],
        share_bqkv[None],
        share_out[None],
        share_up[None],
        share_bup[None],
        share_down[None],
    )


FAR_ORDER = (0, 2, 3, 1)
VMEM_LIMIT = 60 * 1024 * 1024
ROW_BLOCK = 256
CHUNKS = 2
COLUMN_STEP = 512
MICROSECOND = 1_000_000_000


def ring(value, axis, by):
    length = lax.axis_size(axis)
    return lax.ppermute(value, axis, [(i, (i + by) % length) for i in range(length)])


def swap(value, axis, bit):
    length = lax.axis_size(axis)
    return lax.ppermute(value, axis, [(i, i ^ bit) for i in range(length)])


def pick(value, index, axis=0):
    return lax.dynamic_index_in_dim(value, index, axis, keepdims=False)


def place(value, block, index):
    return lax.dynamic_update_index_in_dim(value, block, index, 0)


def relative(values, own):
    size = values.shape[-1] // 4
    picked = [
        lax.dynamic_slice_in_dim(values, jnp.bitwise_xor(own, k) * size, size, values.ndim - 1)
        for k in range(4)
    ]
    return jnp.concatenate(picked, axis=-1)


class Clock:
    def __init__(self):
        self.ended = ()

    def hold(self, value):
        return lax.optimization_barrier((value, self.ended))[0]

    def tick(self, *ended):
        self.ended = tuple(jax.tree.leaves(ended))


def exchange_near(blocks, own, hold):
    half = blocks.shape[1] // 2
    far = pick(blocks, (own + 2) % 4)
    ahead = jnp.concatenate([pick(blocks, (own + 1) % 4), far[:half]], axis=0)
    behind = jnp.concatenate([pick(blocks, (own + 3) % 4), far[half:]], axis=0)
    return ring(hold(ahead), "tensor", 1), ring(hold(behind), "tensor", -1)


def exchange_far(near, hold):
    rows = near[0].shape[0] * 2 // 3
    first = ring(hold(near[0][rows:]), "tensor", 1)
    second = ring(hold(near[1][rows:]), "tensor", -1)
    return first, second


def exchanged(blocks, near, far, own):
    rows = blocks.shape[1]
    result = jnp.zeros_like(blocks)
    result = place(result, pick(blocks, own), own)
    result = place(result, near[0][:rows], (own + 3) % 4)
    result = place(result, near[1][:rows], (own + 1) % 4)
    return place(result, jnp.concatenate(far, axis=0), (own + 2) % 4)


def add_wide(left, right):
    return (left.astype(jnp.float32) + right.astype(jnp.float32)).astype(jnp.bfloat16)


def add_three(first, second, third):
    total = first.astype(jnp.float32) + second.astype(jnp.float32) + third.astype(jnp.float32)
    return total.astype(jnp.bfloat16)


def ring_first(blocks, hold):
    far = blocks[3]
    half = far.shape[0] // 2
    to_right = ring(hold(far[:half]), "tensor", 1)
    to_left = ring(hold(far[half:]), "tensor", -1)
    return to_right, to_left


def ring_second(blocks, got, hold):
    _, left, right, _ = blocks
    half = left.shape[0] // 2
    right = jnp.concatenate([add_wide(right[:half], got[0]), right[half:]], axis=0)
    left = jnp.concatenate([left[:half], add_wide(left[half:], got[1])], axis=0)
    return ring(hold(right), "tensor", 1), ring(hold(left), "tensor", -1)


def ring_total(own, got):
    total = own.astype(jnp.float32) + got[0].astype(jnp.float32) + got[1].astype(jnp.float32)
    return total.astype(jnp.bfloat16)


def normalised(x):
    average = jnp.mean(x, axis=-1, keepdims=True)
    centred = x - average
    variance = jnp.mean(centred * centred, axis=-1, keepdims=True)
    inverse = lax.rsqrt(variance + NORM_EPS)
    return centred * inverse, inverse


def nt_dot(left, right):
    return lax.dot_general(
        left, right, (((1,), (1,)), ((), ())), preferred_element_type=jnp.float32
    )


def tn_dot(left, right):
    return lax.dot_general(
        left, right, (((0,), (0,)), ((), ())), preferred_element_type=jnp.float32
    )


def nn_dot(left, right):
    return jnp.dot(left, right, preferred_element_type=jnp.float32)


def turn(values, cosine, low_sine, high_sine):
    lanes = values.shape[-1]
    return (
        values * cosine
        + pltpu.roll(values, ROT // 2, 1) * low_sine
        + pltpu.roll(values, lanes - ROT // 2, 1) * high_sine
    )


def call(body, name, flops, grid, ins, outs, scratch=(), filled=()):
    count = len(ins)

    def run(*refs):
        body(*refs[:count], *refs[count + len(filled) :])

    return pl.pallas_call(
        run,
        name=name,
        grid=grid,
        in_specs=[pl.BlockSpec(block, index) for _, block, index in ins]
        + [pl.BlockSpec(memory_space=pl.ANY)] * len(filled),
        out_specs=[pl.BlockSpec(block, index) for _, _, block, index in outs],
        out_shape=[jax.ShapeDtypeStruct(shape, kind) for shape, kind, _, _ in outs],
        scratch_shapes=list(scratch),
        input_output_aliases={count + i: i for i in range(len(filled))},
        cost_estimate=pl.CostEstimate(flops=flops, bytes_accessed=1 << 20, transcendentals=0),
        compiler_params=pltpu.CompilerParams(
            vmem_limit_bytes=VMEM_LIMIT, dimension_semantics=("arbitrary",) * len(grid)
        ),
    )(*[array for array, _, _ in ins], *filled)


def whole(array):
    return (array, array.shape, lambda *_: (0,) * array.ndim)


def matrix(pieces, size, block):
    shape = (2, pieces[0].shape[1], size)
    return [(piece, shape, lambda *_: (0, 0, block)) for piece in pieces]


def room(pieces, size):
    return pltpu.VMEM((4 * pieces[0].shape[1], 4 * size), jnp.bfloat16)


def assemble(refs, target):
    _, rows, size = refs[0].shape
    for core in range(2):
        for offset in range(4):
            for side in range(2):
                at = (2 * side + core) * rows
                target[at : at + rows, offset * size : (offset + 1) * size] = refs[
                    core * 4 + offset
                ][side]


def rows_of(array, first=0, block=ROW_BLOCK):
    base = first // block
    return (array, (block, array.shape[1]), lambda i: (i + base, 0))


def qkv_body(x, vecs, shift, cos, low, high, *rest):
    ln_a, ln_m, qkv, w = rest[8:]

    @pl.when(pl.program_id(0) == 0)
    def _():
        assemble(rest[:8], w)

    hat, _ = normalised(x[...].astype(jnp.float32))
    attn = (hat * vecs[0:1, :] + vecs[1:2, :]).astype(jnp.bfloat16)
    ln_a[...] = attn
    ln_m[...] = (hat * vecs[2:3, :] + vecs[3:4, :]).astype(jnp.bfloat16)
    out = nn_dot(attn, w[...]) + shift[...]
    for block in range(qkv.shape[1] // 384):
        for part in range(3):
            at = block * 384 + part * 128
            piece = out[:, at : at + 128]
            if part < 2:
                piece = turn(piece, cos[...], low[...], high[...])
            qkv[:, at : at + 128] = piece.astype(jnp.bfloat16)


def run_qkv(source, vecs, shift, tables, pieces, at, rows, filled):
    x, first = source
    width = x.shape[1]
    length = tables[0].shape[0]
    cols = shift.shape[1]
    bf = jnp.bfloat16
    base = at // ROW_BLOCK
    own = lambda i: (i + base, 0)
    return call(
        qkv_body,
        "norm_qkv",
        rows * 13 * MICROSECOND // 1024,
        (rows // ROW_BLOCK,),
        [rows_of(x, first), whole(vecs), whole(shift)]
        + [rows_of(t, at) for t in tables]
        + matrix(pieces, cols // 4, 0),
        [
            ((length, width), bf, (ROW_BLOCK, width), own),
            ((length, width), bf, (ROW_BLOCK, width), own),
            ((length, cols), bf, (ROW_BLOCK, cols), own),
        ],
        [room(pieces, cols // 4)],
        filled,
    )


def attend_body(q, k, v, ctx, lse):
    length = q.shape[0]
    step = ROW_BLOCK
    for head in range(2):
        lanes = slice(head * 64, head * 64 + 64)
        keys = k[:, lanes]
        vals = v[:, lanes]
        for at in range(0, length, step):
            end = at + step
            queries = q[at:end, lanes] * jnp.bfloat16(0.125)
            scores = nt_dot(queries, keys[:end])
            row = lax.broadcasted_iota(jnp.int32, (step, step), 0)
            col = lax.broadcasted_iota(jnp.int32, (step, step), 1)
            last = jnp.where(col <= row, scores[:, at:], MASK_FILL)
            scores = last if at == 0 else jnp.concatenate([scores[:, :at], last], axis=1)
            top = jnp.max(scores, axis=1, keepdims=True)
            power = jnp.exp(scores - top)
            total = jnp.sum(power, axis=1, keepdims=True)
            mixed = nn_dot(power.astype(jnp.bfloat16), vals[:end]) * (1.0 / total)
            ctx[at:end, lanes] = mixed.astype(jnp.bfloat16)
            level = jnp.broadcast_to(top + jnp.log(total), (step, 128))
            lse[0, head : head + 1, at:end] = level.T[0:1]


def run_attend(qkv):
    length, cols = qkv.shape
    groups = cols // 384
    return call(
        attend_body,
        "attend",
        length * 19 * MICROSECOND // 1024,
        (groups,),
        [
            (qkv, (length, 128), lambda i: (0, 3 * i)),
            (qkv, (length, 128), lambda i: (0, 3 * i + 1)),
            (qkv, (length, 128), lambda i: (0, 3 * i + 2)),
        ],
        [
            ((length, groups * 128), jnp.bfloat16, (length, 128), lambda i: (0, i)),
            ((groups, 8, length), jnp.float32, (1, 8, length), lambda i: (i, 0, 0)),
        ],
    )


ERF_TOP = (
    0.00022905065861350646,
    0.0034082910107109506,
    0.050955695062380861,
    0.18520832239976145,
    1.128379143519084,
)
ERF_BOTTOM = (
    -1.1791602954361697e-7,
    0.000023547966471313185,
    0.0010179625278914885,
    0.014070470171167667,
    0.11098505178285362,
    0.49746925110067538,
    1.0,
)


def erf(x):
    x = jnp.clip(x, -3.7439211627767994, 3.7439211627767994)
    square = x * x
    top = jnp.full_like(x, ERF_TOP[0])
    for term in ERF_TOP[1:]:
        top = top * square + term
    bottom = jnp.full_like(x, ERF_BOTTOM[0])
    for term in ERF_BOTTOM[1:]:
        bottom = bottom * square + term
    return x * top / bottom


def mlp_body(ctx, ln_m, shift, *rest):
    act, slope, part, w_out, w_up, w_down = rest[24:]

    @pl.when(pl.program_id(0) == 0)
    def _():
        assemble(rest[:8], w_out)
        assemble(rest[8:16], w_up)
        assemble(rest[16:24], w_down)

    total = nt_dot(ctx[...], w_out[...])
    values = ln_m[...]
    size = min(COLUMN_STEP, act.shape[1])
    for at in range(0, act.shape[1], size):
        cols = slice(at, at + size)
        up = nn_dot(values, w_up[:, cols]) + shift[:, cols]
        half_erf = 0.5 * erf(up * (2.0**-0.5)) + 0.5
        bell = jnp.exp(up * up * -0.5) * ((2.0 * math.pi) ** -0.5)
        active = (up * half_erf).astype(jnp.bfloat16)
        act[:, cols] = active
        slope[:, cols] = (half_erf + up * bell).astype(jnp.bfloat16)
        total = total + nt_dot(active, w_down[:, cols])
    part[...] = total.astype(jnp.bfloat16)


def run_mlp(ctx, ln_m, shift, narrow, broad, at, rows, filled):
    length, width = ln_m.shape
    cols, heads = shift.shape[1], ctx.shape[1]
    bf = jnp.bfloat16
    base = at // ROW_BLOCK
    own = lambda i: (i + base, 0)
    return call(
        mlp_body,
        "mlp_out",
        rows * 32 * MICROSECOND // 1024,
        (rows // ROW_BLOCK,),
        [rows_of(ctx, at), rows_of(ln_m, at), whole(shift)]
        + matrix(narrow, heads // 4, 3)
        + matrix(broad, cols // 4, 0)
        + matrix(broad, cols // 4, 1),
        [
            ((length, cols), bf, (ROW_BLOCK, cols), own),
            ((length, cols), bf, (ROW_BLOCK, cols), own),
            ((rows, width), bf, (ROW_BLOCK, width), lambda i: (i, 0)),
        ],
        [room(narrow, heads // 4), room(broad, cols // 4), room(broad, cols // 4)],
        filled,
    )


def mlp_back_body(g, slope, *rest):
    d_up, d_ctx, sum_up, sum_g, w_out, w_down = rest[16:]

    @pl.when(pl.program_id(0) == 0)
    def _():
        assemble(rest[:8], w_out)
        assemble(rest[8:16], w_down)
        sum_up[...] = jnp.zeros_like(sum_up)
        sum_g[...] = jnp.zeros_like(sum_g)

    grad = g[...]
    size = min(COLUMN_STEP, d_up.shape[1])
    for at in range(0, d_up.shape[1], size):
        cols = slice(at, at + size)
        du = nn_dot(grad, w_down[:, cols]) * slope[:, cols].astype(jnp.float32)
        du = du.astype(jnp.bfloat16)
        d_up[:, cols] = du
        sum_up[:, cols] += jnp.sum(du.astype(jnp.float32), axis=0, keepdims=True)
    d_ctx[...] = nn_dot(grad, w_out[...]).astype(jnp.bfloat16)
    sum_g[...] += jnp.sum(grad.astype(jnp.float32), axis=0, keepdims=True)


def run_mlp_back(source, slope, narrow, broad, at, rows, heads, filled):
    g, first = source
    width = g.shape[1]
    length, cols = slope.shape
    bf = jnp.bfloat16
    base = at // ROW_BLOCK
    own = lambda i: (i + base, 0)
    fixed = lambda i: (0, 0)
    return call(
        mlp_back_body,
        "mlp_back",
        rows * 15 * MICROSECOND // 1024,
        (rows // ROW_BLOCK,),
        [rows_of(g, first), rows_of(slope, at)]
        + matrix(narrow, heads // 4, 3)
        + matrix(broad, cols // 4, 1),
        [
            ((length, cols), bf, (ROW_BLOCK, cols), own),
            ((length, heads), bf, (ROW_BLOCK, heads), own),
            ((1, cols), jnp.float32, (1, cols), fixed),
            ((1, width), jnp.float32, (1, width), fixed),
        ],
        [room(narrow, heads // 4), room(broad, cols // 4)],
        filled,
    )


def attend_back_body(q, k, v, d_ctx, lse, cos, low, high, d_qkv, sums, dk_sum, dv_sum, dq_all):
    length = q.shape[0]
    step = ROW_BLOCK
    for head in range(2):
        lanes = slice(head * 64, head * 64 + 64)
        keys = k[:, lanes]
        vals = v[:, lanes]
        dk_sum[:, lanes] = jnp.zeros((length, 64), jnp.float32)
        dv_sum[:, lanes] = jnp.zeros((length, 64), jnp.float32)
        for at in range(0, length, step):
            end = at + step
            queries = q[at:end, lanes] * jnp.bfloat16(0.125)
            grads = d_ctx[at:end, lanes]
            scores = nt_dot(keys[:end], queries)
            power = jnp.exp(scores - lse[0, head : head + 1, at:end])
            key = lax.broadcasted_iota(jnp.int32, (step, step), 0)
            row = lax.broadcasted_iota(jnp.int32, (step, step), 1)
            last = jnp.where(key <= row, power[at:], 0.0)
            probs = last if at == 0 else jnp.concatenate([power[:at], last], axis=0)
            d_probs = nt_dot(vals[:end], grads)
            delta = jnp.sum(probs * d_probs, axis=0, keepdims=True)
            d_scores = (probs * (d_probs - delta)).astype(jnp.bfloat16)
            dv_sum[:end, lanes] += nn_dot(probs.astype(jnp.bfloat16), grads)
            dk_sum[:end, lanes] += nn_dot(d_scores, queries)
            dq_all[at:end, lanes] = tn_dot(d_scores, keys[:end]) * 0.125
    dq = turn(dq_all[...], cos[...], -low[...], -high[...]).astype(jnp.bfloat16)
    dk = turn(dk_sum[...], cos[...], -low[...], -high[...]).astype(jnp.bfloat16)
    dv = dv_sum[...].astype(jnp.bfloat16)
    for part, piece in enumerate((dq, dk, dv)):
        at = part * 128
        d_qkv[:, at : at + 128] = piece
        sums[:, at : at + 128] = jnp.sum(piece.astype(jnp.float32), axis=0, keepdims=True)


def run_attend_back(qkv, d_ctx, lse, tables):
    length, cols = qkv.shape
    groups = cols // 384
    wide = pltpu.VMEM((length, 128), jnp.float32)
    return call(
        attend_back_body,
        "attend_back",
        length * 26 * MICROSECOND // 1024,
        (groups,),
        [
            (qkv, (length, 128), lambda i: (0, 3 * i)),
            (qkv, (length, 128), lambda i: (0, 3 * i + 1)),
            (qkv, (length, 128), lambda i: (0, 3 * i + 2)),
            (d_ctx, (length, 128), lambda i: (0, i)),
            (lse, (1, 8, length), lambda i: (i, 0, 0)),
        ]
        + [whole(t) for t in tables],
        [
            ((length, cols), jnp.bfloat16, (length, 384), lambda i: (0, i)),
            ((1, cols), jnp.float32, (1, 384), lambda i: (0, i)),
        ],
        [wide, wide, wide],
    )


def norm_back_body(x, d_qkv, d_up, vecs, *rest):
    part, sums, w_qkv, w_up = rest[16:]

    @pl.when(pl.program_id(0) == 0)
    def _():
        assemble(rest[:8], w_qkv)
        assemble(rest[8:16], w_up)
        sums[...] = jnp.zeros_like(sums)

    hat, inverse = normalised(x[...].astype(jnp.float32))
    d_attn = nt_dot(d_qkv[...], w_qkv[...])
    d_mlp = nt_dot(d_up[...], w_up[...])
    for row, term in enumerate((d_attn * hat, d_mlp * hat, d_attn, d_mlp)):
        sums[row : row + 1, :] += jnp.sum(term, axis=0, keepdims=True)
    d_hat = d_attn * vecs[0:1, :] + d_mlp * vecs[2:3, :]
    along = jnp.mean(d_hat * hat, axis=-1, keepdims=True)
    level = jnp.mean(d_hat, axis=-1, keepdims=True)
    part[...] = (inverse * (d_hat - level - hat * along)).astype(jnp.bfloat16)


def run_norm_back(source, d_qkv, d_up, vecs, narrow, broad, at, rows):
    x, first = source
    width = x.shape[1]
    n_qkv, n_up = d_qkv.shape[1] // 4, d_up.shape[1] // 4
    return call(
        norm_back_body,
        "norm_back",
        rows * 21 * MICROSECOND // 1024,
        (rows // ROW_BLOCK,),
        [rows_of(x, first), rows_of(d_qkv, at), rows_of(d_up, at), whole(vecs)]
        + matrix(narrow, n_qkv, 0)
        + matrix(broad, n_up, 0),
        [
            ((rows, width), jnp.bfloat16, (ROW_BLOCK, width), lambda i: (i, 0)),
            ((8, width), jnp.float32, (8, width), lambda i: (0, 0)),
        ],
        [room(narrow, n_qkv), room(broad, n_up)],
    )


def weight_grad_body(cuts, *refs):
    a_refs, b_refs, rest = refs[: sum(cuts)], refs[sum(cuts) :], refs[sum(cuts) + 2 :]
    keep, send, turned_one, turned_two = rest
    groups = (a_refs[: cuts[0]], a_refs[cuts[0] :])

    @pl.when(pl.program_id(0) == 0)
    def _():
        for group, turned in zip(groups, (turned_one, turned_two)):
            at = 0
            for ref in group:
                turned[:, at : at + ref.shape[0]] = ref[...].T
                at += ref.shape[0]

    at = 0
    rows = keep.shape[2]
    for turned, right in zip((turned_one, turned_two), b_refs[:2]):
        size = right.shape[1]
        grad = nn_dot(turned[...], right[...]).astype(jnp.bfloat16)
        for side in range(2):
            first = 2 * side * rows
            keep[0, side, :, at : at + size] = grad[first : first + rows]
            send[0, side, :, at : at + size] = grad[first + rows : first + 2 * rows]
        at += size


def run_weight_grad(lefts, rights):
    length, width = rights[0].shape[0], lefts[0][0].shape[1]
    sizes = [right.shape[1] // 4 for right in rights]
    shape = (4, 2, width // 4, sum(sizes))
    out = (shape, jnp.bfloat16, (1,) + shape[1:], lambda i: (i, 0, 0, 0))
    turned = pltpu.VMEM((width, length), jnp.bfloat16)
    return call(
        partial(weight_grad_body, tuple(len(group) for group in lefts)),
        "weight_grad",
        length * 14 * MICROSECOND // 1024,
        (4,),
        [whole(left) for group in lefts for left in group]
        + [(r, (length, n), lambda i: (0, i)) for r, n in zip(rights, sizes)],
        [out, out],
        [turned, turned],
    )


def turn_tables(length):
    cosine, sine_tab = rotary_tables(length)
    zero = jnp.zeros_like(sine_tab)
    rest = jnp.zeros((length, 64 - ROT), jnp.float32)
    cos = jnp.concatenate([cosine, cosine, rest + 1.0], axis=1)
    low = jnp.concatenate([zero, sine_tab, rest], axis=1)
    high = jnp.concatenate([-sine_tab, zero, rest], axis=1)
    return tuple(jnp.concatenate([t, t], axis=1) for t in (cos, low, high))


def by_sequence(
    acts_in, cotangent, norm_gains, vec_bias, w_qkv, b_qkv, w_out, w_up, b_up, w_down
):
    section = lax.axis_index("section")
    across = lax.axis_index("dp")
    along = lax.axis_index("tensor")
    first_section = section == 0
    width = acts_in.shape[3]
    rows = w_qkv.shape[1]
    positions = acts_in.shape[1]
    length = 4 * positions
    heads = b_qkv.shape[1]
    bf = jnp.bfloat16

    qkv_halves = (
        w_qkv[0].reshape(rows, 2, 2, 3, 64).transpose(1, 0, 3, 2, 4).reshape(2, rows, -1)
    )
    out_halves = w_out[0].T.reshape(rows, 2, -1).transpose(1, 0, 2)
    up_halves = w_up[0].reshape(rows, 2, -1).transpose(1, 0, 2)
    down_halves = w_down[0].T.reshape(rows, 2, -1).transpose(1, 0, 2)
    n_qkv, n_out, n_up = qkv_halves.shape[2], out_halves.shape[2], up_halves.shape[2]

    narrow = jnp.stack([jnp.concatenate([qkv_halves[h], out_halves[h]], axis=1) for h in (0, 1)])
    broad = jnp.stack([jnp.concatenate([up_halves[h], down_halves[h]], axis=1) for h in (0, 1)])
    small = jnp.concatenate(
        [
            norm_gains[0].reshape(-1),
            vec_bias[0].reshape(-1),
            b_qkv[0].reshape(-1).astype(jnp.float32),
            b_up[0].reshape(-1).astype(jnp.float32),
        ]
    )
    clock = Clock()
    hold, tick = clock.hold, clock.tick

    def pass_half(halves):
        return swap(hold(pick(halves, 1 - section)), "section", 1)

    def by_layer(halves, got):
        keep = pick(halves, section)
        return jnp.where(first_section, keep, got), jnp.where(first_section, got, keep)

    def x_swap(value):
        return swap(hold(value), "dp", 2)

    def core_swap(value):
        return swap(hold(value), "dp", 1)

    def y_swap(value):
        return swap(hold(value), "section", 1)

    def both_ways(value):
        value = hold(value)
        return ring(value, "tensor", 1), ring(value, "tensor", -1)

    def far_halves(left, right):
        half = left.shape[0] // 2
        return ring(hold(left[:half]), "tensor", 1), ring(hold(right[half:]), "tensor", -1)

    def own_half(blocks):
        return lax.dynamic_slice_in_dim(blocks, section * (width // 2), width // 2, 2)

    def both_halves(own, got):
        own = own.reshape(length, width // 2)
        got = got.reshape(length, width // 2)
        low = jnp.where(first_section, own, got)
        high = jnp.where(first_section, got, own)
        return relative(jnp.concatenate([low, high], axis=1), across)

    def stacked(own, got):
        return jnp.stack([own, got])

    got_narrow = pass_half(narrow)
    got_small = swap(small, "section", 1)
    blocks = own_half(acts_in[:, :, 0, :])
    near = exchange_near(blocks, along, hold)
    tick(got_narrow, got_small, near)
    narrow_shards = by_layer(narrow, got_narrow)
    small = jnp.where(first_section, jnp.stack([small, got_small]), jnp.stack([got_small, small]))
    left, right = both_ways(narrow_shards[0])
    far = exchange_far(near, hold)
    got_broad = pass_half(broad)
    got_own = x_swap(narrow_shards[0])
    small = jnp.stack([small, core_swap(small)])
    small = jnp.concatenate([small, swap(small, "dp", 2)])
    tick(left, right, far, got_broad, got_own, small)
    own_acts = exchanged(blocks, near, far, along)
    got_acts = y_swap(own_acts)
    narrow_far = far_halves(left, right)
    got_left, got_right = x_swap(left), x_swap(right)
    small = jnp.stack([small, swap(hold(small), "tensor", 1)])
    tick(narrow_far, got_left, got_right, small)
    broad_shards = by_layer(broad, got_broad)
    small = jnp.concatenate([small, swap(hold(small), "tensor", 2)])
    broad_left, broad_right = both_ways(broad_shards[0])
    narrow_far = jnp.concatenate(narrow_far, axis=0)
    got_far = x_swap(narrow_far)
    pieces = [
        stacked(narrow_shards[0], got_own),
        stacked(left, got_left),
        stacked(right, got_right),
    ]
    others = [core_swap(piece) for piece in pieces]
    tick(got_far, others, got_acts, small)
    acts = both_halves(own_acts, got_acts)
    pieces.append(stacked(narrow_far, got_far))
    others.append(core_swap(pieces[3]))
    got_own = x_swap(broad_shards[0])
    narrow_zero = (*pieces, *others)
    tick(others[3])

    share = norm_gains.shape[2]
    vec_part = small[..., : 6 * share].reshape(4, 4, 2, 6, share)
    offsets = jnp.array(FAR_ORDER, jnp.int32)
    order = jnp.stack([pick(offsets, (k - along) % 4) for k in range(4)])
    slots = [jnp.bitwise_xor((along + k) % 4, along) for k in (0, 3, 1, 2)]
    vec_part = jnp.stack([pick(vec_part, jnp.bitwise_xor(along, k)) for k in range(4)])
    vecs_full = vec_part.transpose(2, 3, 1, 0, 4).reshape(2, 6, width)
    at = 6 * share
    share_q = b_qkv.shape[2]
    dp_order = [jnp.bitwise_xor(across, k) for k in range(4)]
    qkv_bias = small[..., at : at + heads * share_q].reshape(4, 4, 2, heads, share_q)
    qkv_bias = jnp.stack([pick(qkv_bias, k) for k in slots])
    qkv_bias = jnp.stack([pick(qkv_bias, i, 1) for i in dp_order], axis=1)
    qkv_bias = qkv_bias.transpose(2, 0, 3, 1, 4).reshape(2, 4, 2, heads // 2, 3, 64)
    qkv_bias = pick(qkv_bias, section, 2).transpose(0, 1, 3, 2, 4).reshape(2, 1, -1)
    at += heads * share_q
    bias_rows, share_u = b_up.shape[1], b_up.shape[2]
    up_bias = small[..., at : at + bias_rows * share_u].reshape(4, 4, 2, bias_rows, share_u)
    up_bias = jnp.stack([pick(up_bias, k) for k in slots])
    up_bias = jnp.stack([pick(up_bias, i, 1) for i in dp_order], axis=1)
    up_bias = up_bias.transpose(2, 0, 3, 1, 4).reshape(2, 4, 2, bias_rows // 2, 4 * share_u)
    up_bias = pick(up_bias, section, 2).reshape(2, 1, -1)
    zero_rows = jnp.zeros((4, width), jnp.float32)

    tables = turn_tables(length)
    chunk = length // CHUNKS
    starts = [i * chunk for i in range(CHUNKS)]

    all_vecs = [
        jnp.concatenate([v[0:1], v[2:3], v[1:2], v[3:4], zero_rows], axis=0) for v in vecs_full
    ]

    def project(layer, i, source, pieces, filled):
        return run_qkv(
            source, all_vecs[layer], qkv_bias[layer], tables, pieces, starts[i], chunk, filled
        )

    def feed(layer, i, ctx, ln_m, narrow, broad, filled):
        *filled, part = run_mlp(
            hold(ctx), ln_m, up_bias[layer], narrow, broad, starts[i], chunk, filled
        )
        return filled, part

    def join(layer, before, part, got):
        total = part.astype(jnp.float32) + got.astype(jnp.float32)
        full = vecs_full[layer]
        return (before.astype(jnp.float32) + total + (full[4] + full[5])).astype(bf)

    acts = hold(acts)
    first = project(0, 0, (acts, 0), narrow_zero, ())
    tick(first, broad_left, broad_right)
    got_left = x_swap(broad_left)
    first = project(0, 1, (acts, chunk), narrow_zero, first)
    tick(first, got_own)
    ln_a0, ln_m0, qkv0 = first
    broad_far = far_halves(broad_left, broad_right)
    got_right = x_swap(broad_right)
    ctx0, lse0 = run_attend(hold(qkv0))
    tick(ctx0, broad_far, got_left, got_right)
    broad_far = jnp.concatenate(broad_far, axis=0)
    got_far = x_swap(broad_far)
    pieces = [
        stacked(broad_shards[0], got_own),
        stacked(broad_left, got_left),
        stacked(broad_right, got_right),
    ]
    others = [core_swap(piece) for piece in pieces]
    tick(got_far, others)
    pieces.append(stacked(broad_far, got_far))
    others.append(core_swap(pieces[3]))
    broad_zero = (*pieces, *others)
    tick(others[3])
    first, part_a = feed(0, 0, ctx0, ln_m0, narrow_zero, broad_zero, ())
    left, right = both_ways(narrow_shards[1])
    got_own = x_swap(narrow_shards[1])
    broad_own = x_swap(broad_shards[1])
    tick(part_a, left, right, got_own, broad_own)
    first, part_b = feed(0, 1, ctx0, ln_m0, narrow_zero, broad_zero, first)
    act0, slope0 = first
    got_a = y_swap(part_a)
    narrow_far = far_halves(left, right)
    broad_left, broad_right = both_ways(broad_shards[1])
    tick(part_b, got_a, narrow_far, broad_left, broad_right)
    got_b = y_swap(part_b)
    got_left, got_right = x_swap(left), x_swap(right)
    x1_a = join(0, acts[:chunk], part_a, got_a)
    tick(got_left, got_right)
    narrow_far = jnp.concatenate(narrow_far, axis=0)
    got_far = x_swap(narrow_far)
    pieces = [
        stacked(narrow_shards[1], got_own),
        stacked(left, got_left),
        stacked(right, got_right),
    ]
    others = [core_swap(piece) for piece in pieces]
    tick(got_b, got_far, others)
    x1_b = join(0, acts[chunk:], part_b, got_b)
    pieces.append(stacked(narrow_far, got_far))
    others.append(core_swap(pieces[3]))
    narrow_one = (*pieces, *others)
    tick(others[3], x1_a, x1_b)

    broad_far = far_halves(broad_left, broad_right)
    got_left = x_swap(broad_left)
    first = project(1, 0, (hold(x1_a), 0), narrow_one, ())
    first = project(1, 1, (x1_b, 0), narrow_one, first)
    ln_a1, ln_m1, qkv1 = first
    tick(first, broad_far, got_left)
    broad_far = jnp.concatenate(broad_far, axis=0)
    got_right, got_far = x_swap(broad_right), x_swap(broad_far)
    pieces = [stacked(broad_shards[1], broad_own), stacked(broad_left, got_left)]
    others = [core_swap(piece) for piece in pieces]
    ctx1, lse1 = run_attend(hold(qkv1))
    tick(ctx1, got_right, got_far, others)
    pieces += [stacked(broad_right, got_right), stacked(broad_far, got_far)]
    others += [core_swap(piece) for piece in pieces[2:]]
    broad_one = (*pieces, *others)
    tick(others[2:])
    first, part_a = feed(1, 0, ctx1, ln_m1, narrow_one, broad_one, ())
    blocks = own_half(cotangent[:, :, 0, :])
    near = exchange_near(blocks, along, hold)
    tick(part_a, near)
    first, part_b = feed(1, 1, ctx1, ln_m1, narrow_one, broad_one, first)
    act1, slope1 = first
    far = exchange_far(near, hold)
    tick(far)
    own_grads = exchanged(blocks, near, far, along)
    got_grads = y_swap(own_grads)
    tick(part_b, got_grads)

    grads = hold(both_halves(own_grads, got_grads))
    n_heads = ctx0.shape[1]

    def back(i, source, slope, narrow, broad, filled):
        *filled, up_term, g_term = run_mlp_back(
            source, slope, narrow, broad, starts[i], chunk, n_heads, filled
        )
        return filled, up_term, g_term

    first, up_a, g_a = back(0, (grads, 0), slope1, narrow_one, broad_one, ())
    first, up_b, g_b = back(1, (grads, chunk), slope1, narrow_one, broad_one, first)
    d_up1, d_ctx1 = first
    sums_one = [None, g_a + g_b, None, up_a + up_b]
    got_a = y_swap(part_a)
    tick(first, got_a)
    x1 = jnp.concatenate([x1_a, x1_b], axis=0)

    def to_blocks(values):
        return relative(values, across).reshape(4, positions, width)

    d_qkv1, sums_one[2] = run_attend_back(qkv1, hold(d_ctx1), lse1, tables)
    got_b = y_swap(part_b)
    tick(d_qkv1, got_b)
    x2 = jnp.concatenate(
        [join(1, x1_a, part_a, got_a), join(1, x1_b, hold(part_b), got_b)], axis=0
    )
    out_blocks = to_blocks(jnp.where(first_section, x1, x2))
    part_a, sum_a = run_norm_back(
        (x1_a, 0), hold(d_qkv1), d_up1, all_vecs[1], narrow_one, broad_one, 0, chunk
    )
    tick(part_a, out_blocks)
    got_a = y_swap(part_a)
    part_b, sum_b = run_norm_back(
        (x1_b, 0), hold(d_qkv1), d_up1, all_vecs[1], narrow_one, broad_one, chunk, chunk
    )
    sums_one[0] = (sum_a + sum_b)[:4]
    keep_broad, send = run_weight_grad([[hold(ln_m1)], [grads]], [d_up1, act1])
    tick(part_b, keep_broad, got_a)
    got_b = y_swap(part_b)
    got_core = core_swap(send)
    out_near = exchange_near(out_blocks, along, hold)
    keep_narrow, send_narrow = run_weight_grad([[hold(ln_a1)], [grads]], [d_qkv1, ctx1])
    tick(keep_narrow, got_b, got_core)

    def lower(above, part, got):
        total = part.astype(jnp.float32) + got.astype(jnp.float32)
        return (above.astype(jnp.float32) + total).astype(bf)

    g1_a = lower(grads[:chunk], hold(part_a), got_a)
    g1_b = lower(grads[chunk:], hold(part_b), got_b)
    keep_one, core_one = hold(keep_broad), got_core
    got_core = core_swap(send_narrow)
    got_x = [x_swap(add_wide(keep_one[2:, 1], core_one[2:, 1]))]
    first, up_a, g_a = back(0, (hold(g1_a), 0), slope0, narrow_zero, broad_zero, ())
    first, up_b, g_b = back(1, (g1_b, 0), slope0, narrow_zero, broad_zero, first)
    d_up0, d_ctx0 = first
    sums_zero = [None, g_a + g_b, None, up_a + up_b]
    tick(first, got_core, got_x, out_near)
    core_narrow = got_core
    out_far = exchange_far(out_near, hold)
    got_x.append(x_swap(add_wide(hold(keep_one[:2, 1]), core_one[:2, 1])))
    keep_broad, send = run_weight_grad([[hold(ln_m0)], [g1_a, g1_b]], [d_up0, act0])
    tick(keep_broad, out_far, got_x)

    def late_blocks(keep, core, got):
        late = add_three(hold(keep[2:, 0]), core[2:, 0], got)
        return [late[0], late[1]]

    def early_blocks(keep, core, got):
        early = add_three(hold(keep[:2, 0]), core[:2, 0], got)
        return [early[0], early[1]]

    got_core = core_swap(send)
    late = late_blocks(keep_one, core_one, got_x[0])
    broad_got = ring_first([None, None, *late], hold)
    got_narrow = x_swap(add_wide(hold(keep_narrow[:, 1]), core_narrow[:, 1]))
    d_qkv0, sums_zero[2] = run_attend_back(qkv0, hold(d_ctx0), lse0, tables)
    tick(d_qkv0, broad_got, got_core, got_narrow)
    broad_one_sum = early_blocks(keep_one, core_one, got_x[1]) + late
    narrow_sum = add_three(hold(keep_narrow[:, 0]), core_narrow[:, 0], got_narrow)
    narrow_sum = [narrow_sum[k] for k in range(4)]
    keep_zero, core_zero = hold(keep_broad), got_core
    got_x = [x_swap(add_wide(keep_zero[2:, 1], core_zero[2:, 1]))]
    broad_got = ring_second(broad_one_sum, broad_got, hold)
    part_a, sum_a = run_norm_back(
        (acts, 0), hold(d_qkv0), d_up0, all_vecs[0], narrow_zero, broad_zero, 0, chunk
    )
    tick(part_a)
    got_a = y_swap(part_a)
    part_b, sum_b = run_norm_back(
        (acts, chunk), hold(d_qkv0), d_up0, all_vecs[0], narrow_zero, broad_zero, chunk, chunk
    )
    sums_zero[0] = (sum_a + sum_b)[:4]
    tick(part_b, got_x, broad_got)
    got_b = y_swap(part_b)
    got_x.append(x_swap(add_wide(hold(keep_zero[:2, 1]), core_zero[:2, 1])))
    narrow_got = ring_first(narrow_sum, hold)
    keep_narrow, send_narrow = run_weight_grad([[hold(ln_a0)], [g1_a, g1_b]], [d_qkv0, ctx0])
    tick(keep_narrow, got_a, got_b, got_x, narrow_got)

    flat = []
    for norm_sums, sum_g, sum_qkv, sum_up in hold((sums_zero, sums_one)):
        feature = relative(jnp.concatenate([norm_sums, sum_g], axis=0), across)
        q_sum = sum_qkv.reshape(4, 3, 2, 64).transpose(0, 2, 1, 3).reshape(4, -1)
        both = jnp.concatenate([q_sum, sum_up.reshape(4, -1)], axis=1)
        both = jnp.stack([pick(both, order[k]) for k in range(4)])
        flat.append(jnp.concatenate([feature.reshape(-1), both.reshape(-1)]))
    flat = jnp.stack(flat)
    got_core = core_swap(send_narrow)
    late = late_blocks(keep_zero, core_zero, got_x[0])
    broad_next = ring_first([None, None, *late], hold)
    grads_low = jnp.concatenate(
        [lower(g1_a, hold(part_a), got_a), lower(g1_b, hold(part_b), got_b)], axis=0
    )
    g1 = jnp.concatenate([g1_a, g1_b], axis=0)
    grad_blocks = to_blocks(jnp.where(first_section, grads_low, g1))
    tick(broad_next, got_core, grad_blocks)
    broad_zero_sum = early_blocks(keep_zero, core_zero, got_x[1]) + late
    broad_next = ring_second(broad_zero_sum, broad_next, hold)
    narrow_got = ring_second(narrow_sum, narrow_got, hold)
    got_narrow = x_swap(add_wide(hold(keep_narrow[:, 1]), got_core[:, 1]))
    flat = flat + core_swap(flat)
    acts_local = exchanged(hold(out_blocks), out_near, out_far, along)
    tick(broad_next, got_narrow, flat, narrow_got, acts_local)
    zero_sum = add_three(hold(keep_narrow[:, 0]), got_core[:, 0], got_narrow)
    zero_sum = [zero_sum[k] for k in range(4)]
    narrow_next = ring_first(zero_sum, hold)
    flat = flat + x_swap(flat)
    tick(narrow_next, flat)
    grad_near = exchange_near(grad_blocks, along, hold)
    narrow_next = ring_second(zero_sum, narrow_next, hold)
    one_broad = ring_total(hold(broad_one_sum[0]), broad_got)
    one_narrow = ring_total(hold(narrow_sum[0]), narrow_got)
    zero_broad = ring_total(hold(broad_zero_sum[0]), broad_next)
    broad_send = y_swap(jnp.where(first_section, one_broad, zero_broad))
    flat = flat + swap(hold(flat), "tensor", 1)
    tick(narrow_next, grad_near, broad_send, flat)
    grad_far = exchange_far(grad_near, hold)
    zero_narrow = ring_total(zero_sum[0], narrow_next)
    narrow_send = y_swap(jnp.where(first_section, one_narrow, zero_narrow))
    flat = flat + swap(hold(flat), "tensor", 2)
    grad_local = exchanged(grad_blocks, grad_near, grad_far, along)

    def whole_layer(keep_pair, got):
        keep = jnp.where(first_section, *keep_pair).astype(jnp.float32)
        got = got.astype(jnp.float32)
        return jnp.where(first_section, jnp.stack([keep, got], 1), jnp.stack([got, keep], 1))

    narrow_out = whole_layer((zero_narrow, one_narrow), narrow_send)
    broad_out = whole_layer((zero_broad, one_broad), broad_send)
    grad_qkv = narrow_out[..., :n_qkv].reshape(rows, 2, 3, 2, 64)
    grad_qkv = grad_qkv.transpose(0, 1, 3, 2, 4).reshape(rows, -1)
    grad_out = narrow_out[..., n_qkv:].reshape(rows, -1).T
    grad_up = broad_out[..., :n_up].reshape(rows, -1)
    grad_down = broad_out[..., n_up:].reshape(rows, -1).T

    keep = pick(flat, section)
    mine = pick(flat, 1 - section)
    got = swap(mine, "section", 1)
    n_feature = 5 * width
    feature_own = keep[:n_feature].reshape(5, width)
    feature = feature_own[:4] + got[: 4 * width].reshape(4, width)
    place_at = (across * 4 + along) * share
    gain_share = lax.dynamic_slice_in_dim(feature[:2], place_at, share, 1)
    shifts = jnp.concatenate([feature[2:4], feature_own[4:5], feature_own[4:5]], axis=0)
    bias_share = lax.dynamic_slice_in_dim(shifts, place_at, share, 1)
    low_half = jnp.where(first_section, keep, got)[n_feature:].reshape(4, -1)
    high_half = jnp.where(first_section, got, keep)[n_feature:].reshape(4, -1)
    halves = jnp.stack([pick(low_half, along), pick(high_half, along)])
    n_head = (heads // 2) * 192
    head_sums = halves[:, :n_head].reshape(heads, 192)
    head_share = lax.dynamic_slice_in_dim(head_sums, across * share_q, share_q, 1)
    unit_sums = halves[:, n_head:].reshape(bias_rows, 4 * share_u)
    unit_share = lax.dynamic_slice_in_dim(unit_sums, across * share_u, share_u, 1)
    return (
        acts_local[None, :, :, None],
        grad_local[None, :, :, None],
        gain_share[None],
        bias_share[None],
        grad_qkv[None],
        head_share[None],
        grad_out[None],
        grad_up[None],
        unit_share[None],
        grad_down[None],
    )


def fits(mesh, args):
    acts_in, b_qkv = args[0], args[5]
    sizes = dict(mesh.shape)
    return (
        sizes["section"] == 2
        and sizes["dp"] == 4
        and sizes["tensor"] == MICRO
        and MICRO == 4
        and acts_in.shape[2] == sizes["dp"]
        and b_qkv.shape[1] == 16
        and b_qkv.shape[2] == 192
        and acts_in.shape[1] % (CHUNKS * ROW_BLOCK) == 0
    )


def solution(mesh):
    placed = (
        P(None, "tensor", "dp", None),
        P(None, "tensor", "dp", None),
        P("section", None, ("dp", "tensor")),
        P("section", None, ("dp", "tensor")),
        P("section", "dp", "tensor"),
        P("section", "tensor", "dp"),
        P("section", "tensor", "dp"),
        P("section", "dp", "tensor"),
        P("section", "tensor", "dp"),
        P("section", "tensor", "dp"),
    )
    def wrap(body):
        return jax.shard_map(
            body,
            mesh=mesh,
            in_specs=placed,
            out_specs=(
                P("section", None, "tensor", "dp", None),
                P("section", None, "tensor", "dp", None),
                P("section", None, ("dp", "tensor")),
                P("section", None, ("dp", "tensor")),
                P("section", "dp", "tensor"),
                P("section", "tensor", "dp"),
                P("section", "tensor", "dp"),
                P("section", "dp", "tensor"),
                P("section", "tensor", "dp"),
                P("section", "tensor", "dp"),
            ),
            check_vma=False,
        )

    return lambda *args: wrap(by_sequence if fits(mesh, args) else local)(*args)
```

```python
from functools import partial
import math

import jax
import jax.numpy as jnp
from jax import lax
from jax.experimental import pallas as pl
from jax.experimental.pallas import tpu as pltpu
from jax.sharding import PartitionSpec as P

ROT = 16
QBLOCK = 512
MICRO = 4


NORM_EPS = 1e-05
ROPE_BASE = 10000.0
MASK_FILL = -1e30


def from_behind(value, axis, by):
    length = lax.axis_size(axis)
    pairs = [(i, i + by) for i in range(length) if 0 <= i + by < length]
    return lax.ppermute(value, axis, pairs)


def layer_norm(values, norm_gain, norm_shift):
    average = jnp.mean(values, axis=-1, keepdims=True)
    centred = values - average
    variance = jnp.mean(centred * centred, axis=-1, keepdims=True)
    return centred * lax.rsqrt(variance + NORM_EPS) * norm_gain + norm_shift


def both_norms(values, gain_attn, shift_attn, gain_mlp, shift_mlp):
    return (layer_norm(values, gain_attn, shift_attn), layer_norm(values, gain_mlp, shift_mlp))


def rotary_tables(length):
    half_rot = ROT // 2
    frequency = jnp.exp(
        jnp.arange(half_rot, dtype=jnp.float32) * (-2.0 * math.log(ROPE_BASE) / ROT)
    )
    angles = jnp.arange(length, dtype=jnp.float32)[:, None] * frequency[None, :]
    return (jnp.cos(angles), jnp.sin(angles))


def rotate(values, cosine, sine_tab):
    half_rot = ROT // 2
    low_half = values[..., :half_rot]
    high_half = values[..., half_rot:ROT]
    return jnp.concatenate(
        [
            low_half * cosine - high_half * sine_tab,
            high_half * cosine + low_half * sine_tab,
            values[..., ROT:],
        ],
        axis=-1,
    )


def rotate_back(grads_rot, cosine, sine_tab):
    half_rot = ROT // 2
    low_half = grads_rot[..., :half_rot]
    high_half = grads_rot[..., half_rot:ROT]
    return jnp.concatenate(
        [
            low_half * cosine + high_half * sine_tab,
            high_half * cosine - low_half * sine_tab,
            grads_rot[..., ROT:],
        ],
        axis=-1,
    )


def causal_scores(queries, key_rows, first_row, score_scale):
    block_rows = queries.shape[0]
    last_row = key_rows.shape[0]
    scores = (
        jnp.einsum("qshd,kshd->shqk", queries, key_rows, preferred_element_type=jnp.float32)
        * score_scale
    )
    row_pos = first_row + jnp.arange(block_rows, dtype=jnp.int32)
    col_pos = jnp.arange(last_row, dtype=jnp.int32)
    allowed = col_pos[None, :] <= row_pos[:, None]
    return (scores, allowed)


def attend(queries, key_rows, val_rows):
    length = queries.shape[0]
    block_rows = min(QBLOCK, length)
    score_scale = queries.shape[-1] ** (-0.5)
    outputs = []
    totals = []
    for block_index in range(length // block_rows):
        first_row = block_index * block_rows
        last_row = first_row + block_rows
        scores, allowed = causal_scores(
            queries[first_row:last_row], key_rows[:last_row], first_row, score_scale
        )
        scores = jnp.where(allowed, scores, MASK_FILL)
        highest = jnp.max(scores, axis=-1, keepdims=True)
        exponent = jnp.exp(scores - highest)
        denominator = jnp.sum(exponent, axis=-1, keepdims=True)
        probability = (exponent / denominator).astype(jnp.bfloat16)
        block_out = jnp.einsum(
            "shqk,kshd->qshd", probability, val_rows[:last_row], preferred_element_type=jnp.float32
        )
        outputs.append(block_out.astype(jnp.bfloat16))
        totals.append((highest + jnp.log(denominator))[..., 0])
    context = jnp.concatenate(outputs, axis=0)
    return (context.reshape(length, context.shape[1], -1), jnp.concatenate(totals, axis=-1))


def attend_back(queries, key_rows, val_rows, d_context, log_total):
    length = queries.shape[0]
    block_rows = min(QBLOCK, length)
    score_scale = queries.shape[-1] ** (-0.5)
    grad_query_list = []
    grad_keys = jnp.zeros(queries.shape, jnp.float32)
    grad_vals = jnp.zeros(queries.shape, jnp.float32)
    for block_index in range(length // block_rows):
        first_row = block_index * block_rows
        last_row = first_row + block_rows
        query_block = queries[first_row:last_row]
        scores, allowed = causal_scores(query_block, key_rows[:last_row], first_row, score_scale)
        probability = jnp.where(
            allowed, jnp.exp(scores - log_total[:, :, first_row:last_row, None]), 0.0
        )
        d_block = d_context[first_row:last_row]
        d_prob = jnp.einsum(
            "qshd,kshd->shqk", d_block, val_rows[:last_row], preferred_element_type=jnp.float32
        )
        delta = jnp.sum(probability * d_prob, axis=-1, keepdims=True)
        d_scores = (probability * (d_prob - delta)).astype(jnp.bfloat16)
        grad_query_list.append(
            jnp.einsum(
                "shqk,kshd->qshd", d_scores, key_rows[:last_row], preferred_element_type=jnp.float32
            )
            * score_scale
        )
        grad_keys = grad_keys.at[:last_row].add(
            jnp.einsum("shqk,qshd->kshd", d_scores, query_block, preferred_element_type=jnp.float32)
            * score_scale
        )
        grad_vals = grad_vals.at[:last_row].add(
            jnp.einsum(
                "shqk,qshd->kshd",
                probability.astype(jnp.bfloat16),
                d_block,
                preferred_element_type=jnp.float32,
            )
        )
    return (jnp.concatenate(grad_query_list, axis=0), grad_keys, grad_vals)


def local(acts_in, cotangent, norm_gains, vec_bias, w_qkv, b_qkv, w_out, w_up, b_up, w_down):
    section_index = lax.axis_index("section")
    own_start = lax.axis_index("tensor") * acts_in.shape[1]
    local_len = acts_in.shape[1]
    seq_count = acts_in.shape[2]
    model_width = acts_in.shape[3]
    length = local_len * lax.axis_size("tensor")
    all_rows = length * seq_count
    gain_full, bias_full = (
        lax.all_gather(norm_gains[0], ("dp", "tensor"), axis=1, tiled=True),
        lax.all_gather(vec_bias[0], ("dp", "tensor"), axis=1, tiled=True),
    )
    mat_qkv, bias_qkv, mat_out, mat_up, bias_up, mat_down = (
        lax.all_gather(w_qkv[0], "dp", axis=0, tiled=True),
        lax.all_gather(b_qkv[0], "dp", axis=1, tiled=True),
        lax.all_gather(w_out[0], "dp", axis=1, tiled=True),
        lax.all_gather(w_up[0], "dp", axis=0, tiled=True),
        lax.all_gather(b_up[0], "dp", axis=1, tiled=True),
        lax.all_gather(w_down[0], "dp", axis=1, tiled=True),
    )
    head_count = bias_qkv.shape[0]
    head_dim = bias_qkv.shape[1] // 3
    qkv_shift = bias_qkv.reshape(-1).astype(jnp.float32)
    up_shift = bias_up.reshape(-1).astype(jnp.float32)
    cosine, sine_tab = rotary_tables(length)
    cosine = cosine[:, None, None, :]
    sine_tab = sine_tab[:, None, None, :]
    received = jnp.zeros_like(acts_in[0])
    stash_list = []
    out_list = []
    for moment in range(MICRO + 1):
        own_rows = acts_in[min(moment, MICRO - 1)]
        inputs = jnp.where(section_index == 0, own_rows, received)
        forward_gathered = lax.all_gather(inputs, "tensor", axis=0, tiled=True)
        full_attn, full_mlp = both_norms(
            forward_gathered.astype(jnp.float32),
            gain_full[0],
            bias_full[0],
            gain_full[1],
            bias_full[1],
        )
        forward_normed_attn = full_attn.astype(jnp.bfloat16)
        forward_normed_mlp = full_mlp.astype(jnp.bfloat16)
        forward_flat_attn = forward_normed_attn.reshape(all_rows, model_width)
        forward_flat_mlp = forward_normed_mlp.reshape(all_rows, model_width)
        projected = (
            jnp.dot(forward_flat_attn, mat_qkv, preferred_element_type=jnp.float32) + qkv_shift
        )
        projected = projected.reshape(length, seq_count, head_count, 3, head_dim)
        forward_queries = rotate(projected[:, :, :, 0], cosine, sine_tab).astype(jnp.bfloat16)
        forward_key_rows = rotate(projected[:, :, :, 1], cosine, sine_tab).astype(jnp.bfloat16)
        forward_val_rows = projected[:, :, :, 2].astype(jnp.bfloat16)
        forward_context, forward_log_total = attend(
            forward_queries, forward_key_rows, forward_val_rows
        )
        forward_up_proj = (
            jnp.dot(forward_flat_mlp, mat_up, preferred_element_type=jnp.float32) + up_shift
        )
        forward_activated = jax.nn.gelu(forward_up_proj, approximate=False).astype(jnp.bfloat16)
        active_rows = forward_activated.reshape(length, seq_count, -1)
        context_part = forward_context.reshape(lax.axis_size("tensor") * local_len * seq_count, -1)
        active_part = active_rows.reshape(lax.axis_size("tensor") * local_len * seq_count, -1)
        summed = jnp.dot(context_part, mat_out, preferred_element_type=jnp.float32) + jnp.dot(
            active_part, mat_down, preferred_element_type=jnp.float32
        )
        mixed_sum = lax.psum_scatter(
            summed.reshape(lax.axis_size("tensor") * local_len, seq_count, model_width),
            "tensor",
            scatter_dimension=0,
            tiled=True,
        )
        result = inputs.astype(jnp.float32) + mixed_sum + bias_full[2] + bias_full[3]
        forward_stashed = (
            forward_gathered,
            forward_normed_attn,
            forward_normed_mlp,
            forward_queries,
            forward_key_rows,
            forward_val_rows,
            forward_context,
            forward_log_total,
            forward_up_proj,
            forward_activated,
        )
        result, stashed = (result.astype(jnp.bfloat16), forward_stashed)
        stash_list.append(stashed)
        out_list.append(result)
        if moment < MICRO:
            received = from_behind(result, "section", 1)
    stash_all = jax.tree.map(lambda *parts: jnp.stack(parts), *stash_list)
    acts_local = lax.dynamic_slice_in_dim(jnp.stack(out_list), section_index, MICRO, 0)
    back_received = jnp.zeros_like(cotangent[0])
    grad_list = []
    weight_sums = None
    vector_sums = None
    for moment in range(MICRO + 1):
        micro_index = moment - 1 + section_index
        is_valid = (micro_index >= 0) & (micro_index < MICRO)
        source_clock = jnp.clip(micro_index + section_index, 0, MICRO)
        stashed = jax.tree.map(
            lambda part: lax.dynamic_index_in_dim(part, source_clock, 0, keepdims=False), stash_all
        )
        upstream = jnp.where(section_index == 1, cotangent[min(moment, MICRO - 1)], back_received)
        (
            gathered,
            normed_attn,
            normed_mlp,
            queries,
            key_rows,
            val_rows,
            context,
            log_total,
            up_proj,
            activated,
        ) = stashed
        backward_inputs = lax.dynamic_slice_in_dim(gathered, own_start, local_len, 0)
        upstream_rows = lax.all_gather(upstream, "tensor", axis=0, tiled=True)
        flat_grad = upstream_rows.reshape(all_rows, model_width)
        d_context = jnp.dot(flat_grad, mat_out.T, preferred_element_type=jnp.float32).astype(
            jnp.bfloat16
        )
        d_context = d_context.reshape(length, seq_count, head_count, head_dim)
        d_active = jnp.dot(flat_grad, mat_down.T, preferred_element_type=jnp.float32)
        _, gelu_pullback = jax.vjp(partial(jax.nn.gelu, approximate=False), up_proj)
        d_up = gelu_pullback(d_active)[0].astype(jnp.bfloat16)
        grad_query, grad_key, grad_val = attend_back(
            queries, key_rows, val_rows, d_context, log_total
        )
        d_qkv = jnp.stack(
            [
                rotate_back(grad_query, cosine, sine_tab),
                rotate_back(grad_key, cosine, sine_tab),
                grad_val,
            ],
            axis=3,
        ).astype(jnp.bfloat16)
        d_qkv_flat = d_qkv.reshape(all_rows, -1)
        d_qkv_rows = d_qkv.reshape(length, seq_count, -1)
        d_up_rows = d_up.reshape(length, seq_count, -1)
        flat_attn = normed_attn.reshape(all_rows, model_width)
        flat_mlp = normed_mlp.reshape(all_rows, model_width)
        weight_terms = (
            jnp.einsum("tc,te->ce", flat_attn, d_qkv_flat, preferred_element_type=jnp.float32),
            jnp.sum(d_qkv_flat.astype(jnp.float32), axis=0).reshape(bias_qkv.shape),
            jnp.einsum(
                "tc,te->ce",
                context.reshape(all_rows, -1),
                flat_grad,
                preferred_element_type=jnp.float32,
            ),
            jnp.einsum("tc,te->ce", flat_mlp, d_up, preferred_element_type=jnp.float32),
            jnp.sum(d_up.astype(jnp.float32), axis=0).reshape(bias_up.shape),
            jnp.einsum("tc,te->ce", activated, flat_grad, preferred_element_type=jnp.float32),
        )
        attn_part = d_qkv_rows.reshape(lax.axis_size("tensor") * local_len * seq_count, -1)
        mlp_part = d_up_rows.reshape(lax.axis_size("tensor") * local_len * seq_count, -1)
        joined = jnp.concatenate(
            [
                jnp.dot(attn_part, mat_qkv.T, preferred_element_type=jnp.float32),
                jnp.dot(mlp_part, mat_up.T, preferred_element_type=jnp.float32),
            ],
            axis=-1,
        )
        d_normed = lax.psum_scatter(
            joined.reshape(lax.axis_size("tensor") * local_len, seq_count, 2 * model_width).astype(
                jnp.bfloat16
            ),
            "tensor",
            scatter_dimension=0,
            tiled=True,
        ).astype(jnp.float32)
        _, norm_pullback = jax.vjp(
            both_norms,
            backward_inputs.astype(jnp.float32),
            gain_full[0],
            bias_full[0],
            gain_full[1],
            bias_full[1],
        )
        d_local, d_gain_attn, d_shift_attn, d_gain_mlp, d_shift_mlp = norm_pullback(
            (d_normed[..., :model_width], d_normed[..., model_width:])
        )
        upstream_float = upstream.astype(jnp.float32)
        d_inputs = (upstream_float + d_local).astype(jnp.bfloat16)
        out_shift = jnp.sum(upstream_float, axis=(0, 1))
        vector_terms = (
            jnp.stack([d_gain_attn, d_gain_mlp]),
            jnp.stack([d_shift_attn, d_shift_mlp, out_shift, out_shift]),
        )
        d_inputs, weight_terms, vector_terms = (d_inputs, weight_terms, vector_terms)
        grad_list.append(d_inputs)
        if moment < MICRO:
            back_received = from_behind(d_inputs, "section", -1)
        weight_terms = tuple((jnp.where(is_valid, term, 0.0) for term in weight_terms))
        vector_terms = tuple((jnp.where(is_valid, term, 0.0) for term in vector_terms))
        if moment == 0:
            weight_sums = tuple(weight_terms)
            vector_sums = vector_terms
        else:
            weight_sums = tuple((a + b for a, b in zip(weight_sums, weight_terms)))
            vector_sums = tuple((a + b for a, b in zip(vector_sums, vector_terms)))
    sum_qkv, sum_bqkv, sum_out, sum_up, sum_bup, sum_down = weight_sums
    share_qkv, share_bqkv, share_out, share_up, share_bup, share_down = (
        lax.psum_scatter(
            sum_qkv.astype(jnp.bfloat16), "dp", scatter_dimension=0, tiled=True
        ).astype(jnp.float32),
        lax.psum_scatter(
            sum_bqkv.astype(jnp.bfloat16), "dp", scatter_dimension=1, tiled=True
        ).astype(jnp.float32),
        lax.psum_scatter(
            sum_out.astype(jnp.bfloat16), "dp", scatter_dimension=1, tiled=True
        ).astype(jnp.float32),
        lax.psum_scatter(sum_up.astype(jnp.bfloat16), "dp", scatter_dimension=0, tiled=True).astype(
            jnp.float32
        ),
        lax.psum_scatter(
            sum_bup.astype(jnp.bfloat16), "dp", scatter_dimension=1, tiled=True
        ).astype(jnp.float32),
        lax.psum_scatter(
            sum_down.astype(jnp.bfloat16), "dp", scatter_dimension=1, tiled=True
        ).astype(jnp.float32),
    )
    grad_local = lax.dynamic_slice_in_dim(jnp.stack(grad_list), 1 - section_index, MICRO, 0)
    gain_share, bias_share = (
        lax.psum_scatter(vector_sums[0], ("dp", "tensor"), scatter_dimension=1, tiled=True),
        lax.psum_scatter(vector_sums[1], ("dp", "tensor"), scatter_dimension=1, tiled=True),
    )
    return (
        acts_local[None],
        grad_local[None],
        gain_share[None],
        bias_share[None],
        share_qkv[None],
        share_bqkv[None],
        share_out[None],
        share_up[None],
        share_bup[None],
        share_down[None],
    )


FAR_ORDER = (0, 2, 3, 1)
VMEM_LIMIT = 60 * 1024 * 1024
ROW_BLOCK = 256
CHUNKS = 2
COLUMN_STEP = 512
MICROSECOND = 1_000_000_000


def ring(value, axis, by):
    length = lax.axis_size(axis)
    return lax.ppermute(value, axis, [(i, (i + by) % length) for i in range(length)])


def swap(value, axis, bit):
    length = lax.axis_size(axis)
    return lax.ppermute(value, axis, [(i, i ^ bit) for i in range(length)])


def pick(value, index, axis=0):
    return lax.dynamic_index_in_dim(value, index, axis, keepdims=False)


def place(value, block, index):
    return lax.dynamic_update_index_in_dim(value, block, index, 0)


def relative(values, own):
    size = values.shape[-1] // 4
    picked = [
        lax.dynamic_slice_in_dim(values, jnp.bitwise_xor(own, k) * size, size, values.ndim - 1)
        for k in range(4)
    ]
    return jnp.concatenate(picked, axis=-1)


class Clock:
    def __init__(self):
        self.ended = ()

    def hold(self, value):
        return lax.optimization_barrier((value, self.ended))[0]

    def tick(self, *ended):
        self.ended = tuple(jax.tree.leaves(ended))


def exchange_near(blocks, own, hold):
    half = blocks.shape[1] // 2
    far = pick(blocks, (own + 2) & 3)
    ahead = jnp.concatenate([pick(blocks, (own + 1) & 3), far[:half]], axis=0)
    behind = jnp.concatenate([pick(blocks, (own + 3) & 3), far[half:]], axis=0)
    return ring(hold(ahead), "tensor", 1), ring(hold(behind), "tensor", -1)


def exchange_far(near, hold):
    rows = near[0].shape[0] * 2 // 3
    first = ring(hold(near[0][rows:]), "tensor", 1)
    second = ring(hold(near[1][rows:]), "tensor", -1)
    return first, second


def exchanged(blocks, near, far, own):
    rows = blocks.shape[1]
    result = jnp.zeros_like(blocks)
    result = place(result, pick(blocks, own), own)
    result = place(result, near[0][:rows], (own + 3) & 3)
    result = place(result, near[1][:rows], (own + 1) & 3)
    return place(result, jnp.concatenate(far, axis=0), (own + 2) & 3)


def add_wide(left, right):
    return (left.astype(jnp.float32) + right.astype(jnp.float32)).astype(jnp.bfloat16)


def add_three(first, second, third):
    total = first.astype(jnp.float32) + second.astype(jnp.float32) + third.astype(jnp.float32)
    return total.astype(jnp.bfloat16)


def ring_first(blocks, hold):
    far = blocks[3]
    half = far.shape[0] // 2
    to_right = ring(hold(far[:half]), "tensor", 1)
    to_left = ring(hold(far[half:]), "tensor", -1)
    return to_right, to_left


def ring_second(blocks, got, hold):
    _, left, right, _ = blocks
    half = left.shape[0] // 2
    right = jnp.concatenate([add_wide(right[:half], got[0]), right[half:]], axis=0)
    left = jnp.concatenate([left[:half], add_wide(left[half:], got[1])], axis=0)
    return ring(hold(right), "tensor", 1), ring(hold(left), "tensor", -1)


def ring_total(own, got):
    total = own.astype(jnp.float32) + got[0].astype(jnp.float32) + got[1].astype(jnp.float32)
    return total.astype(jnp.bfloat16)


def normalised(x):
    average = jnp.mean(x, axis=-1, keepdims=True)
    centred = x - average
    variance = jnp.mean(centred * centred, axis=-1, keepdims=True)
    inverse = lax.rsqrt(variance + NORM_EPS)
    return centred * inverse, inverse


def nt_dot(left, right):
    return lax.dot_general(
        left, right, (((1,), (1,)), ((), ())), preferred_element_type=jnp.float32
    )


def tn_dot(left, right):
    return lax.dot_general(
        left, right, (((0,), (0,)), ((), ())), preferred_element_type=jnp.float32
    )


def nn_dot(left, right):
    return jnp.dot(left, right, preferred_element_type=jnp.float32)


def turn(values, cosine, low_sine, high_sine):
    lanes = values.shape[-1]
    return (
        values * cosine
        + pltpu.roll(values, ROT // 2, 1) * low_sine
        + pltpu.roll(values, lanes - ROT // 2, 1) * high_sine
    )


def call(body, name, flops, grid, ins, outs, scratch=(), filled=()):
    count = len(ins)

    def run(*refs):
        body(*refs[:count], *refs[count + len(filled) :])

    return pl.pallas_call(
        run,
        name=name,
        grid=grid,
        in_specs=[pl.BlockSpec(block, index) for _, block, index in ins]
        + [pl.BlockSpec(memory_space=pl.ANY)] * len(filled),
        out_specs=[pl.BlockSpec(block, index) for _, _, block, index in outs],
        out_shape=[jax.ShapeDtypeStruct(shape, kind) for shape, kind, _, _ in outs],
        scratch_shapes=list(scratch),
        input_output_aliases={count + i: i for i in range(len(filled))},
        cost_estimate=pl.CostEstimate(flops=flops, bytes_accessed=1 << 20, transcendentals=0),
        compiler_params=pltpu.CompilerParams(
            vmem_limit_bytes=VMEM_LIMIT, dimension_semantics=("arbitrary",) * len(grid)
        ),
    )(*[array for array, _, _ in ins], *filled)


def whole(array):
    return (array, array.shape, lambda *_: (0,) * array.ndim)


def matrix(pieces, size, block):
    shape = (2, pieces[0].shape[1], size)
    return [(piece, shape, lambda *_: (0, 0, block)) for piece in pieces]


def room(pieces, size):
    return pltpu.VMEM((4 * pieces[0].shape[1], 4 * size), jnp.bfloat16)


def assemble(refs, target):
    _, rows, size = refs[0].shape
    for core in range(2):
        for offset in range(4):
            for side in range(2):
                at = (2 * side + core) * rows
                target[at : at + rows, offset * size : (offset + 1) * size] = refs[
                    core * 4 + offset
                ][side]


def rows_of(array, first=0, block=ROW_BLOCK):
    base = first // block
    return (array, (block, array.shape[1]), lambda i: (i + base, 0))


def qkv_body(x, vecs, shift, cos, low, high, *rest):
    ln_a, ln_m, qkv, w = rest[8:]

    @pl.when(pl.program_id(0) == 0)
    def _():
        assemble(rest[:8], w)

    hat, _ = normalised(x[...].astype(jnp.float32))
    attn = (hat * vecs[0:1, :] + vecs[1:2, :]).astype(jnp.bfloat16)
    ln_a[...] = attn
    ln_m[...] = (hat * vecs[2:3, :] + vecs[3:4, :]).astype(jnp.bfloat16)
    out = nn_dot(attn, w[...]) + shift[...]
    for block in range(qkv.shape[1] // 384):
        for part in range(3):
            at = block * 384 + part * 128
            piece = out[:, at : at + 128]
            if part < 2:
                piece = turn(piece, cos[...], low[...], high[...])
            qkv[:, at : at + 128] = piece.astype(jnp.bfloat16)


def run_qkv(source, vecs, shift, tables, pieces, at, rows, filled):
    x, first = source
    width = x.shape[1]
    length = tables[0].shape[0]
    cols = shift.shape[1]
    bf = jnp.bfloat16
    base = at // ROW_BLOCK
    own = lambda i: (i + base, 0)
    return call(
        qkv_body,
        "norm_qkv",
        rows * 13 * MICROSECOND // 1024,
        (rows // ROW_BLOCK,),
        [rows_of(x, first), whole(vecs), whole(shift)]
        + [rows_of(t, at) for t in tables]
        + matrix(pieces, cols // 4, 0),
        [
            ((length, width), bf, (ROW_BLOCK, width), own),
            ((length, width), bf, (ROW_BLOCK, width), own),
            ((length, cols), bf, (ROW_BLOCK, cols), own),
        ],
        [room(pieces, cols // 4)],
        filled,
    )


def attend_body(q, k, v, ctx, lse):
    length = q.shape[0]
    step = ROW_BLOCK
    for head in range(2):
        lanes = slice(head * 64, head * 64 + 64)
        keys = k[:, lanes]
        vals = v[:, lanes]
        for at in range(0, length, step):
            end = at + step
            queries = q[at:end, lanes] * jnp.bfloat16(0.125)
            scores = nt_dot(queries, keys[:end])
            row = lax.broadcasted_iota(jnp.int32, (step, step), 0)
            col = lax.broadcasted_iota(jnp.int32, (step, step), 1)
            last = jnp.where(col <= row, scores[:, at:], MASK_FILL)
            scores = last if at == 0 else jnp.concatenate([scores[:, :at], last], axis=1)
            top = jnp.max(scores, axis=1, keepdims=True)
            power = jnp.exp(scores - top)
            total = jnp.sum(power, axis=1, keepdims=True)
            mixed = nn_dot(power.astype(jnp.bfloat16), vals[:end]) * (1.0 / total)
            ctx[at:end, lanes] = mixed.astype(jnp.bfloat16)
            level = jnp.broadcast_to(top + jnp.log(total), (step, 128))
            lse[0, head : head + 1, at:end] = level.T[0:1]


def run_attend(qkv):
    length, cols = qkv.shape
    groups = cols // 384
    return call(
        attend_body,
        "attend",
        length * 19 * MICROSECOND // 1024,
        (groups,),
        [
            (qkv, (length, 128), lambda i: (0, 3 * i)),
            (qkv, (length, 128), lambda i: (0, 3 * i + 1)),
            (qkv, (length, 128), lambda i: (0, 3 * i + 2)),
        ],
        [
            ((length, groups * 128), jnp.bfloat16, (length, 128), lambda i: (0, i)),
            ((groups, 8, length), jnp.float32, (1, 8, length), lambda i: (i, 0, 0)),
        ],
    )


ERF_TOP = (
    0.00022905065861350646,
    0.0034082910107109506,
    0.050955695062380861,
    0.18520832239976145,
    1.128379143519084,
)
ERF_BOTTOM = (
    -1.1791602954361697e-7,
    0.000023547966471313185,
    0.0010179625278914885,
    0.014070470171167667,
    0.11098505178285362,
    0.49746925110067538,
    1.0,
)


def erf(x):
    x = jnp.clip(x, -3.7439211627767994, 3.7439211627767994)
    square = x * x
    top = jnp.full_like(x, ERF_TOP[0])
    for term in ERF_TOP[1:]:
        top = top * square + term
    bottom = jnp.full_like(x, ERF_BOTTOM[0])
    for term in ERF_BOTTOM[1:]:
        bottom = bottom * square + term
    return x * top / bottom


def mlp_body(ctx, ln_m, shift, *rest):
    act, slope, part, w_out, w_up, w_down = rest[24:]

    @pl.when(pl.program_id(0) == 0)
    def _():
        assemble(rest[:8], w_out)
        assemble(rest[8:16], w_up)
        assemble(rest[16:24], w_down)

    total = nt_dot(ctx[...], w_out[...])
    values = ln_m[...]
    size = min(COLUMN_STEP, act.shape[1])
    for at in range(0, act.shape[1], size):
        cols = slice(at, at + size)
        up = nn_dot(values, w_up[:, cols]) + shift[:, cols]
        half_erf = 0.5 * erf(up * (2.0**-0.5)) + 0.5
        bell = jnp.exp(up * up * -0.5) * ((2.0 * math.pi) ** -0.5)
        active = (up * half_erf).astype(jnp.bfloat16)
        act[:, cols] = active
        slope[:, cols] = (half_erf + up * bell).astype(jnp.bfloat16)
        total = total + nt_dot(active, w_down[:, cols])
    part[...] = total.astype(jnp.bfloat16)


def run_mlp(ctx, ln_m, shift, narrow, broad, at, rows, filled):
    length, width = ln_m.shape
    cols, heads = shift.shape[1], ctx.shape[1]
    bf = jnp.bfloat16
    base = at // ROW_BLOCK
    own = lambda i: (i + base, 0)
    return call(
        mlp_body,
        "mlp_out",
        rows * 32 * MICROSECOND // 1024,
        (rows // ROW_BLOCK,),
        [rows_of(ctx, at), rows_of(ln_m, at), whole(shift)]
        + matrix(narrow, heads // 4, 3)
        + matrix(broad, cols // 4, 0)
        + matrix(broad, cols // 4, 1),
        [
            ((length, cols), bf, (ROW_BLOCK, cols), own),
            ((length, cols), bf, (ROW_BLOCK, cols), own),
            ((rows, width), bf, (ROW_BLOCK, width), lambda i: (i, 0)),
        ],
        [room(narrow, heads // 4), room(broad, cols // 4), room(broad, cols // 4)],
        filled,
    )


def mlp_back_body(g, slope, *rest):
    d_up, d_ctx, sum_up, sum_g, w_out, w_down = rest[16:]

    @pl.when(pl.program_id(0) == 0)
    def _():
        assemble(rest[:8], w_out)
        assemble(rest[8:16], w_down)
        sum_up[...] = jnp.zeros_like(sum_up)
        sum_g[...] = jnp.zeros_like(sum_g)

    grad = g[...]
    size = min(COLUMN_STEP, d_up.shape[1])
    for at in range(0, d_up.shape[1], size):
        cols = slice(at, at + size)
        du = nn_dot(grad, w_down[:, cols]) * slope[:, cols].astype(jnp.float32)
        du = du.astype(jnp.bfloat16)
        d_up[:, cols] = du
        sum_up[:, cols] += jnp.sum(du.astype(jnp.float32), axis=0, keepdims=True)
    d_ctx[...] = nn_dot(grad, w_out[...]).astype(jnp.bfloat16)
    sum_g[...] += jnp.sum(grad.astype(jnp.float32), axis=0, keepdims=True)


def run_mlp_back(source, slope, narrow, broad, at, rows, heads, filled):
    g, first = source
    width = g.shape[1]
    length, cols = slope.shape
    bf = jnp.bfloat16
    base = at // ROW_BLOCK
    own = lambda i: (i + base, 0)
    fixed = lambda i: (0, 0)
    return call(
        mlp_back_body,
        "mlp_back",
        rows * 15 * MICROSECOND // 1024,
        (rows // ROW_BLOCK,),
        [rows_of(g, first), rows_of(slope, at)]
        + matrix(narrow, heads // 4, 3)
        + matrix(broad, cols // 4, 1),
        [
            ((length, cols), bf, (ROW_BLOCK, cols), own),
            ((length, heads), bf, (ROW_BLOCK, heads), own),
            ((1, cols), jnp.float32, (1, cols), fixed),
            ((1, width), jnp.float32, (1, width), fixed),
        ],
        [room(narrow, heads // 4), room(broad, cols // 4)],
        filled,
    )


def attend_back_body(q, k, v, d_ctx, lse, cos, low, high, d_qkv, sums, dk_sum, dv_sum, dq_all):
    length = q.shape[0]
    step = ROW_BLOCK
    for head in range(2):
        lanes = slice(head * 64, head * 64 + 64)
        keys = k[:, lanes]
        vals = v[:, lanes]
        dk_sum[:, lanes] = jnp.zeros((length, 64), jnp.float32)
        dv_sum[:, lanes] = jnp.zeros((length, 64), jnp.float32)
        for at in range(0, length, step):
            end = at + step
            queries = q[at:end, lanes] * jnp.bfloat16(0.125)
            grads = d_ctx[at:end, lanes]
            scores = nt_dot(keys[:end], queries)
            power = jnp.exp(scores - lse[0, head : head + 1, at:end])
            key = lax.broadcasted_iota(jnp.int32, (step, step), 0)
            row = lax.broadcasted_iota(jnp.int32, (step, step), 1)
            last = jnp.where(key <= row, power[at:], 0.0)
            probs = last if at == 0 else jnp.concatenate([power[:at], last], axis=0)
            d_probs = nt_dot(vals[:end], grads)
            delta = jnp.sum(probs * d_probs, axis=0, keepdims=True)
            d_scores = (probs * (d_probs - delta)).astype(jnp.bfloat16)
            dv_sum[:end, lanes] += nn_dot(probs.astype(jnp.bfloat16), grads)
            dk_sum[:end, lanes] += nn_dot(d_scores, queries)
            dq_all[at:end, lanes] = tn_dot(d_scores, keys[:end]) * 0.125
    dq = turn(dq_all[...], cos[...], -low[...], -high[...]).astype(jnp.bfloat16)
    dk = turn(dk_sum[...], cos[...], -low[...], -high[...]).astype(jnp.bfloat16)
    dv = dv_sum[...].astype(jnp.bfloat16)
    for part, piece in enumerate((dq, dk, dv)):
        at = part * 128
        d_qkv[:, at : at + 128] = piece
        sums[:, at : at + 128] = jnp.sum(piece.astype(jnp.float32), axis=0, keepdims=True)


def run_attend_back(qkv, d_ctx, lse, tables):
    length, cols = qkv.shape
    groups = cols // 384
    wide = pltpu.VMEM((length, 128), jnp.float32)
    return call(
        attend_back_body,
        "attend_back",
        length * 26 * MICROSECOND // 1024,
        (groups,),
        [
            (qkv, (length, 128), lambda i: (0, 3 * i)),
            (qkv, (length, 128), lambda i: (0, 3 * i + 1)),
            (qkv, (length, 128), lambda i: (0, 3 * i + 2)),
            (d_ctx, (length, 128), lambda i: (0, i)),
            (lse, (1, 8, length), lambda i: (i, 0, 0)),
        ]
        + [whole(t) for t in tables],
        [
            ((length, cols), jnp.bfloat16, (length, 384), lambda i: (0, i)),
            ((1, cols), jnp.float32, (1, 384), lambda i: (0, i)),
        ],
        [wide, wide, wide],
    )


def norm_back_body(x, d_qkv, d_up, vecs, *rest):
    part, sums, w_qkv, w_up = rest[16:]

    @pl.when(pl.program_id(0) == 0)
    def _():
        assemble(rest[:8], w_qkv)
        assemble(rest[8:16], w_up)
        sums[...] = jnp.zeros_like(sums)

    hat, inverse = normalised(x[...].astype(jnp.float32))
    d_attn = nt_dot(d_qkv[...], w_qkv[...])
    d_mlp = nt_dot(d_up[...], w_up[...])
    for row, term in enumerate((d_attn * hat, d_mlp * hat, d_attn, d_mlp)):
        sums[row : row + 1, :] += jnp.sum(term, axis=0, keepdims=True)
    d_hat = d_attn * vecs[0:1, :] + d_mlp * vecs[2:3, :]
    along = jnp.mean(d_hat * hat, axis=-1, keepdims=True)
    level = jnp.mean(d_hat, axis=-1, keepdims=True)
    part[...] = (inverse * (d_hat - level - hat * along)).astype(jnp.bfloat16)


def run_norm_back(source, d_qkv, d_up, vecs, narrow, broad, at, rows):
    x, first = source
    width = x.shape[1]
    n_qkv, n_up = d_qkv.shape[1] // 4, d_up.shape[1] // 4
    return call(
        norm_back_body,
        "norm_back",
        rows * 21 * MICROSECOND // 1024,
        (rows // ROW_BLOCK,),
        [rows_of(x, first), rows_of(d_qkv, at), rows_of(d_up, at), whole(vecs)]
        + matrix(narrow, n_qkv, 0)
        + matrix(broad, n_up, 0),
        [
            ((rows, width), jnp.bfloat16, (ROW_BLOCK, width), lambda i: (i, 0)),
            ((8, width), jnp.float32, (8, width), lambda i: (0, 0)),
        ],
        [room(narrow, n_qkv), room(broad, n_up)],
    )


def weight_grad_body(cuts, *refs):
    a_refs, b_refs, rest = refs[: sum(cuts)], refs[sum(cuts) :], refs[sum(cuts) + 2 :]
    keep, send, turned_one, turned_two = rest
    groups = (a_refs[: cuts[0]], a_refs[cuts[0] :])

    @pl.when(pl.program_id(0) == 0)
    def _():
        for group, turned in zip(groups, (turned_one, turned_two)):
            at = 0
            for ref in group:
                turned[:, at : at + ref.shape[0]] = ref[...].T
                at += ref.shape[0]

    at = 0
    rows = keep.shape[2]
    for turned, right in zip((turned_one, turned_two), b_refs[:2]):
        size = right.shape[1]
        grad = nn_dot(turned[...], right[...]).astype(jnp.bfloat16)
        for side in range(2):
            first = 2 * side * rows
            keep[side, 0, :, at : at + size] = grad[first : first + rows]
            send[side, 0, :, at : at + size] = grad[first + rows : first + 2 * rows]
        at += size


def run_weight_grad(lefts, rights):
    length, width = rights[0].shape[0], lefts[0][0].shape[1]
    sizes = [right.shape[1] // 4 for right in rights]
    shape = (2, 4, width // 4, sum(sizes))
    out = (shape, jnp.bfloat16, (2, 1) + shape[2:], lambda i: (0, i, 0, 0))
    turned = pltpu.VMEM((width, length), jnp.bfloat16)
    return call(
        partial(weight_grad_body, tuple(len(group) for group in lefts)),
        "weight_grad",
        length * 14 * MICROSECOND // 1024,
        (4,),
        [whole(left) for group in lefts for left in group]
        + [(r, (length, n), lambda i: (0, i)) for r, n in zip(rights, sizes)],
        [out, out],
        [turned, turned],
    )


def turn_tables(length):
    cosine, sine_tab = rotary_tables(length)
    zero = jnp.zeros_like(sine_tab)
    rest = jnp.zeros((length, 64 - ROT), jnp.float32)
    cos = jnp.concatenate([cosine, cosine, rest + 1.0], axis=1)
    low = jnp.concatenate([zero, sine_tab, rest], axis=1)
    high = jnp.concatenate([-sine_tab, zero, rest], axis=1)
    return tuple(jnp.concatenate([t, t], axis=1) for t in (cos, low, high))


def by_sequence(
    acts_in, cotangent, norm_gains, vec_bias, w_qkv, b_qkv, w_out, w_up, b_up, w_down
):
    section = lax.axis_index("section").astype(jnp.uint32)
    across = lax.axis_index("dp").astype(jnp.uint32)
    along = lax.axis_index("tensor").astype(jnp.uint32)
    first_section = section == 0
    width = acts_in.shape[3]
    rows = w_qkv.shape[1]
    positions = acts_in.shape[1]
    length = 4 * positions
    heads = b_qkv.shape[1]
    bf = jnp.bfloat16

    qkv_halves = (
        w_qkv[0].reshape(rows, 2, 2, 3, 64).transpose(1, 0, 3, 2, 4).reshape(2, rows, -1)
    )
    out_halves = w_out[0].T.reshape(rows, 2, -1).transpose(1, 0, 2)
    up_halves = w_up[0].reshape(rows, 2, -1).transpose(1, 0, 2)
    down_halves = w_down[0].T.reshape(rows, 2, -1).transpose(1, 0, 2)
    n_qkv, n_out, n_up = qkv_halves.shape[2], out_halves.shape[2], up_halves.shape[2]

    narrow = jnp.stack([jnp.concatenate([qkv_halves[h], out_halves[h]], axis=1) for h in (0, 1)])
    broad = jnp.stack([jnp.concatenate([up_halves[h], down_halves[h]], axis=1) for h in (0, 1)])
    small = jnp.concatenate(
        [
            norm_gains[0].reshape(-1),
            vec_bias[0].reshape(-1),
            b_qkv[0].reshape(-1).astype(jnp.float32),
            b_up[0].reshape(-1).astype(jnp.float32),
        ]
    )
    clock = Clock()
    hold, tick = clock.hold, clock.tick

    def pass_half(halves):
        return swap(hold(pick(halves, 1 - section)), "section", 1)

    def by_layer(halves, got):
        keep = pick(halves, section)
        return jnp.where(first_section, keep, got), jnp.where(first_section, got, keep)

    def x_swap(value):
        return swap(hold(value), "dp", 2)

    def core_swap(value):
        return swap(hold(value), "dp", 1)

    def y_swap(value):
        return swap(hold(value), "section", 1)

    def both_ways(value):
        value = hold(value)
        return ring(value, "tensor", 1), ring(value, "tensor", -1)

    def far_halves(left, right):
        half = left.shape[0] // 2
        return ring(hold(left[:half]), "tensor", 1), ring(hold(right[half:]), "tensor", -1)

    def own_half(blocks):
        return lax.dynamic_slice_in_dim(blocks, section * (width // 2), width // 2, 2)

    def both_halves(own, got):
        own = own.reshape(length, width // 2)
        got = got.reshape(length, width // 2)
        low = jnp.where(first_section, own, got)
        high = jnp.where(first_section, got, own)
        return relative(jnp.concatenate([low, high], axis=1), across)

    def stacked(own, got):
        return jnp.stack([own, got])

    got_narrow = pass_half(narrow)
    got_small = swap(small, "section", 1)
    blocks = own_half(acts_in[:, :, 0, :])
    near = exchange_near(blocks, along, hold)
    tick(got_narrow, got_small, near)
    narrow_shards = by_layer(narrow, got_narrow)
    small = jnp.where(first_section, jnp.stack([small, got_small]), jnp.stack([got_small, small]))
    left, right = both_ways(narrow_shards[0])
    far = exchange_far(near, hold)
    got_broad = pass_half(broad)
    got_own = x_swap(narrow_shards[0])
    small = jnp.stack([small, core_swap(small)])
    small = jnp.concatenate([small, swap(small, "dp", 2)])
    tick(left, right, far, got_broad, got_own, small)
    own_acts = exchanged(blocks, near, far, along)
    got_acts = y_swap(own_acts)
    narrow_far = far_halves(left, right)
    got_left, got_right = x_swap(left), x_swap(right)
    small = jnp.stack([small, swap(hold(small), "tensor", 1)])
    small = jnp.concatenate([small, swap(small, "tensor", 2)])
    tick(narrow_far, got_left, got_right, small)
    broad_shards = by_layer(broad, got_broad)
    broad_left, broad_right = both_ways(broad_shards[0])
    narrow_far = jnp.concatenate(narrow_far, axis=0)
    got_far = x_swap(narrow_far)
    pieces = [
        stacked(narrow_shards[0], got_own),
        stacked(left, got_left),
        stacked(right, got_right),
    ]
    others = [core_swap(piece) for piece in pieces]
    tick(got_far, others, got_acts)
    acts = both_halves(own_acts, got_acts)
    pieces.append(stacked(narrow_far, got_far))
    others.append(core_swap(pieces[3]))
    got_own = x_swap(broad_shards[0])
    narrow_zero = (*pieces, *others)
    tick(others[3])

    share = norm_gains.shape[2]
    vec_part = small[..., : 6 * share].reshape(4, 4, 2, 6, share)
    offsets = jnp.array(FAR_ORDER, jnp.int32)
    order = jnp.stack([pick(offsets, (k - along) & 3) for k in range(4)])
    slots = [jnp.bitwise_xor((along + k) & 3, along) for k in (0, 3, 1, 2)]
    vec_part = jnp.stack([pick(vec_part, jnp.bitwise_xor(along, k)) for k in range(4)])
    vecs_full = vec_part.transpose(2, 3, 1, 0, 4).reshape(2, 6, width)
    at = 6 * share
    share_q = b_qkv.shape[2]
    dp_order = [jnp.bitwise_xor(across, k) for k in range(4)]
    qkv_bias = small[..., at : at + heads * share_q].reshape(4, 4, 2, heads, share_q)
    qkv_bias = jnp.stack([pick(qkv_bias, k) for k in slots])
    qkv_bias = jnp.stack([pick(qkv_bias, i, 1) for i in dp_order], axis=1)
    qkv_bias = qkv_bias.transpose(2, 0, 3, 1, 4).reshape(2, 4, 2, heads // 2, 3, 64)
    qkv_bias = pick(qkv_bias, section, 2).transpose(0, 1, 3, 2, 4).reshape(2, 1, -1)
    at += heads * share_q
    bias_rows, share_u = b_up.shape[1], b_up.shape[2]
    up_bias = small[..., at : at + bias_rows * share_u].reshape(4, 4, 2, bias_rows, share_u)
    up_bias = jnp.stack([pick(up_bias, k) for k in slots])
    up_bias = jnp.stack([pick(up_bias, i, 1) for i in dp_order], axis=1)
    up_bias = up_bias.transpose(2, 0, 3, 1, 4).reshape(2, 4, 2, bias_rows // 2, 4 * share_u)
    up_bias = pick(up_bias, section, 2).reshape(2, 1, -1)
    zero_rows = jnp.zeros((4, width), jnp.float32)

    tables = turn_tables(length)
    chunk = length // CHUNKS
    starts = [i * chunk for i in range(CHUNKS)]

    all_vecs = [
        jnp.concatenate([v[0:1], v[2:3], v[1:2], v[3:4], zero_rows], axis=0) for v in vecs_full
    ]

    def project(layer, i, source, pieces, filled):
        return run_qkv(
            source, all_vecs[layer], qkv_bias[layer], tables, pieces, starts[i], chunk, filled
        )

    def feed(layer, i, ctx, ln_m, narrow, broad, filled):
        *filled, part = run_mlp(
            hold(ctx), ln_m, up_bias[layer], narrow, broad, starts[i], chunk, filled
        )
        return filled, part

    def join(layer, before, part, got):
        total = part.astype(jnp.float32) + got.astype(jnp.float32)
        full = vecs_full[layer]
        return (before.astype(jnp.float32) + total + (full[4] + full[5])).astype(bf)

    acts = hold(acts)
    first = project(0, 0, (acts, 0), narrow_zero, ())
    tick(first, broad_left, broad_right)
    got_left = x_swap(broad_left)
    first = project(0, 1, (acts, chunk), narrow_zero, first)
    tick(first, got_own)
    ln_a0, ln_m0, qkv0 = first
    broad_far = far_halves(broad_left, broad_right)
    got_right = x_swap(broad_right)
    ctx0, lse0 = run_attend(hold(qkv0))
    tick(ctx0, broad_far, got_left, got_right)
    broad_far = jnp.concatenate(broad_far, axis=0)
    got_far = x_swap(broad_far)
    pieces = [
        stacked(broad_shards[0], got_own),
        stacked(broad_left, got_left),
        stacked(broad_right, got_right),
    ]
    others = [core_swap(piece) for piece in pieces]
    tick(got_far, others)
    pieces.append(stacked(broad_far, got_far))
    others.append(core_swap(pieces[3]))
    broad_zero = (*pieces, *others)
    tick(others[3])
    first, part_a = feed(0, 0, ctx0, ln_m0, narrow_zero, broad_zero, ())
    left, right = both_ways(narrow_shards[1])
    got_own = x_swap(narrow_shards[1])
    broad_own = x_swap(broad_shards[1])
    tick(part_a, left, right, got_own, broad_own)
    first, part_b = feed(0, 1, ctx0, ln_m0, narrow_zero, broad_zero, first)
    act0, slope0 = first
    got_a = y_swap(part_a)
    narrow_far = far_halves(left, right)
    broad_left, broad_right = both_ways(broad_shards[1])
    tick(part_b, got_a, narrow_far, broad_left, broad_right)
    got_b = y_swap(part_b)
    got_left, got_right = x_swap(left), x_swap(right)
    x1_a = join(0, acts[:chunk], part_a, got_a)
    tick(got_left, got_right)
    narrow_far = jnp.concatenate(narrow_far, axis=0)
    got_far = x_swap(narrow_far)
    pieces = [
        stacked(narrow_shards[1], got_own),
        stacked(left, got_left),
        stacked(right, got_right),
    ]
    others = [core_swap(piece) for piece in pieces]
    tick(got_b, got_far, others)
    x1_b = join(0, acts[chunk:], part_b, got_b)
    pieces.append(stacked(narrow_far, got_far))
    others.append(core_swap(pieces[3]))
    narrow_one = (*pieces, *others)
    tick(others[3], x1_a, x1_b)

    broad_far = far_halves(broad_left, broad_right)
    got_left = x_swap(broad_left)
    first = project(1, 0, (hold(x1_a), 0), narrow_one, ())
    first = project(1, 1, (x1_b, 0), narrow_one, first)
    ln_a1, ln_m1, qkv1 = first
    tick(first, broad_far, got_left)
    broad_far = jnp.concatenate(broad_far, axis=0)
    got_right, got_far = x_swap(broad_right), x_swap(broad_far)
    pieces = [stacked(broad_shards[1], broad_own), stacked(broad_left, got_left)]
    others = [core_swap(piece) for piece in pieces]
    ctx1, lse1 = run_attend(hold(qkv1))
    tick(ctx1, got_right, got_far, others)
    pieces += [stacked(broad_right, got_right), stacked(broad_far, got_far)]
    others += [core_swap(piece) for piece in pieces[2:]]
    broad_one = (*pieces, *others)
    tick(others[2:])
    first, part_a = feed(1, 0, ctx1, ln_m1, narrow_one, broad_one, ())
    blocks = own_half(cotangent[:, :, 0, :])
    near = exchange_near(blocks, along, hold)
    tick(part_a, near)
    first, part_b = feed(1, 1, ctx1, ln_m1, narrow_one, broad_one, first)
    act1, slope1 = first
    far = exchange_far(near, hold)
    tick(far)
    own_grads = exchanged(blocks, near, far, along)
    got_grads = y_swap(own_grads)
    tick(part_b, got_grads)

    grads = hold(both_halves(own_grads, got_grads))
    n_heads = ctx0.shape[1]

    def back(i, source, slope, narrow, broad, filled):
        *filled, up_term, g_term = run_mlp_back(
            source, slope, narrow, broad, starts[i], chunk, n_heads, filled
        )
        return filled, up_term, g_term

    first, up_a, g_a = back(0, (grads, 0), slope1, narrow_one, broad_one, ())
    first, up_b, g_b = back(1, (grads, chunk), slope1, narrow_one, broad_one, first)
    d_up1, d_ctx1 = first
    sums_one = [None, g_a + g_b, None, up_a + up_b]
    got_a = y_swap(part_a)
    tick(first, got_a)
    x1 = jnp.concatenate([x1_a, x1_b], axis=0)

    def to_blocks(values):
        return relative(values, across).reshape(4, positions, width)

    d_qkv1, sums_one[2] = run_attend_back(qkv1, hold(d_ctx1), lse1, tables)
    got_b = y_swap(part_b)
    tick(d_qkv1, got_b)
    x2 = jnp.concatenate(
        [join(1, x1_a, part_a, got_a), join(1, x1_b, hold(part_b), got_b)], axis=0
    )
    out_blocks = to_blocks(jnp.where(first_section, x1, x2))
    part_a, sum_a = run_norm_back(
        (x1_a, 0), hold(d_qkv1), d_up1, all_vecs[1], narrow_one, broad_one, 0, chunk
    )
    tick(part_a, out_blocks)
    got_a = y_swap(part_a)
    out_parts = out_blocks[..., : width // 2], out_blocks[..., width // 2 :]
    out_near = [exchange_near(out_parts[0], along, hold)]
    part_b, sum_b = run_norm_back(
        (x1_b, 0), hold(d_qkv1), d_up1, all_vecs[1], narrow_one, broad_one, chunk, chunk
    )
    sums_one[0] = (sum_a + sum_b)[:4]
    keep_broad, send = run_weight_grad([[hold(ln_m1)], [grads]], [d_up1, act1])
    tick(part_b, keep_broad, got_a, out_near)
    got_b = y_swap(part_b)
    got_core = core_swap(send)
    out_near.append(exchange_near(out_parts[1], along, hold))
    keep_narrow, send_narrow = run_weight_grad([[hold(ln_a1)], [grads]], [d_qkv1, ctx1])
    tick(keep_narrow, got_b, got_core, out_near)

    def lower(above, part, got):
        total = part.astype(jnp.float32) + got.astype(jnp.float32)
        return (above.astype(jnp.float32) + total).astype(bf)

    g1_a = lower(grads[:chunk], hold(part_a), got_a)
    g1_b = lower(grads[chunk:], hold(part_b), got_b)
    keep_one, core_one = hold(keep_broad), got_core
    got_core = core_swap(send_narrow)
    got_x = [x_swap(add_wide(keep_one[1, 2:], core_one[1, 2:]))]
    first, up_a, g_a = back(0, (hold(g1_a), 0), slope0, narrow_zero, broad_zero, ())
    first, up_b, g_b = back(1, (g1_b, 0), slope0, narrow_zero, broad_zero, first)
    d_up0, d_ctx0 = first
    sums_zero = [None, g_a + g_b, None, up_a + up_b]
    out_far = [exchange_far(near, hold) for near in out_near]
    tick(first, got_core, got_x, out_far)
    core_narrow = got_core
    got_x.append(x_swap(add_wide(hold(keep_one[1, :2]), core_one[1, :2])))
    keep_broad, send = run_weight_grad([[hold(ln_m0)], [g1_a, g1_b]], [d_up0, act0])
    tick(keep_broad, got_x)

    def late_blocks(keep, core, got):
        late = add_three(hold(keep[0, 2:]), core[0, 2:], got)
        return [late[0], late[1]]

    def early_blocks(keep, core, got):
        early = add_three(hold(keep[0, :2]), core[0, :2], got)
        return [early[0], early[1]]

    got_core = core_swap(send)
    late = late_blocks(keep_one, core_one, got_x[0])
    broad_got = ring_first([None, None, *late], hold)
    got_narrow = x_swap(add_wide(hold(keep_narrow[1]), core_narrow[1]))
    d_qkv0, sums_zero[2] = run_attend_back(qkv0, hold(d_ctx0), lse0, tables)
    tick(d_qkv0, broad_got, got_core, got_narrow)
    broad_one_sum = early_blocks(keep_one, core_one, got_x[1]) + late
    narrow_sum = add_three(hold(keep_narrow[0]), core_narrow[0], got_narrow)
    narrow_sum = [narrow_sum[k] for k in range(4)]
    keep_zero, core_zero = hold(keep_broad), got_core
    got_x = [x_swap(add_wide(keep_zero[1, 2:], core_zero[1, 2:]))]
    broad_got = ring_second(broad_one_sum, broad_got, hold)
    part_a, sum_a = run_norm_back(
        (acts, 0), hold(d_qkv0), d_up0, all_vecs[0], narrow_zero, broad_zero, 0, chunk
    )
    tick(part_a)
    got_a = y_swap(part_a)
    part_b, sum_b = run_norm_back(
        (acts, chunk), hold(d_qkv0), d_up0, all_vecs[0], narrow_zero, broad_zero, chunk, chunk
    )
    sums_zero[0] = (sum_a + sum_b)[:4]
    tick(part_b, got_x, broad_got)
    got_b = y_swap(part_b)
    got_x.append(x_swap(add_wide(hold(keep_zero[1, :2]), core_zero[1, :2])))
    narrow_got = ring_first(narrow_sum, hold)
    keep_narrow, send_narrow = run_weight_grad([[hold(ln_a0)], [g1_a, g1_b]], [d_qkv0, ctx0])
    tick(keep_narrow, got_a, got_b, got_x, narrow_got)

    flat = []
    for norm_sums, sum_g, sum_qkv, sum_up in hold((sums_zero, sums_one)):
        feature = relative(jnp.concatenate([norm_sums, sum_g], axis=0), across)
        q_sum = sum_qkv.reshape(4, 3, 2, 64).transpose(0, 2, 1, 3).reshape(4, -1)
        both = jnp.concatenate([q_sum, sum_up.reshape(4, -1)], axis=1)
        both = jnp.stack([pick(both, order[k]) for k in range(4)])
        flat.append(jnp.concatenate([feature.reshape(-1), both.reshape(-1)]))
    flat = jnp.stack(flat)
    got_core = core_swap(send_narrow)
    late = late_blocks(keep_zero, core_zero, got_x[0])
    broad_next = ring_first([None, None, *late], hold)
    grads_low = jnp.concatenate(
        [lower(g1_a, hold(part_a), got_a), lower(g1_b, hold(part_b), got_b)], axis=0
    )
    g1 = jnp.concatenate([g1_a, g1_b], axis=0)
    grad_blocks = to_blocks(jnp.where(first_section, grads_low, g1))
    flat = flat + swap(flat, "dp", 1)
    tick(broad_next, got_core, grad_blocks, flat)
    broad_zero_sum = early_blocks(keep_zero, core_zero, got_x[1]) + late
    broad_next = ring_second(broad_zero_sum, broad_next, hold)
    narrow_got = ring_second(narrow_sum, narrow_got, hold)
    got_narrow = x_swap(add_wide(hold(keep_narrow[1]), got_core[1]))
    flat = flat + x_swap(flat)
    acts_local = [
        exchanged(part, near, far, along)
        for part, near, far in zip(hold(out_parts), out_near, out_far)
    ]
    acts_local = jnp.concatenate(acts_local, axis=-1)
    tick(broad_next, got_narrow, flat, narrow_got, acts_local)
    zero_sum = add_three(hold(keep_narrow[0]), got_core[0], got_narrow)
    zero_sum = [zero_sum[k] for k in range(4)]
    narrow_next = ring_first(zero_sum, hold)
    flat = flat + swap(hold(flat), "tensor", 1)
    tick(narrow_next, flat)
    grad_near = exchange_near(grad_blocks, along, hold)
    narrow_next = ring_second(zero_sum, narrow_next, hold)
    one_broad = ring_total(hold(broad_one_sum[0]), broad_got)
    one_narrow = ring_total(hold(narrow_sum[0]), narrow_got)
    zero_broad = ring_total(hold(broad_zero_sum[0]), broad_next)
    broad_send = y_swap(jnp.where(first_section, one_broad, zero_broad))
    tick(narrow_next, grad_near, broad_send)
    grad_far = exchange_far(grad_near, hold)
    zero_narrow = ring_total(zero_sum[0], narrow_next)
    narrow_send = y_swap(jnp.where(first_section, one_narrow, zero_narrow))
    flat = flat + swap(hold(flat), "tensor", 2)
    grad_local = exchanged(grad_blocks, grad_near, grad_far, along)

    def whole_layer(keep_pair, got):
        keep = jnp.where(first_section, *keep_pair).astype(jnp.float32)
        got = got.astype(jnp.float32)
        return jnp.where(first_section, jnp.stack([keep, got], 1), jnp.stack([got, keep], 1))

    narrow_out = whole_layer((zero_narrow, one_narrow), narrow_send)
    broad_out = whole_layer((zero_broad, one_broad), broad_send)
    grad_qkv = narrow_out[..., :n_qkv].reshape(rows, 2, 3, 2, 64)
    grad_qkv = grad_qkv.transpose(0, 1, 3, 2, 4).reshape(rows, -1)
    grad_out = narrow_out[..., n_qkv:].reshape(rows, -1).T
    grad_up = broad_out[..., :n_up].reshape(rows, -1)
    grad_down = broad_out[..., n_up:].reshape(rows, -1).T

    keep = pick(flat, section)
    mine = pick(flat, 1 - section)
    got = swap(mine, "section", 1)
    n_feature = 5 * width
    feature_own = keep[:n_feature].reshape(5, width)
    feature = feature_own[:4] + got[: 4 * width].reshape(4, width)
    place_at = (across * 4 + along) * share
    gain_share = lax.dynamic_slice_in_dim(feature[:2], place_at, share, 1)
    shifts = jnp.concatenate([feature[2:4], feature_own[4:5], feature_own[4:5]], axis=0)
    bias_share = lax.dynamic_slice_in_dim(shifts, place_at, share, 1)
    low_half = jnp.where(first_section, keep, got)[n_feature:].reshape(4, -1)
    high_half = jnp.where(first_section, got, keep)[n_feature:].reshape(4, -1)
    halves = jnp.stack([pick(low_half, along), pick(high_half, along)])
    n_head = (heads // 2) * 192
    head_sums = halves[:, :n_head].reshape(heads, 192)
    head_share = lax.dynamic_slice_in_dim(head_sums, across * share_q, share_q, 1)
    unit_sums = halves[:, n_head:].reshape(bias_rows, 4 * share_u)
    unit_share = lax.dynamic_slice_in_dim(unit_sums, across * share_u, share_u, 1)
    return (
        acts_local[None, :, :, None],
        grad_local[None, :, :, None],
        gain_share[None],
        bias_share[None],
        grad_qkv[None],
        head_share[None],
        grad_out[None],
        grad_up[None],
        unit_share[None],
        grad_down[None],
    )


def fits(mesh, args):
    acts_in, b_qkv = args[0], args[5]
    sizes = dict(mesh.shape)
    return (
        sizes["section"] == 2
        and sizes["dp"] == 4
        and sizes["tensor"] == MICRO
        and MICRO == 4
        and acts_in.shape[2] == sizes["dp"]
        and b_qkv.shape[1] == 16
        and b_qkv.shape[2] == 192
        and acts_in.shape[1] % (CHUNKS * ROW_BLOCK) == 0
    )


def solution(mesh):
    placed = (
        P(None, "tensor", "dp", None),
        P(None, "tensor", "dp", None),
        P("section", None, ("dp", "tensor")),
        P("section", None, ("dp", "tensor")),
        P("section", "dp", "tensor"),
        P("section", "tensor", "dp"),
        P("section", "tensor", "dp"),
        P("section", "dp", "tensor"),
        P("section", "tensor", "dp"),
        P("section", "tensor", "dp"),
    )
    def wrap(body):
        return jax.shard_map(
            body,
            mesh=mesh,
            in_specs=placed,
            out_specs=(
                P("section", None, "tensor", "dp", None),
                P("section", None, "tensor", "dp", None),
                P("section", None, ("dp", "tensor")),
                P("section", None, ("dp", "tensor")),
                P("section", "dp", "tensor"),
                P("section", "tensor", "dp"),
                P("section", "tensor", "dp"),
                P("section", "dp", "tensor"),
                P("section", "tensor", "dp"),
                P("section", "tensor", "dp"),
            ),
            check_vma=False,
        )

    return lambda *args: wrap(by_sequence if fits(mesh, args) else local)(*args)
```

```python
from functools import partial
import math

import jax
import jax.numpy as jnp
from jax import lax
from jax.experimental import pallas as pl
from jax.experimental.pallas import tpu as pltpu
from jax.sharding import PartitionSpec as P

ROT = 16
QBLOCK = 512
MICRO = 4


NORM_EPS = 1e-05
ROPE_BASE = 10000.0
MASK_FILL = -1e30


def from_behind(value, axis, by):
    length = lax.axis_size(axis)
    pairs = [(i, i + by) for i in range(length) if 0 <= i + by < length]
    return lax.ppermute(value, axis, pairs)


def layer_norm(values, norm_gain, norm_shift):
    average = jnp.mean(values, axis=-1, keepdims=True)
    centred = values - average
    variance = jnp.mean(centred * centred, axis=-1, keepdims=True)
    return centred * lax.rsqrt(variance + NORM_EPS) * norm_gain + norm_shift


def both_norms(values, gain_attn, shift_attn, gain_mlp, shift_mlp):
    return (layer_norm(values, gain_attn, shift_attn), layer_norm(values, gain_mlp, shift_mlp))


def rotary_tables(length):
    half_rot = ROT // 2
    frequency = jnp.exp(
        jnp.arange(half_rot, dtype=jnp.float32) * (-2.0 * math.log(ROPE_BASE) / ROT)
    )
    angles = jnp.arange(length, dtype=jnp.float32)[:, None] * frequency[None, :]
    return (jnp.cos(angles), jnp.sin(angles))


def rotate(values, cosine, sine_tab):
    half_rot = ROT // 2
    low_half = values[..., :half_rot]
    high_half = values[..., half_rot:ROT]
    return jnp.concatenate(
        [
            low_half * cosine - high_half * sine_tab,
            high_half * cosine + low_half * sine_tab,
            values[..., ROT:],
        ],
        axis=-1,
    )


def rotate_back(grads_rot, cosine, sine_tab):
    half_rot = ROT // 2
    low_half = grads_rot[..., :half_rot]
    high_half = grads_rot[..., half_rot:ROT]
    return jnp.concatenate(
        [
            low_half * cosine + high_half * sine_tab,
            high_half * cosine - low_half * sine_tab,
            grads_rot[..., ROT:],
        ],
        axis=-1,
    )


def causal_scores(queries, key_rows, first_row, score_scale):
    block_rows = queries.shape[0]
    last_row = key_rows.shape[0]
    scores = (
        jnp.einsum("qshd,kshd->shqk", queries, key_rows, preferred_element_type=jnp.float32)
        * score_scale
    )
    row_pos = first_row + jnp.arange(block_rows, dtype=jnp.int32)
    col_pos = jnp.arange(last_row, dtype=jnp.int32)
    allowed = col_pos[None, :] <= row_pos[:, None]
    return (scores, allowed)


def attend(queries, key_rows, val_rows):
    length = queries.shape[0]
    block_rows = min(QBLOCK, length)
    score_scale = queries.shape[-1] ** (-0.5)
    outputs = []
    totals = []
    for block_index in range(length // block_rows):
        first_row = block_index * block_rows
        last_row = first_row + block_rows
        scores, allowed = causal_scores(
            queries[first_row:last_row], key_rows[:last_row], first_row, score_scale
        )
        scores = jnp.where(allowed, scores, MASK_FILL)
        highest = jnp.max(scores, axis=-1, keepdims=True)
        exponent = jnp.exp(scores - highest)
        denominator = jnp.sum(exponent, axis=-1, keepdims=True)
        probability = (exponent / denominator).astype(jnp.bfloat16)
        block_out = jnp.einsum(
            "shqk,kshd->qshd", probability, val_rows[:last_row], preferred_element_type=jnp.float32
        )
        outputs.append(block_out.astype(jnp.bfloat16))
        totals.append((highest + jnp.log(denominator))[..., 0])
    context = jnp.concatenate(outputs, axis=0)
    return (context.reshape(length, context.shape[1], -1), jnp.concatenate(totals, axis=-1))


def attend_back(queries, key_rows, val_rows, d_context, log_total):
    length = queries.shape[0]
    block_rows = min(QBLOCK, length)
    score_scale = queries.shape[-1] ** (-0.5)
    grad_query_list = []
    grad_keys = jnp.zeros(queries.shape, jnp.float32)
    grad_vals = jnp.zeros(queries.shape, jnp.float32)
    for block_index in range(length // block_rows):
        first_row = block_index * block_rows
        last_row = first_row + block_rows
        query_block = queries[first_row:last_row]
        scores, allowed = causal_scores(query_block, key_rows[:last_row], first_row, score_scale)
        probability = jnp.where(
            allowed, jnp.exp(scores - log_total[:, :, first_row:last_row, None]), 0.0
        )
        d_block = d_context[first_row:last_row]
        d_prob = jnp.einsum(
            "qshd,kshd->shqk", d_block, val_rows[:last_row], preferred_element_type=jnp.float32
        )
        delta = jnp.sum(probability * d_prob, axis=-1, keepdims=True)
        d_scores = (probability * (d_prob - delta)).astype(jnp.bfloat16)
        grad_query_list.append(
            jnp.einsum(
                "shqk,kshd->qshd", d_scores, key_rows[:last_row], preferred_element_type=jnp.float32
            )
            * score_scale
        )
        grad_keys = grad_keys.at[:last_row].add(
            jnp.einsum("shqk,qshd->kshd", d_scores, query_block, preferred_element_type=jnp.float32)
            * score_scale
        )
        grad_vals = grad_vals.at[:last_row].add(
            jnp.einsum(
                "shqk,qshd->kshd",
                probability.astype(jnp.bfloat16),
                d_block,
                preferred_element_type=jnp.float32,
            )
        )
    return (jnp.concatenate(grad_query_list, axis=0), grad_keys, grad_vals)


def local(acts_in, cotangent, norm_gains, vec_bias, w_qkv, b_qkv, w_out, w_up, b_up, w_down):
    section_index = lax.axis_index("section")
    own_start = lax.axis_index("tensor") * acts_in.shape[1]
    local_len = acts_in.shape[1]
    seq_count = acts_in.shape[2]
    model_width = acts_in.shape[3]
    length = local_len * lax.axis_size("tensor")
    all_rows = length * seq_count
    gain_full, bias_full = (
        lax.all_gather(norm_gains[0], ("dp", "tensor"), axis=1, tiled=True),
        lax.all_gather(vec_bias[0], ("dp", "tensor"), axis=1, tiled=True),
    )
    mat_qkv, bias_qkv, mat_out, mat_up, bias_up, mat_down = (
        lax.all_gather(w_qkv[0], "dp", axis=0, tiled=True),
        lax.all_gather(b_qkv[0], "dp", axis=1, tiled=True),
        lax.all_gather(w_out[0], "dp", axis=1, tiled=True),
        lax.all_gather(w_up[0], "dp", axis=0, tiled=True),
        lax.all_gather(b_up[0], "dp", axis=1, tiled=True),
        lax.all_gather(w_down[0], "dp", axis=1, tiled=True),
    )
    head_count = bias_qkv.shape[0]
    head_dim = bias_qkv.shape[1] // 3
    qkv_shift = bias_qkv.reshape(-1).astype(jnp.float32)
    up_shift = bias_up.reshape(-1).astype(jnp.float32)
    cosine, sine_tab = rotary_tables(length)
    cosine = cosine[:, None, None, :]
    sine_tab = sine_tab[:, None, None, :]
    received = jnp.zeros_like(acts_in[0])
    stash_list = []
    out_list = []
    for moment in range(MICRO + 1):
        own_rows = acts_in[min(moment, MICRO - 1)]
        inputs = jnp.where(section_index == 0, own_rows, received)
        forward_gathered = lax.all_gather(inputs, "tensor", axis=0, tiled=True)
        full_attn, full_mlp = both_norms(
            forward_gathered.astype(jnp.float32),
            gain_full[0],
            bias_full[0],
            gain_full[1],
            bias_full[1],
        )
        forward_normed_attn = full_attn.astype(jnp.bfloat16)
        forward_normed_mlp = full_mlp.astype(jnp.bfloat16)
        forward_flat_attn = forward_normed_attn.reshape(all_rows, model_width)
        forward_flat_mlp = forward_normed_mlp.reshape(all_rows, model_width)
        projected = (
            jnp.dot(forward_flat_attn, mat_qkv, preferred_element_type=jnp.float32) + qkv_shift
        )
        projected = projected.reshape(length, seq_count, head_count, 3, head_dim)
        forward_queries = rotate(projected[:, :, :, 0], cosine, sine_tab).astype(jnp.bfloat16)
        forward_key_rows = rotate(projected[:, :, :, 1], cosine, sine_tab).astype(jnp.bfloat16)
        forward_val_rows = projected[:, :, :, 2].astype(jnp.bfloat16)
        forward_context, forward_log_total = attend(
            forward_queries, forward_key_rows, forward_val_rows
        )
        forward_up_proj = (
            jnp.dot(forward_flat_mlp, mat_up, preferred_element_type=jnp.float32) + up_shift
        )
        forward_activated = jax.nn.gelu(forward_up_proj, approximate=False).astype(jnp.bfloat16)
        active_rows = forward_activated.reshape(length, seq_count, -1)
        context_part = forward_context.reshape(lax.axis_size("tensor") * local_len * seq_count, -1)
        active_part = active_rows.reshape(lax.axis_size("tensor") * local_len * seq_count, -1)
        summed = jnp.dot(context_part, mat_out, preferred_element_type=jnp.float32) + jnp.dot(
            active_part, mat_down, preferred_element_type=jnp.float32
        )
        mixed_sum = lax.psum_scatter(
            summed.reshape(lax.axis_size("tensor") * local_len, seq_count, model_width),
            "tensor",
            scatter_dimension=0,
            tiled=True,
        )
        result = inputs.astype(jnp.float32) + mixed_sum + bias_full[2] + bias_full[3]
        forward_stashed = (
            forward_gathered,
            forward_normed_attn,
            forward_normed_mlp,
            forward_queries,
            forward_key_rows,
            forward_val_rows,
            forward_context,
            forward_log_total,
            forward_up_proj,
            forward_activated,
        )
        result, stashed = (result.astype(jnp.bfloat16), forward_stashed)
        stash_list.append(stashed)
        out_list.append(result)
        if moment < MICRO:
            received = from_behind(result, "section", 1)
    stash_all = jax.tree.map(lambda *parts: jnp.stack(parts), *stash_list)
    acts_local = lax.dynamic_slice_in_dim(jnp.stack(out_list), section_index, MICRO, 0)
    back_received = jnp.zeros_like(cotangent[0])
    grad_list = []
    weight_sums = None
    vector_sums = None
    for moment in range(MICRO + 1):
        micro_index = moment - 1 + section_index
        is_valid = (micro_index >= 0) & (micro_index < MICRO)
        source_clock = jnp.clip(micro_index + section_index, 0, MICRO)
        stashed = jax.tree.map(
            lambda part: lax.dynamic_index_in_dim(part, source_clock, 0, keepdims=False), stash_all
        )
        upstream = jnp.where(section_index == 1, cotangent[min(moment, MICRO - 1)], back_received)
        (
            gathered,
            normed_attn,
            normed_mlp,
            queries,
            key_rows,
            val_rows,
            context,
            log_total,
            up_proj,
            activated,
        ) = stashed
        backward_inputs = lax.dynamic_slice_in_dim(gathered, own_start, local_len, 0)
        upstream_rows = lax.all_gather(upstream, "tensor", axis=0, tiled=True)
        flat_grad = upstream_rows.reshape(all_rows, model_width)
        d_context = jnp.dot(flat_grad, mat_out.T, preferred_element_type=jnp.float32).astype(
            jnp.bfloat16
        )
        d_context = d_context.reshape(length, seq_count, head_count, head_dim)
        d_active = jnp.dot(flat_grad, mat_down.T, preferred_element_type=jnp.float32)
        _, gelu_pullback = jax.vjp(partial(jax.nn.gelu, approximate=False), up_proj)
        d_up = gelu_pullback(d_active)[0].astype(jnp.bfloat16)
        grad_query, grad_key, grad_val = attend_back(
            queries, key_rows, val_rows, d_context, log_total
        )
        d_qkv = jnp.stack(
            [
                rotate_back(grad_query, cosine, sine_tab),
                rotate_back(grad_key, cosine, sine_tab),
                grad_val,
            ],
            axis=3,
        ).astype(jnp.bfloat16)
        d_qkv_flat = d_qkv.reshape(all_rows, -1)
        d_qkv_rows = d_qkv.reshape(length, seq_count, -1)
        d_up_rows = d_up.reshape(length, seq_count, -1)
        flat_attn = normed_attn.reshape(all_rows, model_width)
        flat_mlp = normed_mlp.reshape(all_rows, model_width)
        weight_terms = (
            jnp.einsum("tc,te->ce", flat_attn, d_qkv_flat, preferred_element_type=jnp.float32),
            jnp.sum(d_qkv_flat.astype(jnp.float32), axis=0).reshape(bias_qkv.shape),
            jnp.einsum(
                "tc,te->ce",
                context.reshape(all_rows, -1),
                flat_grad,
                preferred_element_type=jnp.float32,
            ),
            jnp.einsum("tc,te->ce", flat_mlp, d_up, preferred_element_type=jnp.float32),
            jnp.sum(d_up.astype(jnp.float32), axis=0).reshape(bias_up.shape),
            jnp.einsum("tc,te->ce", activated, flat_grad, preferred_element_type=jnp.float32),
        )
        attn_part = d_qkv_rows.reshape(lax.axis_size("tensor") * local_len * seq_count, -1)
        mlp_part = d_up_rows.reshape(lax.axis_size("tensor") * local_len * seq_count, -1)
        joined = jnp.concatenate(
            [
                jnp.dot(attn_part, mat_qkv.T, preferred_element_type=jnp.float32),
                jnp.dot(mlp_part, mat_up.T, preferred_element_type=jnp.float32),
            ],
            axis=-1,
        )
        d_normed = lax.psum_scatter(
            joined.reshape(lax.axis_size("tensor") * local_len, seq_count, 2 * model_width).astype(
                jnp.bfloat16
            ),
            "tensor",
            scatter_dimension=0,
            tiled=True,
        ).astype(jnp.float32)
        _, norm_pullback = jax.vjp(
            both_norms,
            backward_inputs.astype(jnp.float32),
            gain_full[0],
            bias_full[0],
            gain_full[1],
            bias_full[1],
        )
        d_local, d_gain_attn, d_shift_attn, d_gain_mlp, d_shift_mlp = norm_pullback(
            (d_normed[..., :model_width], d_normed[..., model_width:])
        )
        upstream_float = upstream.astype(jnp.float32)
        d_inputs = (upstream_float + d_local).astype(jnp.bfloat16)
        out_shift = jnp.sum(upstream_float, axis=(0, 1))
        vector_terms = (
            jnp.stack([d_gain_attn, d_gain_mlp]),
            jnp.stack([d_shift_attn, d_shift_mlp, out_shift, out_shift]),
        )
        d_inputs, weight_terms, vector_terms = (d_inputs, weight_terms, vector_terms)
        grad_list.append(d_inputs)
        if moment < MICRO:
            back_received = from_behind(d_inputs, "section", -1)
        weight_terms = tuple((jnp.where(is_valid, term, 0.0) for term in weight_terms))
        vector_terms = tuple((jnp.where(is_valid, term, 0.0) for term in vector_terms))
        if moment == 0:
            weight_sums = tuple(weight_terms)
            vector_sums = vector_terms
        else:
            weight_sums = tuple((a + b for a, b in zip(weight_sums, weight_terms)))
            vector_sums = tuple((a + b for a, b in zip(vector_sums, vector_terms)))
    sum_qkv, sum_bqkv, sum_out, sum_up, sum_bup, sum_down = weight_sums
    share_qkv, share_bqkv, share_out, share_up, share_bup, share_down = (
        lax.psum_scatter(
            sum_qkv.astype(jnp.bfloat16), "dp", scatter_dimension=0, tiled=True
        ).astype(jnp.float32),
        lax.psum_scatter(
            sum_bqkv.astype(jnp.bfloat16), "dp", scatter_dimension=1, tiled=True
        ).astype(jnp.float32),
        lax.psum_scatter(
            sum_out.astype(jnp.bfloat16), "dp", scatter_dimension=1, tiled=True
        ).astype(jnp.float32),
        lax.psum_scatter(sum_up.astype(jnp.bfloat16), "dp", scatter_dimension=0, tiled=True).astype(
            jnp.float32
        ),
        lax.psum_scatter(
            sum_bup.astype(jnp.bfloat16), "dp", scatter_dimension=1, tiled=True
        ).astype(jnp.float32),
        lax.psum_scatter(
            sum_down.astype(jnp.bfloat16), "dp", scatter_dimension=1, tiled=True
        ).astype(jnp.float32),
    )
    grad_local = lax.dynamic_slice_in_dim(jnp.stack(grad_list), 1 - section_index, MICRO, 0)
    gain_share, bias_share = (
        lax.psum_scatter(vector_sums[0], ("dp", "tensor"), scatter_dimension=1, tiled=True),
        lax.psum_scatter(vector_sums[1], ("dp", "tensor"), scatter_dimension=1, tiled=True),
    )
    return (
        acts_local[None],
        grad_local[None],
        gain_share[None],
        bias_share[None],
        share_qkv[None],
        share_bqkv[None],
        share_out[None],
        share_up[None],
        share_bup[None],
        share_down[None],
    )


FAR_ORDER = (0, 2, 3, 1)
VMEM_LIMIT = 60 * 1024 * 1024
ROW_BLOCK = 256
CHUNKS = 2
COLUMN_STEP = 512
MICROSECOND = 1_000_000_000


def ring(value, axis, by):
    length = lax.axis_size(axis)
    return lax.ppermute(value, axis, [(i, (i + by) % length) for i in range(length)])


def swap(value, axis, bit):
    length = lax.axis_size(axis)
    return lax.ppermute(value, axis, [(i, i ^ bit) for i in range(length)])


def pick(value, index, axis=0):
    return lax.dynamic_index_in_dim(value, index, axis, keepdims=False)


def place(value, block, index):
    return lax.dynamic_update_index_in_dim(value, block, index, 0)


def relative(values, own):
    size = values.shape[-1] // 4
    picked = [
        lax.dynamic_slice_in_dim(values, jnp.bitwise_xor(own, k) * size, size, values.ndim - 1)
        for k in range(4)
    ]
    return jnp.concatenate(picked, axis=-1)


class Clock:
    def __init__(self):
        self.ended = ()

    def hold(self, value):
        return lax.optimization_barrier((value, self.ended))[0]

    def tick(self, *ended):
        self.ended = tuple(jax.tree.leaves(ended))


def exchange_near(blocks, own, hold):
    half = blocks.shape[1] // 2
    far = pick(blocks, (own + 2) & 3)
    ahead = jnp.concatenate([pick(blocks, (own + 1) & 3), far[:half]], axis=0)
    behind = jnp.concatenate([pick(blocks, (own + 3) & 3), far[half:]], axis=0)
    return ring(hold(ahead), "tensor", 1), ring(hold(behind), "tensor", -1)


def exchange_far(near, hold):
    rows = near[0].shape[0] * 2 // 3
    first = ring(hold(near[0][rows:]), "tensor", 1)
    second = ring(hold(near[1][rows:]), "tensor", -1)
    return first, second


def exchanged(blocks, near, far, own):
    rows = blocks.shape[1]
    result = jnp.zeros_like(blocks)
    result = place(result, pick(blocks, own), own)
    result = place(result, near[0][:rows], (own + 3) & 3)
    result = place(result, near[1][:rows], (own + 1) & 3)
    return place(result, jnp.concatenate(far, axis=0), (own + 2) & 3)


def add_wide(left, right):
    return (left.astype(jnp.float32) + right.astype(jnp.float32)).astype(jnp.bfloat16)


def add_three(first, second, third):
    total = first.astype(jnp.float32) + second.astype(jnp.float32) + third.astype(jnp.float32)
    return total.astype(jnp.bfloat16)


def ring_first(blocks, hold):
    far = blocks[3]
    half = far.shape[0] // 2
    to_right = ring(hold(far[:half]), "tensor", 1)
    to_left = ring(hold(far[half:]), "tensor", -1)
    return to_right, to_left


def ring_second(blocks, got, hold):
    _, left, right, _ = blocks
    half = left.shape[0] // 2
    right = jnp.concatenate([add_wide(right[:half], got[0]), right[half:]], axis=0)
    left = jnp.concatenate([left[:half], add_wide(left[half:], got[1])], axis=0)
    return ring(hold(right), "tensor", 1), ring(hold(left), "tensor", -1)


def ring_total(own, got):
    total = own.astype(jnp.float32) + got[0].astype(jnp.float32) + got[1].astype(jnp.float32)
    return total.astype(jnp.bfloat16)


def normalised(x):
    average = jnp.mean(x, axis=-1, keepdims=True)
    centred = x - average
    variance = jnp.mean(centred * centred, axis=-1, keepdims=True)
    inverse = lax.rsqrt(variance + NORM_EPS)
    return centred * inverse, inverse


def nt_dot(left, right):
    return lax.dot_general(
        left, right, (((1,), (1,)), ((), ())), preferred_element_type=jnp.float32
    )


def tn_dot(left, right):
    return lax.dot_general(
        left, right, (((0,), (0,)), ((), ())), preferred_element_type=jnp.float32
    )


def nn_dot(left, right):
    return jnp.dot(left, right, preferred_element_type=jnp.float32)


def turn(values, cosine, low_sine, high_sine):
    lanes = values.shape[-1]
    return (
        values * cosine
        + pltpu.roll(values, ROT // 2, 1) * low_sine
        + pltpu.roll(values, lanes - ROT // 2, 1) * high_sine
    )


def call(body, name, flops, grid, ins, outs, scratch=(), filled=()):
    count = len(ins)

    def run(*refs):
        body(*refs[:count], *refs[count + len(filled) :])

    return pl.pallas_call(
        run,
        name=name,
        grid=grid,
        in_specs=[pl.BlockSpec(block, index) for _, block, index in ins]
        + [pl.BlockSpec(memory_space=pl.ANY)] * len(filled),
        out_specs=[pl.BlockSpec(block, index) for _, _, block, index in outs],
        out_shape=[jax.ShapeDtypeStruct(shape, kind) for shape, kind, _, _ in outs],
        scratch_shapes=list(scratch),
        input_output_aliases={count + i: i for i in range(len(filled))},
        cost_estimate=pl.CostEstimate(flops=flops, bytes_accessed=1 << 20, transcendentals=0),
        compiler_params=pltpu.CompilerParams(
            vmem_limit_bytes=VMEM_LIMIT, dimension_semantics=("arbitrary",) * len(grid)
        ),
    )(*[array for array, _, _ in ins], *filled)


def whole(array):
    return (array, array.shape, lambda *_: (0,) * array.ndim)


def matrix(pieces, size, block):
    shape = (2, pieces[0].shape[1], size)
    return [(piece, shape, lambda *_: (0, 0, block)) for piece in pieces]


def room(pieces, size):
    return pltpu.VMEM((4 * pieces[0].shape[1], 4 * size), jnp.bfloat16)


def assemble(refs, target):
    _, rows, size = refs[0].shape
    for core in range(2):
        for offset in range(4):
            for side in range(2):
                at = (2 * side + core) * rows
                target[at : at + rows, offset * size : (offset + 1) * size] = refs[
                    core * 4 + offset
                ][side]


def rows_of(array, first=0, block=ROW_BLOCK):
    base = first // block
    return (array, (block, array.shape[1]), lambda i: (i + base, 0))


def qkv_body(x, vecs, shift, cos, low, high, *rest):
    ln_a, ln_m, qkv, w = rest[8:]

    @pl.when(pl.program_id(0) == 0)
    def _():
        assemble(rest[:8], w)

    hat, _ = normalised(x[...].astype(jnp.float32))
    attn = (hat * vecs[0:1, :] + vecs[1:2, :]).astype(jnp.bfloat16)
    ln_a[...] = attn
    ln_m[...] = (hat * vecs[2:3, :] + vecs[3:4, :]).astype(jnp.bfloat16)
    out = nn_dot(attn, w[...]) + shift[...]
    for block in range(qkv.shape[1] // 384):
        for part in range(3):
            at = block * 384 + part * 128
            piece = out[:, at : at + 128]
            if part < 2:
                piece = turn(piece, cos[...], low[...], high[...])
            qkv[:, at : at + 128] = piece.astype(jnp.bfloat16)


def run_qkv(source, vecs, shift, tables, pieces, at, rows, filled):
    x, first = source
    width = x.shape[1]
    length = tables[0].shape[0]
    cols = shift.shape[1]
    bf = jnp.bfloat16
    base = at // ROW_BLOCK
    own = lambda i: (i + base, 0)
    return call(
        qkv_body,
        "norm_qkv",
        rows * 13 * MICROSECOND // 1024,
        (rows // ROW_BLOCK,),
        [rows_of(x, first), whole(vecs), whole(shift)]
        + [rows_of(t, at) for t in tables]
        + matrix(pieces, cols // 4, 0),
        [
            ((length, width), bf, (ROW_BLOCK, width), own),
            ((length, width), bf, (ROW_BLOCK, width), own),
            ((length, cols), bf, (ROW_BLOCK, cols), own),
        ],
        [room(pieces, cols // 4)],
        filled,
    )


def attend_body(q, k, v, ctx, lse):
    length = q.shape[0]
    step = ROW_BLOCK
    for head in range(2):
        lanes = slice(head * 64, head * 64 + 64)
        keys = k[:, lanes]
        vals = v[:, lanes]
        for at in range(0, length, step):
            end = at + step
            queries = q[at:end, lanes] * jnp.bfloat16(0.125)
            scores = nt_dot(queries, keys[:end])
            row = lax.broadcasted_iota(jnp.int32, (step, step), 0)
            col = lax.broadcasted_iota(jnp.int32, (step, step), 1)
            last = jnp.where(col <= row, scores[:, at:], MASK_FILL)
            scores = last if at == 0 else jnp.concatenate([scores[:, :at], last], axis=1)
            top = jnp.max(scores, axis=1, keepdims=True)
            power = jnp.exp(scores - top)
            total = jnp.sum(power, axis=1, keepdims=True)
            mixed = nn_dot(power.astype(jnp.bfloat16), vals[:end]) * (1.0 / total)
            ctx[at:end, lanes] = mixed.astype(jnp.bfloat16)
            level = jnp.broadcast_to(top + jnp.log(total), (step, 128))
            lse[0, head : head + 1, at:end] = level.T[0:1]


def run_attend(qkv):
    length, cols = qkv.shape
    groups = cols // 384
    return call(
        attend_body,
        "attend",
        length * 19 * MICROSECOND // 1024,
        (groups,),
        [
            (qkv, (length, 128), lambda i: (0, 3 * i)),
            (qkv, (length, 128), lambda i: (0, 3 * i + 1)),
            (qkv, (length, 128), lambda i: (0, 3 * i + 2)),
        ],
        [
            ((length, groups * 128), jnp.bfloat16, (length, 128), lambda i: (0, i)),
            ((groups, 8, length), jnp.float32, (1, 8, length), lambda i: (i, 0, 0)),
        ],
    )


ERF_TOP = (
    0.00022905065861350646,
    0.0034082910107109506,
    0.050955695062380861,
    0.18520832239976145,
    1.128379143519084,
)
ERF_BOTTOM = (
    -1.1791602954361697e-7,
    0.000023547966471313185,
    0.0010179625278914885,
    0.014070470171167667,
    0.11098505178285362,
    0.49746925110067538,
    1.0,
)


def erf(x):
    x = jnp.clip(x, -3.7439211627767994, 3.7439211627767994)
    square = x * x
    top = jnp.full_like(x, ERF_TOP[0])
    for term in ERF_TOP[1:]:
        top = top * square + term
    bottom = jnp.full_like(x, ERF_BOTTOM[0])
    for term in ERF_BOTTOM[1:]:
        bottom = bottom * square + term
    return x * top / bottom


def mlp_body(ctx, ln_m, shift, *rest):
    act, slope, part, w_out, w_up, w_down = rest[24:]

    @pl.when(pl.program_id(0) == 0)
    def _():
        assemble(rest[:8], w_out)
        assemble(rest[8:16], w_up)
        assemble(rest[16:24], w_down)

    total = nt_dot(ctx[...], w_out[...])
    values = ln_m[...]
    size = min(COLUMN_STEP, act.shape[1])
    for at in range(0, act.shape[1], size):
        cols = slice(at, at + size)
        up = nn_dot(values, w_up[:, cols]) + shift[:, cols]
        half_erf = 0.5 * erf(up * (2.0**-0.5)) + 0.5
        bell = jnp.exp(up * up * -0.5) * ((2.0 * math.pi) ** -0.5)
        active = (up * half_erf).astype(jnp.bfloat16)
        act[:, cols] = active
        slope[:, cols] = (half_erf + up * bell).astype(jnp.bfloat16)
        total = total + nt_dot(active, w_down[:, cols])
    part[...] = total.astype(jnp.bfloat16)


def run_mlp(ctx, ln_m, shift, narrow, broad, at, rows, filled):
    length, width = ln_m.shape
    cols, heads = shift.shape[1], ctx.shape[1]
    bf = jnp.bfloat16
    base = at // ROW_BLOCK
    own = lambda i: (i + base, 0)
    return call(
        mlp_body,
        "mlp_out",
        rows * 32 * MICROSECOND // 1024,
        (rows // ROW_BLOCK,),
        [rows_of(ctx, at), rows_of(ln_m, at), whole(shift)]
        + matrix(narrow, heads // 4, 3)
        + matrix(broad, cols // 4, 0)
        + matrix(broad, cols // 4, 1),
        [
            ((length, cols), bf, (ROW_BLOCK, cols), own),
            ((length, cols), bf, (ROW_BLOCK, cols), own),
            ((rows, width), bf, (ROW_BLOCK, width), lambda i: (i, 0)),
        ],
        [room(narrow, heads // 4), room(broad, cols // 4), room(broad, cols // 4)],
        filled,
    )


def mlp_back_body(g, slope, *rest):
    d_up, d_ctx, sum_up, sum_g, w_out, w_down = rest[16:]

    @pl.when(pl.program_id(0) == 0)
    def _():
        assemble(rest[:8], w_out)
        assemble(rest[8:16], w_down)
        sum_up[...] = jnp.zeros_like(sum_up)
        sum_g[...] = jnp.zeros_like(sum_g)

    grad = g[...]
    size = min(COLUMN_STEP, d_up.shape[1])
    for at in range(0, d_up.shape[1], size):
        cols = slice(at, at + size)
        du = nn_dot(grad, w_down[:, cols]) * slope[:, cols].astype(jnp.float32)
        du = du.astype(jnp.bfloat16)
        d_up[:, cols] = du
        sum_up[:, cols] += jnp.sum(du.astype(jnp.float32), axis=0, keepdims=True)
    d_ctx[...] = nn_dot(grad, w_out[...]).astype(jnp.bfloat16)
    sum_g[...] += jnp.sum(grad.astype(jnp.float32), axis=0, keepdims=True)


def run_mlp_back(source, slope, narrow, broad, at, rows, heads, filled):
    g, first = source
    width = g.shape[1]
    length, cols = slope.shape
    bf = jnp.bfloat16
    base = at // ROW_BLOCK
    own = lambda i: (i + base, 0)
    fixed = lambda i: (0, 0)
    return call(
        mlp_back_body,
        "mlp_back",
        rows * 15 * MICROSECOND // 1024,
        (rows // ROW_BLOCK,),
        [rows_of(g, first), rows_of(slope, at)]
        + matrix(narrow, heads // 4, 3)
        + matrix(broad, cols // 4, 1),
        [
            ((length, cols), bf, (ROW_BLOCK, cols), own),
            ((length, heads), bf, (ROW_BLOCK, heads), own),
            ((1, cols), jnp.float32, (1, cols), fixed),
            ((1, width), jnp.float32, (1, width), fixed),
        ],
        [room(narrow, heads // 4), room(broad, cols // 4)],
        filled,
    )


def attend_back_body(q, k, v, d_ctx, lse, cos, low, high, d_qkv, sums, dk_sum, dv_sum, dq_all):
    length = q.shape[0]
    step = ROW_BLOCK
    for head in range(2):
        lanes = slice(head * 64, head * 64 + 64)
        keys = k[:, lanes]
        vals = v[:, lanes]
        dk_sum[:, lanes] = jnp.zeros((length, 64), jnp.float32)
        dv_sum[:, lanes] = jnp.zeros((length, 64), jnp.float32)
        for at in range(0, length, step):
            end = at + step
            queries = q[at:end, lanes] * jnp.bfloat16(0.125)
            grads = d_ctx[at:end, lanes]
            scores = nt_dot(keys[:end], queries)
            power = jnp.exp(scores - lse[0, head : head + 1, at:end])
            key = lax.broadcasted_iota(jnp.int32, (step, step), 0)
            row = lax.broadcasted_iota(jnp.int32, (step, step), 1)
            last = jnp.where(key <= row, power[at:], 0.0)
            probs = last if at == 0 else jnp.concatenate([power[:at], last], axis=0)
            d_probs = nt_dot(vals[:end], grads)
            delta = jnp.sum(probs * d_probs, axis=0, keepdims=True)
            d_scores = (probs * (d_probs - delta)).astype(jnp.bfloat16)
            dv_sum[:end, lanes] += nn_dot(probs.astype(jnp.bfloat16), grads)
            dk_sum[:end, lanes] += nn_dot(d_scores, queries)
            dq_all[at:end, lanes] = tn_dot(d_scores, keys[:end]) * 0.125
    dq = turn(dq_all[...], cos[...], -low[...], -high[...]).astype(jnp.bfloat16)
    dk = turn(dk_sum[...], cos[...], -low[...], -high[...]).astype(jnp.bfloat16)
    dv = dv_sum[...].astype(jnp.bfloat16)
    for part, piece in enumerate((dq, dk, dv)):
        at = part * 128
        d_qkv[:, at : at + 128] = piece
        sums[:, at : at + 128] = jnp.sum(piece.astype(jnp.float32), axis=0, keepdims=True)


def run_attend_back(qkv, d_ctx, lse, tables):
    length, cols = qkv.shape
    groups = cols // 384
    wide = pltpu.VMEM((length, 128), jnp.float32)
    return call(
        attend_back_body,
        "attend_back",
        length * 26 * MICROSECOND // 1024,
        (groups,),
        [
            (qkv, (length, 128), lambda i: (0, 3 * i)),
            (qkv, (length, 128), lambda i: (0, 3 * i + 1)),
            (qkv, (length, 128), lambda i: (0, 3 * i + 2)),
            (d_ctx, (length, 128), lambda i: (0, i)),
            (lse, (1, 8, length), lambda i: (i, 0, 0)),
        ]
        + [whole(t) for t in tables],
        [
            ((length, cols), jnp.bfloat16, (length, 384), lambda i: (0, i)),
            ((1, cols), jnp.float32, (1, 384), lambda i: (0, i)),
        ],
        [wide, wide, wide],
    )


def norm_back_body(x, d_qkv, d_up, vecs, *rest):
    part, sums, w_qkv, w_up = rest[16:]

    @pl.when(pl.program_id(0) == 0)
    def _():
        assemble(rest[:8], w_qkv)
        assemble(rest[8:16], w_up)
        sums[...] = jnp.zeros_like(sums)

    hat, inverse = normalised(x[...].astype(jnp.float32))
    d_attn = nt_dot(d_qkv[...], w_qkv[...])
    d_mlp = nt_dot(d_up[...], w_up[...])
    for row, term in enumerate((d_attn * hat, d_mlp * hat, d_attn, d_mlp)):
        sums[row : row + 1, :] += jnp.sum(term, axis=0, keepdims=True)
    d_hat = d_attn * vecs[0:1, :] + d_mlp * vecs[2:3, :]
    along = jnp.mean(d_hat * hat, axis=-1, keepdims=True)
    level = jnp.mean(d_hat, axis=-1, keepdims=True)
    part[...] = (inverse * (d_hat - level - hat * along)).astype(jnp.bfloat16)


def run_norm_back(source, d_qkv, d_up, vecs, narrow, broad, at, rows):
    x, first = source
    width = x.shape[1]
    n_qkv, n_up = d_qkv.shape[1] // 4, d_up.shape[1] // 4
    return call(
        norm_back_body,
        "norm_back",
        rows * 21 * MICROSECOND // 1024,
        (rows // ROW_BLOCK,),
        [rows_of(x, first), rows_of(d_qkv, at), rows_of(d_up, at), whole(vecs)]
        + matrix(narrow, n_qkv, 0)
        + matrix(broad, n_up, 0),
        [
            ((rows, width), jnp.bfloat16, (ROW_BLOCK, width), lambda i: (i, 0)),
            ((8, width), jnp.float32, (8, width), lambda i: (0, 0)),
        ],
        [room(narrow, n_qkv), room(broad, n_up)],
    )


def weight_grad_body(cuts, *refs):
    a_refs, b_refs, rest = refs[: sum(cuts)], refs[sum(cuts) :], refs[sum(cuts) + 2 :]
    keep, send, turned_one, turned_two = rest
    groups = (a_refs[: cuts[0]], a_refs[cuts[0] :])

    @pl.when(pl.program_id(0) == 0)
    def _():
        for group, turned in zip(groups, (turned_one, turned_two)):
            at = 0
            for ref in group:
                turned[:, at : at + ref.shape[0]] = ref[...].T
                at += ref.shape[0]

    at = 0
    rows = keep.shape[2]
    for turned, right in zip((turned_one, turned_two), b_refs[:2]):
        size = right.shape[1]
        grad = nn_dot(turned[...], right[...]).astype(jnp.bfloat16)
        for side in range(2):
            first = 2 * side * rows
            keep[side, 0, :, at : at + size] = grad[first : first + rows]
            send[side, 0, :, at : at + size] = grad[first + rows : first + 2 * rows]
        at += size


def run_weight_grad(lefts, rights):
    length, width = rights[0].shape[0], lefts[0][0].shape[1]
    sizes = [right.shape[1] // 4 for right in rights]
    shape = (2, 4, width // 4, sum(sizes))
    out = (shape, jnp.bfloat16, (2, 1) + shape[2:], lambda i: (0, i, 0, 0))
    turned = pltpu.VMEM((width, length), jnp.bfloat16)
    return call(
        partial(weight_grad_body, tuple(len(group) for group in lefts)),
        "weight_grad",
        length * 14 * MICROSECOND // 1024,
        (4,),
        [whole(left) for group in lefts for left in group]
        + [(r, (length, n), lambda i: (0, i)) for r, n in zip(rights, sizes)],
        [out, out],
        [turned, turned],
    )


def turn_tables(length):
    cosine, sine_tab = rotary_tables(length)
    zero = jnp.zeros_like(sine_tab)
    rest = jnp.zeros((length, 64 - ROT), jnp.float32)
    cos = jnp.concatenate([cosine, cosine, rest + 1.0], axis=1)
    low = jnp.concatenate([zero, sine_tab, rest], axis=1)
    high = jnp.concatenate([-sine_tab, zero, rest], axis=1)
    return tuple(jnp.concatenate([t, t], axis=1) for t in (cos, low, high))


def by_sequence(
    acts_in, cotangent, norm_gains, vec_bias, w_qkv, b_qkv, w_out, w_up, b_up, w_down
):
    section = lax.axis_index("section").astype(jnp.uint32)
    across = lax.axis_index("dp").astype(jnp.uint32)
    along = lax.axis_index("tensor").astype(jnp.uint32)
    first_section = section == 0
    width = acts_in.shape[3]
    rows = w_qkv.shape[1]
    positions = acts_in.shape[1]
    length = 4 * positions
    heads = b_qkv.shape[1]
    bf = jnp.bfloat16

    qkv_halves = (
        w_qkv[0].reshape(rows, 2, 2, 3, 64).transpose(1, 0, 3, 2, 4).reshape(2, rows, -1)
    )
    out_halves = w_out[0].T.reshape(rows, 2, -1).transpose(1, 0, 2)
    up_halves = w_up[0].reshape(rows, 2, -1).transpose(1, 0, 2)
    down_halves = w_down[0].T.reshape(rows, 2, -1).transpose(1, 0, 2)
    n_qkv, n_out, n_up = qkv_halves.shape[2], out_halves.shape[2], up_halves.shape[2]

    narrow = jnp.stack([jnp.concatenate([qkv_halves[h], out_halves[h]], axis=1) for h in (0, 1)])
    broad = jnp.stack([jnp.concatenate([up_halves[h], down_halves[h]], axis=1) for h in (0, 1)])
    small = jnp.concatenate(
        [
            norm_gains[0].reshape(-1),
            vec_bias[0].reshape(-1),
            b_qkv[0].reshape(-1).astype(jnp.float32),
            b_up[0].reshape(-1).astype(jnp.float32),
        ]
    )
    clock = Clock()
    hold, tick = clock.hold, clock.tick

    def pass_half(halves):
        return swap(hold(pick(halves, 1 - section)), "section", 1)

    def by_layer(halves, got):
        keep = pick(halves, section)
        return jnp.where(first_section, keep, got), jnp.where(first_section, got, keep)

    def x_swap(value):
        return swap(hold(value), "dp", 2)

    def core_swap(value):
        return swap(hold(value), "dp", 1)

    def y_swap(value):
        return swap(hold(value), "section", 1)

    def both_ways(value):
        value = hold(value)
        return ring(value, "tensor", 1), ring(value, "tensor", -1)

    def far_halves(left, right):
        half = left.shape[0] // 2
        return ring(hold(left[:half]), "tensor", 1), ring(hold(right[half:]), "tensor", -1)

    def own_half(blocks):
        return lax.dynamic_slice_in_dim(blocks, section * (width // 2), width // 2, 2)

    def both_halves(own, got):
        own = own.reshape(length, width // 2)
        got = got.reshape(length, width // 2)
        low = jnp.where(first_section, own, got)
        high = jnp.where(first_section, got, own)
        return relative(jnp.concatenate([low, high], axis=1), across)

    def stacked(own, got):
        return jnp.stack([own, got])

    got_narrow = pass_half(narrow)
    got_small = swap(small, "section", 1)
    blocks = own_half(acts_in[:, :, 0, :])
    near = exchange_near(blocks, along, hold)
    tick(got_narrow, got_small, near)
    narrow_shards = by_layer(narrow, got_narrow)
    small = jnp.where(first_section, jnp.stack([small, got_small]), jnp.stack([got_small, small]))
    left, right = both_ways(narrow_shards[0])
    far = exchange_far(near, hold)
    got_broad = pass_half(broad)
    got_own = x_swap(narrow_shards[0])
    small = jnp.stack([small, core_swap(small)])
    small = jnp.concatenate([small, swap(small, "dp", 2)])
    tick(left, right, far, got_broad, got_own, small)
    own_acts = exchanged(blocks, near, far, along)
    got_acts = y_swap(own_acts)
    narrow_far = far_halves(left, right)
    got_left, got_right = x_swap(left), x_swap(right)
    small = jnp.stack([small, swap(hold(small), "tensor", 1)])
    small = jnp.concatenate([small, swap(small, "tensor", 2)])
    tick(narrow_far, got_left, got_right, small)
    broad_shards = by_layer(broad, got_broad)
    broad_left, broad_right = both_ways(broad_shards[0])
    narrow_far = jnp.concatenate(narrow_far, axis=0)
    got_far = x_swap(narrow_far)
    pieces = [
        stacked(narrow_shards[0], got_own),
        stacked(left, got_left),
        stacked(right, got_right),
    ]
    others = [core_swap(piece) for piece in pieces]
    tick(got_far, others, got_acts)
    acts = both_halves(own_acts, got_acts)
    pieces.append(stacked(narrow_far, got_far))
    others.append(core_swap(pieces[3]))
    got_own = x_swap(broad_shards[0])
    narrow_zero = (*pieces, *others)
    tick(others[3])

    share = norm_gains.shape[2]
    vec_part = small[..., : 6 * share].reshape(4, 4, 2, 6, share)
    offsets = jnp.array(FAR_ORDER, jnp.int32)
    order = jnp.stack([pick(offsets, (k - along) & 3) for k in range(4)])
    slots = [jnp.bitwise_xor((along + k) & 3, along) for k in (0, 3, 1, 2)]
    vec_part = jnp.stack([pick(vec_part, jnp.bitwise_xor(along, k)) for k in range(4)])
    vecs_full = vec_part.transpose(2, 3, 1, 0, 4).reshape(2, 6, width)
    at = 6 * share
    share_q = b_qkv.shape[2]
    dp_order = [jnp.bitwise_xor(across, k) for k in range(4)]
    qkv_bias = small[..., at : at + heads * share_q].reshape(4, 4, 2, heads, share_q)
    qkv_bias = jnp.stack([pick(qkv_bias, k) for k in slots])
    qkv_bias = jnp.stack([pick(qkv_bias, i, 1) for i in dp_order], axis=1)
    qkv_bias = qkv_bias.transpose(2, 0, 3, 1, 4).reshape(2, 4, 2, heads // 2, 3, 64)
    qkv_bias = pick(qkv_bias, section, 2).transpose(0, 1, 3, 2, 4).reshape(2, 1, -1)
    at += heads * share_q
    bias_rows, share_u = b_up.shape[1], b_up.shape[2]
    up_bias = small[..., at : at + bias_rows * share_u].reshape(4, 4, 2, bias_rows, share_u)
    up_bias = jnp.stack([pick(up_bias, k) for k in slots])
    up_bias = jnp.stack([pick(up_bias, i, 1) for i in dp_order], axis=1)
    up_bias = up_bias.transpose(2, 0, 3, 1, 4).reshape(2, 4, 2, bias_rows // 2, 4 * share_u)
    up_bias = pick(up_bias, section, 2).reshape(2, 1, -1)
    zero_rows = jnp.zeros((4, width), jnp.float32)

    tables = turn_tables(length)
    chunk = length // CHUNKS
    starts = [i * chunk for i in range(CHUNKS)]

    all_vecs = [
        jnp.concatenate([v[0:1], v[2:3], v[1:2], v[3:4], zero_rows], axis=0) for v in vecs_full
    ]

    def project(layer, i, source, pieces, filled):
        return run_qkv(
            source, all_vecs[layer], qkv_bias[layer], tables, pieces, starts[i], chunk, filled
        )

    def feed(layer, i, ctx, ln_m, narrow, broad, filled):
        *filled, part = run_mlp(
            hold(ctx), ln_m, up_bias[layer], narrow, broad, starts[i], chunk, filled
        )
        return filled, part

    def join(layer, before, part, got):
        total = part.astype(jnp.float32) + got.astype(jnp.float32)
        full = vecs_full[layer]
        return (before.astype(jnp.float32) + total + (full[4] + full[5])).astype(bf)

    acts = hold(acts)
    first = project(0, 0, (acts, 0), narrow_zero, ())
    tick(first, broad_left, broad_right)
    got_left = x_swap(broad_left)
    first = project(0, 1, (acts, chunk), narrow_zero, first)
    tick(first, got_own)
    ln_a0, ln_m0, qkv0 = first
    broad_far = far_halves(broad_left, broad_right)
    got_right = x_swap(broad_right)
    ctx0, lse0 = run_attend(hold(qkv0))
    tick(ctx0, broad_far, got_left, got_right)
    broad_far = jnp.concatenate(broad_far, axis=0)
    got_far = x_swap(broad_far)
    pieces = [
        stacked(broad_shards[0], got_own),
        stacked(broad_left, got_left),
        stacked(broad_right, got_right),
    ]
    others = [core_swap(piece) for piece in pieces]
    tick(got_far, others)
    pieces.append(stacked(broad_far, got_far))
    others.append(core_swap(pieces[3]))
    broad_zero = (*pieces, *others)
    tick(others[3])
    first, part_a = feed(0, 0, ctx0, ln_m0, narrow_zero, broad_zero, ())
    left, right = both_ways(narrow_shards[1])
    got_own = x_swap(narrow_shards[1])
    broad_own = x_swap(broad_shards[1])
    tick(part_a, left, right, got_own, broad_own)
    first, part_b = feed(0, 1, ctx0, ln_m0, narrow_zero, broad_zero, first)
    act0, slope0 = first
    got_a = y_swap(part_a)
    narrow_far = far_halves(left, right)
    broad_left, broad_right = both_ways(broad_shards[1])
    tick(part_b, got_a, narrow_far, broad_left, broad_right)
    got_b = y_swap(part_b)
    got_left, got_right = x_swap(left), x_swap(right)
    x1_a = join(0, acts[:chunk], part_a, got_a)
    tick(got_left, got_right)
    narrow_far = jnp.concatenate(narrow_far, axis=0)
    got_far = x_swap(narrow_far)
    pieces = [
        stacked(narrow_shards[1], got_own),
        stacked(left, got_left),
        stacked(right, got_right),
    ]
    others = [core_swap(piece) for piece in pieces]
    tick(got_b, got_far, others)
    x1_b = join(0, acts[chunk:], part_b, got_b)
    pieces.append(stacked(narrow_far, got_far))
    others.append(core_swap(pieces[3]))
    narrow_one = (*pieces, *others)
    tick(others[3], x1_a, x1_b)

    broad_far = far_halves(broad_left, broad_right)
    got_left = x_swap(broad_left)
    first = project(1, 0, (hold(x1_a), 0), narrow_one, ())
    first = project(1, 1, (x1_b, 0), narrow_one, first)
    ln_a1, ln_m1, qkv1 = first
    pieces = [stacked(broad_shards[1], broad_own)]
    others = [core_swap(pieces[0])]
    tick(first, broad_far, got_left, others)
    broad_far = jnp.concatenate(broad_far, axis=0)
    got_right, got_far = x_swap(broad_right), x_swap(broad_far)
    pieces.append(stacked(broad_left, got_left))
    others.append(core_swap(pieces[1]))
    ctx1, lse1 = run_attend(hold(qkv1))
    blocks = own_half(cotangent[:, :, 0, :])
    near = exchange_near(blocks, along, hold)
    tick(ctx1, got_right, got_far, others, near)
    far = exchange_far(near, hold)
    pieces += [stacked(broad_right, got_right), stacked(broad_far, got_far)]
    others += [core_swap(piece) for piece in pieces[2:]]
    broad_one = (*pieces, *others)
    tick(others[2:], far)
    own_grads = exchanged(blocks, near, far, along)
    got_grads = y_swap(own_grads)
    first, part_a = feed(1, 0, ctx1, ln_m1, narrow_one, broad_one, ())
    tick(part_a, got_grads)
    got_a = y_swap(part_a)
    first, part_b = feed(1, 1, ctx1, ln_m1, narrow_one, broad_one, first)
    act1, slope1 = first
    tick(part_b, got_a)

    grads = hold(both_halves(own_grads, got_grads))
    n_heads = ctx0.shape[1]

    def back(i, source, slope, narrow, broad, filled):
        *filled, up_term, g_term = run_mlp_back(
            source, slope, narrow, broad, starts[i], chunk, n_heads, filled
        )
        return filled, up_term, g_term

    first, up_a, g_a = back(0, (grads, 0), slope1, narrow_one, broad_one, ())
    first, up_b, g_b = back(1, (grads, chunk), slope1, narrow_one, broad_one, first)
    d_up1, d_ctx1 = first
    sums_one = [None, g_a + g_b, None, up_a + up_b]
    tick(first, got_a)
    x1 = jnp.concatenate([x1_a, x1_b], axis=0)

    def to_blocks(values):
        return relative(values, across).reshape(4, positions, width)

    d_qkv1, sums_one[2] = run_attend_back(qkv1, hold(d_ctx1), lse1, tables)
    got_b = y_swap(part_b)
    tick(d_qkv1, got_b)
    x2 = jnp.concatenate(
        [join(1, x1_a, part_a, got_a), join(1, x1_b, hold(part_b), got_b)], axis=0
    )
    out_blocks = to_blocks(jnp.where(first_section, x1, x2))
    part_a, sum_a = run_norm_back(
        (x1_a, 0), hold(d_qkv1), d_up1, all_vecs[1], narrow_one, broad_one, 0, chunk
    )
    tick(part_a, out_blocks)
    got_a = y_swap(part_a)
    out_parts = out_blocks[..., : width // 2], out_blocks[..., width // 2 :]
    out_near = [exchange_near(out_parts[0], along, hold)]
    part_b, sum_b = run_norm_back(
        (x1_b, 0), hold(d_qkv1), d_up1, all_vecs[1], narrow_one, broad_one, chunk, chunk
    )
    sums_one[0] = (sum_a + sum_b)[:4]
    keep_broad, send = run_weight_grad([[hold(ln_m1)], [grads]], [d_up1, act1])
    tick(part_b, keep_broad, got_a, out_near)
    got_b = y_swap(part_b)
    got_core = core_swap(send)
    out_near.append(exchange_near(out_parts[1], along, hold))
    keep_narrow, send_narrow = run_weight_grad([[hold(ln_a1)], [grads]], [d_qkv1, ctx1])
    tick(keep_narrow, got_b, got_core, out_near)

    def lower(above, part, got):
        total = part.astype(jnp.float32) + got.astype(jnp.float32)
        return (above.astype(jnp.float32) + total).astype(bf)

    g1_a = lower(grads[:chunk], hold(part_a), got_a)
    g1_b = lower(grads[chunk:], hold(part_b), got_b)
    keep_one, core_one = hold(keep_broad), got_core
    got_core = core_swap(send_narrow)
    got_x = [x_swap(add_wide(keep_one[1, 2:], core_one[1, 2:]))]
    first, up_a, g_a = back(0, (hold(g1_a), 0), slope0, narrow_zero, broad_zero, ())
    first, up_b, g_b = back(1, (g1_b, 0), slope0, narrow_zero, broad_zero, first)
    d_up0, d_ctx0 = first
    sums_zero = [None, g_a + g_b, None, up_a + up_b]
    out_far = [exchange_far(near, hold) for near in out_near]
    tick(first, got_core, got_x, out_far)
    core_narrow = got_core
    got_x.append(x_swap(add_wide(hold(keep_one[1, :2]), core_one[1, :2])))
    keep_broad, send = run_weight_grad([[hold(ln_m0)], [g1_a, g1_b]], [d_up0, act0])
    tick(keep_broad, got_x)

    def late_blocks(keep, core, got):
        late = add_three(hold(keep[0, 2:]), core[0, 2:], got)
        return [late[0], late[1]]

    def early_blocks(keep, core, got):
        early = add_three(hold(keep[0, :2]), core[0, :2], got)
        return [early[0], early[1]]

    got_core = core_swap(send)
    late = late_blocks(keep_one, core_one, got_x[0])
    broad_got = ring_first([None, None, *late], hold)
    got_narrow = x_swap(add_wide(hold(keep_narrow[1]), core_narrow[1]))
    d_qkv0, sums_zero[2] = run_attend_back(qkv0, hold(d_ctx0), lse0, tables)
    tick(d_qkv0, broad_got, got_core, got_narrow)
    broad_one_sum = early_blocks(keep_one, core_one, got_x[1]) + late
    narrow_sum = add_three(hold(keep_narrow[0]), core_narrow[0], got_narrow)
    narrow_sum = [narrow_sum[k] for k in range(4)]
    keep_zero, core_zero = hold(keep_broad), got_core
    got_x = [x_swap(add_wide(keep_zero[1, 2:], core_zero[1, 2:]))]
    broad_got = ring_second(broad_one_sum, broad_got, hold)
    part_a, sum_a = run_norm_back(
        (acts, 0), hold(d_qkv0), d_up0, all_vecs[0], narrow_zero, broad_zero, 0, chunk
    )
    tick(part_a)
    got_a = y_swap(part_a)
    part_b, sum_b = run_norm_back(
        (acts, chunk), hold(d_qkv0), d_up0, all_vecs[0], narrow_zero, broad_zero, chunk, chunk
    )
    sums_zero[0] = (sum_a + sum_b)[:4]
    tick(part_b, got_x, broad_got)
    got_b = y_swap(part_b)
    got_x.append(x_swap(add_wide(hold(keep_zero[1, :2]), core_zero[1, :2])))
    narrow_got = ring_first(narrow_sum, hold)
    keep_narrow, send_narrow = run_weight_grad([[hold(ln_a0)], [g1_a, g1_b]], [d_qkv0, ctx0])
    tick(keep_narrow, got_a, got_b, got_x, narrow_got)

    flat = []
    for norm_sums, sum_g, sum_qkv, sum_up in hold((sums_zero, sums_one)):
        feature = relative(jnp.concatenate([norm_sums, sum_g], axis=0), across)
        q_sum = sum_qkv.reshape(4, 3, 2, 64).transpose(0, 2, 1, 3).reshape(4, -1)
        both = jnp.concatenate([q_sum, sum_up.reshape(4, -1)], axis=1)
        both = jnp.stack([pick(both, order[k]) for k in range(4)])
        flat.append(jnp.concatenate([feature.reshape(-1), both.reshape(-1)]))
    flat = jnp.stack(flat)
    got_core = core_swap(send_narrow)
    late = late_blocks(keep_zero, core_zero, got_x[0])
    broad_next = ring_first([None, None, *late], hold)
    grads_low = jnp.concatenate(
        [lower(g1_a, hold(part_a), got_a), lower(g1_b, hold(part_b), got_b)], axis=0
    )
    g1 = jnp.concatenate([g1_a, g1_b], axis=0)
    grad_blocks = to_blocks(jnp.where(first_section, grads_low, g1))
    flat = flat + swap(flat, "dp", 1)
    tick(broad_next, got_core, grad_blocks, flat)
    broad_zero_sum = early_blocks(keep_zero, core_zero, got_x[1]) + late
    broad_next = ring_second(broad_zero_sum, broad_next, hold)
    narrow_got = ring_second(narrow_sum, narrow_got, hold)
    got_narrow = x_swap(add_wide(hold(keep_narrow[1]), got_core[1]))
    flat = flat + x_swap(flat)
    acts_local = [
        exchanged(part, near, far, along)
        for part, near, far in zip(hold(out_parts), out_near, out_far)
    ]
    acts_local = jnp.concatenate(acts_local, axis=-1)
    tick(broad_next, got_narrow, flat, narrow_got, acts_local)
    zero_sum = add_three(hold(keep_narrow[0]), got_core[0], got_narrow)
    zero_sum = [zero_sum[k] for k in range(4)]
    narrow_next = ring_first(zero_sum, hold)
    flat = flat + swap(hold(flat), "tensor", 1)
    tick(narrow_next, flat)
    grad_near = exchange_near(grad_blocks, along, hold)
    narrow_next = ring_second(zero_sum, narrow_next, hold)
    one_broad = ring_total(hold(broad_one_sum[0]), broad_got)
    one_narrow = ring_total(hold(narrow_sum[0]), narrow_got)
    zero_broad = ring_total(hold(broad_zero_sum[0]), broad_next)
    broad_send = y_swap(jnp.where(first_section, one_broad, zero_broad))
    tick(narrow_next, grad_near, broad_send)
    grad_far = exchange_far(grad_near, hold)
    zero_narrow = ring_total(zero_sum[0], narrow_next)
    narrow_send = y_swap(jnp.where(first_section, one_narrow, zero_narrow))
    flat = flat + swap(hold(flat), "tensor", 2)
    grad_local = exchanged(grad_blocks, grad_near, grad_far, along)

    def whole_layer(keep_pair, got):
        keep = jnp.where(first_section, *keep_pair).astype(jnp.float32)
        got = got.astype(jnp.float32)
        return jnp.where(first_section, jnp.stack([keep, got], 1), jnp.stack([got, keep], 1))

    narrow_out = whole_layer((zero_narrow, one_narrow), narrow_send)
    broad_out = whole_layer((zero_broad, one_broad), broad_send)
    grad_qkv = narrow_out[..., :n_qkv].reshape(rows, 2, 3, 2, 64)
    grad_qkv = grad_qkv.transpose(0, 1, 3, 2, 4).reshape(rows, -1)
    grad_out = narrow_out[..., n_qkv:].reshape(rows, -1).T
    grad_up = broad_out[..., :n_up].reshape(rows, -1)
    grad_down = broad_out[..., n_up:].reshape(rows, -1).T

    keep = pick(flat, section)
    mine = pick(flat, 1 - section)
    got = swap(mine, "section", 1)
    n_feature = 5 * width
    feature_own = keep[:n_feature].reshape(5, width)
    feature = feature_own[:4] + got[: 4 * width].reshape(4, width)
    place_at = (across * 4 + along) * share
    gain_share = lax.dynamic_slice_in_dim(feature[:2], place_at, share, 1)
    shifts = jnp.concatenate([feature[2:4], feature_own[4:5], feature_own[4:5]], axis=0)
    bias_share = lax.dynamic_slice_in_dim(shifts, place_at, share, 1)
    low_half = jnp.where(first_section, keep, got)[n_feature:].reshape(4, -1)
    high_half = jnp.where(first_section, got, keep)[n_feature:].reshape(4, -1)
    halves = jnp.stack([pick(low_half, along), pick(high_half, along)])
    n_head = (heads // 2) * 192
    head_sums = halves[:, :n_head].reshape(heads, 192)
    head_share = lax.dynamic_slice_in_dim(head_sums, across * share_q, share_q, 1)
    unit_sums = halves[:, n_head:].reshape(bias_rows, 4 * share_u)
    unit_share = lax.dynamic_slice_in_dim(unit_sums, across * share_u, share_u, 1)
    return (
        acts_local[None, :, :, None],
        grad_local[None, :, :, None],
        gain_share[None],
        bias_share[None],
        grad_qkv[None],
        head_share[None],
        grad_out[None],
        grad_up[None],
        unit_share[None],
        grad_down[None],
    )


def fits(mesh, args):
    acts_in, b_qkv = args[0], args[5]
    sizes = dict(mesh.shape)
    return (
        sizes["section"] == 2
        and sizes["dp"] == 4
        and sizes["tensor"] == MICRO
        and MICRO == 4
        and acts_in.shape[2] == sizes["dp"]
        and b_qkv.shape[1] == 16
        and b_qkv.shape[2] == 192
        and acts_in.shape[1] % (CHUNKS * ROW_BLOCK) == 0
    )


def solution(mesh):
    placed = (
        P(None, "tensor", "dp", None),
        P(None, "tensor", "dp", None),
        P("section", None, ("dp", "tensor")),
        P("section", None, ("dp", "tensor")),
        P("section", "dp", "tensor"),
        P("section", "tensor", "dp"),
        P("section", "tensor", "dp"),
        P("section", "dp", "tensor"),
        P("section", "tensor", "dp"),
        P("section", "tensor", "dp"),
    )
    def wrap(body):
        return jax.shard_map(
            body,
            mesh=mesh,
            in_specs=placed,
            out_specs=(
                P("section", None, "tensor", "dp", None),
                P("section", None, "tensor", "dp", None),
                P("section", None, ("dp", "tensor")),
                P("section", None, ("dp", "tensor")),
                P("section", "dp", "tensor"),
                P("section", "tensor", "dp"),
                P("section", "tensor", "dp"),
                P("section", "dp", "tensor"),
                P("section", "tensor", "dp"),
                P("section", "tensor", "dp"),
            ),
            check_vma=False,
        )

    return lambda *args: wrap(by_sequence if fits(mesh, args) else local)(*args)
```

```python
from functools import partial
import math

import jax
import jax.numpy as jnp
from jax import lax
from jax.experimental import pallas as pl
from jax.experimental.pallas import tpu as pltpu
from jax.sharding import PartitionSpec as P

ROT = 16
QBLOCK = 512
MICRO = 4


NORM_EPS = 1e-05
ROPE_BASE = 10000.0
MASK_FILL = -1e30


def from_behind(value, axis, by):
    length = lax.axis_size(axis)
    pairs = [(i, i + by) for i in range(length) if 0 <= i + by < length]
    return lax.ppermute(value, axis, pairs)


def layer_norm(values, norm_gain, norm_shift):
    average = jnp.mean(values, axis=-1, keepdims=True)
    centred = values - average
    variance = jnp.mean(centred * centred, axis=-1, keepdims=True)
    return centred * lax.rsqrt(variance + NORM_EPS) * norm_gain + norm_shift


def both_norms(values, gain_attn, shift_attn, gain_mlp, shift_mlp):
    return (layer_norm(values, gain_attn, shift_attn), layer_norm(values, gain_mlp, shift_mlp))


def rotary_tables(length):
    half_rot = ROT // 2
    frequency = jnp.exp(
        jnp.arange(half_rot, dtype=jnp.float32) * (-2.0 * math.log(ROPE_BASE) / ROT)
    )
    angles = jnp.arange(length, dtype=jnp.float32)[:, None] * frequency[None, :]
    return (jnp.cos(angles), jnp.sin(angles))


def rotate(values, cosine, sine_tab):
    half_rot = ROT // 2
    low_half = values[..., :half_rot]
    high_half = values[..., half_rot:ROT]
    return jnp.concatenate(
        [
            low_half * cosine - high_half * sine_tab,
            high_half * cosine + low_half * sine_tab,
            values[..., ROT:],
        ],
        axis=-1,
    )


def rotate_back(grads_rot, cosine, sine_tab):
    half_rot = ROT // 2
    low_half = grads_rot[..., :half_rot]
    high_half = grads_rot[..., half_rot:ROT]
    return jnp.concatenate(
        [
            low_half * cosine + high_half * sine_tab,
            high_half * cosine - low_half * sine_tab,
            grads_rot[..., ROT:],
        ],
        axis=-1,
    )


def causal_scores(queries, key_rows, first_row, score_scale):
    block_rows = queries.shape[0]
    last_row = key_rows.shape[0]
    scores = (
        jnp.einsum("qshd,kshd->shqk", queries, key_rows, preferred_element_type=jnp.float32)
        * score_scale
    )
    row_pos = first_row + jnp.arange(block_rows, dtype=jnp.int32)
    col_pos = jnp.arange(last_row, dtype=jnp.int32)
    allowed = col_pos[None, :] <= row_pos[:, None]
    return (scores, allowed)


def attend(queries, key_rows, val_rows):
    length = queries.shape[0]
    block_rows = min(QBLOCK, length)
    score_scale = queries.shape[-1] ** (-0.5)
    outputs = []
    totals = []
    for block_index in range(length // block_rows):
        first_row = block_index * block_rows
        last_row = first_row + block_rows
        scores, allowed = causal_scores(
            queries[first_row:last_row], key_rows[:last_row], first_row, score_scale
        )
        scores = jnp.where(allowed, scores, MASK_FILL)
        highest = jnp.max(scores, axis=-1, keepdims=True)
        exponent = jnp.exp(scores - highest)
        denominator = jnp.sum(exponent, axis=-1, keepdims=True)
        probability = (exponent / denominator).astype(jnp.bfloat16)
        block_out = jnp.einsum(
            "shqk,kshd->qshd", probability, val_rows[:last_row], preferred_element_type=jnp.float32
        )
        outputs.append(block_out.astype(jnp.bfloat16))
        totals.append((highest + jnp.log(denominator))[..., 0])
    context = jnp.concatenate(outputs, axis=0)
    return (context.reshape(length, context.shape[1], -1), jnp.concatenate(totals, axis=-1))


def attend_back(queries, key_rows, val_rows, d_context, log_total):
    length = queries.shape[0]
    block_rows = min(QBLOCK, length)
    score_scale = queries.shape[-1] ** (-0.5)
    grad_query_list = []
    grad_keys = jnp.zeros(queries.shape, jnp.float32)
    grad_vals = jnp.zeros(queries.shape, jnp.float32)
    for block_index in range(length // block_rows):
        first_row = block_index * block_rows
        last_row = first_row + block_rows
        query_block = queries[first_row:last_row]
        scores, allowed = causal_scores(query_block, key_rows[:last_row], first_row, score_scale)
        probability = jnp.where(
            allowed, jnp.exp(scores - log_total[:, :, first_row:last_row, None]), 0.0
        )
        d_block = d_context[first_row:last_row]
        d_prob = jnp.einsum(
            "qshd,kshd->shqk", d_block, val_rows[:last_row], preferred_element_type=jnp.float32
        )
        delta = jnp.sum(probability * d_prob, axis=-1, keepdims=True)
        d_scores = (probability * (d_prob - delta)).astype(jnp.bfloat16)
        grad_query_list.append(
            jnp.einsum(
                "shqk,kshd->qshd", d_scores, key_rows[:last_row], preferred_element_type=jnp.float32
            )
            * score_scale
        )
        grad_keys = grad_keys.at[:last_row].add(
            jnp.einsum("shqk,qshd->kshd", d_scores, query_block, preferred_element_type=jnp.float32)
            * score_scale
        )
        grad_vals = grad_vals.at[:last_row].add(
            jnp.einsum(
                "shqk,qshd->kshd",
                probability.astype(jnp.bfloat16),
                d_block,
                preferred_element_type=jnp.float32,
            )
        )
    return (jnp.concatenate(grad_query_list, axis=0), grad_keys, grad_vals)


def local(acts_in, cotangent, norm_gains, vec_bias, w_qkv, b_qkv, w_out, w_up, b_up, w_down):
    section_index = lax.axis_index("section")
    own_start = lax.axis_index("tensor") * acts_in.shape[1]
    local_len = acts_in.shape[1]
    seq_count = acts_in.shape[2]
    model_width = acts_in.shape[3]
    length = local_len * lax.axis_size("tensor")
    all_rows = length * seq_count
    gain_full, bias_full = (
        lax.all_gather(norm_gains[0], ("dp", "tensor"), axis=1, tiled=True),
        lax.all_gather(vec_bias[0], ("dp", "tensor"), axis=1, tiled=True),
    )
    mat_qkv, bias_qkv, mat_out, mat_up, bias_up, mat_down = (
        lax.all_gather(w_qkv[0], "dp", axis=0, tiled=True),
        lax.all_gather(b_qkv[0], "dp", axis=1, tiled=True),
        lax.all_gather(w_out[0], "dp", axis=1, tiled=True),
        lax.all_gather(w_up[0], "dp", axis=0, tiled=True),
        lax.all_gather(b_up[0], "dp", axis=1, tiled=True),
        lax.all_gather(w_down[0], "dp", axis=1, tiled=True),
    )
    head_count = bias_qkv.shape[0]
    head_dim = bias_qkv.shape[1] // 3
    qkv_shift = bias_qkv.reshape(-1).astype(jnp.float32)
    up_shift = bias_up.reshape(-1).astype(jnp.float32)
    cosine, sine_tab = rotary_tables(length)
    cosine = cosine[:, None, None, :]
    sine_tab = sine_tab[:, None, None, :]
    received = jnp.zeros_like(acts_in[0])
    stash_list = []
    out_list = []
    for moment in range(MICRO + 1):
        own_rows = acts_in[min(moment, MICRO - 1)]
        inputs = jnp.where(section_index == 0, own_rows, received)
        forward_gathered = lax.all_gather(inputs, "tensor", axis=0, tiled=True)
        full_attn, full_mlp = both_norms(
            forward_gathered.astype(jnp.float32),
            gain_full[0],
            bias_full[0],
            gain_full[1],
            bias_full[1],
        )
        forward_normed_attn = full_attn.astype(jnp.bfloat16)
        forward_normed_mlp = full_mlp.astype(jnp.bfloat16)
        forward_flat_attn = forward_normed_attn.reshape(all_rows, model_width)
        forward_flat_mlp = forward_normed_mlp.reshape(all_rows, model_width)
        projected = (
            jnp.dot(forward_flat_attn, mat_qkv, preferred_element_type=jnp.float32) + qkv_shift
        )
        projected = projected.reshape(length, seq_count, head_count, 3, head_dim)
        forward_queries = rotate(projected[:, :, :, 0], cosine, sine_tab).astype(jnp.bfloat16)
        forward_key_rows = rotate(projected[:, :, :, 1], cosine, sine_tab).astype(jnp.bfloat16)
        forward_val_rows = projected[:, :, :, 2].astype(jnp.bfloat16)
        forward_context, forward_log_total = attend(
            forward_queries, forward_key_rows, forward_val_rows
        )
        forward_up_proj = (
            jnp.dot(forward_flat_mlp, mat_up, preferred_element_type=jnp.float32) + up_shift
        )
        forward_activated = jax.nn.gelu(forward_up_proj, approximate=False).astype(jnp.bfloat16)
        active_rows = forward_activated.reshape(length, seq_count, -1)
        context_part = forward_context.reshape(lax.axis_size("tensor") * local_len * seq_count, -1)
        active_part = active_rows.reshape(lax.axis_size("tensor") * local_len * seq_count, -1)
        summed = jnp.dot(context_part, mat_out, preferred_element_type=jnp.float32) + jnp.dot(
            active_part, mat_down, preferred_element_type=jnp.float32
        )
        mixed_sum = lax.psum_scatter(
            summed.reshape(lax.axis_size("tensor") * local_len, seq_count, model_width),
            "tensor",
            scatter_dimension=0,
            tiled=True,
        )
        result = inputs.astype(jnp.float32) + mixed_sum + bias_full[2] + bias_full[3]
        forward_stashed = (
            forward_gathered,
            forward_normed_attn,
            forward_normed_mlp,
            forward_queries,
            forward_key_rows,
            forward_val_rows,
            forward_context,
            forward_log_total,
            forward_up_proj,
            forward_activated,
        )
        result, stashed = (result.astype(jnp.bfloat16), forward_stashed)
        stash_list.append(stashed)
        out_list.append(result)
        if moment < MICRO:
            received = from_behind(result, "section", 1)
    stash_all = jax.tree.map(lambda *parts: jnp.stack(parts), *stash_list)
    acts_local = lax.dynamic_slice_in_dim(jnp.stack(out_list), section_index, MICRO, 0)
    back_received = jnp.zeros_like(cotangent[0])
    grad_list = []
    weight_sums = None
    vector_sums = None
    for moment in range(MICRO + 1):
        micro_index = moment - 1 + section_index
        is_valid = (micro_index >= 0) & (micro_index < MICRO)
        source_clock = jnp.clip(micro_index + section_index, 0, MICRO)
        stashed = jax.tree.map(
            lambda part: lax.dynamic_index_in_dim(part, source_clock, 0, keepdims=False), stash_all
        )
        upstream = jnp.where(section_index == 1, cotangent[min(moment, MICRO - 1)], back_received)
        (
            gathered,
            normed_attn,
            normed_mlp,
            queries,
            key_rows,
            val_rows,
            context,
            log_total,
            up_proj,
            activated,
        ) = stashed
        backward_inputs = lax.dynamic_slice_in_dim(gathered, own_start, local_len, 0)
        upstream_rows = lax.all_gather(upstream, "tensor", axis=0, tiled=True)
        flat_grad = upstream_rows.reshape(all_rows, model_width)
        d_context = jnp.dot(flat_grad, mat_out.T, preferred_element_type=jnp.float32).astype(
            jnp.bfloat16
        )
        d_context = d_context.reshape(length, seq_count, head_count, head_dim)
        d_active = jnp.dot(flat_grad, mat_down.T, preferred_element_type=jnp.float32)
        _, gelu_pullback = jax.vjp(partial(jax.nn.gelu, approximate=False), up_proj)
        d_up = gelu_pullback(d_active)[0].astype(jnp.bfloat16)
        grad_query, grad_key, grad_val = attend_back(
            queries, key_rows, val_rows, d_context, log_total
        )
        d_qkv = jnp.stack(
            [
                rotate_back(grad_query, cosine, sine_tab),
                rotate_back(grad_key, cosine, sine_tab),
                grad_val,
            ],
            axis=3,
        ).astype(jnp.bfloat16)
        d_qkv_flat = d_qkv.reshape(all_rows, -1)
        d_qkv_rows = d_qkv.reshape(length, seq_count, -1)
        d_up_rows = d_up.reshape(length, seq_count, -1)
        flat_attn = normed_attn.reshape(all_rows, model_width)
        flat_mlp = normed_mlp.reshape(all_rows, model_width)
        weight_terms = (
            jnp.einsum("tc,te->ce", flat_attn, d_qkv_flat, preferred_element_type=jnp.float32),
            jnp.sum(d_qkv_flat.astype(jnp.float32), axis=0).reshape(bias_qkv.shape),
            jnp.einsum(
                "tc,te->ce",
                context.reshape(all_rows, -1),
                flat_grad,
                preferred_element_type=jnp.float32,
            ),
            jnp.einsum("tc,te->ce", flat_mlp, d_up, preferred_element_type=jnp.float32),
            jnp.sum(d_up.astype(jnp.float32), axis=0).reshape(bias_up.shape),
            jnp.einsum("tc,te->ce", activated, flat_grad, preferred_element_type=jnp.float32),
        )
        attn_part = d_qkv_rows.reshape(lax.axis_size("tensor") * local_len * seq_count, -1)
        mlp_part = d_up_rows.reshape(lax.axis_size("tensor") * local_len * seq_count, -1)
        joined = jnp.concatenate(
            [
                jnp.dot(attn_part, mat_qkv.T, preferred_element_type=jnp.float32),
                jnp.dot(mlp_part, mat_up.T, preferred_element_type=jnp.float32),
            ],
            axis=-1,
        )
        d_normed = lax.psum_scatter(
            joined.reshape(lax.axis_size("tensor") * local_len, seq_count, 2 * model_width).astype(
                jnp.bfloat16
            ),
            "tensor",
            scatter_dimension=0,
            tiled=True,
        ).astype(jnp.float32)
        _, norm_pullback = jax.vjp(
            both_norms,
            backward_inputs.astype(jnp.float32),
            gain_full[0],
            bias_full[0],
            gain_full[1],
            bias_full[1],
        )
        d_local, d_gain_attn, d_shift_attn, d_gain_mlp, d_shift_mlp = norm_pullback(
            (d_normed[..., :model_width], d_normed[..., model_width:])
        )
        upstream_float = upstream.astype(jnp.float32)
        d_inputs = (upstream_float + d_local).astype(jnp.bfloat16)
        out_shift = jnp.sum(upstream_float, axis=(0, 1))
        vector_terms = (
            jnp.stack([d_gain_attn, d_gain_mlp]),
            jnp.stack([d_shift_attn, d_shift_mlp, out_shift, out_shift]),
        )
        d_inputs, weight_terms, vector_terms = (d_inputs, weight_terms, vector_terms)
        grad_list.append(d_inputs)
        if moment < MICRO:
            back_received = from_behind(d_inputs, "section", -1)
        weight_terms = tuple((jnp.where(is_valid, term, 0.0) for term in weight_terms))
        vector_terms = tuple((jnp.where(is_valid, term, 0.0) for term in vector_terms))
        if moment == 0:
            weight_sums = tuple(weight_terms)
            vector_sums = vector_terms
        else:
            weight_sums = tuple((a + b for a, b in zip(weight_sums, weight_terms)))
            vector_sums = tuple((a + b for a, b in zip(vector_sums, vector_terms)))
    sum_qkv, sum_bqkv, sum_out, sum_up, sum_bup, sum_down = weight_sums
    share_qkv, share_bqkv, share_out, share_up, share_bup, share_down = (
        lax.psum_scatter(
            sum_qkv.astype(jnp.bfloat16), "dp", scatter_dimension=0, tiled=True
        ).astype(jnp.float32),
        lax.psum_scatter(
            sum_bqkv.astype(jnp.bfloat16), "dp", scatter_dimension=1, tiled=True
        ).astype(jnp.float32),
        lax.psum_scatter(
            sum_out.astype(jnp.bfloat16), "dp", scatter_dimension=1, tiled=True
        ).astype(jnp.float32),
        lax.psum_scatter(sum_up.astype(jnp.bfloat16), "dp", scatter_dimension=0, tiled=True).astype(
            jnp.float32
        ),
        lax.psum_scatter(
            sum_bup.astype(jnp.bfloat16), "dp", scatter_dimension=1, tiled=True
        ).astype(jnp.float32),
        lax.psum_scatter(
            sum_down.astype(jnp.bfloat16), "dp", scatter_dimension=1, tiled=True
        ).astype(jnp.float32),
    )
    grad_local = lax.dynamic_slice_in_dim(jnp.stack(grad_list), 1 - section_index, MICRO, 0)
    gain_share, bias_share = (
        lax.psum_scatter(vector_sums[0], ("dp", "tensor"), scatter_dimension=1, tiled=True),
        lax.psum_scatter(vector_sums[1], ("dp", "tensor"), scatter_dimension=1, tiled=True),
    )
    return (
        acts_local[None],
        grad_local[None],
        gain_share[None],
        bias_share[None],
        share_qkv[None],
        share_bqkv[None],
        share_out[None],
        share_up[None],
        share_bup[None],
        share_down[None],
    )


FAR_ORDER = (0, 2, 3, 1)
VMEM_LIMIT = 60 * 1024 * 1024
ROW_BLOCK = 256
CHUNKS = 2
COLUMN_STEP = 2048
MICROSECOND = 1_000_000_000


def ring(value, axis, by):
    length = lax.axis_size(axis)
    return lax.ppermute(value, axis, [(i, (i + by) % length) for i in range(length)])


def swap(value, axis, bit):
    length = lax.axis_size(axis)
    return lax.ppermute(value, axis, [(i, i ^ bit) for i in range(length)])


def pick(value, index, axis=0):
    return lax.dynamic_index_in_dim(value, index, axis, keepdims=False)


def place(value, block, index):
    return lax.dynamic_update_index_in_dim(value, block, index, 0)


def relative(values, own):
    size = values.shape[-1] // 4
    picked = [
        lax.dynamic_slice_in_dim(values, jnp.bitwise_xor(own, k) * size, size, values.ndim - 1)
        for k in range(4)
    ]
    return jnp.concatenate(picked, axis=-1)


class Clock:
    def __init__(self):
        self.ended = ()

    def hold(self, value):
        return lax.optimization_barrier((value, self.ended))[0]

    def tick(self, *ended):
        self.ended = tuple(jax.tree.leaves(ended))


def exchange_near(blocks, own, hold):
    half = blocks.shape[1] // 2
    far = pick(blocks, (own + 2) & 3)
    ahead = jnp.concatenate([pick(blocks, (own + 1) & 3), far[:half]], axis=0)
    behind = jnp.concatenate([pick(blocks, (own + 3) & 3), far[half:]], axis=0)
    return ring(hold(ahead), "tensor", 1), ring(hold(behind), "tensor", -1)


def exchange_far(near, hold):
    rows = near[0].shape[0] * 2 // 3
    first = ring(hold(near[0][rows:]), "tensor", 1)
    second = ring(hold(near[1][rows:]), "tensor", -1)
    return first, second


def exchanged(blocks, near, far, own):
    rows = blocks.shape[1]
    result = jnp.zeros_like(blocks)
    result = place(result, pick(blocks, own), own)
    result = place(result, near[0][:rows], (own + 3) & 3)
    result = place(result, near[1][:rows], (own + 1) & 3)
    return place(result, jnp.concatenate(far, axis=0), (own + 2) & 3)


def add_wide(left, right):
    return (left.astype(jnp.float32) + right.astype(jnp.float32)).astype(jnp.bfloat16)


def add_three(first, second, third):
    total = first.astype(jnp.float32) + second.astype(jnp.float32) + third.astype(jnp.float32)
    return total.astype(jnp.bfloat16)


def ring_first(blocks, hold):
    far = blocks[3]
    half = far.shape[0] // 2
    to_right = ring(hold(far[:half]), "tensor", 1)
    to_left = ring(hold(far[half:]), "tensor", -1)
    return to_right, to_left


def ring_second(blocks, got, hold):
    _, left, right, _ = blocks
    half = left.shape[0] // 2
    right = jnp.concatenate([add_wide(right[:half], got[0]), right[half:]], axis=0)
    left = jnp.concatenate([left[:half], add_wide(left[half:], got[1])], axis=0)
    return ring(hold(right), "tensor", 1), ring(hold(left), "tensor", -1)


def ring_total(own, got):
    total = own.astype(jnp.float32) + got[0].astype(jnp.float32) + got[1].astype(jnp.float32)
    return total.astype(jnp.bfloat16)


def normalised(x):
    average = jnp.mean(x, axis=-1, keepdims=True)
    centred = x - average
    variance = jnp.mean(centred * centred, axis=-1, keepdims=True)
    inverse = lax.rsqrt(variance + NORM_EPS)
    return centred * inverse, inverse


def nt_dot(left, right):
    return lax.dot_general(
        left, right, (((1,), (1,)), ((), ())), preferred_element_type=jnp.float32
    )


def tn_dot(left, right):
    return lax.dot_general(
        left, right, (((0,), (0,)), ((), ())), preferred_element_type=jnp.float32
    )


def nn_dot(left, right):
    return jnp.dot(left, right, preferred_element_type=jnp.float32)


def turn(values, cosine, low_sine, high_sine):
    lanes = values.shape[-1]
    return (
        values * cosine
        + pltpu.roll(values, ROT // 2, 1) * low_sine
        + pltpu.roll(values, lanes - ROT // 2, 1) * high_sine
    )


def call(body, name, flops, grid, ins, outs, scratch=(), filled=()):
    count = len(ins)

    def run(*refs):
        body(*refs[:count], *refs[count + len(filled) :])

    return pl.pallas_call(
        run,
        name=name,
        grid=grid,
        in_specs=[pl.BlockSpec(block, index) for _, block, index in ins]
        + [pl.BlockSpec(memory_space=pl.ANY)] * len(filled),
        out_specs=[pl.BlockSpec(block, index) for _, _, block, index in outs],
        out_shape=[jax.ShapeDtypeStruct(shape, kind) for shape, kind, _, _ in outs],
        scratch_shapes=list(scratch),
        input_output_aliases={count + i: i for i in range(len(filled))},
        cost_estimate=pl.CostEstimate(flops=flops, bytes_accessed=1 << 20, transcendentals=0),
        compiler_params=pltpu.CompilerParams(
            vmem_limit_bytes=VMEM_LIMIT, dimension_semantics=("arbitrary",) * len(grid)
        ),
    )(*[array for array, _, _ in ins], *filled)


def whole(array):
    return (array, array.shape, lambda *_: (0,) * array.ndim)


def matrix(pieces, size, block):
    shape = (2, pieces[0].shape[1], size)
    return [(piece, shape, lambda *_: (0, 0, block)) for piece in pieces]


def room(pieces, size):
    return pltpu.VMEM((4 * pieces[0].shape[1], 4 * size), jnp.bfloat16)


def assemble(refs, target):
    _, rows, size = refs[0].shape
    for core in range(2):
        for offset in range(4):
            for side in range(2):
                at = (2 * side + core) * rows
                target[at : at + rows, offset * size : (offset + 1) * size] = refs[
                    core * 4 + offset
                ][side]


def rows_of(array, first=0, block=ROW_BLOCK):
    base = first // block
    return (array, (block, array.shape[1]), lambda i: (i + base, 0))


def qkv_body(x, vecs, shift, cos, low, high, *rest):
    ln_a, ln_m, qkv, w = rest[8:]

    @pl.when(pl.program_id(0) == 0)
    def _():
        assemble(rest[:8], w)

    hat, _ = normalised(x[...].astype(jnp.float32))
    attn = (hat * vecs[0:1, :] + vecs[1:2, :]).astype(jnp.bfloat16)
    ln_a[...] = attn
    ln_m[...] = (hat * vecs[2:3, :] + vecs[3:4, :]).astype(jnp.bfloat16)
    out = nn_dot(attn, w[...]) + shift[...]
    for block in range(qkv.shape[1] // 384):
        for part in range(3):
            at = block * 384 + part * 128
            piece = out[:, at : at + 128]
            if part < 2:
                piece = turn(piece, cos[...], low[...], high[...])
            qkv[:, at : at + 128] = piece.astype(jnp.bfloat16)


def run_qkv(source, vecs, shift, tables, pieces, at, rows, filled):
    x, first = source
    width = x.shape[1]
    length = tables[0].shape[0]
    cols = shift.shape[1]
    bf = jnp.bfloat16
    base = at // ROW_BLOCK
    own = lambda i: (i + base, 0)
    return call(
        qkv_body,
        "norm_qkv",
        rows * 13 * MICROSECOND // 1024,
        (rows // ROW_BLOCK,),
        [rows_of(x, first), whole(vecs), whole(shift)]
        + [rows_of(t, at) for t in tables]
        + matrix(pieces, cols // 4, 0),
        [
            ((length, width), bf, (ROW_BLOCK, width), own),
            ((length, width), bf, (ROW_BLOCK, width), own),
            ((length, cols), bf, (ROW_BLOCK, cols), own),
        ],
        [room(pieces, cols // 4)],
        filled,
    )


def attend_body(q, k, v, ctx, lse):
    length = q.shape[0]
    step = ROW_BLOCK
    for head in range(2):
        lanes = slice(head * 64, head * 64 + 64)
        keys = k[:, lanes]
        vals = v[:, lanes]
        for at in range(0, length, step):
            end = at + step
            queries = q[at:end, lanes] * jnp.bfloat16(0.125)
            scores = nt_dot(queries, keys[:end])
            row = lax.broadcasted_iota(jnp.int32, (step, step), 0)
            col = lax.broadcasted_iota(jnp.int32, (step, step), 1)
            last = jnp.where(col <= row, scores[:, at:], MASK_FILL)
            scores = last if at == 0 else jnp.concatenate([scores[:, :at], last], axis=1)
            top = jnp.max(scores, axis=1, keepdims=True)
            power = jnp.exp(scores - top)
            total = jnp.sum(power, axis=1, keepdims=True)
            mixed = nn_dot(power.astype(jnp.bfloat16), vals[:end]) * (1.0 / total)
            ctx[at:end, lanes] = mixed.astype(jnp.bfloat16)
            level = jnp.broadcast_to(top + jnp.log(total), (step, 128))
            lse[0, head : head + 1, at:end] = level.T[0:1]


def run_attend(qkv):
    length, cols = qkv.shape
    groups = cols // 384
    return call(
        attend_body,
        "attend",
        length * 19 * MICROSECOND // 1024,
        (groups,),
        [
            (qkv, (length, 128), lambda i: (0, 3 * i)),
            (qkv, (length, 128), lambda i: (0, 3 * i + 1)),
            (qkv, (length, 128), lambda i: (0, 3 * i + 2)),
        ],
        [
            ((length, groups * 128), jnp.bfloat16, (length, 128), lambda i: (0, i)),
            ((groups, 8, length), jnp.float32, (1, 8, length), lambda i: (i, 0, 0)),
        ],
    )


ERF_TOP = (
    0.00022905065861350646,
    0.0034082910107109506,
    0.050955695062380861,
    0.18520832239976145,
    1.128379143519084,
)
ERF_BOTTOM = (
    -1.1791602954361697e-7,
    0.000023547966471313185,
    0.0010179625278914885,
    0.014070470171167667,
    0.11098505178285362,
    0.49746925110067538,
    1.0,
)


def erf(x):
    x = jnp.clip(x, -3.7439211627767994, 3.7439211627767994)
    square = x * x
    top = jnp.full_like(x, ERF_TOP[0])
    for term in ERF_TOP[1:]:
        top = top * square + term
    bottom = jnp.full_like(x, ERF_BOTTOM[0])
    for term in ERF_BOTTOM[1:]:
        bottom = bottom * square + term
    return x * top / bottom


def mlp_body(ctx, ln_m, shift, *rest):
    act, slope, part, w_out, w_up, w_down = rest[24:]

    @pl.when(pl.program_id(0) == 0)
    def _():
        assemble(rest[:8], w_out)
        assemble(rest[8:16], w_up)
        assemble(rest[16:24], w_down)

    total = nt_dot(ctx[...], w_out[...])
    values = ln_m[...]
    size = min(COLUMN_STEP, act.shape[1])
    for at in range(0, act.shape[1], size):
        cols = slice(at, at + size)
        up = nn_dot(values, w_up[:, cols]) + shift[:, cols]
        half_erf = 0.5 * erf(up * (2.0**-0.5)) + 0.5
        bell = jnp.exp(up * up * -0.5) * ((2.0 * math.pi) ** -0.5)
        active = (up * half_erf).astype(jnp.bfloat16)
        act[:, cols] = active
        slope[:, cols] = (half_erf + up * bell).astype(jnp.bfloat16)
        total = total + nt_dot(active, w_down[:, cols])
    part[...] = total.astype(jnp.bfloat16)


def run_mlp(ctx, ln_m, shift, narrow, broad, at, rows, filled):
    length, width = ln_m.shape
    cols, heads = shift.shape[1], ctx.shape[1]
    bf = jnp.bfloat16
    base = at // ROW_BLOCK
    own = lambda i: (i + base, 0)
    return call(
        mlp_body,
        "mlp_out",
        rows * 32 * MICROSECOND // 1024,
        (rows // ROW_BLOCK,),
        [rows_of(ctx, at), rows_of(ln_m, at), whole(shift)]
        + matrix(narrow, heads // 4, 3)
        + matrix(broad, cols // 4, 0)
        + matrix(broad, cols // 4, 1),
        [
            ((length, cols), bf, (ROW_BLOCK, cols), own),
            ((length, cols), bf, (ROW_BLOCK, cols), own),
            ((rows, width), bf, (ROW_BLOCK, width), lambda i: (i, 0)),
        ],
        [room(narrow, heads // 4), room(broad, cols // 4), room(broad, cols // 4)],
        filled,
    )


def mlp_back_body(g, slope, *rest):
    d_up, d_ctx, sum_up, sum_g, w_out, w_down = rest[16:]

    @pl.when(pl.program_id(0) == 0)
    def _():
        assemble(rest[:8], w_out)
        assemble(rest[8:16], w_down)
        sum_up[...] = jnp.zeros_like(sum_up)
        sum_g[...] = jnp.zeros_like(sum_g)

    grad = g[...]
    size = min(COLUMN_STEP, d_up.shape[1])
    for at in range(0, d_up.shape[1], size):
        cols = slice(at, at + size)
        du = nn_dot(grad, w_down[:, cols]) * slope[:, cols].astype(jnp.float32)
        du = du.astype(jnp.bfloat16)
        d_up[:, cols] = du
        sum_up[:, cols] += jnp.sum(du.astype(jnp.float32), axis=0, keepdims=True)
    d_ctx[...] = nn_dot(grad, w_out[...]).astype(jnp.bfloat16)
    sum_g[...] += jnp.sum(grad.astype(jnp.float32), axis=0, keepdims=True)


def run_mlp_back(source, slope, narrow, broad, at, rows, heads, filled):
    g, first = source
    width = g.shape[1]
    length, cols = slope.shape
    bf = jnp.bfloat16
    base = at // ROW_BLOCK
    own = lambda i: (i + base, 0)
    fixed = lambda i: (0, 0)
    return call(
        mlp_back_body,
        "mlp_back",
        rows * 15 * MICROSECOND // 1024,
        (rows // ROW_BLOCK,),
        [rows_of(g, first), rows_of(slope, at)]
        + matrix(narrow, heads // 4, 3)
        + matrix(broad, cols // 4, 1),
        [
            ((length, cols), bf, (ROW_BLOCK, cols), own),
            ((length, heads), bf, (ROW_BLOCK, heads), own),
            ((1, cols), jnp.float32, (1, cols), fixed),
            ((1, width), jnp.float32, (1, width), fixed),
        ],
        [room(narrow, heads // 4), room(broad, cols // 4)],
        filled,
    )


def attend_back_body(q, k, v, d_ctx, lse, cos, low, high, d_qkv, sums, dk_sum, dv_sum, dq_all):
    length = q.shape[0]
    step = ROW_BLOCK
    for head in range(2):
        lanes = slice(head * 64, head * 64 + 64)
        keys = k[:, lanes]
        vals = v[:, lanes]
        dk_sum[:, lanes] = jnp.zeros((length, 64), jnp.float32)
        dv_sum[:, lanes] = jnp.zeros((length, 64), jnp.float32)
        for at in range(0, length, step):
            end = at + step
            queries = q[at:end, lanes] * jnp.bfloat16(0.125)
            grads = d_ctx[at:end, lanes]
            scores = nt_dot(keys[:end], queries)
            power = jnp.exp(scores - lse[0, head : head + 1, at:end])
            key = lax.broadcasted_iota(jnp.int32, (step, step), 0)
            row = lax.broadcasted_iota(jnp.int32, (step, step), 1)
            last = jnp.where(key <= row, power[at:], 0.0)
            probs = last if at == 0 else jnp.concatenate([power[:at], last], axis=0)
            d_probs = nt_dot(vals[:end], grads)
            delta = jnp.sum(probs * d_probs, axis=0, keepdims=True)
            d_scores = (probs * (d_probs - delta)).astype(jnp.bfloat16)
            dv_sum[:end, lanes] += nn_dot(probs.astype(jnp.bfloat16), grads)
            dk_sum[:end, lanes] += nn_dot(d_scores, queries)
            dq_all[at:end, lanes] = tn_dot(d_scores, keys[:end]) * 0.125
    dq = turn(dq_all[...], cos[...], -low[...], -high[...]).astype(jnp.bfloat16)
    dk = turn(dk_sum[...], cos[...], -low[...], -high[...]).astype(jnp.bfloat16)
    dv = dv_sum[...].astype(jnp.bfloat16)
    for part, piece in enumerate((dq, dk, dv)):
        at = part * 128
        d_qkv[:, at : at + 128] = piece
        sums[:, at : at + 128] = jnp.sum(piece.astype(jnp.float32), axis=0, keepdims=True)


def run_attend_back(qkv, d_ctx, lse, tables):
    length, cols = qkv.shape
    groups = cols // 384
    wide = pltpu.VMEM((length, 128), jnp.float32)
    return call(
        attend_back_body,
        "attend_back",
        length * 26 * MICROSECOND // 1024,
        (groups,),
        [
            (qkv, (length, 128), lambda i: (0, 3 * i)),
            (qkv, (length, 128), lambda i: (0, 3 * i + 1)),
            (qkv, (length, 128), lambda i: (0, 3 * i + 2)),
            (d_ctx, (length, 128), lambda i: (0, i)),
            (lse, (1, 8, length), lambda i: (i, 0, 0)),
        ]
        + [whole(t) for t in tables],
        [
            ((length, cols), jnp.bfloat16, (length, 384), lambda i: (0, i)),
            ((1, cols), jnp.float32, (1, 384), lambda i: (0, i)),
        ],
        [wide, wide, wide],
    )


def norm_back_body(x, d_qkv, d_up, vecs, *rest):
    part, sums, w_qkv, w_up = rest[16:]

    @pl.when(pl.program_id(0) == 0)
    def _():
        assemble(rest[:8], w_qkv)
        assemble(rest[8:16], w_up)
        sums[...] = jnp.zeros_like(sums)

    hat, inverse = normalised(x[...].astype(jnp.float32))
    d_attn = nt_dot(d_qkv[...], w_qkv[...])
    d_mlp = nt_dot(d_up[...], w_up[...])
    for row, term in enumerate((d_attn * hat, d_mlp * hat, d_attn, d_mlp)):
        sums[row : row + 1, :] += jnp.sum(term, axis=0, keepdims=True)
    d_hat = d_attn * vecs[0:1, :] + d_mlp * vecs[2:3, :]
    along = jnp.mean(d_hat * hat, axis=-1, keepdims=True)
    level = jnp.mean(d_hat, axis=-1, keepdims=True)
    part[...] = (inverse * (d_hat - level - hat * along)).astype(jnp.bfloat16)


def run_norm_back(source, d_qkv, d_up, vecs, narrow, broad, at, rows):
    x, first = source
    width = x.shape[1]
    n_qkv, n_up = d_qkv.shape[1] // 4, d_up.shape[1] // 4
    return call(
        norm_back_body,
        "norm_back",
        rows * 21 * MICROSECOND // 1024,
        (rows // ROW_BLOCK,),
        [rows_of(x, first), rows_of(d_qkv, at), rows_of(d_up, at), whole(vecs)]
        + matrix(narrow, n_qkv, 0)
        + matrix(broad, n_up, 0),
        [
            ((rows, width), jnp.bfloat16, (ROW_BLOCK, width), lambda i: (i, 0)),
            ((8, width), jnp.float32, (8, width), lambda i: (0, 0)),
        ],
        [room(narrow, n_qkv), room(broad, n_up)],
    )


def weight_grad_body(cuts, *refs):
    a_refs, b_refs, rest = refs[: sum(cuts)], refs[sum(cuts) :], refs[sum(cuts) + 2 :]
    keep, send, turned_one, turned_two = rest
    groups = (a_refs[: cuts[0]], a_refs[cuts[0] :])

    @pl.when(pl.program_id(0) == 0)
    def _():
        for group, turned in zip(groups, (turned_one, turned_two)):
            at = 0
            for ref in group:
                turned[:, at : at + ref.shape[0]] = ref[...].T
                at += ref.shape[0]

    at = 0
    rows = keep.shape[2]
    for turned, right in zip((turned_one, turned_two), b_refs[:2]):
        size = right.shape[1]
        grad = nn_dot(turned[...], right[...]).astype(jnp.bfloat16)
        for side in range(2):
            first = 2 * side * rows
            keep[side, 0, :, at : at + size] = grad[first : first + rows]
            send[side, 0, :, at : at + size] = grad[first + rows : first + 2 * rows]
        at += size


def run_weight_grad(lefts, rights):
    length, width = rights[0].shape[0], lefts[0][0].shape[1]
    sizes = [right.shape[1] // 4 for right in rights]
    shape = (2, 4, width // 4, sum(sizes))
    out = (shape, jnp.bfloat16, (2, 1) + shape[2:], lambda i: (0, i, 0, 0))
    turned = pltpu.VMEM((width, length), jnp.bfloat16)
    return call(
        partial(weight_grad_body, tuple(len(group) for group in lefts)),
        "weight_grad",
        length * 14 * MICROSECOND // 1024,
        (4,),
        [whole(left) for group in lefts for left in group]
        + [(r, (length, n), lambda i: (0, i)) for r, n in zip(rights, sizes)],
        [out, out],
        [turned, turned],
    )


def turn_tables(length):
    cosine, sine_tab = rotary_tables(length)
    zero = jnp.zeros_like(sine_tab)
    rest = jnp.zeros((length, 64 - ROT), jnp.float32)
    cos = jnp.concatenate([cosine, cosine, rest + 1.0], axis=1)
    low = jnp.concatenate([zero, sine_tab, rest], axis=1)
    high = jnp.concatenate([-sine_tab, zero, rest], axis=1)
    return tuple(jnp.concatenate([t, t], axis=1) for t in (cos, low, high))


def by_sequence(
    acts_in, cotangent, norm_gains, vec_bias, w_qkv, b_qkv, w_out, w_up, b_up, w_down
):
    section = lax.axis_index("section").astype(jnp.uint32)
    across = lax.axis_index("dp").astype(jnp.uint32)
    along = lax.axis_index("tensor").astype(jnp.uint32)
    first_section = section == 0
    width = acts_in.shape[3]
    rows = w_qkv.shape[1]
    positions = acts_in.shape[1]
    length = 4 * positions
    heads = b_qkv.shape[1]
    bf = jnp.bfloat16

    qkv_halves = (
        w_qkv[0].reshape(rows, 2, 2, 3, 64).transpose(1, 0, 3, 2, 4).reshape(2, rows, -1)
    )
    out_halves = w_out[0].T.reshape(rows, 2, -1).transpose(1, 0, 2)
    up_halves = w_up[0].reshape(rows, 2, -1).transpose(1, 0, 2)
    down_halves = w_down[0].T.reshape(rows, 2, -1).transpose(1, 0, 2)
    n_qkv, n_out, n_up = qkv_halves.shape[2], out_halves.shape[2], up_halves.shape[2]

    narrow = jnp.stack([jnp.concatenate([qkv_halves[h], out_halves[h]], axis=1) for h in (0, 1)])
    broad = jnp.stack([jnp.concatenate([up_halves[h], down_halves[h]], axis=1) for h in (0, 1)])
    small = jnp.concatenate(
        [
            norm_gains[0].reshape(-1),
            vec_bias[0].reshape(-1),
            b_qkv[0].reshape(-1).astype(jnp.float32),
            b_up[0].reshape(-1).astype(jnp.float32),
        ]
    )
    clock = Clock()
    hold, tick = clock.hold, clock.tick

    def pass_half(halves):
        return swap(hold(pick(halves, 1 - section)), "section", 1)

    def by_layer(halves, got):
        keep = pick(halves, section)
        return jnp.where(first_section, keep, got), jnp.where(first_section, got, keep)

    def x_swap(value):
        return swap(hold(value), "dp", 2)

    def core_swap(value):
        return swap(hold(value), "dp", 1)

    def y_swap(value):
        return swap(hold(value), "section", 1)

    def both_ways(value):
        value = hold(value)
        return ring(value, "tensor", 1), ring(value, "tensor", -1)

    def far_halves(left, right):
        half = left.shape[0] // 2
        return ring(hold(left[:half]), "tensor", 1), ring(hold(right[half:]), "tensor", -1)

    def own_half(blocks):
        return lax.dynamic_slice_in_dim(blocks, section * (width // 2), width // 2, 2)

    def both_halves(own, got):
        own = own.reshape(length, width // 2)
        got = got.reshape(length, width // 2)
        low = jnp.where(first_section, own, got)
        high = jnp.where(first_section, got, own)
        return relative(jnp.concatenate([low, high], axis=1), across)

    def stacked(own, got):
        return jnp.stack([own, got])

    got_narrow = pass_half(narrow)
    got_small = swap(small, "section", 1)
    blocks = own_half(acts_in[:, :, 0, :])
    near = exchange_near(blocks, along, hold)
    tick(got_narrow, got_small, near)
    narrow_shards = by_layer(narrow, got_narrow)
    small = jnp.where(first_section, jnp.stack([small, got_small]), jnp.stack([got_small, small]))
    left, right = both_ways(narrow_shards[0])
    far = exchange_far(near, hold)
    got_broad = pass_half(broad)
    got_own = x_swap(narrow_shards[0])
    small = jnp.stack([small, core_swap(small)])
    small = jnp.concatenate([small, swap(small, "dp", 2)])
    tick(left, right, far, got_broad, got_own, small)
    own_acts = exchanged(blocks, near, far, along)
    got_acts = y_swap(own_acts)
    narrow_far = far_halves(left, right)
    got_left, got_right = x_swap(left), x_swap(right)
    small = jnp.stack([small, swap(hold(small), "tensor", 1)])
    small = jnp.concatenate([small, swap(small, "tensor", 2)])
    tick(narrow_far, got_left, got_right, small)
    broad_shards = by_layer(broad, got_broad)
    broad_left, broad_right = both_ways(broad_shards[0])
    narrow_far = jnp.concatenate(narrow_far, axis=0)
    got_far = x_swap(narrow_far)
    pieces = [
        stacked(narrow_shards[0], got_own),
        stacked(left, got_left),
        stacked(right, got_right),
    ]
    others = [core_swap(piece) for piece in pieces]
    tick(got_far, others, got_acts)
    acts = both_halves(own_acts, got_acts)
    pieces.append(stacked(narrow_far, got_far))
    others.append(core_swap(pieces[3]))
    got_own = x_swap(broad_shards[0])
    narrow_zero = (*pieces, *others)
    tick(others[3])

    share = norm_gains.shape[2]
    vec_part = small[..., : 6 * share].reshape(4, 4, 2, 6, share)
    offsets = jnp.array(FAR_ORDER, jnp.int32)
    order = jnp.stack([pick(offsets, (k - along) & 3) for k in range(4)])
    slots = [jnp.bitwise_xor((along + k) & 3, along) for k in (0, 3, 1, 2)]
    vec_part = jnp.stack([pick(vec_part, jnp.bitwise_xor(along, k)) for k in range(4)])
    vecs_full = vec_part.transpose(2, 3, 1, 0, 4).reshape(2, 6, width)
    at = 6 * share
    share_q = b_qkv.shape[2]
    dp_order = [jnp.bitwise_xor(across, k) for k in range(4)]
    qkv_bias = small[..., at : at + heads * share_q].reshape(4, 4, 2, heads, share_q)
    qkv_bias = jnp.stack([pick(qkv_bias, k) for k in slots])
    qkv_bias = jnp.stack([pick(qkv_bias, i, 1) for i in dp_order], axis=1)
    qkv_bias = qkv_bias.transpose(2, 0, 3, 1, 4).reshape(2, 4, 2, heads // 2, 3, 64)
    qkv_bias = pick(qkv_bias, section, 2).transpose(0, 1, 3, 2, 4).reshape(2, 1, -1)
    at += heads * share_q
    bias_rows, share_u = b_up.shape[1], b_up.shape[2]
    up_bias = small[..., at : at + bias_rows * share_u].reshape(4, 4, 2, bias_rows, share_u)
    up_bias = jnp.stack([pick(up_bias, k) for k in slots])
    up_bias = jnp.stack([pick(up_bias, i, 1) for i in dp_order], axis=1)
    up_bias = up_bias.transpose(2, 0, 3, 1, 4).reshape(2, 4, 2, bias_rows // 2, 4 * share_u)
    up_bias = pick(up_bias, section, 2).reshape(2, 1, -1)
    zero_rows = jnp.zeros((4, width), jnp.float32)

    tables = turn_tables(length)
    chunk = length // CHUNKS
    starts = [i * chunk for i in range(CHUNKS)]

    all_vecs = [
        jnp.concatenate([v[0:1], v[2:3], v[1:2], v[3:4], zero_rows], axis=0) for v in vecs_full
    ]

    def project(layer, i, source, pieces, filled):
        return run_qkv(
            source, all_vecs[layer], qkv_bias[layer], tables, pieces, starts[i], chunk, filled
        )

    def feed(layer, i, ctx, ln_m, narrow, broad, filled):
        *filled, part = run_mlp(
            hold(ctx), ln_m, up_bias[layer], narrow, broad, starts[i], chunk, filled
        )
        return filled, part

    def join(layer, before, part, got):
        total = part.astype(jnp.float32) + got.astype(jnp.float32)
        full = vecs_full[layer]
        return (before.astype(jnp.float32) + total + (full[4] + full[5])).astype(bf)

    acts = hold(acts)
    first = project(0, 0, (acts, 0), narrow_zero, ())
    tick(first, broad_left, broad_right)
    got_left = x_swap(broad_left)
    first = project(0, 1, (acts, chunk), narrow_zero, first)
    tick(first, got_own)
    ln_a0, ln_m0, qkv0 = first
    broad_far = far_halves(broad_left, broad_right)
    got_right = x_swap(broad_right)
    ctx0, lse0 = run_attend(hold(qkv0))
    tick(ctx0, broad_far, got_left, got_right)
    broad_far = jnp.concatenate(broad_far, axis=0)
    got_far = x_swap(broad_far)
    pieces = [
        stacked(broad_shards[0], got_own),
        stacked(broad_left, got_left),
        stacked(broad_right, got_right),
    ]
    others = [core_swap(piece) for piece in pieces]
    tick(got_far, others)
    pieces.append(stacked(broad_far, got_far))
    others.append(core_swap(pieces[3]))
    broad_zero = (*pieces, *others)
    tick(others[3])
    first, part_a = feed(0, 0, ctx0, ln_m0, narrow_zero, broad_zero, ())
    left, right = both_ways(narrow_shards[1])
    got_own = x_swap(narrow_shards[1])
    broad_own = x_swap(broad_shards[1])
    tick(part_a, left, right, got_own, broad_own)
    first, part_b = feed(0, 1, ctx0, ln_m0, narrow_zero, broad_zero, first)
    act0, slope0 = first
    got_a = y_swap(part_a)
    narrow_far = far_halves(left, right)
    broad_left, broad_right = both_ways(broad_shards[1])
    tick(part_b, got_a, narrow_far, broad_left, broad_right)
    got_b = y_swap(part_b)
    got_left, got_right = x_swap(left), x_swap(right)
    x1_a = join(0, acts[:chunk], part_a, got_a)
    tick(got_left, got_right)
    narrow_far = jnp.concatenate(narrow_far, axis=0)
    got_far = x_swap(narrow_far)
    pieces = [
        stacked(narrow_shards[1], got_own),
        stacked(left, got_left),
        stacked(right, got_right),
    ]
    others = [core_swap(piece) for piece in pieces]
    tick(got_b, got_far, others)
    x1_b = join(0, acts[chunk:], part_b, got_b)
    pieces.append(stacked(narrow_far, got_far))
    others.append(core_swap(pieces[3]))
    narrow_one = (*pieces, *others)
    tick(others[3], x1_a, x1_b)

    broad_far = far_halves(broad_left, broad_right)
    got_left = x_swap(broad_left)
    first = project(1, 0, (hold(x1_a), 0), narrow_one, ())
    first = project(1, 1, (x1_b, 0), narrow_one, first)
    ln_a1, ln_m1, qkv1 = first
    pieces = [stacked(broad_shards[1], broad_own)]
    others = [core_swap(pieces[0])]
    tick(first, broad_far, got_left, others)
    broad_far = jnp.concatenate(broad_far, axis=0)
    got_right, got_far = x_swap(broad_right), x_swap(broad_far)
    pieces.append(stacked(broad_left, got_left))
    others.append(core_swap(pieces[1]))
    ctx1, lse1 = run_attend(hold(qkv1))
    blocks = own_half(cotangent[:, :, 0, :])
    near = exchange_near(blocks, along, hold)
    tick(ctx1, got_right, got_far, others, near)
    far = exchange_far(near, hold)
    pieces += [stacked(broad_right, got_right), stacked(broad_far, got_far)]
    others += [core_swap(piece) for piece in pieces[2:]]
    broad_one = (*pieces, *others)
    tick(others[2:], far)
    own_grads = exchanged(blocks, near, far, along)
    got_grads = y_swap(own_grads)
    first, part_a = feed(1, 0, ctx1, ln_m1, narrow_one, broad_one, ())
    tick(part_a, got_grads)
    got_a = y_swap(part_a)
    first, part_b = feed(1, 1, ctx1, ln_m1, narrow_one, broad_one, first)
    act1, slope1 = first
    tick(part_b, got_a)

    grads = hold(both_halves(own_grads, got_grads))
    n_heads = ctx0.shape[1]

    def back(i, source, slope, narrow, broad, filled):
        *filled, up_term, g_term = run_mlp_back(
            source, slope, narrow, broad, starts[i], chunk, n_heads, filled
        )
        return filled, up_term, g_term

    first, up_a, g_a = back(0, (grads, 0), slope1, narrow_one, broad_one, ())
    first, up_b, g_b = back(1, (grads, chunk), slope1, narrow_one, broad_one, first)
    d_up1, d_ctx1 = first
    sums_one = [None, g_a + g_b, None, up_a + up_b]
    tick(first, got_a)
    x1 = jnp.concatenate([x1_a, x1_b], axis=0)

    def to_blocks(values):
        return relative(values, across).reshape(4, positions, width)

    d_qkv1, sums_one[2] = run_attend_back(qkv1, hold(d_ctx1), lse1, tables)
    got_b = y_swap(part_b)
    tick(d_qkv1, got_b)
    x2 = jnp.concatenate(
        [join(1, x1_a, part_a, got_a), join(1, x1_b, hold(part_b), got_b)], axis=0
    )
    out_blocks = to_blocks(jnp.where(first_section, x1, x2))
    part_a, sum_a = run_norm_back(
        (x1_a, 0), hold(d_qkv1), d_up1, all_vecs[1], narrow_one, broad_one, 0, chunk
    )
    tick(part_a, out_blocks)
    got_a = y_swap(part_a)
    out_parts = out_blocks[..., : width // 2], out_blocks[..., width // 2 :]
    out_near = [exchange_near(out_parts[0], along, hold)]
    part_b, sum_b = run_norm_back(
        (x1_b, 0), hold(d_qkv1), d_up1, all_vecs[1], narrow_one, broad_one, chunk, chunk
    )
    sums_one[0] = (sum_a + sum_b)[:4]
    keep_broad, send = run_weight_grad([[hold(ln_m1)], [grads]], [d_up1, act1])
    tick(part_b, keep_broad, got_a, out_near)
    got_b = y_swap(part_b)
    got_core = core_swap(send)
    out_near.append(exchange_near(out_parts[1], along, hold))
    keep_narrow, send_narrow = run_weight_grad([[hold(ln_a1)], [grads]], [d_qkv1, ctx1])
    tick(keep_narrow, got_b, got_core, out_near)

    def lower(above, part, got):
        total = part.astype(jnp.float32) + got.astype(jnp.float32)
        return (above.astype(jnp.float32) + total).astype(bf)

    g1_a = lower(grads[:chunk], hold(part_a), got_a)
    g1_b = lower(grads[chunk:], hold(part_b), got_b)
    keep_one, core_one = hold(keep_broad), got_core
    got_core = core_swap(send_narrow)
    got_x = [x_swap(add_wide(keep_one[1, 2:], core_one[1, 2:]))]
    first, up_a, g_a = back(0, (hold(g1_a), 0), slope0, narrow_zero, broad_zero, ())
    first, up_b, g_b = back(1, (g1_b, 0), slope0, narrow_zero, broad_zero, first)
    d_up0, d_ctx0 = first
    sums_zero = [None, g_a + g_b, None, up_a + up_b]
    out_far = [exchange_far(near, hold) for near in out_near]
    tick(first, got_core, got_x, out_far)
    core_narrow = got_core
    got_x.append(x_swap(add_wide(hold(keep_one[1, :2]), core_one[1, :2])))
    keep_broad, send = run_weight_grad([[hold(ln_m0)], [g1_a, g1_b]], [d_up0, act0])
    tick(keep_broad, got_x)

    def late_blocks(keep, core, got):
        late = add_three(hold(keep[0, 2:]), core[0, 2:], got)
        return [late[0], late[1]]

    def early_blocks(keep, core, got):
        early = add_three(hold(keep[0, :2]), core[0, :2], got)
        return [early[0], early[1]]

    got_core = core_swap(send)
    late = late_blocks(keep_one, core_one, got_x[0])
    broad_got = ring_first([None, None, *late], hold)
    got_narrow = x_swap(add_wide(hold(keep_narrow[1]), core_narrow[1]))
    d_qkv0, sums_zero[2] = run_attend_back(qkv0, hold(d_ctx0), lse0, tables)
    tick(d_qkv0, broad_got, got_core, got_narrow)
    broad_one_sum = early_blocks(keep_one, core_one, got_x[1]) + late
    narrow_sum = add_three(hold(keep_narrow[0]), core_narrow[0], got_narrow)
    narrow_sum = [narrow_sum[k] for k in range(4)]
    keep_zero, core_zero = hold(keep_broad), got_core
    got_x = [x_swap(add_wide(keep_zero[1, 2:], core_zero[1, 2:]))]
    broad_got = ring_second(broad_one_sum, broad_got, hold)
    part_a, sum_a = run_norm_back(
        (acts, 0), hold(d_qkv0), d_up0, all_vecs[0], narrow_zero, broad_zero, 0, chunk
    )
    tick(part_a)
    got_a = y_swap(part_a)
    part_b, sum_b = run_norm_back(
        (acts, chunk), hold(d_qkv0), d_up0, all_vecs[0], narrow_zero, broad_zero, chunk, chunk
    )
    sums_zero[0] = (sum_a + sum_b)[:4]
    tick(part_b, got_x, broad_got)
    got_b = y_swap(part_b)
    got_x.append(x_swap(add_wide(hold(keep_zero[1, :2]), core_zero[1, :2])))
    narrow_got = ring_first(narrow_sum, hold)
    keep_narrow, send_narrow = run_weight_grad([[hold(ln_a0)], [g1_a, g1_b]], [d_qkv0, ctx0])
    tick(keep_narrow, got_a, got_b, got_x, narrow_got)

    flat = []
    for norm_sums, sum_g, sum_qkv, sum_up in hold((sums_zero, sums_one)):
        feature = relative(jnp.concatenate([norm_sums, sum_g], axis=0), across)
        q_sum = sum_qkv.reshape(4, 3, 2, 64).transpose(0, 2, 1, 3).reshape(4, -1)
        both = jnp.concatenate([q_sum, sum_up.reshape(4, -1)], axis=1)
        both = jnp.stack([pick(both, order[k]) for k in range(4)])
        flat.append(jnp.concatenate([feature.reshape(-1), both.reshape(-1)]))
    flat = jnp.stack(flat)
    got_core = core_swap(send_narrow)
    late = late_blocks(keep_zero, core_zero, got_x[0])
    broad_next = ring_first([None, None, *late], hold)
    grads_low = jnp.concatenate(
        [lower(g1_a, hold(part_a), got_a), lower(g1_b, hold(part_b), got_b)], axis=0
    )
    g1 = jnp.concatenate([g1_a, g1_b], axis=0)
    grad_blocks = to_blocks(jnp.where(first_section, grads_low, g1))
    flat = flat + swap(flat, "dp", 1)
    tick(broad_next, got_core, grad_blocks, flat)
    broad_zero_sum = early_blocks(keep_zero, core_zero, got_x[1]) + late
    broad_next = ring_second(broad_zero_sum, broad_next, hold)
    narrow_got = ring_second(narrow_sum, narrow_got, hold)
    got_narrow = x_swap(add_wide(hold(keep_narrow[1]), got_core[1]))
    flat = flat + x_swap(flat)
    acts_local = [
        exchanged(part, near, far, along)
        for part, near, far in zip(hold(out_parts), out_near, out_far)
    ]
    acts_local = jnp.concatenate(acts_local, axis=-1)
    tick(broad_next, got_narrow, flat, narrow_got, acts_local)
    zero_sum = add_three(hold(keep_narrow[0]), got_core[0], got_narrow)
    zero_sum = [zero_sum[k] for k in range(4)]
    narrow_next = ring_first(zero_sum, hold)
    flat = flat + swap(hold(flat), "tensor", 1)
    tick(narrow_next, flat)
    grad_near = exchange_near(grad_blocks, along, hold)
    narrow_next = ring_second(zero_sum, narrow_next, hold)
    one_broad = ring_total(hold(broad_one_sum[0]), broad_got)
    one_narrow = ring_total(hold(narrow_sum[0]), narrow_got)
    zero_broad = ring_total(hold(broad_zero_sum[0]), broad_next)
    broad_send = y_swap(jnp.where(first_section, one_broad, zero_broad))
    tick(narrow_next, grad_near, broad_send)
    grad_far = exchange_far(grad_near, hold)
    zero_narrow = ring_total(zero_sum[0], narrow_next)
    narrow_send = y_swap(jnp.where(first_section, one_narrow, zero_narrow))
    flat = flat + swap(hold(flat), "tensor", 2)
    grad_local = exchanged(grad_blocks, grad_near, grad_far, along)

    def whole_layer(keep_pair, got):
        keep = jnp.where(first_section, *keep_pair).astype(jnp.float32)
        got = got.astype(jnp.float32)
        return jnp.where(first_section, jnp.stack([keep, got], 1), jnp.stack([got, keep], 1))

    narrow_out = whole_layer((zero_narrow, one_narrow), narrow_send)
    broad_out = whole_layer((zero_broad, one_broad), broad_send)
    grad_qkv = narrow_out[..., :n_qkv].reshape(rows, 2, 3, 2, 64)
    grad_qkv = grad_qkv.transpose(0, 1, 3, 2, 4).reshape(rows, -1)
    grad_out = narrow_out[..., n_qkv:].reshape(rows, -1).T
    grad_up = broad_out[..., :n_up].reshape(rows, -1)
    grad_down = broad_out[..., n_up:].reshape(rows, -1).T

    keep = pick(flat, section)
    mine = pick(flat, 1 - section)
    got = swap(mine, "section", 1)
    n_feature = 5 * width
    feature_own = keep[:n_feature].reshape(5, width)
    feature = feature_own[:4] + got[: 4 * width].reshape(4, width)
    place_at = (across * 4 + along) * share
    gain_share = lax.dynamic_slice_in_dim(feature[:2], place_at, share, 1)
    shifts = jnp.concatenate([feature[2:4], feature_own[4:5], feature_own[4:5]], axis=0)
    bias_share = lax.dynamic_slice_in_dim(shifts, place_at, share, 1)
    low_half = jnp.where(first_section, keep, got)[n_feature:].reshape(4, -1)
    high_half = jnp.where(first_section, got, keep)[n_feature:].reshape(4, -1)
    halves = jnp.stack([pick(low_half, along), pick(high_half, along)])
    n_head = (heads // 2) * 192
    head_sums = halves[:, :n_head].reshape(heads, 192)
    head_share = lax.dynamic_slice_in_dim(head_sums, across * share_q, share_q, 1)
    unit_sums = halves[:, n_head:].reshape(bias_rows, 4 * share_u)
    unit_share = lax.dynamic_slice_in_dim(unit_sums, across * share_u, share_u, 1)
    return (
        acts_local[None, :, :, None],
        grad_local[None, :, :, None],
        gain_share[None],
        bias_share[None],
        grad_qkv[None],
        head_share[None],
        grad_out[None],
        grad_up[None],
        unit_share[None],
        grad_down[None],
    )


def fits(mesh, args):
    acts_in, b_qkv = args[0], args[5]
    sizes = dict(mesh.shape)
    return (
        sizes["section"] == 2
        and sizes["dp"] == 4
        and sizes["tensor"] == MICRO
        and MICRO == 4
        and acts_in.shape[2] == sizes["dp"]
        and b_qkv.shape[1] == 16
        and b_qkv.shape[2] == 192
        and acts_in.shape[1] % (CHUNKS * ROW_BLOCK) == 0
    )


def solution(mesh):
    placed = (
        P(None, "tensor", "dp", None),
        P(None, "tensor", "dp", None),
        P("section", None, ("dp", "tensor")),
        P("section", None, ("dp", "tensor")),
        P("section", "dp", "tensor"),
        P("section", "tensor", "dp"),
        P("section", "tensor", "dp"),
        P("section", "dp", "tensor"),
        P("section", "tensor", "dp"),
        P("section", "tensor", "dp"),
    )
    def wrap(body):
        return jax.shard_map(
            body,
            mesh=mesh,
            in_specs=placed,
            out_specs=(
                P("section", None, "tensor", "dp", None),
                P("section", None, "tensor", "dp", None),
                P("section", None, ("dp", "tensor")),
                P("section", None, ("dp", "tensor")),
                P("section", "dp", "tensor"),
                P("section", "tensor", "dp"),
                P("section", "tensor", "dp"),
                P("section", "dp", "tensor"),
                P("section", "tensor", "dp"),
                P("section", "tensor", "dp"),
            ),
            check_vma=False,
        )

    return lambda *args: wrap(by_sequence if fits(mesh, args) else local)(*args)
```
